32 devices in a mesh: batch: 2 (over y), seq: 4 (over x, core), kv: 4 (over z).
Axes of the slice: x: 2, y: 2, z: 4, core: 2. Of those that a mesh axis runs over, the one named last changes fastest.
Arguments:
- tokens: bfloat16 [4, 2048, 1536], P('batch', ('seq', 'kv')), may hold values from -6 to 6
- cotangent: bfloat16 [4, 2048, 1536], P('batch', ('seq', 'kv')), may hold values from -6 to 6
- segments: int32 [4, 2048], P('batch', 'seq'), may hold values from 0 to 2, as said below
- positions: int32 [4, 2048], P('batch', 'seq'), may hold values from 0 to 1535, as said below
- norm_in: float32 [1, 1536], P(None, ('batch', 'seq', 'kv')), may hold values from 0.5 to 1.5
- w_query: bfloat16 [1, 1536, 1536], P(None, ('batch', 'seq'), 'kv'), may hold values from -0.15625 to 0.15625
- w_key: bfloat16 [1, 1536, 768], P(None, ('batch', 'seq'), 'kv'), may hold values from -0.15625 to 0.15625
- w_value: bfloat16 [1, 1536, 768], P(None, ('batch', 'seq'), 'kv'), may hold values from -0.15625 to 0.15625
- w_out: bfloat16 [1, 1536, 1536], P(None, 'kv', ('batch', 'seq')), may hold values from -0.75 to 0.75
- norm_mid: float32 [1, 1536], P(None, ('batch', 'seq', 'kv')), may hold values from 0.5 to 1.5
- w_gate: bfloat16 [1, 1536, 4096], P(None, ('batch', 'seq'), 'kv'), may hold values from -0.15625 to 0.15625
- w_up: bfloat16 [1, 1536, 4096], P(None, ('batch', 'seq'), 'kv'), may hold values from -0.15625 to 0.15625
- w_down: bfloat16 [1, 4096, 1536], P(None, 'kv', ('batch', 'seq')), may hold values from -0.09375 to 0.09375
Outputs:
- out: float32 [4, 2048, 1536], P('batch', ('seq', 'kv'))
- grad_tokens: float32 [4, 2048, 1536], P('batch', ('seq', 'kv'))
- grad_norm_in: float32 [1, 1536], P(None, ('batch', 'seq', 'kv'))
- grad_w_query: float32 [1, 1536, 1536], P(None, ('batch', 'seq'), 'kv')
- grad_w_key: float32 [1, 1536, 768], P(None, ('batch', 'seq'), 'kv')
- grad_w_value: float32 [1, 1536, 768], P(None, ('batch', 'seq'), 'kv')
- grad_w_out: float32 [1, 1536, 1536], P(None, 'kv', ('batch', 'seq'))
- grad_norm_mid: float32 [1, 1536], P(None, ('batch', 'seq', 'kv'))
- grad_w_gate: float32 [1, 1536, 4096], P(None, ('batch', 'seq'), 'kv')
- grad_w_up: float32 [1, 1536, 4096], P(None, ('batch', 'seq'), 'kv')
- grad_w_down: float32 [1, 4096, 1536], P(None, 'kv', ('batch', 'seq'))
The draws below stay inside these ranges and needn't reach their ends.
Inputs may be any that keep to these rules, and one draw needn't show every extreme that they name: `segments`: each row holds three documents with ids 0, 1, 2 in order; document 1 begins within the first 256 tokens of the row and is exactly 1536 tokens long, so document 2 begins within its last quarter. `positions`: the place of a token in its document, counted from 0.
All inputs are finite; a program needn't handle non-finite values.
Results may differ from the reference program's by a relative error of at most 0.02.
Values may be sent and summed in bfloat16 or wider, within the bound.
No kernel may reach another device: no remote copies, remote signals or barrier semaphores. Data moves between devices by JAX's collectives and lax.ppermute only.
A program may use at most 128 MiB of HBM per device.

```python
import jax
import jax.numpy as jnp
from jax import lax

D = 1536
HQ = 16
KVH = 8
HD = 96
FF = 4096
LAYERS = 1
ROWS = 4
L = 2048


def doc_starts(key):
    doc_key = jax.random.fold_in(key, 11)
    start_one = jax.random.randint(doc_key, (ROWS,), 1, max(L // 8, 2), dtype=jnp.int32)
    start_two = start_one + 3 * L // 4
    return (start_one, start_two)


def draw_segments(key, part):
    start_one, start_two = doc_starts(key)
    places = jnp.arange(L, dtype=jnp.int32)[None, :]
    return (places >= start_one[:, None]).astype(jnp.int32) + (places >= start_two[:, None]).astype(jnp.int32)


def draw_positions(key, part):
    start_one, start_two = doc_starts(key)
    places = jnp.arange(L, dtype=jnp.int32)[None, :]
    begins = jnp.where(places >= start_two[:, None], start_two[:, None], jnp.where(places >= start_one[:, None], start_one[:, None], 0))
    return (places - begins).astype(jnp.int32)


def levels(own_key, extent, split, low, largest):
    def one(dim, shards_of):
        draws = jax.random.uniform(jax.random.fold_in(jax.random.fold_in(own_key, 6), dim), (shards_of,), jnp.float32, low / len(split), largest / len(split))
        return jnp.repeat(jnp.exp(draws), extent[dim] // shards_of).reshape((-1,) + (1,) * (len(extent) - dim - 1))

    loudness = one(*split[0])
    for cut in split[1:]:
        loudness = loudness * one(*cut)
    return loudness


def scatter_about(own_key, shape, scale, limit, shards=(), kind=jnp.bfloat16):
    factor_of = levels(own_key, shape, shards, -0.22, 0.18) if shards else 1.0
    values = jax.random.normal(own_key, shape, jnp.float32) * scale * factor_of
    return jnp.minimum(jnp.maximum(values, -limit), limit).astype(kind)


def setup_inputs(seed: int = 0) -> dict:
    key_list = jax.random.split(jax.random.key(seed), 14)
    tokens = scatter_about(key_list[0], (ROWS, L, D), 1.0, 6.0, ((0, 2), (1, 16)))
    cotangent = scatter_about(key_list[1], (ROWS, L, D), 1.0, 6.0, ((0, 2), (1, 16)))
    segments = draw_segments(jax.random.fold_in(key_list[13], 71), 0)
    positions = draw_positions(jax.random.fold_in(key_list[13], 71), 0)
    norm_in = jnp.clip(1.0 + 0.1 * jax.random.normal(key_list[4], (LAYERS, D), jnp.float32), 0.5, 1.5)
    w_query = scatter_about(key_list[5], (LAYERS, D, HQ * HD), D ** -0.5, 0.15625, ((1, 8), (2, 4)))
    w_key = scatter_about(key_list[6], (LAYERS, D, KVH * HD), D ** -0.5, 0.15625, ((1, 8), (2, 4)))
    w_value = scatter_about(key_list[7], (LAYERS, D, KVH * HD), D ** -0.5, 0.15625, ((1, 8), (2, 4)))
    w_out = scatter_about(key_list[8], (LAYERS, HQ * HD, D), 64 ** -0.5, 0.75, ((1, 4), (2, 8)))
    norm_mid = jnp.clip(1.0 + 0.1 * jax.random.normal(key_list[9], (LAYERS, D), jnp.float32), 0.5, 1.5)
    w_gate = scatter_about(key_list[10], (LAYERS, D, FF), D ** -0.5, 0.15625, ((1, 8), (2, 4)))
    w_up = scatter_about(key_list[11], (LAYERS, D, FF), D ** -0.5, 0.15625, ((1, 8), (2, 4)))
    w_down = scatter_about(key_list[12], (LAYERS, FF, D), FF ** -0.5, 0.09375, ((1, 4), (2, 8)))
    return dict(tokens=tokens, cotangent=cotangent, segments=segments, positions=positions, norm_in=norm_in, w_query=w_query, w_key=w_key, w_value=w_value, w_out=w_out, norm_mid=norm_mid, w_gate=w_gate, w_up=w_up, w_down=w_down)


EPS = 1e-05
THETA = 100000.0
BIG_NEG = -1e+30
HIGH = lax.Precision.HIGHEST

@jax.custom_vjp
def low(v):
    return lax.optimization_barrier(v.astype(jnp.bfloat16)).astype(jnp.float32)

@jax.custom_vjp
def low_back(v):
    return v

def low_keep(v):
    return (low(v), None)

def low_pass(kept, grad):
    return (grad,)

def back_keep(v):
    return (v, None)

def back_low(kept, grad):
    return (low(grad),)
low.defvjp(low_keep, low_pass)
low_back.defvjp(back_keep, back_low)

def rotary(positions_row):
    half_width = HD // 2
    frequency = THETA ** (-(2.0 * jnp.arange(half_width, dtype=jnp.float32)) / HD)
    angles = positions_row.astype(jnp.float32)[:, None] * frequency[None, :]
    cosine = jnp.concatenate([jnp.cos(angles), jnp.cos(angles)], axis=1)
    sine_table = jnp.concatenate([jnp.sin(angles), jnp.sin(angles)], axis=1)
    return (cosine, sine_table)

def rotate(head_vals, cosine, sine_table):
    half_width = head_vals.shape[-1] // 2
    swapped = jnp.concatenate([-head_vals[..., half_width:], head_vals[..., :half_width]], axis=-1)
    return head_vals * cosine[:, None, :] + swapped * sine_table[:, None, :]

def rms_scale(stream, gain):
    return stream * lax.rsqrt(lax.optimization_barrier(jnp.mean(stream * stream, axis=-1, keepdims=True)) + EPS) * gain

def matmul(left_side, right_side):
    return jnp.dot(left_side, right_side, precision=HIGH, preferred_element_type=jnp.float32)

def attend_row(row_args):
    queries, keys_row, values_row, seg_row = row_args
    length = queries.shape[0]
    block_len = min(512, length)
    group_size = HQ // KVH
    score_scale = HD ** (-0.5)
    query_blocks = queries.reshape(length // block_len, block_len, KVH, group_size, HD)
    seg_blocks = seg_row.reshape(length // block_len, block_len)
    index_blocks = jnp.arange(length, dtype=jnp.int32).reshape(length // block_len, block_len)
    key_index = jnp.arange(length, dtype=jnp.int32)

    def one_block(block_args):
        query_block, seg_block, index_block = block_args
        scores = jnp.einsum('qkgd,pkd->kgqp', query_block, keys_row, precision=HIGH) * score_scale
        scores = low_back(scores)
        allowed = (seg_block[:, None] == seg_row[None, :]) & (key_index[None, :] <= index_block[:, None])
        scores = jnp.where(allowed, scores, BIG_NEG)
        row_max = lax.optimization_barrier(jnp.max(scores, axis=-1, keepdims=True))
        weights = jnp.where(allowed, jnp.exp(scores - row_max), 0.0)
        probs = low(weights / lax.optimization_barrier(jnp.sum(weights, axis=-1, keepdims=True)))
        return jnp.einsum('kgqp,pkd->qkgd', probs, values_row, precision=HIGH)
    attended = lax.map(jax.checkpoint(one_block), (query_blocks, seg_blocks, index_blocks))
    return attended.reshape(length, HQ * HD)

def apply_layer(stream, params, cosine, sine_table, segments):
    norm_in, w_query, w_key, w_value, w_out, norm_mid, w_gate, w_up, w_down = params
    row_count, length, width = stream.shape
    flat = stream.reshape(row_count * length, width)
    normed = low(rms_scale(flat, norm_in))
    queries = low_back(matmul(normed, w_query)).reshape(row_count, length, HQ, HD)
    keys_all = low_back(matmul(normed, w_key)).reshape(row_count, length, KVH, HD)
    values_all = low(low_back(matmul(normed, w_value))).reshape(row_count, length, KVH, HD)
    queries = low(jax.vmap(rotate)(queries, cosine, sine_table))
    keys_all = low(jax.vmap(rotate)(keys_all, cosine, sine_table))
    queries = queries.reshape(row_count, length, KVH, HQ // KVH, HD)
    attended = lax.map(attend_row, (queries, keys_all, values_all, segments))
    attended = low(low_back(attended.reshape(row_count * length, HQ * HD)))
    middle = flat + low_back(matmul(attended, w_out))
    normed_mid = low(rms_scale(middle, norm_mid))
    gate_val = low_back(matmul(normed_mid, w_gate))
    up_val = low_back(matmul(normed_mid, w_up))
    hidden = low(jax.nn.silu(gate_val) * up_val)
    result = middle + low_back(matmul(hidden, w_down))
    return result.reshape(row_count, length, width)

def reference(tokens, cotangent, segments, positions, norm_in, w_query, w_key, w_value, w_out, norm_mid, w_gate, w_up, w_down):
    cosine, sine_table = jax.vmap(rotary)(positions)
    params = tuple((weight.astype(jnp.float32) for weight in (norm_in, w_query, w_key, w_value, w_out, norm_mid, w_gate, w_up, w_down)))

    def forward(stream, weight_set):
        for layer_index in range(LAYERS):
            stream = apply_layer(stream, tuple((weight[layer_index] for weight in weight_set)), cosine, sine_table, segments)
        return stream
    result, pullback = jax.vjp(forward, tokens.astype(jnp.float32), params)
    grad_input, grad_parts = pullback(cotangent.astype(jnp.float32))
    return (result, grad_input, grad_parts[0], grad_parts[1], grad_parts[2], grad_parts[3], grad_parts[4], grad_parts[5], grad_parts[6], grad_parts[7], grad_parts[8])
```

```python
import functools
import math
from functools import partial

import jax
import jax.numpy as jnp
from jax import lax
from jax.experimental import pallas as pl
from jax.experimental.pallas import tpu as pltpu
from jax.sharding import Mesh
from jax.sharding import PartitionSpec as P

HD = 96
LAYERS = 1


EPS = 1e-05
THETA = 100000.0
BIG_NEG = -1e30


def rotary(positions_row):
    half_width = HD // 2
    frequency = THETA ** (-(2.0 * jnp.arange(half_width, dtype=jnp.float32)) / HD)
    angles = positions_row.astype(jnp.float32)[:, None] * frequency[None, :]
    cosine = jnp.concatenate([jnp.cos(angles), jnp.cos(angles)], axis=1)
    sine_table = jnp.concatenate([jnp.sin(angles), jnp.sin(angles)], axis=1)
    return (cosine, sine_table)


def rotate(head_vals, cosine, sine_table):
    half_width = head_vals.shape[-1] // 2
    swapped = jnp.concatenate([-head_vals[..., half_width:], head_vals[..., :half_width]], axis=-1)
    return head_vals * cosine[:, None, :] + swapped * sine_table[:, None, :]


def rms_norm(stream, gain):
    factor = lax.rsqrt(jnp.mean(stream * stream, axis=-1, keepdims=True) + EPS)
    return (stream * factor * gain, factor)


def norm_back(stream, factor, gain, upstream):
    scaled_grad = upstream * gain
    inner_mean = jnp.mean(scaled_grad * stream, axis=-1, keepdims=True)
    grad_stream = factor * scaled_grad - stream * factor**3 * inner_mean
    return (grad_stream, jnp.sum(upstream * stream * factor, axis=0))


def key_width(key_count):
    return math.gcd(key_count, 1024)


def contract(left_side, right_side, left_dim, right_dim):
    return lax.dot_general(
        left_side,
        right_side,
        (((left_dim,), (right_dim,)), ((), ())),
        preferred_element_type=jnp.float32,
    )


def spread(shard_rows):
    return lax.all_gather(shard_rows, "kv", axis=0, tiled=True)


def token_sum(pairs):
    summed = None
    for left_part, right_part, right_dim in pairs:
        product = contract(left_part, right_part, 1, right_dim)
        summed = product if summed is None else summed + product
    return lax.psum_scatter(
        summed.astype(jnp.bfloat16), "kv", scatter_dimension=0, tiled=True
    ).astype(jnp.float32)


def split_block(kv_both, seg_keys, offset, step_width, kv_local, head_size):
    kv_block = lax.dynamic_slice_in_dim(kv_both, offset, step_width, 0)
    key_block = kv_block[:, : kv_local * head_size].reshape(step_width, kv_local, head_size)
    value_block = kv_block[:, kv_local * head_size :].reshape(step_width, kv_local, head_size)
    seg_block = lax.dynamic_slice_in_dim(seg_keys, offset, step_width, 0)
    return (key_block, value_block, seg_block)


def forward_row(queries, seg_query, fold_state, kv_both, seg_keys, first_query, key_start):
    key_count = kv_both.shape[0]
    step_width = key_width(key_count)
    query_count, kv_local, group_size, head_size = queries.shape
    query_index = first_query + jnp.arange(query_count, dtype=jnp.int32)
    score_scale = head_size ** (-0.5)

    def forward_one_step(step_index, inner_state):
        running_max, weight_total, value_total = inner_state
        offset = step_index * step_width
        key_block, value_block, seg_block = split_block(
            kv_both, seg_keys, offset, step_width, kv_local, head_size
        )
        key_index = offset + jnp.arange(step_width, dtype=jnp.int32)
        allowed = (seg_query[:, None] == seg_block[None, :]) & (
            key_index[None, :] <= query_index[:, None]
        )
        scores = (
            jnp.einsum("qkgd,pkd->kgqp", queries, key_block, preferred_element_type=jnp.float32)
            * score_scale
        )
        scores = jnp.where(allowed, scores, BIG_NEG)
        new_max = jnp.maximum(running_max, jnp.max(scores, axis=-1))
        weights = jnp.where(allowed, jnp.exp(scores - new_max[..., None]), 0.0)
        rescale = jnp.exp(running_max - new_max)
        weight_total = rescale * weight_total + jnp.sum(weights, axis=-1)
        update = jnp.einsum(
            "kgqp,pkd->qkgd",
            weights.astype(jnp.bfloat16),
            value_block,
            preferred_element_type=jnp.float32,
        )
        value_total = jnp.transpose(rescale, (2, 0, 1))[..., None] * value_total + update
        return (new_max, weight_total, value_total)

    return lax.fori_loop(0, key_count // step_width, forward_one_step, fold_state)


def forward_fold(queries, seg_query, first_query, fold_state, pieces, key_start):
    kv_both, seg_keys = pieces
    row_fn = partial(forward_row, first_query=first_query, key_start=key_start)
    return jax.vmap(row_fn, in_axes=(0, 0, 0, 1, 1))(
        queries, seg_query, fold_state, kv_both, seg_keys
    )


def backward_row(
    queries,
    grad_attn,
    log_total,
    row_delta,
    seg_query,
    fold_state,
    kv_both,
    seg_keys,
    first_query,
    key_start,
):
    key_count = kv_both.shape[0]
    step_width = key_width(key_count)
    query_count, kv_local, group_size, head_size = queries.shape
    query_index = first_query + jnp.arange(query_count, dtype=jnp.int32)
    score_scale = head_size ** (-0.5)

    def backward_one_step(step_index, inner_state):
        grad_queries, grad_buffer = inner_state
        offset = step_index * step_width
        key_block, value_block, seg_block = split_block(
            kv_both, seg_keys, offset, step_width, kv_local, head_size
        )
        key_index = offset + jnp.arange(step_width, dtype=jnp.int32)
        allowed = (seg_query[:, None] == seg_block[None, :]) & (
            key_index[None, :] <= query_index[:, None]
        )
        scores = (
            jnp.einsum("qkgd,pkd->kgqp", queries, key_block, preferred_element_type=jnp.float32)
            * score_scale
        )
        probs_block = jnp.where(allowed, jnp.exp(scores - log_total[..., None]), 0.0)
        grad_probs = jnp.einsum(
            "qkgd,pkd->kgqp", grad_attn, value_block, preferred_element_type=jnp.float32
        )
        grad_scores = (probs_block * (grad_probs - row_delta[..., None])).astype(jnp.bfloat16)
        grad_queries = (
            grad_queries
            + jnp.einsum(
                "kgqp,pkd->qkgd", grad_scores, key_block, preferred_element_type=jnp.float32
            )
            * score_scale
        )
        grad_keys = (
            jnp.einsum("kgqp,qkgd->pkd", grad_scores, queries, preferred_element_type=jnp.float32)
            * score_scale
        )
        grad_values = jnp.einsum(
            "kgqp,qkgd->pkd",
            probs_block.astype(jnp.bfloat16),
            grad_attn,
            preferred_element_type=jnp.float32,
        )
        joined = jnp.concatenate(
            [grad_keys.reshape(step_width, -1), grad_values.reshape(step_width, -1)], axis=1
        )
        grad_buffer = lax.dynamic_update_slice_in_dim(grad_buffer, joined, offset, 0)
        return (grad_queries, grad_buffer)

    return lax.fori_loop(0, key_count // step_width, backward_one_step, fold_state)


def backward_fold(
    queries, grad_attn, log_total, row_delta, seg_query, first_query, fold_state, pieces, key_start
):
    kv_both, seg_keys = pieces
    row_fn = partial(backward_row, first_query=first_query, key_start=key_start)
    return jax.vmap(row_fn, in_axes=(0, 0, 0, 0, 0, 0, 1, 1))(
        queries, grad_attn, log_total, row_delta, seg_query, fold_state, kv_both, seg_keys
    )


def layer_forward(stream, gain_pair, matrices, seg_info, tables):
    gain_in, gain_mid = gain_pair
    w_query, w_key, w_value, w_out, w_gate, w_up, w_down = matrices
    seg_query, seg_keys = seg_info
    cosine, sine_table = tables
    row_count = seg_query.shape[0]
    kv_local = w_key.shape[1] // HD
    head_local = w_query.shape[1] // HD
    group_size = head_local // kv_local
    normed_a, factor_a = rms_norm(stream, gain_in)
    spread_a = spread(normed_a.astype(jnp.bfloat16))
    flat_count = spread_a.shape[0]
    token_count = flat_count // row_count
    raw_queries = jnp.dot(spread_a, w_query, preferred_element_type=jnp.float32).reshape(
        flat_count, head_local, HD
    )
    queries = (
        rotate(raw_queries, cosine, sine_table)
        .astype(jnp.bfloat16)
        .reshape(token_count, row_count, kv_local, group_size, HD)
    )
    queries = jnp.transpose(queries, (1, 0, 2, 3, 4))
    raw_keys = jnp.dot(spread_a, w_key, preferred_element_type=jnp.float32).reshape(
        flat_count, kv_local, HD
    )
    keys_low = (
        rotate(raw_keys, cosine, sine_table).astype(jnp.bfloat16).reshape(flat_count, kv_local * HD)
    )
    values_low = jnp.dot(spread_a, w_value, preferred_element_type=jnp.float32).astype(jnp.bfloat16)
    kv_both = jnp.concatenate([keys_low, values_low], axis=1).reshape(
        token_count, row_count, 2 * kv_local * HD
    )
    first_query = lax.axis_index("seq") * token_count
    start_state = (
        jnp.full((row_count, kv_local, group_size, token_count), BIG_NEG, jnp.float32),
        jnp.zeros((row_count, kv_local, group_size, token_count), jnp.float32),
        jnp.zeros((row_count, token_count, kv_local, group_size, HD), jnp.float32),
    )
    running_max, weight_total, value_total = forward_fold(
        queries,
        seg_query,
        first_query,
        start_state,
        (
            lax.all_gather(kv_both, "seq", axis=0, tiled=True),
            lax.all_gather(seg_keys, "seq", axis=0, tiled=True),
        ),
        jnp.int32(0),
    )
    attn_float = value_total / jnp.transpose(weight_total, (0, 3, 1, 2))[..., None]
    log_total = running_max + jnp.log(weight_total)
    attn_low = (
        jnp.transpose(attn_float, (1, 0, 2, 3, 4))
        .reshape(flat_count, head_local * HD)
        .astype(jnp.bfloat16)
    )
    stream_mid = stream + token_sum(((attn_low, w_out, 0),))
    normed_b, factor_b = rms_norm(stream_mid, gain_mid)
    spread_b = spread(normed_b.astype(jnp.bfloat16))
    gate_val = jnp.dot(spread_b, w_gate, preferred_element_type=jnp.float32)
    up_val = jnp.dot(spread_b, w_up, preferred_element_type=jnp.float32)
    hidden = (jax.nn.silu(gate_val) * up_val).astype(jnp.bfloat16)
    stream_out = stream_mid + token_sum(((hidden, w_down, 0),))
    saved_state = (
        stream,
        factor_a,
        spread_a,
        queries,
        kv_both,
        attn_float,
        attn_low,
        log_total,
        stream_mid,
        factor_b,
        spread_b,
        gate_val,
        up_val,
        hidden,
    )
    return (stream_out, saved_state)


def layer_backward(saved_state, grad_stream, gain_pair, matrices, seg_info, tables):
    (
        stream,
        factor_a,
        spread_a,
        queries,
        kv_both,
        attn_float,
        attn_low,
        log_total,
        stream_mid,
        factor_b,
        spread_b,
        gate_val,
        up_val,
        hidden,
    ) = saved_state
    gain_in, gain_mid = gain_pair
    w_query, w_key, w_value, w_out, w_gate, w_up, w_down = matrices
    seg_query, seg_keys = seg_info
    cosine, sine_table = tables
    row_count, token_count, kv_local, group_size, head_size = queries.shape
    head_local = kv_local * group_size
    flat_count = row_count * token_count
    grad_low = spread(grad_stream.astype(jnp.bfloat16))
    grad_down_w = contract(hidden, grad_low, 0, 0)
    grad_hidden = contract(grad_low, w_down, 1, 1)
    sigmoid_gate = jax.nn.sigmoid(gate_val)
    silu_gate = gate_val * sigmoid_gate
    grad_gate_low = (
        grad_hidden * up_val * sigmoid_gate * (1.0 + gate_val * (1.0 - sigmoid_gate))
    ).astype(jnp.bfloat16)
    grad_up_low = (grad_hidden * silu_gate).astype(jnp.bfloat16)
    grad_gate_w = contract(spread_b, grad_gate_low, 0, 0)
    grad_up_w = contract(spread_b, grad_up_low, 0, 0)
    grad_normed_b = token_sum(((grad_gate_low, w_gate, 1), (grad_up_low, w_up, 1)))
    back_mid, grad_gain_mid = norm_back(stream_mid, factor_b, gain_mid, grad_normed_b)
    grad_mid = grad_stream + back_mid
    grad_attn_full = spread(grad_mid.astype(jnp.bfloat16))
    grad_out_w = contract(attn_low, grad_attn_full, 0, 0)
    grad_attn = (
        contract(grad_attn_full, w_out, 1, 1)
        .astype(jnp.bfloat16)
        .reshape(token_count, row_count, kv_local, group_size, head_size)
    )
    grad_attn = jnp.transpose(grad_attn, (1, 0, 2, 3, 4))
    row_delta = jnp.transpose(jnp.sum(grad_attn * attn_float, axis=-1), (0, 2, 3, 1))
    first_query = lax.axis_index("seq") * token_count
    row_length = token_count * lax.axis_size("seq")
    start_state = (
        jnp.zeros((row_count, token_count, kv_local, group_size, head_size), jnp.float32),
        jnp.zeros((row_count, row_length, 2 * kv_local * head_size), jnp.float32),
    )
    grad_queries, grad_buffer = backward_fold(
        queries,
        grad_attn,
        log_total,
        row_delta,
        seg_query,
        first_query,
        start_state,
        (
            lax.all_gather(kv_both, "seq", axis=0, tiled=True),
            lax.all_gather(seg_keys, "seq", axis=0, tiled=True),
        ),
        jnp.int32(0),
    )
    grad_kv = lax.psum_scatter(
        grad_buffer.astype(jnp.bfloat16), "seq", scatter_dimension=1, tiled=True
    ).astype(jnp.float32)
    grad_kv = jnp.transpose(grad_kv, (1, 0, 2)).reshape(flat_count, 2 * kv_local * head_size)
    grad_queries = jnp.transpose(grad_queries, (1, 0, 2, 3, 4)).reshape(
        flat_count, head_local, head_size
    )
    grad_q_low = (
        rotate(grad_queries, cosine, -sine_table)
        .astype(jnp.bfloat16)
        .reshape(flat_count, head_local * head_size)
    )
    grad_k_low = (
        rotate(
            grad_kv[:, : kv_local * head_size].reshape(flat_count, kv_local, head_size),
            cosine,
            -sine_table,
        )
        .astype(jnp.bfloat16)
        .reshape(flat_count, kv_local * head_size)
    )
    grad_v_low = grad_kv[:, kv_local * head_size :].astype(jnp.bfloat16)
    grad_query_w = contract(spread_a, grad_q_low, 0, 0)
    grad_key_w = contract(spread_a, grad_k_low, 0, 0)
    grad_value_w = contract(spread_a, grad_v_low, 0, 0)
    grad_normed_a = token_sum(
        ((grad_q_low, w_query, 1), (grad_k_low, w_key, 1), (grad_v_low, w_value, 1))
    )
    back_in, grad_gain_in = norm_back(stream, factor_a, gain_in, grad_normed_a)
    grad_input = grad_mid + back_in
    weight_grads = (
        lax.psum_scatter(
            grad_query_w.astype(jnp.bfloat16), ("batch", "seq"), scatter_dimension=0, tiled=True
        ).astype(jnp.float32),
        lax.psum_scatter(
            grad_key_w.astype(jnp.bfloat16), ("batch", "seq"), scatter_dimension=0, tiled=True
        ).astype(jnp.float32),
        lax.psum_scatter(
            grad_value_w.astype(jnp.bfloat16), ("batch", "seq"), scatter_dimension=0, tiled=True
        ).astype(jnp.float32),
        lax.psum_scatter(
            grad_out_w.astype(jnp.bfloat16), ("batch", "seq"), scatter_dimension=1, tiled=True
        ).astype(jnp.float32),
        lax.psum_scatter(
            grad_gate_w.astype(jnp.bfloat16), ("batch", "seq"), scatter_dimension=0, tiled=True
        ).astype(jnp.float32),
        lax.psum_scatter(
            grad_up_w.astype(jnp.bfloat16), ("batch", "seq"), scatter_dimension=0, tiled=True
        ).astype(jnp.float32),
        lax.psum_scatter(
            grad_down_w.astype(jnp.bfloat16), ("batch", "seq"), scatter_dimension=1, tiled=True
        ).astype(jnp.float32),
    )
    return (grad_input, weight_grads, grad_gain_in, grad_gain_mid)


def to_flat(shard_rows):
    row_count, token_part, width = shard_rows.shape
    return jnp.transpose(shard_rows.astype(jnp.float32), (1, 0, 2)).reshape(
        token_part * row_count, width
    )


def from_flat(flat_rows, row_count):
    token_part = flat_rows.shape[0] // row_count
    return jnp.transpose(flat_rows.reshape(token_part, row_count, flat_rows.shape[1]), (1, 0, 2))


def general_local(
    tokens,
    cotangent,
    segments,
    positions,
    norm_in,
    w_query,
    w_key,
    w_value,
    w_out,
    norm_mid,
    w_gate,
    w_up,
    w_down,
):
    gains_in, gains_mid = (
        lax.all_gather(norm_in, ("batch", "seq", "kv"), axis=1, tiled=True),
        lax.all_gather(norm_mid, ("batch", "seq", "kv"), axis=1, tiled=True),
    )
    row_count = tokens.shape[0]
    seg_info = (segments, jnp.transpose(segments, (1, 0)))
    tables = rotary(jnp.transpose(positions, (1, 0)).reshape(-1))

    def fetch_layer(layer_index):
        return (
            lax.all_gather(w_query[layer_index], ("batch", "seq"), axis=0, tiled=True),
            lax.all_gather(w_key[layer_index], ("batch", "seq"), axis=0, tiled=True),
            lax.all_gather(w_value[layer_index], ("batch", "seq"), axis=0, tiled=True),
            lax.all_gather(w_out[layer_index], ("batch", "seq"), axis=1, tiled=True),
            lax.all_gather(w_gate[layer_index], ("batch", "seq"), axis=0, tiled=True),
            lax.all_gather(w_up[layer_index], ("batch", "seq"), axis=0, tiled=True),
            lax.all_gather(w_down[layer_index], ("batch", "seq"), axis=1, tiled=True),
        )

    stream = to_flat(tokens)
    fetched = []
    states = []
    layer_index = 0
    matrices = fetch_layer(layer_index)
    layer_inputs = [stream]
    stream, saved_state = layer_forward(
        stream, (gains_in[layer_index], gains_mid[layer_index]), matrices, seg_info, tables
    )
    fetched.append(matrices)
    states.append(saved_state)
    grad_stream = to_flat(cotangent)
    grads_in = []
    grads_mid = []
    weight_lists = []
    for layer_index in reversed(range(LAYERS)):
        gain_pair = (gains_in[layer_index], gains_mid[layer_index])
        matrices = fetch_layer(layer_index)
        saved_state = layer_forward(
            layer_inputs[layer_index], gain_pair, matrices, seg_info, tables
        )[1]
        grad_stream, weight_grads, grad_gain_in, grad_gain_mid = layer_backward(
            saved_state, grad_stream, gain_pair, matrices, seg_info, tables
        )
        grads_in.insert(0, grad_gain_in)
        grads_mid.insert(0, grad_gain_mid)
        weight_lists.insert(0, weight_grads)
    gain_grads_in, gain_grads_mid = (
        lax.psum_scatter(
            jnp.stack(grads_in), ("batch", "seq", "kv"), scatter_dimension=1, tiled=True
        ),
        lax.psum_scatter(
            jnp.stack(grads_mid), ("batch", "seq", "kv"), scatter_dimension=1, tiled=True
        ),
    )
    stacked_grads = [
        jnp.stack([grad_set[member] for grad_set in weight_lists]) for member in range(7)
    ]
    return (
        from_flat(stream, row_count),
        from_flat(grad_stream, row_count),
        gain_grads_in,
        stacked_grads[0],
        stacked_grads[1],
        stacked_grads[2],
        stacked_grads[3],
        gain_grads_mid,
        stacked_grads[4],
        stacked_grads[5],
        stacked_grads[6],
    )


def general_solution(mesh):
    in_specs = (
        P("batch", ("seq", "kv"), None),
        P("batch", ("seq", "kv"), None),
        P("batch", "seq"),
        P("batch", "seq"),
        P(None, ("batch", "seq", "kv")),
        P(None, ("batch", "seq"), "kv"),
        P(None, ("batch", "seq"), "kv"),
        P(None, ("batch", "seq"), "kv"),
        P(None, "kv", ("batch", "seq")),
        P(None, ("batch", "seq", "kv")),
        P(None, ("batch", "seq"), "kv"),
        P(None, ("batch", "seq"), "kv"),
        P(None, "kv", ("batch", "seq")),
    )
    out_specs = (
        P("batch", ("seq", "kv"), None),
        P("batch", ("seq", "kv"), None),
        P(None, ("batch", "seq", "kv")),
        P(None, ("batch", "seq"), "kv"),
        P(None, ("batch", "seq"), "kv"),
        P(None, ("batch", "seq"), "kv"),
        P(None, "kv", ("batch", "seq")),
        P(None, ("batch", "seq", "kv")),
        P(None, ("batch", "seq"), "kv"),
        P(None, ("batch", "seq"), "kv"),
        P(None, "kv", ("batch", "seq")),
    )
    return jax.shard_map(general_local, mesh=mesh, in_specs=in_specs, out_specs=out_specs, check_vma=False)


LN = 128
NEG=-1e30
C2 = (96 ** -0.5) * 1.4426950408889634

def lane_iota(rows):
    return lax.broadcasted_iota(jnp.int32, (rows, LN), 1)

def unpack4(t0, t1, t2):
    lane = lane_iota(t0.shape[0])
    live = lane < HD
    zero = jnp.zeros_like(t0)
    a = t0
    b = pltpu.roll(jnp.where(lane >= 96, t0, t1), 32, 1)
    c = pltpu.roll(jnp.where(lane >= 64, t1, t2), 64, 1)
    d = pltpu.roll(t2, 96, 1)
    return tuple(jnp.where(live, v, zero) for v in (a, b, c, d))

def pack4(a, b, c, d):
    lane = lane_iota(a.shape[0])
    b, c, d = pltpu.roll(b, 96, 1), pltpu.roll(c, 64, 1), pltpu.roll(d, 32, 1)
    return (jnp.where(lane < 96, a, b), jnp.where(lane < 64, b, c), jnp.where(lane < 32, c, d))

def split3(x):
    x = x.astype(jnp.float32)
    return x[:, :LN], x[:, LN:2*LN], x[:, 2*LN:]

def doc_low(index, first, length):
    second = first + 3 * length // 4
    return jnp.where(index >= second, second, jnp.where(index >= first, first, 0))

BQ = 256

def dotf(a, b, dims):
    return lax.dot_general(a, b, (dims, ((), ())), preferred_element_type=jnp.float32)

def attn_fwd_kernel(length, first_ref, x_ref, o_ref, of_ref, lse_ref, q_s, k_s, v_s, s_s):
    i = pl.program_id(0)
    blocks = length // BQ
    first = first_ref[0]
    @pl.when(i == 0)
    def _():
        def body(j, carry):
            rows = pl.ds(pl.multiple_of(j * BQ, BQ), BQ)
            q0, q1, k, v = unpack4(*split3(x_ref[rows, :]))
            q_s[j, :BQ, :] = q0.astype(jnp.bfloat16)
            q_s[j, BQ:, :] = q1.astype(jnp.bfloat16)
            k_s[j] = k.astype(jnp.bfloat16)
            v_s[j] = v.astype(jnp.bfloat16)
            return carry
        lax.fori_loop(0, blocks, body, 0)
    q = q_s[i]
    clean_from = (length // 8 + BQ - 1) // BQ
    clean_to = 3 * length // 4 // BQ
    late = (3 * length // 4 + length // 8) // BQ
    start = jnp.where(i >= late, 3 * length // 4 // BQ, 0)
    head_masked = jnp.where(i < clean_to, jnp.minimum(clean_from, i), i)
    q_index = i * BQ + lax.broadcasted_iota(jnp.int32, (BQ, 1), 0)
    low = doc_low(q_index, first, length)

    def halves(v, op):
        return op(v[:, :LN], v[:, LN:])

    def score(j, top, masked):
        s = dotf(q, k_s[j], ((1,), (1,)))
        if masked:
            key = j * BQ + lax.broadcasted_iota(jnp.int32, (1, BQ), 1)
            ok = (key <= q_index) & (key >= low)
            s = jnp.where(jnp.concatenate([ok, ok], axis=0), s, NEG)
        s_s[j] = s
        return jnp.maximum(top, halves(s, jnp.maximum))

    top = jnp.full((2 * BQ, LN), NEG, jnp.float32)
    top = lax.fori_loop(start, head_masked, lambda j, t: score(j, t, True), top)
    top = lax.fori_loop(jnp.maximum(head_masked, start), i, lambda j, t: score(j, t, False), top)
    top = score(i, top, True)
    m = jnp.max(top, axis=1, keepdims=True) * C2

    def add(j, state):
        total, acc = state
        p = jnp.exp2(s_s[j] * C2 - m)
        total = total + halves(p, jnp.add)
        acc = acc + dotf(p.astype(jnp.bfloat16), v_s[j], ((1,), (0,)))
        return total, acc

    zero = jnp.zeros((2 * BQ, LN), jnp.float32)
    total, acc = lax.fori_loop(start, i + 1, add, (zero, zero))
    total = jnp.sum(total, axis=1, keepdims=True)
    out = acc / total
    lse = jnp.broadcast_to(m + jnp.log2(total), (2 * BQ, LN))
    lse_ref[0] = jnp.transpose(lse, (1, 0))[:8, :]
    of_ref[0] = out
    for d in range(2):
        parts = []
        for h in range(2):
            parts.append(out[BQ*0 + d*128 + h*64: d*128 + h*64 + 64])
            parts.append(out[BQ + d*128 + h*64: BQ + d*128 + h*64 + 64])
        t = pack4(*parts)
        for n in range(3):
            o_ref[d, :, n*LN:(n+1)*LN] = t[n].astype(jnp.bfloat16)

def attn_fwd(first, x):
    length = x.shape[0]
    blocks = length // BQ
    return pl.pallas_call(
        functools.partial(attn_fwd_kernel, length),
        grid=(blocks,),
        in_specs=[pl.BlockSpec(memory_space=pltpu.SMEM),
                  pl.BlockSpec((length, 3*LN), lambda i: (0, 0))],
        out_specs=[pl.BlockSpec((2, 64, 3*LN), lambda i: (i, 0, 0)),
                   pl.BlockSpec((1, 2*BQ, LN), lambda i: (i, 0, 0)),
                   pl.BlockSpec((1, 8, 2*BQ), lambda i: (i, 0, 0))],
        out_shape=[jax.ShapeDtypeStruct((length//128, 64, 3*LN), jnp.bfloat16),
                   jax.ShapeDtypeStruct((blocks, 2*BQ, LN), jnp.float32),
                   jax.ShapeDtypeStruct((blocks, 8, 2*BQ), jnp.float32)],
        scratch_shapes=[pltpu.VMEM((blocks, 2*BQ, LN), jnp.bfloat16),
                        pltpu.VMEM((blocks, BQ, LN), jnp.bfloat16),
                        pltpu.VMEM((blocks, BQ, LN), jnp.bfloat16),
                        pltpu.VMEM((blocks, 2*BQ, BQ), jnp.float32)],
        compiler_params=pltpu.CompilerParams(vmem_limit_bytes=48 << 20),
        name="attend",
    )(first, x)

def attn_bwd_kernel(length, first_ref, x_ref, do_ref, of_ref, lse_ref, cos_ref, sin_ref, out_ref,
                    q_s, k_s, v_s, do_s, dl_s, dq_s, dk_s, dv_s):
    j = pl.program_id(0)
    blocks = length // BQ
    first = first_ref[0]
    @pl.when(j == 0)
    def _():
        def body(b, carry):
            rows = pl.ds(pl.multiple_of(b * BQ, BQ), BQ)
            q0, q1, k, v = unpack4(*split3(x_ref[rows, :]))
            q_s[b, :BQ, :] = q0.astype(jnp.bfloat16)
            q_s[b, BQ:, :] = q1.astype(jnp.bfloat16)
            k_s[b] = k.astype(jnp.bfloat16)
            v_s[b] = v.astype(jnp.bfloat16)
            for d in range(2):
                parts = unpack4(*split3(do_ref[2*b + d]))
                for n, part in enumerate(parts):
                    at = (n % 2) * BQ + d*128 + (n // 2) * 64
                    do_s[b, at:at+64, :] = part.astype(jnp.bfloat16)
            prod = do_s[b].astype(jnp.float32) * of_ref[b]
            delta = jnp.broadcast_to(jnp.sum(prod, axis=1, keepdims=True), (2*BQ, LN))
            dl_s[b] = jnp.transpose(delta, (1, 0))[:8, :]
            dq_s[b] = jnp.zeros((2*BQ, LN), jnp.float32)
            return carry
        lax.fori_loop(0, blocks, body, 0)
    clean_from = (length // 8 + BQ - 1) // BQ
    clean_to = 3 * length // 4 // BQ
    late = (3 * length // 4 + length // 8) // BQ
    third = 3 * length // 4 // BQ
    stop = jnp.where(j >= third, blocks, late)
    k = k_s[j]
    v = v_s[j]
    dk_s[j] = jnp.zeros((BQ, LN), jnp.float32)
    dv_s[j] = jnp.zeros((BQ, LN), jnp.float32)
    key = j * BQ + lax.broadcasted_iota(jnp.int32, (BQ, 1), 0)

    def step(i, masked):
        q, do = q_s[i], do_s[i]
        s = dotf(k, q, ((1,), (1,)))
        p = jnp.exp2(s * C2 - lse_ref[i, 0:1, :])
        if masked:
            q_index = i * BQ + lax.broadcasted_iota(jnp.int32, (1, BQ), 1)
            ok = (key <= q_index) & (key >= doc_low(q_index, first, length))
            p = jnp.where(jnp.concatenate([ok, ok], axis=1), p, 0.0)
        dp = dotf(v, do, ((1,), (1,)))
        ds = (p * (dp - dl_s[i, 0:1, :])).astype(jnp.bfloat16)
        dv_s[j] += dotf(p.astype(jnp.bfloat16), do, ((1,), (0,)))
        dk_s[j] += dotf(ds, q, ((1,), (0,)))
        dq_s[i] += dotf(ds, k, ((0,), (0,)))

    def loop(lo, hi, masked):
        def body(i, carry):
            step(i, masked)
            return carry
        lax.fori_loop(lo, hi, body, 0)

    step(j, True)
    clean_lo = j + 1
    clean_hi = jnp.where(j >= clean_from, jnp.maximum(clean_to, j + 1), j + 1)
    loop(clean_lo, clean_hi, False)
    loop(clean_hi, stop, True)

    @pl.when(j == blocks - 1)
    def _():
        scale = HD ** -0.5
        def body(b, carry):
            rows = pl.ds(pl.multiple_of(b * BQ, BQ), BQ)
            t = pack4(dq_s[b, :BQ, :] * scale, dq_s[b, BQ:, :] * scale, dk_s[b] * scale, dv_s[b])
            t = jnp.concatenate(t, axis=1)
            cosine, sine, lower = cos_sin3(cos_ref[rows, :], sin_ref[rows, :])
            out_ref[rows, :] = turn(t, cosine, -sine, lower).astype(jnp.bfloat16)
            return carry
        lax.fori_loop(0, blocks, body, 0)

def attn_bwd(first, x, do, of, lse, cos, sin):
    length = x.shape[0]
    blocks = length // BQ
    whole = lambda a: pl.BlockSpec(a.shape, lambda j: (0,) * a.ndim)
    return pl.pallas_call(
        functools.partial(attn_bwd_kernel, length),
        grid=(blocks,),
        in_specs=[pl.BlockSpec(memory_space=pltpu.SMEM)] + [whole(a) for a in (x, do, of, lse, cos, sin)],
        out_specs=pl.BlockSpec((length, 3*LN), lambda j: (0, 0)),
        out_shape=jax.ShapeDtypeStruct((length, 3*LN), jnp.bfloat16),
        scratch_shapes=[pltpu.VMEM((blocks, 2*BQ, LN), jnp.bfloat16),
                        pltpu.VMEM((blocks, BQ, LN), jnp.bfloat16),
                        pltpu.VMEM((blocks, BQ, LN), jnp.bfloat16),
                        pltpu.VMEM((blocks, 2*BQ, LN), jnp.bfloat16),
                        pltpu.VMEM((blocks, 8, 2*BQ), jnp.float32),
                        pltpu.VMEM((blocks, 2*BQ, LN), jnp.float32),
                        pltpu.VMEM((blocks, BQ, LN), jnp.float32),
                        pltpu.VMEM((blocks, BQ, LN), jnp.float32)],
        compiler_params=pltpu.CompilerParams(vmem_limit_bytes=56 << 20),
        name="attend_back",
    )(first, x, do, of, lse, cos, sin)


def widen(table):
    lane = lane_iota(table.shape[0])
    second = jnp.where(lane < 96, pltpu.roll(table, 96, 1), pltpu.roll(table, 16, 1))
    third = jnp.where(lane < 112, pltpu.roll(table, 112, 1), pltpu.roll(table, 32, 1))
    return second, third


def cos_sin3(cos, sin):
    lane = lane_iota(cos.shape[0])
    live = lane < 32
    cos_two, cos_three = widen(cos)
    sin_two, sin_three = widen(sin)
    cosine = jnp.concatenate([cos, cos_two, jnp.where(live, cos_three, 1.0)], axis=1)
    sine = jnp.concatenate([sin, sin_two, jnp.where(live, sin_three, 0.0)], axis=1)
    wide = lax.broadcasted_iota(jnp.int32, cosine.shape, 1)
    lower = (wide % HD) < HD // 2
    return cosine, jnp.where(lower, -sine, sine), lower


def turn(values, cosine, sine, lower):
    width = values.shape[1]
    swapped = jnp.where(
        lower, pltpu.roll(values, width - HD // 2, 1), pltpu.roll(values, HD // 2, 1)
    )
    return values * cosine + swapped * sine


def full_spec(array):
    rank = array.ndim
    return pl.BlockSpec(array.shape, lambda *_: (0,) * rank)


def qkv_kernel(parts, rows, place_ref, *refs):
    blocks = refs[:parts]
    gain_ref, w_ref, cos_ref, sin_ref, a_ref, out_ref = refs[parts:]
    tokens = blocks[0].shape[0] // rows
    for k in range(parts):
        z = lax.rem(place_ref[0] + (parts - k), parts)
        stream = blocks[k][...].astype(jnp.float32)
        factor = lax.rsqrt(jnp.mean(stream * stream, axis=-1, keepdims=True) + EPS)
        normed = (stream * factor * gain_ref[...]).astype(jnp.bfloat16)
        at = pl.ds(pl.multiple_of(z * tokens, tokens), tokens)
        for r in range(rows):
            a_ref[r, at, :] = normed[r * tokens : (r + 1) * tokens]
        product = dotf(normed, w_ref[...], ((1,), (0,)))
        for r in range(rows):
            cosine, sine, lower = cos_sin3(cos_ref[r, at, :], sin_ref[r, at, :])
            for h in range(product.shape[1] // (3 * LN)):
                piece = product[r * tokens : (r + 1) * tokens, h * 3 * LN : (h + 1) * 3 * LN]
                out_ref[h * rows + r, at, :] = turn(piece, cosine, sine, lower).astype(jnp.bfloat16)


def qkv_call(place, blocks, gain, weight, cos, sin, rows):
    parts = len(blocks)
    count, width = blocks[0].shape
    tokens = count // rows * parts
    groups = weight.shape[1] // (3 * LN)
    operands = (*blocks, gain, weight, cos, sin)
    return pl.pallas_call(
        partial(qkv_kernel, parts, rows),
        grid=(1,),
        in_specs=[pl.BlockSpec(memory_space=pltpu.SMEM)] + [full_spec(v) for v in operands],
        out_specs=[
            pl.BlockSpec((rows, tokens, width), lambda i: (0, 0, 0)),
            pl.BlockSpec((groups * rows, tokens, 3 * LN), lambda i: (0, 0, 0)),
        ],
        out_shape=[
            jax.ShapeDtypeStruct((rows, tokens, width), jnp.bfloat16),
            jax.ShapeDtypeStruct((groups * rows, tokens, 3 * LN), jnp.bfloat16),
        ],
        compiler_params=pltpu.CompilerParams(vmem_limit_bytes=48 << 20),
        name="norm_qkv",
    )(place, *operands)


def thirds(values):
    return values[:, :LN], values[:, LN : 2 * LN], values[:, 2 * LN :]


def join_pairs(left, right):
    l0, l1, l2 = thirds(left)
    r0, r1, r2 = thirds(right)
    low = lane_iota(left.shape[0]) < 64
    s0, s1, s2 = (pltpu.roll(v, 64, 1) for v in (r0, r1, r2))
    firsts = (l0, jnp.where(low, l1, s0), jnp.where(low, s0, s1))
    m1, m2 = pltpu.roll(l1, 64, 1), pltpu.roll(l2, 64, 1)
    lasts = (jnp.where(low, m1, m2), jnp.where(low, m2, r1), r2)
    return jnp.concatenate(firsts, axis=1), jnp.concatenate(lasts, axis=1)


def out_kernel(rows, parts, o_ref, w_ref, tok_ref, gain_ref, mid_ref, b_ref, oo_ref, o_s):
    half = o_ref.shape[1]
    for r in range(rows):
        for z in range(parts):
            left = o_ref[r * parts + z].astype(jnp.float32)
            right = o_ref[(rows + r) * parts + z].astype(jnp.float32)
            for n, piece in enumerate(join_pairs(left, right)):
                at = (2 * r + n) * half
                o_s[at : at + half, z * 3 * LN : (z + 1) * 3 * LN] = piece.astype(jnp.bfloat16)
    attended = o_s[...]
    oo_ref[...] = attended
    middle = tok_ref[...].astype(jnp.float32) + dotf(attended, w_ref[...], ((1,), (1,)))
    mid_ref[...] = middle
    factor = lax.rsqrt(jnp.mean(middle * middle, axis=-1, keepdims=True) + EPS)
    b_ref[...] = (middle * factor * gain_ref[...]).astype(jnp.bfloat16)


def out_call(o_parts, weight, tokens, gain, rows):
    count, width = tokens.shape
    inner = weight.shape[1]
    operands = (o_parts, weight, tokens, gain)
    shapes = [
        jax.ShapeDtypeStruct((count, width), jnp.float32),
        jax.ShapeDtypeStruct((count, width), jnp.bfloat16),
        jax.ShapeDtypeStruct((count, inner), jnp.bfloat16),
    ]
    return pl.pallas_call(
        partial(out_kernel, rows, o_parts.shape[0] // (2 * rows)),
        grid=(1,),
        in_specs=[full_spec(v) for v in operands],
        out_specs=[full_spec(v) for v in shapes],
        out_shape=shapes,
        scratch_shapes=[pltpu.VMEM((count, inner), jnp.bfloat16)],
        compiler_params=pltpu.CompilerParams(vmem_limit_bytes=48 << 20),
        name="out_norm",
    )(*operands)


def split_pairs(firsts, lasts):
    f0, f1, f2 = thirds(firsts)
    g0, g1, g2 = thirds(lasts)
    low = lane_iota(firsts.shape[0]) < 64
    t0, t1 = pltpu.roll(g0, 64, 1), pltpu.roll(g1, 64, 1)
    left = (f0, jnp.where(low, f1, t0), jnp.where(low, t0, t1))
    u1, u2 = pltpu.roll(f1, 64, 1), pltpu.roll(f2, 64, 1)
    right = (jnp.where(low, u1, u2), jnp.where(low, u2, g1), g2)
    return jnp.concatenate(left, axis=1), jnp.concatenate(right, axis=1)


def mid_back_kernel(
    rows, parts, db_ref, mid_ref, cot_ref, gain_ref, w_ref, gmid_ref, go_ref, do_ref, gg_ref
):
    db = db_ref[...]
    middle = mid_ref[...]
    factor = lax.rsqrt(jnp.mean(middle * middle, axis=-1, keepdims=True) + EPS)
    scaled = db * gain_ref[...]
    inner = jnp.mean(scaled * middle, axis=-1, keepdims=True)
    grad = cot_ref[...].astype(jnp.float32) + factor * scaled - middle * (factor**3 * inner)
    gmid_ref[...] = grad
    gg_ref[...] = jnp.sum(db * middle * factor, axis=0, keepdims=True)
    low = grad.astype(jnp.bfloat16)
    go_ref[...] = low
    back = dotf(low, w_ref[...], ((1,), (0,)))
    half = do_ref.shape[1]
    for r in range(rows):
        for z in range(parts):
            cols = slice(z * 3 * LN, (z + 1) * 3 * LN)
            at = 2 * r * half
            left, right = split_pairs(back[at : at + half, cols], back[at + half : at + 2 * half, cols])
            do_ref[r * parts + z] = left.astype(jnp.bfloat16)
            do_ref[(rows + r) * parts + z] = right.astype(jnp.bfloat16)


def mid_back_call(db, middle, cot, gain, weight, rows, parts):
    count, width = middle.shape
    operands = (db, middle, cot, gain, weight)
    shapes = [
        jax.ShapeDtypeStruct((count, width), jnp.float32),
        jax.ShapeDtypeStruct((count, width), jnp.bfloat16),
        jax.ShapeDtypeStruct((2 * rows * parts, count // rows // 2, 3 * LN), jnp.bfloat16),
        jax.ShapeDtypeStruct((1, width), jnp.float32),
    ]
    return pl.pallas_call(
        partial(mid_back_kernel, rows, parts),
        grid=(1,),
        in_specs=[full_spec(v) for v in operands],
        out_specs=[full_spec(v) for v in shapes],
        out_shape=shapes,
        compiler_params=pltpu.CompilerParams(vmem_limit_bytes=48 << 20),
        name="mid_back",
    )(*operands)


def da_kernel(parts, rows, place_ref, *refs):
    blocks = refs[:parts]
    d_ref, w_ref, da_ref, gg_ref = refs[parts:]
    tokens = blocks[0].shape[0] // rows
    groups = d_ref.shape[0]
    total = jnp.zeros(gg_ref.shape, jnp.float32)
    for k in range(parts):
        z = lax.rem(place_ref[0] + (parts - k), parts)
        at = pl.ds(pl.multiple_of(z * tokens, tokens), tokens)
        left = jnp.concatenate(
            [jnp.concatenate([d_ref[g, r, at, :] for r in range(rows)], axis=0) for g in range(groups)],
            axis=1,
        )
        back = dotf(left, w_ref[...], ((1,), (1,)))
        stream = blocks[k][...].astype(jnp.float32)
        factor = lax.rsqrt(jnp.mean(stream * stream, axis=-1, keepdims=True) + EPS)
        total = total + jnp.sum(back * stream * factor, axis=0, keepdims=True)
        count = rows * tokens
        da_ref[pl.ds(pl.multiple_of(z * count, count), count), :] = back.astype(jnp.bfloat16)
    gg_ref[...] = total


def da_call(place, blocks, grads, weight, rows):
    parts = len(blocks)
    count, width = blocks[0].shape
    operands = (*blocks, grads, weight)
    shapes = [
        jax.ShapeDtypeStruct((parts * count, width), jnp.bfloat16),
        jax.ShapeDtypeStruct((1, width), jnp.float32),
    ]
    return pl.pallas_call(
        partial(da_kernel, parts, rows),
        grid=(1,),
        in_specs=[pl.BlockSpec(memory_space=pltpu.SMEM)] + [full_spec(v) for v in operands],
        out_specs=[full_spec(v) for v in shapes],
        out_shape=shapes,
        compiler_params=pltpu.CompilerParams(vmem_limit_bytes=48 << 20),
        name="da_part",
    )(place, *operands)


EVERY = ("y", "x", "c", "z")
SWAP = ((0, 1), (1, 0))


def swap(value, axis):
    return lax.ppermute(value, axis, SWAP)


def gather_blocks(value, size):
    shift = lambda k: [(i, (i + k) % size) for i in range(size)]
    order = sorted(range(1, size), key=lambda k: -min(k, size - k))
    got = {k: lax.ppermute(value, "z", shift(k)) for k in order}
    return [value] + [got[k] for k in range(1, size)]


def gather_square(value):
    half = value.shape[0] // 2
    xn, yn = swap(value, "x"), swap(value, "y")
    dg_first, dg_last = swap(yn[:half], "x"), swap(xn[half:], "y")
    return jnp.concatenate([value, xn[:half], dg_first, yn[half:], dg_last, xn[half:], yn[:half]], axis=0)


def reduce_square(part):
    low = jnp.bfloat16
    half = part.shape[0] // 8
    piece = lambda n, m=1: part[n * half : (n + m) * half]
    from_x = swap(piece(2, 2).astype(low), "x").astype(jnp.float32)
    from_y = swap(piece(4, 2).astype(low), "y").astype(jnp.float32)
    pass_y = swap((piece(7) + from_x[half:]).astype(low), "y").astype(jnp.float32)
    pass_x = swap((piece(6) + from_y[half:]).astype(low), "x").astype(jnp.float32)
    return jnp.concatenate(
        [piece(0) + from_x[:half] + pass_y, piece(1) + from_y[:half] + pass_x], axis=0
    )


def all_to_all(value, axes):
    return lax.all_to_all(value, axes, 0, 0, tiled=True)


def tie(*values):
    return lax.optimization_barrier(values)


def dot(left, right, left_dim, right_dim, kind=jnp.float32):
    return contract(left, right, left_dim, right_dim).astype(kind)


def fast_local(sizes, *args):
    (tokens, cotangent, segments, positions, norm_in, w_query, w_key, w_value, w_out, norm_mid, w_gate, w_up, w_down) = args
    low = jnp.bfloat16
    nz = sizes["z"]
    devices = sizes["y"] * sizes["x"] * sizes["c"] * nz
    plane = devices // nz
    rows, span, width = tokens.shape
    count = rows * span
    chunk = segments.shape[1]
    length = chunk * sizes["x"] * sizes["c"]
    x_at, c_at, z_at = lax.axis_index("x"), lax.axis_index("c"), lax.axis_index("z")
    place = z_at.reshape(1).astype(jnp.int32)

    own = tokens.reshape(count, width)
    blocks = gather_blocks(own, nz)

    gains = jnp.concatenate([norm_in, norm_mid], axis=1)
    share = norm_in.shape[1]
    gains = jnp.pad(gains, ((0, 0), (0, LN - 2 * share)))
    gains = all_to_all(jnp.broadcast_to(gains, (devices, LN)), EVERY)
    gain_in = gains[:, :share].reshape(1, width)
    gain_mid = gains[:, share : 2 * share].reshape(1, width)

    kv_local = w_key.shape[2] // HD
    per_head = lambda w: w[0].reshape(w.shape[1], kv_local, -1)
    w_qkv = jnp.concatenate([per_head(w_query), per_head(w_key), per_head(w_value)], axis=2)
    w_qkv = w_qkv.reshape(w_qkv.shape[0], -1)
    w_qkv = lax.all_gather(w_qkv, ("y", "x", "c"), axis=0, tiled=True)

    units = w_gate.shape[2] // plane
    by_unit = lambda w: w.reshape(w.shape[0], plane, units)
    w_ff = jnp.stack([by_unit(w_gate[0]), by_unit(w_up[0]), by_unit(w_down[0].T)], axis=2)
    w_ff = jnp.transpose(w_ff, (1, 0, 2, 3)).reshape(width, 3 * units)
    w_ff = all_to_all(w_ff, ("y", "x", "c"))

    last = (x_at * sizes["c"] + c_at + 1) * chunk - 1
    begin = last - positions[:, -1] - jnp.where(segments[:, -1] == 2, 3 * length // 4, 0)
    lanes = jnp.arange(LN, dtype=jnp.int32) % (HD // 2)
    frequency = THETA ** (-(2.0 * lanes.astype(jnp.float32)) / HD)
    token_angle = positions.astype(jnp.float32)[:, :, None] * frequency
    first = lax.dynamic_slice_in_dim(begin, c_at, 1).astype(jnp.int32)
    index = jnp.arange(length, dtype=jnp.int32)
    row_angle = (index - doc_low(index, first[0], length)).astype(jnp.float32)[:, None] * frequency
    token_cos, token_sin = jnp.cos(token_angle), jnp.sin(token_angle)
    row_cos, row_sin = jnp.cos(row_angle), jnp.sin(row_angle)

    normed, qkv = qkv_call(place, blocks, gain_in, w_qkv, token_cos, token_sin, rows)
    qkv = all_to_all(qkv, ("x", "c")).reshape(length, 3 * LN)

    w_ff, *blocks = tie(w_ff, *blocks)
    w_ff = lax.all_gather(w_ff, "z", axis=0, tiled=True).reshape(nz, width, 3, units)
    w_ff = jnp.stack([w_ff, swap(w_ff, "c")], axis=0)
    w_ff = jnp.transpose(w_ff, (3, 2, 0, 1, 4)).reshape(3, width, 2 * nz * units)
    w_gu = jnp.transpose(w_ff[:2], (1, 0, 2)).reshape(width, -1)
    w_d = w_ff[2]
    w_o = lax.all_gather(w_out[0].T, EVERY, axis=0, tiled=True)
    w_o = jnp.transpose(w_o.reshape(plane, nz, -1, w_out.shape[1]), (0, 2, 1, 3)).reshape(width, -1)
    cot_low = cotangent.reshape(count, width)
    cot_all = gather_square(cot_low)

    attended, attended_float, log_total = attn_fwd(first, qkv)
    attended = all_to_all(attended, ("x", "c", "z"))
    middle, normed_b, attended_low = out_call(attended, w_o, own, gain_mid, rows)
    b_all = gather_square(normed_b)

    hidden_width = w_d.shape[1]
    gate_up = dot(b_all, w_gu, 1, 0)
    gate, up = gate_up[:, :hidden_width], gate_up[:, hidden_width:]
    grad_hidden = dot(cot_all, w_d, 1, 0)
    sigma = jax.nn.sigmoid(gate)
    silu = gate * sigma
    hidden = (silu * up).astype(low)
    grad_gate = (grad_hidden * up * sigma * (1.0 + gate * (1.0 - sigma))).astype(low)
    grad_up = (grad_hidden * silu).astype(low)
    grad_gu = jnp.concatenate([grad_gate, grad_up], axis=1)
    grad_b = reduce_square(dot(grad_gu, w_gu, 1, 1))
    out = middle + reduce_square(dot(hidden, w_d, 1, 1))

    grad_ff = jnp.concatenate(
        [dot(b_all, grad_gu, 0, 0, low), dot(cot_all, hidden, 0, 0, low)], axis=1
    )
    grad_ff = jnp.transpose(grad_ff.reshape(width, 3, 2, nz, units), (2, 3, 0, 1, 4))
    grad_ff = grad_ff.reshape(2, nz * width, 3 * units)
    grad_ff = (grad_ff[0].astype(jnp.float32) + swap(grad_ff[1], "c").astype(jnp.float32)).astype(low)
    grad_ff = lax.psum_scatter(grad_ff, "z", scatter_dimension=0, tiled=True)
    grad_ff = all_to_all(grad_ff, ("y", "x", "c")).reshape(plane, width // plane, 3, units)
    grad_ff = jnp.transpose(grad_ff.astype(jnp.float32), (2, 1, 0, 3)).reshape(3, width // plane, -1)

    grad_mid, grad_low, grad_o, gain_grad_mid = mid_back_call(
        grad_b, middle, cot_low, gain_mid, w_o, rows, nz
    )
    grad_o = all_to_all(grad_o, ("x", "c", "z"))
    grad_wo = dot(grad_low, attended_low, 0, 0, low)
    grad_wo = jnp.transpose(grad_wo.reshape(plane, -1, nz, w_out.shape[1]), (0, 2, 1, 3))
    grad_wo = grad_wo.reshape(-1, w_out.shape[1])
    grad_wo = lax.psum_scatter(grad_wo, EVERY, scatter_dimension=0, tiled=True)

    grad_qkv = attn_bwd(first, qkv, grad_o, attended_float, log_total, row_cos, row_sin)
    grad_qkv = all_to_all(grad_qkv.reshape(-1, chunk, 3 * LN), ("x", "c"))
    grad_qkv = grad_qkv.reshape(kv_local, rows, chunk, 3 * LN)
    part, gain_grad_in = da_call(place, blocks, grad_qkv, w_qkv, rows)
    grad_a = lax.psum_scatter(part, "z", scatter_dimension=0, tiled=True)
    normed = normed.reshape(rows * chunk, width)
    grad_wqkv = jnp.concatenate(
        [dot(normed, grad_qkv[h].reshape(rows * chunk, 3 * LN), 0, 0, low) for h in range(kv_local)], axis=1
    )
    grad_wqkv = lax.psum_scatter(grad_wqkv, ("y", "x", "c"), scatter_dimension=0, tiled=True)

    gain_grads = jnp.concatenate(
        [gain_grad_in.reshape(devices, share), gain_grad_mid.reshape(devices, share)], axis=1
    )
    gain_grads = jnp.pad(gain_grads, ((0, 0), (0, LN - 2 * share)))
    gain_grads = jnp.sum(all_to_all(gain_grads, EVERY), axis=0, keepdims=True)

    back_in, _ = norm_back(
        own.astype(jnp.float32),
        lax.rsqrt(jnp.mean(jnp.square(own.astype(jnp.float32)), axis=-1, keepdims=True) + EPS),
        gain_in,
        grad_a.astype(jnp.float32),
    )
    grad_tokens = grad_mid + back_in
    grad_wqkv = grad_wqkv.astype(jnp.float32).reshape(-1, kv_local, 4 * HD)
    flat = lambda g: g.reshape(1, g.shape[0], -1)
    return (
        out.reshape(tokens.shape),
        grad_tokens.reshape(tokens.shape),
        gain_grads[:, :share],
        flat(grad_wqkv[:, :, : 2 * HD]),
        flat(grad_wqkv[:, :, 2 * HD : 3 * HD]),
        flat(grad_wqkv[:, :, 3 * HD :]),
        grad_wo.astype(jnp.float32).T[None],
        gain_grads[:, share : 2 * share],
        grad_ff[0][None],
        grad_ff[1][None],
        grad_ff[2].T[None],
    )


def fast_solution(mesh, cores):
    batch, seq, kv = mesh.devices.shape
    fine = Mesh(mesh.devices.reshape(batch, seq // cores, cores, kv), EVERY)
    sizes = dict(fine.shape)
    row_spec = P("y", ("x", "c", "z"), None)
    seq_spec = P("y", ("x", "c"))
    gain_spec = P(None, EVERY)
    in_w = P(None, ("y", "x", "c"), "z")
    out_w = P(None, "z", ("y", "x", "c"))
    in_specs = (row_spec, row_spec, seq_spec, seq_spec, gain_spec, in_w, in_w, in_w, out_w, gain_spec, in_w, in_w, out_w)
    out_specs = (row_spec, row_spec, gain_spec, in_w, in_w, in_w, out_w, gain_spec, in_w, in_w, out_w)
    return jax.shard_map(
        partial(fast_local, sizes), mesh=fine, in_specs=in_specs, out_specs=out_specs, check_vma=False
    )


def solution(mesh):
    batch, seq, kv = (mesh.shape[name] for name in ("batch", "seq", "kv"))
    general = general_solution(mesh)
    if (batch, seq) != (2, 4):
        return general
    fast = fast_solution(mesh, 2)

    def run(*args):
        rows, length, width = args[0].shape
        kv_heads, q_heads = args[6].shape[2] // HD, args[5].shape[2] // HD
        fits = (
            rows == 2 * batch
            and kv_heads == 2 * kv
            and q_heads == 2 * kv_heads
            and length == 128 * seq * kv
            and length % (4 * BQ) == 0
            and width % LN == 0
            and 2 * width // (batch * seq * kv) <= LN
            and args[10].shape[2] == LN * batch * seq * kv
        )
        return (fast if fits else general)(*args)

    return run
```

```python
import functools
import math
from functools import partial

import jax
import jax.numpy as jnp
from jax import lax
from jax.experimental import pallas as pl
from jax.experimental.pallas import tpu as pltpu
from jax.sharding import Mesh
from jax.sharding import PartitionSpec as P

HD = 96
LAYERS = 1


EPS = 1e-05
THETA = 100000.0
BIG_NEG = -1e30


def rotary(positions_row):
    half_width = HD // 2
    frequency = THETA ** (-(2.0 * jnp.arange(half_width, dtype=jnp.float32)) / HD)
    angles = positions_row.astype(jnp.float32)[:, None] * frequency[None, :]
    cosine = jnp.concatenate([jnp.cos(angles), jnp.cos(angles)], axis=1)
    sine_table = jnp.concatenate([jnp.sin(angles), jnp.sin(angles)], axis=1)
    return (cosine, sine_table)


def rotate(head_vals, cosine, sine_table):
    half_width = head_vals.shape[-1] // 2
    swapped = jnp.concatenate([-head_vals[..., half_width:], head_vals[..., :half_width]], axis=-1)
    return head_vals * cosine[:, None, :] + swapped * sine_table[:, None, :]


def rms_norm(stream, gain):
    factor = lax.rsqrt(jnp.mean(stream * stream, axis=-1, keepdims=True) + EPS)
    return (stream * factor * gain, factor)


def norm_back(stream, factor, gain, upstream):
    scaled_grad = upstream * gain
    inner_mean = jnp.mean(scaled_grad * stream, axis=-1, keepdims=True)
    grad_stream = factor * scaled_grad - stream * factor**3 * inner_mean
    return (grad_stream, jnp.sum(upstream * stream * factor, axis=0))


def key_width(key_count):
    return math.gcd(key_count, 1024)


def contract(left_side, right_side, left_dim, right_dim):
    return lax.dot_general(
        left_side,
        right_side,
        (((left_dim,), (right_dim,)), ((), ())),
        preferred_element_type=jnp.float32,
    )


def spread(shard_rows):
    return lax.all_gather(shard_rows, "kv", axis=0, tiled=True)


def token_sum(pairs):
    summed = None
    for left_part, right_part, right_dim in pairs:
        product = contract(left_part, right_part, 1, right_dim)
        summed = product if summed is None else summed + product
    return lax.psum_scatter(
        summed.astype(jnp.bfloat16), "kv", scatter_dimension=0, tiled=True
    ).astype(jnp.float32)


def split_block(kv_both, seg_keys, offset, step_width, kv_local, head_size):
    kv_block = lax.dynamic_slice_in_dim(kv_both, offset, step_width, 0)
    key_block = kv_block[:, : kv_local * head_size].reshape(step_width, kv_local, head_size)
    value_block = kv_block[:, kv_local * head_size :].reshape(step_width, kv_local, head_size)
    seg_block = lax.dynamic_slice_in_dim(seg_keys, offset, step_width, 0)
    return (key_block, value_block, seg_block)


def forward_row(queries, seg_query, fold_state, kv_both, seg_keys, first_query, key_start):
    key_count = kv_both.shape[0]
    step_width = key_width(key_count)
    query_count, kv_local, group_size, head_size = queries.shape
    query_index = first_query + jnp.arange(query_count, dtype=jnp.int32)
    score_scale = head_size ** (-0.5)

    def forward_one_step(step_index, inner_state):
        running_max, weight_total, value_total = inner_state
        offset = step_index * step_width
        key_block, value_block, seg_block = split_block(
            kv_both, seg_keys, offset, step_width, kv_local, head_size
        )
        key_index = offset + jnp.arange(step_width, dtype=jnp.int32)
        allowed = (seg_query[:, None] == seg_block[None, :]) & (
            key_index[None, :] <= query_index[:, None]
        )
        scores = (
            jnp.einsum("qkgd,pkd->kgqp", queries, key_block, preferred_element_type=jnp.float32)
            * score_scale
        )
        scores = jnp.where(allowed, scores, BIG_NEG)
        new_max = jnp.maximum(running_max, jnp.max(scores, axis=-1))
        weights = jnp.where(allowed, jnp.exp(scores - new_max[..., None]), 0.0)
        rescale = jnp.exp(running_max - new_max)
        weight_total = rescale * weight_total + jnp.sum(weights, axis=-1)
        update = jnp.einsum(
            "kgqp,pkd->qkgd",
            weights.astype(jnp.bfloat16),
            value_block,
            preferred_element_type=jnp.float32,
        )
        value_total = jnp.transpose(rescale, (2, 0, 1))[..., None] * value_total + update
        return (new_max, weight_total, value_total)

    return lax.fori_loop(0, key_count // step_width, forward_one_step, fold_state)


def forward_fold(queries, seg_query, first_query, fold_state, pieces, key_start):
    kv_both, seg_keys = pieces
    row_fn = partial(forward_row, first_query=first_query, key_start=key_start)
    return jax.vmap(row_fn, in_axes=(0, 0, 0, 1, 1))(
        queries, seg_query, fold_state, kv_both, seg_keys
    )


def backward_row(
    queries,
    grad_attn,
    log_total,
    row_delta,
    seg_query,
    fold_state,
    kv_both,
    seg_keys,
    first_query,
    key_start,
):
    key_count = kv_both.shape[0]
    step_width = key_width(key_count)
    query_count, kv_local, group_size, head_size = queries.shape
    query_index = first_query + jnp.arange(query_count, dtype=jnp.int32)
    score_scale = head_size ** (-0.5)

    def backward_one_step(step_index, inner_state):
        grad_queries, grad_buffer = inner_state
        offset = step_index * step_width
        key_block, value_block, seg_block = split_block(
            kv_both, seg_keys, offset, step_width, kv_local, head_size
        )
        key_index = offset + jnp.arange(step_width, dtype=jnp.int32)
        allowed = (seg_query[:, None] == seg_block[None, :]) & (
            key_index[None, :] <= query_index[:, None]
        )
        scores = (
            jnp.einsum("qkgd,pkd->kgqp", queries, key_block, preferred_element_type=jnp.float32)
            * score_scale
        )
        probs_block = jnp.where(allowed, jnp.exp(scores - log_total[..., None]), 0.0)
        grad_probs = jnp.einsum(
            "qkgd,pkd->kgqp", grad_attn, value_block, preferred_element_type=jnp.float32
        )
        grad_scores = (probs_block * (grad_probs - row_delta[..., None])).astype(jnp.bfloat16)
        grad_queries = (
            grad_queries
            + jnp.einsum(
                "kgqp,pkd->qkgd", grad_scores, key_block, preferred_element_type=jnp.float32
            )
            * score_scale
        )
        grad_keys = (
            jnp.einsum("kgqp,qkgd->pkd", grad_scores, queries, preferred_element_type=jnp.float32)
            * score_scale
        )
        grad_values = jnp.einsum(
            "kgqp,qkgd->pkd",
            probs_block.astype(jnp.bfloat16),
            grad_attn,
            preferred_element_type=jnp.float32,
        )
        joined = jnp.concatenate(
            [grad_keys.reshape(step_width, -1), grad_values.reshape(step_width, -1)], axis=1
        )
        grad_buffer = lax.dynamic_update_slice_in_dim(grad_buffer, joined, offset, 0)
        return (grad_queries, grad_buffer)

    return lax.fori_loop(0, key_count // step_width, backward_one_step, fold_state)


def backward_fold(
    queries, grad_attn, log_total, row_delta, seg_query, first_query, fold_state, pieces, key_start
):
    kv_both, seg_keys = pieces
    row_fn = partial(backward_row, first_query=first_query, key_start=key_start)
    return jax.vmap(row_fn, in_axes=(0, 0, 0, 0, 0, 0, 1, 1))(
        queries, grad_attn, log_total, row_delta, seg_query, fold_state, kv_both, seg_keys
    )


def layer_forward(stream, gain_pair, matrices, seg_info, tables):
    gain_in, gain_mid = gain_pair
    w_query, w_key, w_value, w_out, w_gate, w_up, w_down = matrices
    seg_query, seg_keys = seg_info
    cosine, sine_table = tables
    row_count = seg_query.shape[0]
    kv_local = w_key.shape[1] // HD
    head_local = w_query.shape[1] // HD
    group_size = head_local // kv_local
    normed_a, factor_a = rms_norm(stream, gain_in)
    spread_a = spread(normed_a.astype(jnp.bfloat16))
    flat_count = spread_a.shape[0]
    token_count = flat_count // row_count
    raw_queries = jnp.dot(spread_a, w_query, preferred_element_type=jnp.float32).reshape(
        flat_count, head_local, HD
    )
    queries = (
        rotate(raw_queries, cosine, sine_table)
        .astype(jnp.bfloat16)
        .reshape(token_count, row_count, kv_local, group_size, HD)
    )
    queries = jnp.transpose(queries, (1, 0, 2, 3, 4))
    raw_keys = jnp.dot(spread_a, w_key, preferred_element_type=jnp.float32).reshape(
        flat_count, kv_local, HD
    )
    keys_low = (
        rotate(raw_keys, cosine, sine_table).astype(jnp.bfloat16).reshape(flat_count, kv_local * HD)
    )
    values_low = jnp.dot(spread_a, w_value, preferred_element_type=jnp.float32).astype(jnp.bfloat16)
    kv_both = jnp.concatenate([keys_low, values_low], axis=1).reshape(
        token_count, row_count, 2 * kv_local * HD
    )
    first_query = lax.axis_index("seq") * token_count
    start_state = (
        jnp.full((row_count, kv_local, group_size, token_count), BIG_NEG, jnp.float32),
        jnp.zeros((row_count, kv_local, group_size, token_count), jnp.float32),
        jnp.zeros((row_count, token_count, kv_local, group_size, HD), jnp.float32),
    )
    running_max, weight_total, value_total = forward_fold(
        queries,
        seg_query,
        first_query,
        start_state,
        (
            lax.all_gather(kv_both, "seq", axis=0, tiled=True),
            lax.all_gather(seg_keys, "seq", axis=0, tiled=True),
        ),
        jnp.int32(0),
    )
    attn_float = value_total / jnp.transpose(weight_total, (0, 3, 1, 2))[..., None]
    log_total = running_max + jnp.log(weight_total)
    attn_low = (
        jnp.transpose(attn_float, (1, 0, 2, 3, 4))
        .reshape(flat_count, head_local * HD)
        .astype(jnp.bfloat16)
    )
    stream_mid = stream + token_sum(((attn_low, w_out, 0),))
    normed_b, factor_b = rms_norm(stream_mid, gain_mid)
    spread_b = spread(normed_b.astype(jnp.bfloat16))
    gate_val = jnp.dot(spread_b, w_gate, preferred_element_type=jnp.float32)
    up_val = jnp.dot(spread_b, w_up, preferred_element_type=jnp.float32)
    hidden = (jax.nn.silu(gate_val) * up_val).astype(jnp.bfloat16)
    stream_out = stream_mid + token_sum(((hidden, w_down, 0),))
    saved_state = (
        stream,
        factor_a,
        spread_a,
        queries,
        kv_both,
        attn_float,
        attn_low,
        log_total,
        stream_mid,
        factor_b,
        spread_b,
        gate_val,
        up_val,
        hidden,
    )
    return (stream_out, saved_state)


def layer_backward(saved_state, grad_stream, gain_pair, matrices, seg_info, tables):
    (
        stream,
        factor_a,
        spread_a,
        queries,
        kv_both,
        attn_float,
        attn_low,
        log_total,
        stream_mid,
        factor_b,
        spread_b,
        gate_val,
        up_val,
        hidden,
    ) = saved_state
    gain_in, gain_mid = gain_pair
    w_query, w_key, w_value, w_out, w_gate, w_up, w_down = matrices
    seg_query, seg_keys = seg_info
    cosine, sine_table = tables
    row_count, token_count, kv_local, group_size, head_size = queries.shape
    head_local = kv_local * group_size
    flat_count = row_count * token_count
    grad_low = spread(grad_stream.astype(jnp.bfloat16))
    grad_down_w = contract(hidden, grad_low, 0, 0)
    grad_hidden = contract(grad_low, w_down, 1, 1)
    sigmoid_gate = jax.nn.sigmoid(gate_val)
    silu_gate = gate_val * sigmoid_gate
    grad_gate_low = (
        grad_hidden * up_val * sigmoid_gate * (1.0 + gate_val * (1.0 - sigmoid_gate))
    ).astype(jnp.bfloat16)
    grad_up_low = (grad_hidden * silu_gate).astype(jnp.bfloat16)
    grad_gate_w = contract(spread_b, grad_gate_low, 0, 0)
    grad_up_w = contract(spread_b, grad_up_low, 0, 0)
    grad_normed_b = token_sum(((grad_gate_low, w_gate, 1), (grad_up_low, w_up, 1)))
    back_mid, grad_gain_mid = norm_back(stream_mid, factor_b, gain_mid, grad_normed_b)
    grad_mid = grad_stream + back_mid
    grad_attn_full = spread(grad_mid.astype(jnp.bfloat16))
    grad_out_w = contract(attn_low, grad_attn_full, 0, 0)
    grad_attn = (
        contract(grad_attn_full, w_out, 1, 1)
        .astype(jnp.bfloat16)
        .reshape(token_count, row_count, kv_local, group_size, head_size)
    )
    grad_attn = jnp.transpose(grad_attn, (1, 0, 2, 3, 4))
    row_delta = jnp.transpose(jnp.sum(grad_attn * attn_float, axis=-1), (0, 2, 3, 1))
    first_query = lax.axis_index("seq") * token_count
    row_length = token_count * lax.axis_size("seq")
    start_state = (
        jnp.zeros((row_count, token_count, kv_local, group_size, head_size), jnp.float32),
        jnp.zeros((row_count, row_length, 2 * kv_local * head_size), jnp.float32),
    )
    grad_queries, grad_buffer = backward_fold(
        queries,
        grad_attn,
        log_total,
        row_delta,
        seg_query,
        first_query,
        start_state,
        (
            lax.all_gather(kv_both, "seq", axis=0, tiled=True),
            lax.all_gather(seg_keys, "seq", axis=0, tiled=True),
        ),
        jnp.int32(0),
    )
    grad_kv = lax.psum_scatter(
        grad_buffer.astype(jnp.bfloat16), "seq", scatter_dimension=1, tiled=True
    ).astype(jnp.float32)
    grad_kv = jnp.transpose(grad_kv, (1, 0, 2)).reshape(flat_count, 2 * kv_local * head_size)
    grad_queries = jnp.transpose(grad_queries, (1, 0, 2, 3, 4)).reshape(
        flat_count, head_local, head_size
    )
    grad_q_low = (
        rotate(grad_queries, cosine, -sine_table)
        .astype(jnp.bfloat16)
        .reshape(flat_count, head_local * head_size)
    )
    grad_k_low = (
        rotate(
            grad_kv[:, : kv_local * head_size].reshape(flat_count, kv_local, head_size),
            cosine,
            -sine_table,
        )
        .astype(jnp.bfloat16)
        .reshape(flat_count, kv_local * head_size)
    )
    grad_v_low = grad_kv[:, kv_local * head_size :].astype(jnp.bfloat16)
    grad_query_w = contract(spread_a, grad_q_low, 0, 0)
    grad_key_w = contract(spread_a, grad_k_low, 0, 0)
    grad_value_w = contract(spread_a, grad_v_low, 0, 0)
    grad_normed_a = token_sum(
        ((grad_q_low, w_query, 1), (grad_k_low, w_key, 1), (grad_v_low, w_value, 1))
    )
    back_in, grad_gain_in = norm_back(stream, factor_a, gain_in, grad_normed_a)
    grad_input = grad_mid + back_in
    weight_grads = (
        lax.psum_scatter(
            grad_query_w.astype(jnp.bfloat16), ("batch", "seq"), scatter_dimension=0, tiled=True
        ).astype(jnp.float32),
        lax.psum_scatter(
            grad_key_w.astype(jnp.bfloat16), ("batch", "seq"), scatter_dimension=0, tiled=True
        ).astype(jnp.float32),
        lax.psum_scatter(
            grad_value_w.astype(jnp.bfloat16), ("batch", "seq"), scatter_dimension=0, tiled=True
        ).astype(jnp.float32),
        lax.psum_scatter(
            grad_out_w.astype(jnp.bfloat16), ("batch", "seq"), scatter_dimension=1, tiled=True
        ).astype(jnp.float32),
        lax.psum_scatter(
            grad_gate_w.astype(jnp.bfloat16), ("batch", "seq"), scatter_dimension=0, tiled=True
        ).astype(jnp.float32),
        lax.psum_scatter(
            grad_up_w.astype(jnp.bfloat16), ("batch", "seq"), scatter_dimension=0, tiled=True
        ).astype(jnp.float32),
        lax.psum_scatter(
            grad_down_w.astype(jnp.bfloat16), ("batch", "seq"), scatter_dimension=1, tiled=True
        ).astype(jnp.float32),
    )
    return (grad_input, weight_grads, grad_gain_in, grad_gain_mid)


def to_flat(shard_rows):
    row_count, token_part, width = shard_rows.shape
    return jnp.transpose(shard_rows.astype(jnp.float32), (1, 0, 2)).reshape(
        token_part * row_count, width
    )


def from_flat(flat_rows, row_count):
    token_part = flat_rows.shape[0] // row_count
    return jnp.transpose(flat_rows.reshape(token_part, row_count, flat_rows.shape[1]), (1, 0, 2))


def general_local(
    tokens,
    cotangent,
    segments,
    positions,
    norm_in,
    w_query,
    w_key,
    w_value,
    w_out,
    norm_mid,
    w_gate,
    w_up,
    w_down,
):
    gains_in, gains_mid = (
        lax.all_gather(norm_in, ("batch", "seq", "kv"), axis=1, tiled=True),
        lax.all_gather(norm_mid, ("batch", "seq", "kv"), axis=1, tiled=True),
    )
    row_count = tokens.shape[0]
    seg_info = (segments, jnp.transpose(segments, (1, 0)))
    tables = rotary(jnp.transpose(positions, (1, 0)).reshape(-1))

    def fetch_layer(layer_index):
        return (
            lax.all_gather(w_query[layer_index], ("batch", "seq"), axis=0, tiled=True),
            lax.all_gather(w_key[layer_index], ("batch", "seq"), axis=0, tiled=True),
            lax.all_gather(w_value[layer_index], ("batch", "seq"), axis=0, tiled=True),
            lax.all_gather(w_out[layer_index], ("batch", "seq"), axis=1, tiled=True),
            lax.all_gather(w_gate[layer_index], ("batch", "seq"), axis=0, tiled=True),
            lax.all_gather(w_up[layer_index], ("batch", "seq"), axis=0, tiled=True),
            lax.all_gather(w_down[layer_index], ("batch", "seq"), axis=1, tiled=True),
        )

    stream = to_flat(tokens)
    fetched = []
    states = []
    layer_index = 0
    matrices = fetch_layer(layer_index)
    layer_inputs = [stream]
    stream, saved_state = layer_forward(
        stream, (gains_in[layer_index], gains_mid[layer_index]), matrices, seg_info, tables
    )
    fetched.append(matrices)
    states.append(saved_state)
    grad_stream = to_flat(cotangent)
    grads_in = []
    grads_mid = []
    weight_lists = []
    for layer_index in reversed(range(LAYERS)):
        gain_pair = (gains_in[layer_index], gains_mid[layer_index])
        matrices = fetch_layer(layer_index)
        saved_state = layer_forward(
            layer_inputs[layer_index], gain_pair, matrices, seg_info, tables
        )[1]
        grad_stream, weight_grads, grad_gain_in, grad_gain_mid = layer_backward(
            saved_state, grad_stream, gain_pair, matrices, seg_info, tables
        )
        grads_in.insert(0, grad_gain_in)
        grads_mid.insert(0, grad_gain_mid)
        weight_lists.insert(0, weight_grads)
    gain_grads_in, gain_grads_mid = (
        lax.psum_scatter(
            jnp.stack(grads_in), ("batch", "seq", "kv"), scatter_dimension=1, tiled=True
        ),
        lax.psum_scatter(
            jnp.stack(grads_mid), ("batch", "seq", "kv"), scatter_dimension=1, tiled=True
        ),
    )
    stacked_grads = [
        jnp.stack([grad_set[member] for grad_set in weight_lists]) for member in range(7)
    ]
    return (
        from_flat(stream, row_count),
        from_flat(grad_stream, row_count),
        gain_grads_in,
        stacked_grads[0],
        stacked_grads[1],
        stacked_grads[2],
        stacked_grads[3],
        gain_grads_mid,
        stacked_grads[4],
        stacked_grads[5],
        stacked_grads[6],
    )


def general_solution(mesh):
    in_specs = (
        P("batch", ("seq", "kv"), None),
        P("batch", ("seq", "kv"), None),
        P("batch", "seq"),
        P("batch", "seq"),
        P(None, ("batch", "seq", "kv")),
        P(None, ("batch", "seq"), "kv"),
        P(None, ("batch", "seq"), "kv"),
        P(None, ("batch", "seq"), "kv"),
        P(None, "kv", ("batch", "seq")),
        P(None, ("batch", "seq", "kv")),
        P(None, ("batch", "seq"), "kv"),
        P(None, ("batch", "seq"), "kv"),
        P(None, "kv", ("batch", "seq")),
    )
    out_specs = (
        P("batch", ("seq", "kv"), None),
        P("batch", ("seq", "kv"), None),
        P(None, ("batch", "seq", "kv")),
        P(None, ("batch", "seq"), "kv"),
        P(None, ("batch", "seq"), "kv"),
        P(None, ("batch", "seq"), "kv"),
        P(None, "kv", ("batch", "seq")),
        P(None, ("batch", "seq", "kv")),
        P(None, ("batch", "seq"), "kv"),
        P(None, ("batch", "seq"), "kv"),
        P(None, "kv", ("batch", "seq")),
    )
    return jax.shard_map(general_local, mesh=mesh, in_specs=in_specs, out_specs=out_specs, check_vma=False)


LN = 128
NEG=-1e30
C2 = (96 ** -0.5) * 1.4426950408889634

def lane_iota(rows):
    return lax.broadcasted_iota(jnp.int32, (rows, LN), 1)

def unpack4(t0, t1, t2):
    lane = lane_iota(t0.shape[0])
    live = lane < HD
    zero = jnp.zeros_like(t0)
    a = t0
    b = pltpu.roll(jnp.where(lane >= 96, t0, t1), 32, 1)
    c = pltpu.roll(jnp.where(lane >= 64, t1, t2), 64, 1)
    d = pltpu.roll(t2, 96, 1)
    return tuple(jnp.where(live, v, zero) for v in (a, b, c, d))

def pack4(a, b, c, d):
    lane = lane_iota(a.shape[0])
    b, c, d = pltpu.roll(b, 96, 1), pltpu.roll(c, 64, 1), pltpu.roll(d, 32, 1)
    return (jnp.where(lane < 96, a, b), jnp.where(lane < 64, b, c), jnp.where(lane < 32, c, d))

def split3(x):
    x = x.astype(jnp.float32)
    return x[:, :LN], x[:, LN:2*LN], x[:, 2*LN:]

def doc_low(index, first, length):
    second = first + 3 * length // 4
    return jnp.where(index >= second, second, jnp.where(index >= first, first, 0))

BQ = 256

def dotf(a, b, dims):
    return lax.dot_general(a, b, (dims, ((), ())), preferred_element_type=jnp.float32)

def attn_fwd_kernel(length, first_ref, x_ref, o_ref, of_ref, lse_ref, q_s, k_s, v_s, s_s):
    i = pl.program_id(0)
    blocks = length // BQ
    first = first_ref[0]
    @pl.when(i == 0)
    def _():
        def body(j, carry):
            rows = pl.ds(pl.multiple_of(j * BQ, BQ), BQ)
            q0, q1, k, v = unpack4(*split3(x_ref[rows, :]))
            q_s[j, :BQ, :] = q0.astype(jnp.bfloat16)
            q_s[j, BQ:, :] = q1.astype(jnp.bfloat16)
            k_s[j] = k.astype(jnp.bfloat16)
            v_s[j] = v.astype(jnp.bfloat16)
            return carry
        lax.fori_loop(0, blocks, body, 0)
    q = q_s[i]
    clean_from = (length // 8 + BQ - 1) // BQ
    clean_to = 3 * length // 4 // BQ
    late = (3 * length // 4 + length // 8) // BQ
    start = jnp.where(i >= late, 3 * length // 4 // BQ, 0)
    head_masked = jnp.where(i < clean_to, jnp.minimum(clean_from, i), i)
    q_index = i * BQ + lax.broadcasted_iota(jnp.int32, (BQ, 1), 0)
    low = doc_low(q_index, first, length)

    def halves(v, op):
        return op(v[:, :LN], v[:, LN:])

    def score(j, top, masked):
        s = dotf(q, k_s[j], ((1,), (1,)))
        if masked:
            key = j * BQ + lax.broadcasted_iota(jnp.int32, (1, BQ), 1)
            ok = (key <= q_index) & (key >= low)
            s = jnp.where(jnp.concatenate([ok, ok], axis=0), s, NEG)
        s_s[j] = s
        return jnp.maximum(top, halves(s, jnp.maximum))

    top = jnp.full((2 * BQ, LN), NEG, jnp.float32)
    top = lax.fori_loop(start, head_masked, lambda j, t: score(j, t, True), top)
    top = lax.fori_loop(jnp.maximum(head_masked, start), i, lambda j, t: score(j, t, False), top)
    top = score(i, top, True)
    m = jnp.max(top, axis=1, keepdims=True) * C2

    def add(j, state):
        total, acc = state
        p = jnp.exp2(s_s[j] * C2 - m)
        total = total + halves(p, jnp.add)
        acc = acc + dotf(p.astype(jnp.bfloat16), v_s[j], ((1,), (0,)))
        return total, acc

    zero = jnp.zeros((2 * BQ, LN), jnp.float32)
    total, acc = lax.fori_loop(start, i + 1, add, (zero, zero))
    total = jnp.sum(total, axis=1, keepdims=True)
    out = acc / total
    lse = jnp.broadcast_to(m + jnp.log2(total), (2 * BQ, LN))
    lse_ref[0] = jnp.transpose(lse, (1, 0))[:8, :]
    of_ref[0] = out
    for d in range(2):
        parts = []
        for h in range(2):
            parts.append(out[BQ*0 + d*128 + h*64: d*128 + h*64 + 64])
            parts.append(out[BQ + d*128 + h*64: BQ + d*128 + h*64 + 64])
        t = pack4(*parts)
        for n in range(3):
            o_ref[d, :, n*LN:(n+1)*LN] = t[n].astype(jnp.bfloat16)

def attn_fwd(first, x):
    length = x.shape[0]
    blocks = length // BQ
    return pl.pallas_call(
        functools.partial(attn_fwd_kernel, length),
        grid=(blocks,),
        in_specs=[pl.BlockSpec(memory_space=pltpu.SMEM),
                  pl.BlockSpec((length, 3*LN), lambda i: (0, 0))],
        out_specs=[pl.BlockSpec((2, 64, 3*LN), lambda i: (i, 0, 0)),
                   pl.BlockSpec((1, 2*BQ, LN), lambda i: (i, 0, 0)),
                   pl.BlockSpec((1, 8, 2*BQ), lambda i: (i, 0, 0))],
        out_shape=[jax.ShapeDtypeStruct((length//128, 64, 3*LN), jnp.bfloat16),
                   jax.ShapeDtypeStruct((blocks, 2*BQ, LN), jnp.float32),
                   jax.ShapeDtypeStruct((blocks, 8, 2*BQ), jnp.float32)],
        scratch_shapes=[pltpu.VMEM((blocks, 2*BQ, LN), jnp.bfloat16),
                        pltpu.VMEM((blocks, BQ, LN), jnp.bfloat16),
                        pltpu.VMEM((blocks, BQ, LN), jnp.bfloat16),
                        pltpu.VMEM((blocks, 2*BQ, BQ), jnp.float32)],
        compiler_params=pltpu.CompilerParams(vmem_limit_bytes=48 << 20),
        name="attend",
    )(first, x)

def attn_bwd_kernel(length, first_ref, x_ref, do_ref, of_ref, lse_ref, cos_ref, sin_ref, out_ref,
                    q_s, k_s, v_s, do_s, dl_s, dq_s, dk_s, dv_s):
    j = pl.program_id(0)
    blocks = length // BQ
    first = first_ref[0]
    @pl.when(j == 0)
    def _():
        def body(b, carry):
            rows = pl.ds(pl.multiple_of(b * BQ, BQ), BQ)
            q0, q1, k, v = unpack4(*split3(x_ref[rows, :]))
            q_s[b, :BQ, :] = q0.astype(jnp.bfloat16)
            q_s[b, BQ:, :] = q1.astype(jnp.bfloat16)
            k_s[b] = k.astype(jnp.bfloat16)
            v_s[b] = v.astype(jnp.bfloat16)
            for d in range(2):
                parts = unpack4(*split3(do_ref[2*b + d]))
                for n, part in enumerate(parts):
                    at = (n % 2) * BQ + d*128 + (n // 2) * 64
                    do_s[b, at:at+64, :] = part.astype(jnp.bfloat16)
            prod = do_s[b].astype(jnp.float32) * of_ref[b]
            delta = jnp.broadcast_to(jnp.sum(prod, axis=1, keepdims=True), (2*BQ, LN))
            dl_s[b] = jnp.transpose(delta, (1, 0))[:8, :]
            dq_s[b] = jnp.zeros((2*BQ, LN), jnp.float32)
            return carry
        lax.fori_loop(0, blocks, body, 0)
    clean_from = (length // 8 + BQ - 1) // BQ
    clean_to = 3 * length // 4 // BQ
    late = (3 * length // 4 + length // 8) // BQ
    third = 3 * length // 4 // BQ
    stop = jnp.where(j >= third, blocks, late)
    k = k_s[j]
    v = v_s[j]
    dk_s[j] = jnp.zeros((BQ, LN), jnp.float32)
    dv_s[j] = jnp.zeros((BQ, LN), jnp.float32)
    key = j * BQ + lax.broadcasted_iota(jnp.int32, (BQ, 1), 0)

    def step(i, masked):
        q, do = q_s[i], do_s[i]
        s = dotf(k, q, ((1,), (1,)))
        p = jnp.exp2(s * C2 - lse_ref[i, 0:1, :])
        if masked:
            q_index = i * BQ + lax.broadcasted_iota(jnp.int32, (1, BQ), 1)
            ok = (key <= q_index) & (key >= doc_low(q_index, first, length))
            p = jnp.where(jnp.concatenate([ok, ok], axis=1), p, 0.0)
        dp = dotf(v, do, ((1,), (1,)))
        ds = (p * (dp - dl_s[i, 0:1, :])).astype(jnp.bfloat16)
        dv_s[j] += dotf(p.astype(jnp.bfloat16), do, ((1,), (0,)))
        dk_s[j] += dotf(ds, q, ((1,), (0,)))
        dq_s[i] += dotf(ds, k, ((0,), (0,)))

    def loop(lo, hi, masked):
        def body(i, carry):
            step(i, masked)
            return carry
        lax.fori_loop(lo, hi, body, 0)

    step(j, True)
    clean_lo = j + 1
    clean_hi = jnp.where(j >= clean_from, jnp.maximum(clean_to, j + 1), j + 1)
    loop(clean_lo, clean_hi, False)
    loop(clean_hi, stop, True)

    @pl.when(j == blocks - 1)
    def _():
        scale = HD ** -0.5
        def body(b, carry):
            rows = pl.ds(pl.multiple_of(b * BQ, BQ), BQ)
            t = pack4(dq_s[b, :BQ, :] * scale, dq_s[b, BQ:, :] * scale, dk_s[b] * scale, dv_s[b])
            t = jnp.concatenate(t, axis=1)
            cosine, sine, lower = cos_sin3(cos_ref[rows, :], sin_ref[rows, :])
            out_ref[rows, :] = turn(t, cosine, -sine, lower).astype(jnp.bfloat16)
            return carry
        lax.fori_loop(0, blocks, body, 0)

def attn_bwd(first, x, do, of, lse, cos, sin):
    length = x.shape[0]
    blocks = length // BQ
    whole = lambda a: pl.BlockSpec(a.shape, lambda j: (0,) * a.ndim)
    return pl.pallas_call(
        functools.partial(attn_bwd_kernel, length),
        grid=(blocks,),
        in_specs=[pl.BlockSpec(memory_space=pltpu.SMEM)] + [whole(a) for a in (x, do, of, lse, cos, sin)],
        out_specs=pl.BlockSpec((length, 3*LN), lambda j: (0, 0)),
        out_shape=jax.ShapeDtypeStruct((length, 3*LN), jnp.bfloat16),
        scratch_shapes=[pltpu.VMEM((blocks, 2*BQ, LN), jnp.bfloat16),
                        pltpu.VMEM((blocks, BQ, LN), jnp.bfloat16),
                        pltpu.VMEM((blocks, BQ, LN), jnp.bfloat16),
                        pltpu.VMEM((blocks, 2*BQ, LN), jnp.bfloat16),
                        pltpu.VMEM((blocks, 8, 2*BQ), jnp.float32),
                        pltpu.VMEM((blocks, 2*BQ, LN), jnp.float32),
                        pltpu.VMEM((blocks, BQ, LN), jnp.float32),
                        pltpu.VMEM((blocks, BQ, LN), jnp.float32)],
        compiler_params=pltpu.CompilerParams(vmem_limit_bytes=56 << 20),
        name="attend_back",
    )(first, x, do, of, lse, cos, sin)


def widen(table):
    lane = lane_iota(table.shape[0])
    second = jnp.where(lane < 96, pltpu.roll(table, 96, 1), pltpu.roll(table, 16, 1))
    third = jnp.where(lane < 112, pltpu.roll(table, 112, 1), pltpu.roll(table, 32, 1))
    return second, third


def cos_sin3(cos, sin):
    lane = lane_iota(cos.shape[0])
    live = lane < 32
    cos_two, cos_three = widen(cos)
    sin_two, sin_three = widen(sin)
    cosine = jnp.concatenate([cos, cos_two, jnp.where(live, cos_three, 1.0)], axis=1)
    sine = jnp.concatenate([sin, sin_two, jnp.where(live, sin_three, 0.0)], axis=1)
    wide = lax.broadcasted_iota(jnp.int32, cosine.shape, 1)
    lower = (wide % HD) < HD // 2
    return cosine, jnp.where(lower, -sine, sine), lower


def turn(values, cosine, sine, lower):
    width = values.shape[1]
    swapped = jnp.where(
        lower, pltpu.roll(values, width - HD // 2, 1), pltpu.roll(values, HD // 2, 1)
    )
    return values * cosine + swapped * sine


def full_spec(array):
    rank = array.ndim
    return pl.BlockSpec(array.shape, lambda *_: (0,) * rank)


def qkv_kernel(parts, rows, place_ref, *refs):
    blocks = refs[:parts]
    gain_ref, w_ref, cos_ref, sin_ref, a_ref, out_ref = refs[parts:]
    tokens = blocks[0].shape[0] // rows
    for k in range(parts):
        z = lax.rem(place_ref[0] + (parts - k), parts)
        stream = blocks[k][...].astype(jnp.float32)
        factor = lax.rsqrt(jnp.mean(stream * stream, axis=-1, keepdims=True) + EPS)
        normed = (stream * factor * gain_ref[...]).astype(jnp.bfloat16)
        at = pl.ds(pl.multiple_of(z * tokens, tokens), tokens)
        for r in range(rows):
            a_ref[r, at, :] = normed[r * tokens : (r + 1) * tokens]
        product = dotf(normed, w_ref[...], ((1,), (0,)))
        for r in range(rows):
            cosine, sine, lower = cos_sin3(cos_ref[r, at, :], sin_ref[r, at, :])
            for h in range(product.shape[1] // (3 * LN)):
                piece = product[r * tokens : (r + 1) * tokens, h * 3 * LN : (h + 1) * 3 * LN]
                out_ref[h * rows + r, at, :] = turn(piece, cosine, sine, lower).astype(jnp.bfloat16)


def qkv_call(place, blocks, gain, weight, cos, sin, rows):
    parts = len(blocks)
    count, width = blocks[0].shape
    tokens = count // rows * parts
    groups = weight.shape[1] // (3 * LN)
    operands = (*blocks, gain, weight, cos, sin)
    return pl.pallas_call(
        partial(qkv_kernel, parts, rows),
        grid=(1,),
        in_specs=[pl.BlockSpec(memory_space=pltpu.SMEM)] + [full_spec(v) for v in operands],
        out_specs=[
            pl.BlockSpec((rows, tokens, width), lambda i: (0, 0, 0)),
            pl.BlockSpec((groups * rows, tokens, 3 * LN), lambda i: (0, 0, 0)),
        ],
        out_shape=[
            jax.ShapeDtypeStruct((rows, tokens, width), jnp.bfloat16),
            jax.ShapeDtypeStruct((groups * rows, tokens, 3 * LN), jnp.bfloat16),
        ],
        compiler_params=pltpu.CompilerParams(vmem_limit_bytes=48 << 20),
        name="norm_qkv",
    )(place, *operands)


def thirds(values):
    return values[:, :LN], values[:, LN : 2 * LN], values[:, 2 * LN :]


def join_pairs(left, right):
    l0, l1, l2 = thirds(left)
    r0, r1, r2 = thirds(right)
    low = lane_iota(left.shape[0]) < 64
    s0, s1, s2 = (pltpu.roll(v, 64, 1) for v in (r0, r1, r2))
    firsts = (l0, jnp.where(low, l1, s0), jnp.where(low, s0, s1))
    m1, m2 = pltpu.roll(l1, 64, 1), pltpu.roll(l2, 64, 1)
    lasts = (jnp.where(low, m1, m2), jnp.where(low, m2, r1), r2)
    return jnp.concatenate(firsts, axis=1), jnp.concatenate(lasts, axis=1)


def out_kernel(rows, parts, o_ref, w_ref, tok_ref, gain_ref, mid_ref, b_ref, oo_ref, o_s):
    half = o_ref.shape[1]
    for r in range(rows):
        for z in range(parts):
            left = o_ref[r * parts + z].astype(jnp.float32)
            right = o_ref[(rows + r) * parts + z].astype(jnp.float32)
            for n, piece in enumerate(join_pairs(left, right)):
                at = (2 * r + n) * half
                o_s[at : at + half, z * 3 * LN : (z + 1) * 3 * LN] = piece.astype(jnp.bfloat16)
    attended = o_s[...]
    oo_ref[...] = attended
    middle = tok_ref[...].astype(jnp.float32) + dotf(attended, w_ref[...], ((1,), (1,)))
    mid_ref[...] = middle
    factor = lax.rsqrt(jnp.mean(middle * middle, axis=-1, keepdims=True) + EPS)
    b_ref[...] = (middle * factor * gain_ref[...]).astype(jnp.bfloat16)


def out_call(o_parts, weight, tokens, gain, rows):
    count, width = tokens.shape
    inner = weight.shape[1]
    operands = (o_parts, weight, tokens, gain)
    shapes = [
        jax.ShapeDtypeStruct((count, width), jnp.float32),
        jax.ShapeDtypeStruct((count, width), jnp.bfloat16),
        jax.ShapeDtypeStruct((count, inner), jnp.bfloat16),
    ]
    return pl.pallas_call(
        partial(out_kernel, rows, o_parts.shape[0] // (2 * rows)),
        grid=(1,),
        in_specs=[full_spec(v) for v in operands],
        out_specs=[full_spec(v) for v in shapes],
        out_shape=shapes,
        scratch_shapes=[pltpu.VMEM((count, inner), jnp.bfloat16)],
        compiler_params=pltpu.CompilerParams(vmem_limit_bytes=48 << 20),
        name="out_norm",
    )(*operands)


def split_pairs(firsts, lasts):
    f0, f1, f2 = thirds(firsts)
    g0, g1, g2 = thirds(lasts)
    low = lane_iota(firsts.shape[0]) < 64
    t0, t1 = pltpu.roll(g0, 64, 1), pltpu.roll(g1, 64, 1)
    left = (f0, jnp.where(low, f1, t0), jnp.where(low, t0, t1))
    u1, u2 = pltpu.roll(f1, 64, 1), pltpu.roll(f2, 64, 1)
    right = (jnp.where(low, u1, u2), jnp.where(low, u2, g1), g2)
    return jnp.concatenate(left, axis=1), jnp.concatenate(right, axis=1)


def mid_back_kernel(
    rows, parts, keep_ref, fx_ref, fy_ref, px_ref, py_ref, mid_ref, cot_ref, gain_ref, w_ref,
    gmid_ref, go_ref, do_ref, gg_ref
):
    half = px_ref.shape[0]
    wide = lambda v: v.astype(jnp.float32)
    db = jnp.concatenate(
        [
            keep_ref[:half] + wide(fx_ref[:half]) + wide(py_ref[...]),
            keep_ref[half:] + wide(fy_ref[:half]) + wide(px_ref[...]),
        ],
        axis=0,
    )
    middle = mid_ref[...]
    factor = lax.rsqrt(jnp.mean(middle * middle, axis=-1, keepdims=True) + EPS)
    scaled = db * gain_ref[...]
    inner = jnp.mean(scaled * middle, axis=-1, keepdims=True)
    grad = cot_ref[...].astype(jnp.float32) + factor * scaled - middle * (factor**3 * inner)
    gmid_ref[...] = grad
    gg_ref[...] = jnp.sum(db * middle * factor, axis=0, keepdims=True)
    low = grad.astype(jnp.bfloat16)
    go_ref[...] = low
    back = dotf(low, w_ref[...], ((1,), (0,)))
    half = do_ref.shape[1]
    for r in range(rows):
        for z in range(parts):
            cols = slice(z * 3 * LN, (z + 1) * 3 * LN)
            at = 2 * r * half
            left, right = split_pairs(back[at : at + half, cols], back[at + half : at + 2 * half, cols])
            do_ref[r * parts + z] = left.astype(jnp.bfloat16)
            do_ref[(rows + r) * parts + z] = right.astype(jnp.bfloat16)


def mid_back_call(pieces, middle, cot, gain, weight, rows, parts):
    count, width = middle.shape
    operands = (*pieces, middle, cot, gain, weight)
    shapes = [
        jax.ShapeDtypeStruct((count, width), jnp.float32),
        jax.ShapeDtypeStruct((count, width), jnp.bfloat16),
        jax.ShapeDtypeStruct((2 * rows * parts, count // rows // 2, 3 * LN), jnp.bfloat16),
        jax.ShapeDtypeStruct((1, width), jnp.float32),
    ]
    return pl.pallas_call(
        partial(mid_back_kernel, rows, parts),
        grid=(1,),
        in_specs=[pl.BlockSpec((count, width), lambda i: (0, 0))] + [full_spec(v) for v in operands[1:]],
        out_specs=[full_spec(v) for v in shapes],
        out_shape=shapes,
        compiler_params=pltpu.CompilerParams(vmem_limit_bytes=48 << 20),
        name="mid_back",
    )(*operands)


def da_kernel(parts, rows, place_ref, *refs):
    blocks = refs[:parts]
    d_ref, w_ref, da_ref, gg_ref = refs[parts:]
    tokens = blocks[0].shape[0] // rows
    groups = d_ref.shape[0]
    total = jnp.zeros(gg_ref.shape, jnp.float32)
    for k in range(parts):
        z = lax.rem(place_ref[0] + (parts - k), parts)
        at = pl.ds(pl.multiple_of(z * tokens, tokens), tokens)
        left = jnp.concatenate(
            [jnp.concatenate([d_ref[g, r, at, :] for r in range(rows)], axis=0) for g in range(groups)],
            axis=1,
        )
        back = dotf(left, w_ref[...], ((1,), (1,)))
        stream = blocks[k][...].astype(jnp.float32)
        factor = lax.rsqrt(jnp.mean(stream * stream, axis=-1, keepdims=True) + EPS)
        total = total + jnp.sum(back * stream * factor, axis=0, keepdims=True)
        count = rows * tokens
        da_ref[pl.ds(pl.multiple_of(z * count, count), count), :] = back.astype(jnp.bfloat16)
    gg_ref[...] = total


def da_call(place, blocks, grads, weight, rows):
    parts = len(blocks)
    count, width = blocks[0].shape
    operands = (*blocks, grads, weight)
    shapes = [
        jax.ShapeDtypeStruct((parts * count, width), jnp.bfloat16),
        jax.ShapeDtypeStruct((1, width), jnp.float32),
    ]
    return pl.pallas_call(
        partial(da_kernel, parts, rows),
        grid=(1,),
        in_specs=[pl.BlockSpec(memory_space=pltpu.SMEM)] + [full_spec(v) for v in operands],
        out_specs=[full_spec(v) for v in shapes],
        out_shape=shapes,
        compiler_params=pltpu.CompilerParams(vmem_limit_bytes=48 << 20),
        name="da_part",
    )(place, *operands)


def cut_kernel(gate_ref, up_ref, down_ref, out_ref):
    for n in range(out_ref.shape[0]):
        at = slice(n * LN, (n + 1) * LN)
        out_ref[n, :, :LN] = gate_ref[:, at]
        out_ref[n, :, LN : 2 * LN] = up_ref[:, at]
        out_ref[n, :, 2 * LN :] = jnp.transpose(down_ref[at, :].astype(jnp.float32)).astype(jnp.bfloat16)


def cut_call(gate, up, down):
    shape = jax.ShapeDtypeStruct((gate.shape[1] // LN, gate.shape[0], 3 * LN), jnp.bfloat16)
    operands = (gate, up, down)
    return pl.pallas_call(
        cut_kernel,
        grid=(1,),
        in_specs=[full_spec(v) for v in operands],
        out_specs=full_spec(shape),
        out_shape=shape,
        name="cut_units",
    )(*operands)


def uncut_kernel(in_ref, gate_ref, up_ref, down_ref):
    for n in range(in_ref.shape[0]):
        at = slice(n * LN, (n + 1) * LN)
        gate_ref[:, at] = in_ref[n, :, :LN].astype(jnp.float32)
        up_ref[:, at] = in_ref[n, :, LN : 2 * LN].astype(jnp.float32)
        down_ref[at, :] = jnp.transpose(in_ref[n, :, 2 * LN :].astype(jnp.float32))


def uncut_call(value):
    units, rows = value.shape[0] * LN, value.shape[1]
    shapes = [jax.ShapeDtypeStruct(s, jnp.float32) for s in ((rows, units), (rows, units), (units, rows))]
    return pl.pallas_call(
        uncut_kernel,
        grid=(1,),
        in_specs=[full_spec(value)],
        out_specs=[full_spec(v) for v in shapes],
        out_shape=shapes,
        name="uncut_units",
    )(value)


def place_kernel(parts, at_ref, mine_ref, other_ref, out_ref):
    size = mine_ref.shape[1]
    z = at_ref[3]
    for c, ref in enumerate((mine_ref, other_ref)):
        for n in range(parts):
            y, x = at_ref[0] ^ (n // 2), at_ref[1] ^ (n % 2)
            rows = pl.multiple_of(((y * 2 + x) * 2 + (at_ref[2] ^ c)) * size, size)
            for k in range(ref.shape[0] // parts):
                count = ref.shape[0] // parts
                source = lax.rem(z + (count - k), count)
                cols = pl.multiple_of(source * 3 * LN, 3 * LN)
                out_ref[pl.ds(rows, size), pl.ds(cols, 3 * LN)] = ref[n * count + k]


def place_call(at, mine, other):
    size = mine.shape[1]
    shape = jax.ShapeDtypeStruct((8 * size, mine.shape[0] // 4 * mine.shape[2]), mine.dtype)
    return pl.pallas_call(
        partial(place_kernel, 4),
        grid=(1,),
        in_specs=[pl.BlockSpec(memory_space=pltpu.SMEM), full_spec(mine), full_spec(other)],
        out_specs=full_spec(shape),
        out_shape=shape,
        compiler_params=pltpu.CompilerParams(vmem_limit_bytes=32 << 20),
        name="place_out",
    )(at, mine, other)


def fill_square(refs, out_ref):
    own, xn, yn, first, last = refs
    half = first.shape[0]
    out_ref[0, :half], out_ref[0, half:] = own[:half], own[half:]
    out_ref[1, :half], out_ref[1, half:] = xn[:half], first[...]
    out_ref[2, :half], out_ref[2, half:] = yn[half:], last[...]
    out_ref[3, :half], out_ref[3, half:] = xn[half:], yn[:half]


def down_back_kernel(*refs):
    pieces, (w0_ref, w1_ref, out_ref, g_s) = refs[:5], refs[5:]

    @pl.when(pl.program_id(0) == 0)
    def _():
        fill_square(pieces, g_s)

    weight = jnp.concatenate([w0_ref[0, :, 2 * LN :], w1_ref[0, :, 2 * LN :]], axis=1)

    def body(m, carry):
        out_ref[0, m] = dotf(g_s[m], weight, ((1,), (0,)))
        return carry

    lax.fori_loop(0, 4, body, 0)


def unit_spec(weight):
    return pl.BlockSpec((1,) + weight.shape[1:], lambda z: (z, 0, 0))


def down_back_call(pieces, mine, other):
    count, width = pieces[0].shape
    parts = mine.shape[0]
    shape = jax.ShapeDtypeStruct((parts, 4, count, 2 * LN), jnp.float32)
    return pl.pallas_call(
        down_back_kernel,
        grid=(parts,),
        in_specs=[full_spec(v) for v in pieces] + [unit_spec(mine), unit_spec(other)],
        out_specs=pl.BlockSpec((1, 4, count, 2 * LN), lambda z: (z, 0, 0, 0)),
        out_shape=shape,
        scratch_shapes=[pltpu.VMEM((4, count, width), jnp.bfloat16)],
        compiler_params=pltpu.CompilerParams(vmem_limit_bytes=40 << 20),
        name="down_back",
    )(*pieces, mine, other)


def emit_square(acc_ref, keep_ref, sx_ref, sy_ref):
    count = sx_ref.shape[0]
    keep_ref[:count] = acc_ref[0]
    keep_ref[count:] = acc_ref[3]
    sx_ref[...] = acc_ref[1].astype(jnp.bfloat16)
    sy_ref[...] = acc_ref[2].astype(jnp.bfloat16)


def units_kernel(*refs):
    pieces, (w0_ref, w1_ref, dh_ref) = refs[:5], refs[5:8]
    dgu_ref, hid_ref, keep_ref, sx_ref, sy_ref, b_s, acc_s = refs[8:]
    step = pl.program_id(0)

    @pl.when(step == 0)
    def _():
        fill_square(pieces, b_s)

    def body(m, carry):
        b = b_s[m]
        total = None
        for n, w_ref in enumerate((w0_ref, w1_ref)):
            weight = w_ref[0, :, : 2 * LN]
            both = dotf(b, weight, ((1,), (0,)))
            gate, up = both[:, :LN], both[:, LN:]
            dh = dh_ref[0, m, :, n * LN : (n + 1) * LN]
            sigma = 1.0 / (1.0 + jnp.exp(-gate))
            silu = gate * sigma
            hid_ref[0, m, :, n * LN : (n + 1) * LN] = (silu * up).astype(jnp.bfloat16)
            grad_gate = dh * up * sigma * (1.0 + gate * (1.0 - sigma))
            grads = jnp.concatenate([grad_gate, dh * silu], axis=1).astype(jnp.bfloat16)
            dgu_ref[0, n, m] = grads
            back = dotf(grads, weight, ((1,), (1,)))
            total = back if total is None else total + back

        @pl.when(step == 0)
        def _():
            acc_s[m] = total

        @pl.when(step > 0)
        def _():
            acc_s[m] += total

        return carry

    lax.fori_loop(0, 4, body, 0)

    @pl.when(step == pl.num_programs(0) - 1)
    def _():
        emit_square(acc_s, keep_ref, sx_ref, sy_ref)


def square_shapes(count, width):
    return [
        jax.ShapeDtypeStruct((2 * count, width), jnp.float32),
        jax.ShapeDtypeStruct((count, width), jnp.bfloat16),
        jax.ShapeDtypeStruct((count, width), jnp.bfloat16),
    ]


def units_call(pieces, mine, other, grad_hidden):
    count, width = pieces[0].shape
    parts = mine.shape[0]
    low = jnp.bfloat16
    shapes = [
        jax.ShapeDtypeStruct((parts, 2, 4, count, 2 * LN), low),
        jax.ShapeDtypeStruct((parts, 4, count, 2 * LN), low),
    ] + square_shapes(count, width)
    return pl.pallas_call(
        units_kernel,
        grid=(parts,),
        in_specs=[full_spec(v) for v in pieces]
        + [unit_spec(mine), unit_spec(other), pl.BlockSpec((1, 4, count, 2 * LN), lambda z: (z, 0, 0, 0))],
        out_specs=[
            pl.BlockSpec((1, 2, 4, count, 2 * LN), lambda z: (z, 0, 0, 0, 0)),
            pl.BlockSpec((1, 4, count, 2 * LN), lambda z: (z, 0, 0, 0)),
        ]
        + [full_spec(v) for v in shapes[2:]],
        out_shape=shapes,
        scratch_shapes=[pltpu.VMEM((4, count, width), low), pltpu.VMEM((4, count, width), jnp.float32)],
        compiler_params=pltpu.CompilerParams(vmem_limit_bytes=56 << 20),
        name="units",
    )(*pieces, mine, other, grad_hidden)


def down_kernel(hid_ref, w0_ref, w1_ref, keep_ref, sx_ref, sy_ref, acc_s):
    step = pl.program_id(0)
    weight = jnp.concatenate([w0_ref[0, :, 2 * LN :], w1_ref[0, :, 2 * LN :]], axis=1)

    def body(m, carry):
        total = dotf(hid_ref[0, m], weight, ((1,), (1,)))

        @pl.when(step == 0)
        def _():
            acc_s[m] = total

        @pl.when(step > 0)
        def _():
            acc_s[m] += total

        return carry

    lax.fori_loop(0, 4, body, 0)

    @pl.when(step == pl.num_programs(0) - 1)
    def _():
        emit_square(acc_s, keep_ref, sx_ref, sy_ref)


def down_call(hidden, mine, other):
    parts, _, count, _ = hidden.shape
    width = mine.shape[1]
    shapes = square_shapes(count, width)
    return pl.pallas_call(
        down_kernel,
        grid=(parts,),
        in_specs=[pl.BlockSpec((1,) + hidden.shape[1:], lambda z: (z, 0, 0, 0)), unit_spec(mine), unit_spec(other)],
        out_specs=[full_spec(v) for v in shapes],
        out_shape=shapes,
        scratch_shapes=[pltpu.VMEM((4, count, width), jnp.float32)],
        compiler_params=pltpu.CompilerParams(vmem_limit_bytes=40 << 20),
        name="down",
    )(hidden, mine, other)


def unit_grads_kernel(*refs):
    b_pieces, g_pieces = refs[:5], refs[5:10]
    dgu_ref, hid_ref, out_ref, fill_s, b_s, g_s = refs[10:]
    count = fill_s.shape[1]

    @pl.when(pl.program_id(0) == 0)
    def _():
        for pieces, side in ((b_pieces, b_s), (g_pieces, g_s)):
            fill_square(pieces, fill_s)
            for m in range(4):
                side[:, m * count : (m + 1) * count] = jnp.transpose(fill_s[m])

    hidden = hid_ref[0].reshape(4 * count, 2 * LN)
    grads = [dgu_ref[0, n].reshape(4 * count, 2 * LN) for n in range(2)]
    rows = b_s.shape[0] // 4

    def body(m, carry):
        at = pl.ds(pl.multiple_of(m * rows, rows), rows)
        left, right = b_s[at, :], g_s[at, :]
        down = dotf(right, hidden, ((1,), (0,)))
        for n in range(2):
            out_ref[n, 0, at, : 2 * LN] = dotf(left, grads[n], ((1,), (0,))).astype(jnp.bfloat16)
            out_ref[n, 0, at, 2 * LN :] = down[:, n * LN : (n + 1) * LN].astype(jnp.bfloat16)
        return carry

    lax.fori_loop(0, 4, body, 0)


def unit_grads_call(b_pieces, g_pieces, grads, hidden):
    count, width = b_pieces[0].shape
    parts = hidden.shape[0]
    low = jnp.bfloat16
    operands = (*b_pieces, *g_pieces)
    return pl.pallas_call(
        unit_grads_kernel,
        grid=(parts,),
        in_specs=[full_spec(v) for v in operands]
        + [
            pl.BlockSpec((1,) + grads.shape[1:], lambda z: (z, 0, 0, 0, 0)),
            pl.BlockSpec((1,) + hidden.shape[1:], lambda z: (z, 0, 0, 0)),
        ],
        out_specs=pl.BlockSpec((2, 1, width, 3 * LN), lambda z: (0, z, 0, 0)),
        out_shape=jax.ShapeDtypeStruct((2, parts, width, 3 * LN), low),
        scratch_shapes=[pltpu.VMEM((4, count, width), low)] + [pltpu.VMEM((width, 4 * count), low)] * 2,
        compiler_params=pltpu.CompilerParams(vmem_limit_bytes=56 << 20),
        name="unit_grads",
    )(*operands, grads, hidden)


def qkv_grads_kernel(a_ref, d_ref, out_ref):
    left = jnp.transpose(a_ref[...])
    for g in range(d_ref.shape[0]):
        cols = slice(g * 3 * LN, (g + 1) * 3 * LN)
        out_ref[:, cols] = dotf(left, d_ref[g], ((1,), (0,))).astype(out_ref.dtype)


def qkv_grads_call(normed, grads):
    count, width = normed.shape
    shape = jax.ShapeDtypeStruct((width, grads.shape[0] * 3 * LN), jnp.bfloat16)
    tile = 2 * LN
    return pl.pallas_call(
        qkv_grads_kernel,
        grid=(width // tile,),
        in_specs=[pl.BlockSpec((count, tile), lambda i: (0, i)), full_spec(grads)],
        out_specs=pl.BlockSpec((tile, shape.shape[1]), lambda i: (i, 0)),
        out_shape=shape,
        compiler_params=pltpu.CompilerParams(vmem_limit_bytes=32 << 20),
        name="qkv_grads",
    )(normed, grads)


def out_grads_kernel(at_ref, go_ref, o_ref, out_ref, full_s):
    tile = 2 * LN
    right = o_ref[...]
    for n in range(full_s.shape[0] // tile):
        left = jnp.transpose(go_ref[:, n * tile : (n + 1) * tile])
        full_s[n * tile : (n + 1) * tile, :] = dotf(left, right, ((1,), (0,))).astype(jnp.bfloat16)
    half = out_ref.shape[2]
    size = 2 * half
    order = ((0, 0, 0), (0, 0, 1), (0, 1, 0), (1, 1, 0), (1, 0, 1), (1, 1, 1), (0, 1, 1), (1, 0, 0))
    for c in range(2):
        for n, (y, x, last) in enumerate(order):
            block = ((at_ref[0] ^ y) * 2 + (at_ref[1] ^ x)) * 2 + (at_ref[2] ^ c)
            rows = pl.multiple_of(block * size + last * half, 32)
            out_ref[c, n] = full_s[pl.ds(rows, half), :]


def out_grads_call(at, grad, attended):
    width, inner = grad.shape[1], attended.shape[1]
    shape = jax.ShapeDtypeStruct((2, 8, width // 16, inner), jnp.bfloat16)
    return pl.pallas_call(
        out_grads_kernel,
        grid=(1,),
        in_specs=[pl.BlockSpec(memory_space=pltpu.SMEM), full_spec(grad), full_spec(attended)],
        out_specs=full_spec(shape),
        out_shape=shape,
        scratch_shapes=[pltpu.VMEM((width, inner), jnp.bfloat16)],
        compiler_params=pltpu.CompilerParams(vmem_limit_bytes=32 << 20),
        name="out_grads",
    )(at, grad, attended)


EVERY = ("y", "x", "c", "z")
SWAP = ((0, 1), (1, 0))


def swap(value, axis):
    return lax.ppermute(value, axis, SWAP)


def gather_blocks(value, size):
    shift = lambda k: [(i, (i + k) % size) for i in range(size)]
    order = sorted(range(1, size), key=lambda k: -min(k, size - k))
    got = {k: lax.ppermute(value, "z", shift(k)) for k in order}
    return [value] + [got[k] for k in range(1, size)]


def gather_square(value):
    half = value.shape[0] // 2
    xn, yn = swap(value, "x"), swap(value, "y")
    return value, xn, yn, swap(yn[:half], "x"), swap(xn[half:], "y")


def reduce_square(keep, send_x, send_y):
    low = jnp.bfloat16
    half = send_x.shape[0] // 2
    from_x, from_y = swap(send_x, "x"), swap(send_y, "y")
    pass_y = swap((keep[3 * half :] + from_x[half:].astype(jnp.float32)).astype(low), "y")
    pass_x = swap((keep[2 * half : 3 * half] + from_y[half:].astype(jnp.float32)).astype(low), "x")
    return keep, from_x, from_y, pass_x, pass_y


def total_square(pieces):
    keep, from_x, from_y, pass_x, pass_y = pieces
    half = pass_x.shape[0]
    wide = lambda v: v.astype(jnp.float32)
    return jnp.concatenate(
        [
            keep[:half] + wide(from_x[:half]) + wide(pass_y),
            keep[half : 2 * half] + wide(from_y[:half]) + wide(pass_x),
        ],
        axis=0,
    )


def reduce_line(part, at, size):
    block = lambda k: lax.dynamic_index_in_dim(part, jnp.clip(at + k, 0, size - 1), 0, keepdims=False)
    wide = lambda v: v.astype(jnp.float32)
    up, down = None, None
    for step in range(1, size):
        k = size - step
        send_up, send_down = block(k), block(-k)
        if up is not None:
            send_up = (wide(send_up) + wide(up)).astype(part.dtype)
            send_down = (wide(send_down) + wide(down)).astype(part.dtype)
        up = lax.ppermute(send_up, "z", [(i, i + 1) for i in range(step)])
        down = lax.ppermute(send_down, "z", [(size - 1 - i, size - 2 - i) for i in range(step)])
    return wide(block(0)) + wide(up) + wide(down)


def all_to_all(value, axes):
    return lax.all_to_all(value, axes, 0, 0, tiled=True)


def tie(*values):
    return lax.optimization_barrier(values)


def fast_local(sizes, *args):
    (tokens, cotangent, segments, positions, norm_in, w_query, w_key, w_value, w_out, norm_mid, w_gate, w_up, w_down) = args
    nz = sizes["z"]
    devices = sizes["y"] * sizes["x"] * sizes["c"] * nz
    plane = devices // nz
    rows, span, width = tokens.shape
    count = rows * span
    chunk = segments.shape[1]
    length = chunk * sizes["x"] * sizes["c"]
    x_at, c_at, z_at = lax.axis_index("x"), lax.axis_index("c"), lax.axis_index("z")
    place = z_at.reshape(1).astype(jnp.int32)
    at = jnp.stack([lax.axis_index("y"), x_at, c_at, z_at]).astype(jnp.int32)

    own = tokens.reshape(count, width)
    blocks = gather_blocks(own, nz)

    gains = jnp.concatenate([norm_in, norm_mid], axis=1)
    share = norm_in.shape[1]
    gains = jnp.pad(gains, ((0, 0), (0, LN - 2 * share)))
    gains = all_to_all(jnp.broadcast_to(gains, (devices, LN)), EVERY)
    gain_in = gains[:, :share].reshape(1, width)
    gain_mid = gains[:, share : 2 * share].reshape(1, width)

    kv_local = w_key.shape[2] // HD
    per_head = lambda w: w[0].reshape(w.shape[1], kv_local, -1)
    w_qkv = jnp.concatenate([per_head(w_query), per_head(w_key), per_head(w_value)], axis=2)
    w_qkv = w_qkv.reshape(w_qkv.shape[0], -1)
    w_qkv = lax.all_gather(w_qkv, ("y", "x", "c"), axis=0, tiled=True)

    gate, up, down, early = tie(w_gate[0], w_up[0], w_down[0], blocks[1])
    w_ff = all_to_all(cut_call(gate, up, down), ("y", "x", "c"))
    w_ff = w_ff.reshape(width, 3 * LN)

    last = (x_at * sizes["c"] + c_at + 1) * chunk - 1
    begin = last - positions[:, -1] - jnp.where(segments[:, -1] == 2, 3 * length // 4, 0)
    lanes = jnp.arange(LN, dtype=jnp.int32) % (HD // 2)
    frequency = THETA ** (-(2.0 * lanes.astype(jnp.float32)) / HD)
    token_angle = positions.astype(jnp.float32)[:, :, None] * frequency
    first = lax.dynamic_slice_in_dim(begin, c_at, 1).astype(jnp.int32)
    index = jnp.arange(length, dtype=jnp.int32)
    row_angle = (index - doc_low(index, first[0], length)).astype(jnp.float32)[:, None] * frequency
    token_cos, token_sin = jnp.cos(token_angle), jnp.sin(token_angle)
    row_cos, row_sin = jnp.cos(row_angle), jnp.sin(row_angle)

    normed, qkv = qkv_call(place, blocks, gain_in, w_qkv, token_cos, token_sin, rows)
    w_ff, w_o, *_ = tie(w_ff, w_out[0].T, *blocks)
    qkv = all_to_all(qkv, ("x", "c")).reshape(length, 3 * LN)

    w_mine = lax.all_gather(w_ff, "z", axis=0, tiled=True).reshape(nz, width, 3 * LN)
    w_other = swap(w_mine, "c")
    w_o = jnp.stack(gather_blocks(w_o, nz))
    cot_low = cotangent.reshape(count, width)
    cot_low, w_o, _ = tie(cot_low, w_o, qkv)
    own_o, xn_o, yn_o, first_o, last_o = gather_square(w_o)
    w_o = jnp.concatenate([own_o, xn_o, yn_o, first_o, last_o], axis=0)
    w_o = place_call(at, w_o, swap(w_o, "c"))
    cot_pieces = gather_square(cot_low)

    attended, attended_float, log_total = attn_fwd(first, qkv)
    attended = all_to_all(attended, ("x", "c", "z"))
    middle, normed_b, attended_low = out_call(attended, w_o, own, gain_mid, rows)
    b_pieces = gather_square(normed_b)

    grad_hidden = down_back_call(cot_pieces, w_mine, w_other)
    grad_gu, hidden, *sends = units_call(b_pieces, w_mine, w_other, grad_hidden)
    grad_b = reduce_square(*sends)
    grad_ff = unit_grads_call(b_pieces, cot_pieces, grad_gu, hidden)
    grad_ff = grad_ff.reshape(2, nz * width, 3 * LN)
    grad_ff = (grad_ff[0].astype(jnp.float32) + swap(grad_ff[1], "c").astype(jnp.float32)).astype(jnp.bfloat16)
    grad_ff = lax.psum_scatter(grad_ff, "z", scatter_dimension=0, tiled=True)
    grad_ff = all_to_all(grad_ff.reshape(plane, width // plane, 3 * LN), ("y", "x", "c"))

    grad_mid, grad_low, grad_o, gain_grad_mid = mid_back_call(
        grad_b, middle, cot_low, gain_mid, w_o, rows, nz
    )
    hidden, grad_o = tie(hidden, grad_o)
    grad_o = all_to_all(grad_o, ("x", "c", "z"))
    out = middle + total_square(reduce_square(*down_call(hidden, w_mine, w_other)))

    grad_wo = out_grads_call(at, grad_low, attended_low)
    grad_wo = grad_wo[0].astype(jnp.float32) + swap(grad_wo[1], "c").astype(jnp.float32)
    step = width // 16
    flat_wo = grad_wo.reshape(8 * step, -1)
    keep_wo = jnp.concatenate([flat_wo[: 2 * step], flat_wo[6 * step :]], axis=0)
    grad_wo = total_square(
        reduce_square(
            keep_wo,
            flat_wo[2 * step : 4 * step].astype(jnp.bfloat16),
            flat_wo[4 * step : 6 * step].astype(jnp.bfloat16),
        )
    ).astype(jnp.bfloat16)
    grad_wo = jnp.stack([grad_wo[:, z * 3 * LN : (z + 1) * 3 * LN] for z in range(nz)])
    grad_wo = jnp.sum(all_to_all(grad_wo, "z").astype(jnp.float32), axis=0)

    grad_qkv = attn_bwd(first, qkv, grad_o, attended_float, log_total, row_cos, row_sin)
    grad_qkv = all_to_all(grad_qkv.reshape(-1, chunk, 3 * LN), ("x", "c"))
    grad_qkv = grad_qkv.reshape(kv_local, rows, chunk, 3 * LN)
    part, gain_grad_in = da_call(place, blocks, grad_qkv, w_qkv, rows)
    grad_wqkv = qkv_grads_call(
        normed.reshape(rows * chunk, width), grad_qkv.reshape(kv_local, rows * chunk, 3 * LN)
    )
    grad_wqkv = lax.psum_scatter(grad_wqkv, ("y", "x", "c"), scatter_dimension=0, tiled=True)
    grad_a = reduce_line(part.reshape(nz, count, width), z_at, nz)

    gain_grads = jnp.concatenate(
        [gain_grad_in.reshape(devices, share), gain_grad_mid.reshape(devices, share)], axis=1
    )
    gain_grads = jnp.pad(gain_grads, ((0, 0), (0, LN - 2 * share)))
    gain_grads = jnp.sum(all_to_all(gain_grads, EVERY), axis=0, keepdims=True)

    stream = own.astype(jnp.float32)
    factor = lax.rsqrt(jnp.mean(stream * stream, axis=-1, keepdims=True) + EPS)
    back_in, _ = norm_back(stream, factor, gain_in, grad_a)
    grad_tokens = grad_mid + back_in
    grad_wqkv = grad_wqkv.astype(jnp.float32).reshape(-1, kv_local, 4 * HD)
    flat = lambda g: g.reshape(1, g.shape[0], -1)
    grad_gate, grad_up, grad_down = uncut_call(grad_ff)
    return (
        out.reshape(tokens.shape),
        grad_tokens.reshape(tokens.shape),
        gain_grads[:, :share],
        flat(grad_wqkv[:, :, : 2 * HD]),
        flat(grad_wqkv[:, :, 2 * HD : 3 * HD]),
        flat(grad_wqkv[:, :, 3 * HD :]),
        grad_wo.T[None],
        gain_grads[:, share : 2 * share],
        grad_gate[None],
        grad_up[None],
        grad_down[None],
    )


def fast_solution(mesh, cores):
    batch, seq, kv = mesh.devices.shape
    fine = Mesh(mesh.devices.reshape(batch, seq // cores, cores, kv), EVERY)
    sizes = dict(fine.shape)
    row_spec = P("y", ("x", "c", "z"), None)
    seq_spec = P("y", ("x", "c"))
    gain_spec = P(None, EVERY)
    in_w = P(None, ("y", "x", "c"), "z")
    out_w = P(None, "z", ("y", "x", "c"))
    in_specs = (row_spec, row_spec, seq_spec, seq_spec, gain_spec, in_w, in_w, in_w, out_w, gain_spec, in_w, in_w, out_w)
    out_specs = (row_spec, row_spec, gain_spec, in_w, in_w, in_w, out_w, gain_spec, in_w, in_w, out_w)
    return jax.shard_map(
        partial(fast_local, sizes), mesh=fine, in_specs=in_specs, out_specs=out_specs, check_vma=False
    )


def solution(mesh):
    batch, seq, kv = (mesh.shape[name] for name in ("batch", "seq", "kv"))
    general = general_solution(mesh)
    if (batch, seq) != (2, 4):
        return general
    fast = fast_solution(mesh, 2)

    def run(*args):
        rows, length, width = args[0].shape
        kv_heads, q_heads = args[6].shape[2] // HD, args[5].shape[2] // HD
        fits = (
            rows == 2 * batch
            and kv_heads == 2 * kv
            and q_heads == 2 * kv_heads
            and length == 128 * seq * kv
            and length % (4 * BQ) == 0
            and width % LN == 0
            and 2 * width // (batch * seq * kv) <= LN
            and args[10].shape[2] == LN * batch * seq * kv
        )
        return (fast if fits else general)(*args)

    return run
```

```python
import functools
import math
from functools import partial

import jax
import jax.numpy as jnp
from jax import lax
from jax.experimental import pallas as pl
from jax.experimental.pallas import tpu as pltpu
from jax.sharding import Mesh
from jax.sharding import PartitionSpec as P

HD = 96
LAYERS = 1


EPS = 1e-05
THETA = 100000.0
BIG_NEG = -1e30


def rotary(positions_row):
    half_width = HD // 2
    frequency = THETA ** (-(2.0 * jnp.arange(half_width, dtype=jnp.float32)) / HD)
    angles = positions_row.astype(jnp.float32)[:, None] * frequency[None, :]
    cosine = jnp.concatenate([jnp.cos(angles), jnp.cos(angles)], axis=1)
    sine_table = jnp.concatenate([jnp.sin(angles), jnp.sin(angles)], axis=1)
    return (cosine, sine_table)


def rotate(head_vals, cosine, sine_table):
    half_width = head_vals.shape[-1] // 2
    swapped = jnp.concatenate([-head_vals[..., half_width:], head_vals[..., :half_width]], axis=-1)
    return head_vals * cosine[:, None, :] + swapped * sine_table[:, None, :]


def rms_norm(stream, gain):
    factor = lax.rsqrt(jnp.mean(stream * stream, axis=-1, keepdims=True) + EPS)
    return (stream * factor * gain, factor)


def norm_back(stream, factor, gain, upstream):
    scaled_grad = upstream * gain
    inner_mean = jnp.mean(scaled_grad * stream, axis=-1, keepdims=True)
    grad_stream = factor * scaled_grad - stream * factor**3 * inner_mean
    return (grad_stream, jnp.sum(upstream * stream * factor, axis=0))


def key_width(key_count):
    return math.gcd(key_count, 1024)


def contract(left_side, right_side, left_dim, right_dim):
    return lax.dot_general(
        left_side,
        right_side,
        (((left_dim,), (right_dim,)), ((), ())),
        preferred_element_type=jnp.float32,
    )


def spread(shard_rows):
    return lax.all_gather(shard_rows, "kv", axis=0, tiled=True)


def token_sum(pairs):
    summed = None
    for left_part, right_part, right_dim in pairs:
        product = contract(left_part, right_part, 1, right_dim)
        summed = product if summed is None else summed + product
    return lax.psum_scatter(
        summed.astype(jnp.bfloat16), "kv", scatter_dimension=0, tiled=True
    ).astype(jnp.float32)


def split_block(kv_both, seg_keys, offset, step_width, kv_local, head_size):
    kv_block = lax.dynamic_slice_in_dim(kv_both, offset, step_width, 0)
    key_block = kv_block[:, : kv_local * head_size].reshape(step_width, kv_local, head_size)
    value_block = kv_block[:, kv_local * head_size :].reshape(step_width, kv_local, head_size)
    seg_block = lax.dynamic_slice_in_dim(seg_keys, offset, step_width, 0)
    return (key_block, value_block, seg_block)


def forward_row(queries, seg_query, fold_state, kv_both, seg_keys, first_query, key_start):
    key_count = kv_both.shape[0]
    step_width = key_width(key_count)
    query_count, kv_local, group_size, head_size = queries.shape
    query_index = first_query + jnp.arange(query_count, dtype=jnp.int32)
    score_scale = head_size ** (-0.5)

    def forward_one_step(step_index, inner_state):
        running_max, weight_total, value_total = inner_state
        offset = step_index * step_width
        key_block, value_block, seg_block = split_block(
            kv_both, seg_keys, offset, step_width, kv_local, head_size
        )
        key_index = offset + jnp.arange(step_width, dtype=jnp.int32)
        allowed = (seg_query[:, None] == seg_block[None, :]) & (
            key_index[None, :] <= query_index[:, None]
        )
        scores = (
            jnp.einsum("qkgd,pkd->kgqp", queries, key_block, preferred_element_type=jnp.float32)
            * score_scale
        )
        scores = jnp.where(allowed, scores, BIG_NEG)
        new_max = jnp.maximum(running_max, jnp.max(scores, axis=-1))
        weights = jnp.where(allowed, jnp.exp(scores - new_max[..., None]), 0.0)
        rescale = jnp.exp(running_max - new_max)
        weight_total = rescale * weight_total + jnp.sum(weights, axis=-1)
        update = jnp.einsum(
            "kgqp,pkd->qkgd",
            weights.astype(jnp.bfloat16),
            value_block,
            preferred_element_type=jnp.float32,
        )
        value_total = jnp.transpose(rescale, (2, 0, 1))[..., None] * value_total + update
        return (new_max, weight_total, value_total)

    return lax.fori_loop(0, key_count // step_width, forward_one_step, fold_state)


def forward_fold(queries, seg_query, first_query, fold_state, pieces, key_start):
    kv_both, seg_keys = pieces
    row_fn = partial(forward_row, first_query=first_query, key_start=key_start)
    return jax.vmap(row_fn, in_axes=(0, 0, 0, 1, 1))(
        queries, seg_query, fold_state, kv_both, seg_keys
    )


def backward_row(
    queries,
    grad_attn,
    log_total,
    row_delta,
    seg_query,
    fold_state,
    kv_both,
    seg_keys,
    first_query,
    key_start,
):
    key_count = kv_both.shape[0]
    step_width = key_width(key_count)
    query_count, kv_local, group_size, head_size = queries.shape
    query_index = first_query + jnp.arange(query_count, dtype=jnp.int32)
    score_scale = head_size ** (-0.5)

    def backward_one_step(step_index, inner_state):
        grad_queries, grad_buffer = inner_state
        offset = step_index * step_width
        key_block, value_block, seg_block = split_block(
            kv_both, seg_keys, offset, step_width, kv_local, head_size
        )
        key_index = offset + jnp.arange(step_width, dtype=jnp.int32)
        allowed = (seg_query[:, None] == seg_block[None, :]) & (
            key_index[None, :] <= query_index[:, None]
        )
        scores = (
            jnp.einsum("qkgd,pkd->kgqp", queries, key_block, preferred_element_type=jnp.float32)
            * score_scale
        )
        probs_block = jnp.where(allowed, jnp.exp(scores - log_total[..., None]), 0.0)
        grad_probs = jnp.einsum(
            "qkgd,pkd->kgqp", grad_attn, value_block, preferred_element_type=jnp.float32
        )
        grad_scores = (probs_block * (grad_probs - row_delta[..., None])).astype(jnp.bfloat16)
        grad_queries = (
            grad_queries
            + jnp.einsum(
                "kgqp,pkd->qkgd", grad_scores, key_block, preferred_element_type=jnp.float32
            )
            * score_scale
        )
        grad_keys = (
            jnp.einsum("kgqp,qkgd->pkd", grad_scores, queries, preferred_element_type=jnp.float32)
            * score_scale
        )
        grad_values = jnp.einsum(
            "kgqp,qkgd->pkd",
            probs_block.astype(jnp.bfloat16),
            grad_attn,
            preferred_element_type=jnp.float32,
        )
        joined = jnp.concatenate(
            [grad_keys.reshape(step_width, -1), grad_values.reshape(step_width, -1)], axis=1
        )
        grad_buffer = lax.dynamic_update_slice_in_dim(grad_buffer, joined, offset, 0)
        return (grad_queries, grad_buffer)

    return lax.fori_loop(0, key_count // step_width, backward_one_step, fold_state)


def backward_fold(
    queries, grad_attn, log_total, row_delta, seg_query, first_query, fold_state, pieces, key_start
):
    kv_both, seg_keys = pieces
    row_fn = partial(backward_row, first_query=first_query, key_start=key_start)
    return jax.vmap(row_fn, in_axes=(0, 0, 0, 0, 0, 0, 1, 1))(
        queries, grad_attn, log_total, row_delta, seg_query, fold_state, kv_both, seg_keys
    )


def layer_forward(stream, gain_pair, matrices, seg_info, tables):
    gain_in, gain_mid = gain_pair
    w_query, w_key, w_value, w_out, w_gate, w_up, w_down = matrices
    seg_query, seg_keys = seg_info
    cosine, sine_table = tables
    row_count = seg_query.shape[0]
    kv_local = w_key.shape[1] // HD
    head_local = w_query.shape[1] // HD
    group_size = head_local // kv_local
    normed_a, factor_a = rms_norm(stream, gain_in)
    spread_a = spread(normed_a.astype(jnp.bfloat16))
    flat_count = spread_a.shape[0]
    token_count = flat_count // row_count
    raw_queries = jnp.dot(spread_a, w_query, preferred_element_type=jnp.float32).reshape(
        flat_count, head_local, HD
    )
    queries = (
        rotate(raw_queries, cosine, sine_table)
        .astype(jnp.bfloat16)
        .reshape(token_count, row_count, kv_local, group_size, HD)
    )
    queries = jnp.transpose(queries, (1, 0, 2, 3, 4))
    raw_keys = jnp.dot(spread_a, w_key, preferred_element_type=jnp.float32).reshape(
        flat_count, kv_local, HD
    )
    keys_low = (
        rotate(raw_keys, cosine, sine_table).astype(jnp.bfloat16).reshape(flat_count, kv_local * HD)
    )
    values_low = jnp.dot(spread_a, w_value, preferred_element_type=jnp.float32).astype(jnp.bfloat16)
    kv_both = jnp.concatenate([keys_low, values_low], axis=1).reshape(
        token_count, row_count, 2 * kv_local * HD
    )
    first_query = lax.axis_index("seq") * token_count
    start_state = (
        jnp.full((row_count, kv_local, group_size, token_count), BIG_NEG, jnp.float32),
        jnp.zeros((row_count, kv_local, group_size, token_count), jnp.float32),
        jnp.zeros((row_count, token_count, kv_local, group_size, HD), jnp.float32),
    )
    running_max, weight_total, value_total = forward_fold(
        queries,
        seg_query,
        first_query,
        start_state,
        (
            lax.all_gather(kv_both, "seq", axis=0, tiled=True),
            lax.all_gather(seg_keys, "seq", axis=0, tiled=True),
        ),
        jnp.int32(0),
    )
    attn_float = value_total / jnp.transpose(weight_total, (0, 3, 1, 2))[..., None]
    log_total = running_max + jnp.log(weight_total)
    attn_low = (
        jnp.transpose(attn_float, (1, 0, 2, 3, 4))
        .reshape(flat_count, head_local * HD)
        .astype(jnp.bfloat16)
    )
    stream_mid = stream + token_sum(((attn_low, w_out, 0),))
    normed_b, factor_b = rms_norm(stream_mid, gain_mid)
    spread_b = spread(normed_b.astype(jnp.bfloat16))
    gate_val = jnp.dot(spread_b, w_gate, preferred_element_type=jnp.float32)
    up_val = jnp.dot(spread_b, w_up, preferred_element_type=jnp.float32)
    hidden = (jax.nn.silu(gate_val) * up_val).astype(jnp.bfloat16)
    stream_out = stream_mid + token_sum(((hidden, w_down, 0),))
    saved_state = (
        stream,
        factor_a,
        spread_a,
        queries,
        kv_both,
        attn_float,
        attn_low,
        log_total,
        stream_mid,
        factor_b,
        spread_b,
        gate_val,
        up_val,
        hidden,
    )
    return (stream_out, saved_state)


def layer_backward(saved_state, grad_stream, gain_pair, matrices, seg_info, tables):
    (
        stream,
        factor_a,
        spread_a,
        queries,
        kv_both,
        attn_float,
        attn_low,
        log_total,
        stream_mid,
        factor_b,
        spread_b,
        gate_val,
        up_val,
        hidden,
    ) = saved_state
    gain_in, gain_mid = gain_pair
    w_query, w_key, w_value, w_out, w_gate, w_up, w_down = matrices
    seg_query, seg_keys = seg_info
    cosine, sine_table = tables
    row_count, token_count, kv_local, group_size, head_size = queries.shape
    head_local = kv_local * group_size
    flat_count = row_count * token_count
    grad_low = spread(grad_stream.astype(jnp.bfloat16))
    grad_down_w = contract(hidden, grad_low, 0, 0)
    grad_hidden = contract(grad_low, w_down, 1, 1)
    sigmoid_gate = jax.nn.sigmoid(gate_val)
    silu_gate = gate_val * sigmoid_gate
    grad_gate_low = (
        grad_hidden * up_val * sigmoid_gate * (1.0 + gate_val * (1.0 - sigmoid_gate))
    ).astype(jnp.bfloat16)
    grad_up_low = (grad_hidden * silu_gate).astype(jnp.bfloat16)
    grad_gate_w = contract(spread_b, grad_gate_low, 0, 0)
    grad_up_w = contract(spread_b, grad_up_low, 0, 0)
    grad_normed_b = token_sum(((grad_gate_low, w_gate, 1), (grad_up_low, w_up, 1)))
    back_mid, grad_gain_mid = norm_back(stream_mid, factor_b, gain_mid, grad_normed_b)
    grad_mid = grad_stream + back_mid
    grad_attn_full = spread(grad_mid.astype(jnp.bfloat16))
    grad_out_w = contract(attn_low, grad_attn_full, 0, 0)
    grad_attn = (
        contract(grad_attn_full, w_out, 1, 1)
        .astype(jnp.bfloat16)
        .reshape(token_count, row_count, kv_local, group_size, head_size)
    )
    grad_attn = jnp.transpose(grad_attn, (1, 0, 2, 3, 4))
    row_delta = jnp.transpose(jnp.sum(grad_attn * attn_float, axis=-1), (0, 2, 3, 1))
    first_query = lax.axis_index("seq") * token_count
    row_length = token_count * lax.axis_size("seq")
    start_state = (
        jnp.zeros((row_count, token_count, kv_local, group_size, head_size), jnp.float32),
        jnp.zeros((row_count, row_length, 2 * kv_local * head_size), jnp.float32),
    )
    grad_queries, grad_buffer = backward_fold(
        queries,
        grad_attn,
        log_total,
        row_delta,
        seg_query,
        first_query,
        start_state,
        (
            lax.all_gather(kv_both, "seq", axis=0, tiled=True),
            lax.all_gather(seg_keys, "seq", axis=0, tiled=True),
        ),
        jnp.int32(0),
    )
    grad_kv = lax.psum_scatter(
        grad_buffer.astype(jnp.bfloat16), "seq", scatter_dimension=1, tiled=True
    ).astype(jnp.float32)
    grad_kv = jnp.transpose(grad_kv, (1, 0, 2)).reshape(flat_count, 2 * kv_local * head_size)
    grad_queries = jnp.transpose(grad_queries, (1, 0, 2, 3, 4)).reshape(
        flat_count, head_local, head_size
    )
    grad_q_low = (
        rotate(grad_queries, cosine, -sine_table)
        .astype(jnp.bfloat16)
        .reshape(flat_count, head_local * head_size)
    )
    grad_k_low = (
        rotate(
            grad_kv[:, : kv_local * head_size].reshape(flat_count, kv_local, head_size),
            cosine,
            -sine_table,
        )
        .astype(jnp.bfloat16)
        .reshape(flat_count, kv_local * head_size)
    )
    grad_v_low = grad_kv[:, kv_local * head_size :].astype(jnp.bfloat16)
    grad_query_w = contract(spread_a, grad_q_low, 0, 0)
    grad_key_w = contract(spread_a, grad_k_low, 0, 0)
    grad_value_w = contract(spread_a, grad_v_low, 0, 0)
    grad_normed_a = token_sum(
        ((grad_q_low, w_query, 1), (grad_k_low, w_key, 1), (grad_v_low, w_value, 1))
    )
    back_in, grad_gain_in = norm_back(stream, factor_a, gain_in, grad_normed_a)
    grad_input = grad_mid + back_in
    weight_grads = (
        lax.psum_scatter(
            grad_query_w.astype(jnp.bfloat16), ("batch", "seq"), scatter_dimension=0, tiled=True
        ).astype(jnp.float32),
        lax.psum_scatter(
            grad_key_w.astype(jnp.bfloat16), ("batch", "seq"), scatter_dimension=0, tiled=True
        ).astype(jnp.float32),
        lax.psum_scatter(
            grad_value_w.astype(jnp.bfloat16), ("batch", "seq"), scatter_dimension=0, tiled=True
        ).astype(jnp.float32),
        lax.psum_scatter(
            grad_out_w.astype(jnp.bfloat16), ("batch", "seq"), scatter_dimension=1, tiled=True
        ).astype(jnp.float32),
        lax.psum_scatter(
            grad_gate_w.astype(jnp.bfloat16), ("batch", "seq"), scatter_dimension=0, tiled=True
        ).astype(jnp.float32),
        lax.psum_scatter(
            grad_up_w.astype(jnp.bfloat16), ("batch", "seq"), scatter_dimension=0, tiled=True
        ).astype(jnp.float32),
        lax.psum_scatter(
            grad_down_w.astype(jnp.bfloat16), ("batch", "seq"), scatter_dimension=1, tiled=True
        ).astype(jnp.float32),
    )
    return (grad_input, weight_grads, grad_gain_in, grad_gain_mid)


def to_flat(shard_rows):
    row_count, token_part, width = shard_rows.shape
    return jnp.transpose(shard_rows.astype(jnp.float32), (1, 0, 2)).reshape(
        token_part * row_count, width
    )


def from_flat(flat_rows, row_count):
    token_part = flat_rows.shape[0] // row_count
    return jnp.transpose(flat_rows.reshape(token_part, row_count, flat_rows.shape[1]), (1, 0, 2))


def general_local(
    tokens,
    cotangent,
    segments,
    positions,
    norm_in,
    w_query,
    w_key,
    w_value,
    w_out,
    norm_mid,
    w_gate,
    w_up,
    w_down,
):
    gains_in, gains_mid = (
        lax.all_gather(norm_in, ("batch", "seq", "kv"), axis=1, tiled=True),
        lax.all_gather(norm_mid, ("batch", "seq", "kv"), axis=1, tiled=True),
    )
    row_count = tokens.shape[0]
    seg_info = (segments, jnp.transpose(segments, (1, 0)))
    tables = rotary(jnp.transpose(positions, (1, 0)).reshape(-1))

    def fetch_layer(layer_index):
        return (
            lax.all_gather(w_query[layer_index], ("batch", "seq"), axis=0, tiled=True),
            lax.all_gather(w_key[layer_index], ("batch", "seq"), axis=0, tiled=True),
            lax.all_gather(w_value[layer_index], ("batch", "seq"), axis=0, tiled=True),
            lax.all_gather(w_out[layer_index], ("batch", "seq"), axis=1, tiled=True),
            lax.all_gather(w_gate[layer_index], ("batch", "seq"), axis=0, tiled=True),
            lax.all_gather(w_up[layer_index], ("batch", "seq"), axis=0, tiled=True),
            lax.all_gather(w_down[layer_index], ("batch", "seq"), axis=1, tiled=True),
        )

    stream = to_flat(tokens)
    fetched = []
    states = []
    layer_index = 0
    matrices = fetch_layer(layer_index)
    layer_inputs = [stream]
    stream, saved_state = layer_forward(
        stream, (gains_in[layer_index], gains_mid[layer_index]), matrices, seg_info, tables
    )
    fetched.append(matrices)
    states.append(saved_state)
    grad_stream = to_flat(cotangent)
    grads_in = []
    grads_mid = []
    weight_lists = []
    for layer_index in reversed(range(LAYERS)):
        gain_pair = (gains_in[layer_index], gains_mid[layer_index])
        matrices = fetch_layer(layer_index)
        saved_state = layer_forward(
            layer_inputs[layer_index], gain_pair, matrices, seg_info, tables
        )[1]
        grad_stream, weight_grads, grad_gain_in, grad_gain_mid = layer_backward(
            saved_state, grad_stream, gain_pair, matrices, seg_info, tables
        )
        grads_in.insert(0, grad_gain_in)
        grads_mid.insert(0, grad_gain_mid)
        weight_lists.insert(0, weight_grads)
    gain_grads_in, gain_grads_mid = (
        lax.psum_scatter(
            jnp.stack(grads_in), ("batch", "seq", "kv"), scatter_dimension=1, tiled=True
        ),
        lax.psum_scatter(
            jnp.stack(grads_mid), ("batch", "seq", "kv"), scatter_dimension=1, tiled=True
        ),
    )
    stacked_grads = [
        jnp.stack([grad_set[member] for grad_set in weight_lists]) for member in range(7)
    ]
    return (
        from_flat(stream, row_count),
        from_flat(grad_stream, row_count),
        gain_grads_in,
        stacked_grads[0],
        stacked_grads[1],
        stacked_grads[2],
        stacked_grads[3],
        gain_grads_mid,
        stacked_grads[4],
        stacked_grads[5],
        stacked_grads[6],
    )


def general_solution(mesh):
    in_specs = (
        P("batch", ("seq", "kv"), None),
        P("batch", ("seq", "kv"), None),
        P("batch", "seq"),
        P("batch", "seq"),
        P(None, ("batch", "seq", "kv")),
        P(None, ("batch", "seq"), "kv"),
        P(None, ("batch", "seq"), "kv"),
        P(None, ("batch", "seq"), "kv"),
        P(None, "kv", ("batch", "seq")),
        P(None, ("batch", "seq", "kv")),
        P(None, ("batch", "seq"), "kv"),
        P(None, ("batch", "seq"), "kv"),
        P(None, "kv", ("batch", "seq")),
    )
    out_specs = (
        P("batch", ("seq", "kv"), None),
        P("batch", ("seq", "kv"), None),
        P(None, ("batch", "seq", "kv")),
        P(None, ("batch", "seq"), "kv"),
        P(None, ("batch", "seq"), "kv"),
        P(None, ("batch", "seq"), "kv"),
        P(None, "kv", ("batch", "seq")),
        P(None, ("batch", "seq", "kv")),
        P(None, ("batch", "seq"), "kv"),
        P(None, ("batch", "seq"), "kv"),
        P(None, "kv", ("batch", "seq")),
    )
    return jax.shard_map(general_local, mesh=mesh, in_specs=in_specs, out_specs=out_specs, check_vma=False)


LN = 128
NEG=-1e30
C2 = (96 ** -0.5) * 1.4426950408889634

def cost(microseconds):
    return pl.CostEstimate(
        flops=microseconds * 10**9, bytes_accessed=microseconds * 3 * 10**6, transcendentals=0
    )


def lane_iota(rows):
    return lax.broadcasted_iota(jnp.int32, (rows, LN), 1)

def unpack4(t0, t1, t2):
    lane = lane_iota(t0.shape[0])
    live = lane < HD
    zero = jnp.zeros_like(t0)
    a = t0
    b = pltpu.roll(jnp.where(lane >= 96, t0, t1), 32, 1)
    c = pltpu.roll(jnp.where(lane >= 64, t1, t2), 64, 1)
    d = pltpu.roll(t2, 96, 1)
    return tuple(jnp.where(live, v, zero) for v in (a, b, c, d))

def pack4(a, b, c, d):
    lane = lane_iota(a.shape[0])
    b, c, d = pltpu.roll(b, 96, 1), pltpu.roll(c, 64, 1), pltpu.roll(d, 32, 1)
    return (jnp.where(lane < 96, a, b), jnp.where(lane < 64, b, c), jnp.where(lane < 32, c, d))

def split3(x):
    x = x.astype(jnp.float32)
    return x[:, :LN], x[:, LN:2*LN], x[:, 2*LN:]

def doc_low(index, first, length):
    second = first + 3 * length // 4
    return jnp.where(index >= second, second, jnp.where(index >= first, first, 0))

BQ = 256

def dotf(a, b, dims):
    return lax.dot_general(a, b, (dims, ((), ())), preferred_element_type=jnp.float32)

def attn_fwd_kernel(length, first_ref, x_ref, o_ref, of_ref, lse_ref, q_s, k_s, v_s, s_s):
    i = pl.program_id(0)
    blocks = length // BQ
    first = first_ref[0]
    @pl.when(i == 0)
    def _():
        def body(j, carry):
            rows = pl.ds(pl.multiple_of(j * BQ, BQ), BQ)
            q0, q1, k, v = unpack4(*split3(x_ref[rows, :]))
            q_s[j, :BQ, :] = q0.astype(jnp.bfloat16)
            q_s[j, BQ:, :] = q1.astype(jnp.bfloat16)
            k_s[j] = k.astype(jnp.bfloat16)
            v_s[j] = v.astype(jnp.bfloat16)
            return carry
        lax.fori_loop(0, blocks, body, 0)
    q = q_s[i]
    clean_from = (length // 8 + BQ - 1) // BQ
    clean_to = 3 * length // 4 // BQ
    late = (3 * length // 4 + length // 8) // BQ
    start = jnp.where(i >= late, 3 * length // 4 // BQ, 0)
    head_masked = jnp.where(i < clean_to, jnp.minimum(clean_from, i), i)
    q_index = i * BQ + lax.broadcasted_iota(jnp.int32, (BQ, 1), 0)
    low = doc_low(q_index, first, length)

    def halves(v, op):
        return op(v[:, :LN], v[:, LN:])

    def score(j, top, masked):
        s = dotf(q, k_s[j], ((1,), (1,)))
        if masked:
            key = j * BQ + lax.broadcasted_iota(jnp.int32, (1, BQ), 1)
            ok = (key <= q_index) & (key >= low)
            s = jnp.where(jnp.concatenate([ok, ok], axis=0), s, NEG)
        s_s[j] = s
        return jnp.maximum(top, halves(s, jnp.maximum))

    top = jnp.full((2 * BQ, LN), NEG, jnp.float32)
    top = lax.fori_loop(start, head_masked, lambda j, t: score(j, t, True), top)
    top = lax.fori_loop(jnp.maximum(head_masked, start), i, lambda j, t: score(j, t, False), top)
    top = score(i, top, True)
    m = jnp.max(top, axis=1, keepdims=True) * C2

    def add(j, state):
        total, acc = state
        p = jnp.exp2(s_s[j] * C2 - m)
        total = total + halves(p, jnp.add)
        acc = acc + dotf(p.astype(jnp.bfloat16), v_s[j], ((1,), (0,)))
        return total, acc

    zero = jnp.zeros((2 * BQ, LN), jnp.float32)
    total, acc = lax.fori_loop(start, i + 1, add, (zero, zero))
    total = jnp.sum(total, axis=1, keepdims=True)
    out = acc / total
    lse = jnp.broadcast_to(m + jnp.log2(total), (2 * BQ, LN))
    lse_ref[0] = jnp.transpose(lse, (1, 0))[:8, :]
    of_ref[0] = out
    for d in range(2):
        parts = []
        for h in range(2):
            parts.append(out[BQ*0 + d*128 + h*64: d*128 + h*64 + 64])
            parts.append(out[BQ + d*128 + h*64: BQ + d*128 + h*64 + 64])
        t = pack4(*parts)
        for n in range(3):
            o_ref[d, :, n*LN:(n+1)*LN] = t[n].astype(jnp.bfloat16)

def attn_fwd(first, x):
    length = x.shape[0]
    blocks = length // BQ
    return pl.pallas_call(
        functools.partial(attn_fwd_kernel, length),
        grid=(blocks,),
        in_specs=[pl.BlockSpec(memory_space=pltpu.SMEM),
                  pl.BlockSpec((length, 3*LN), lambda i: (0, 0))],
        out_specs=[pl.BlockSpec((2, 64, 3*LN), lambda i: (i, 0, 0)),
                   pl.BlockSpec((1, 2*BQ, LN), lambda i: (i, 0, 0)),
                   pl.BlockSpec((1, 8, 2*BQ), lambda i: (i, 0, 0))],
        out_shape=[jax.ShapeDtypeStruct((length//128, 64, 3*LN), jnp.bfloat16),
                   jax.ShapeDtypeStruct((blocks, 2*BQ, LN), jnp.float32),
                   jax.ShapeDtypeStruct((blocks, 8, 2*BQ), jnp.float32)],
        scratch_shapes=[pltpu.VMEM((blocks, 2*BQ, LN), jnp.bfloat16),
                        pltpu.VMEM((blocks, BQ, LN), jnp.bfloat16),
                        pltpu.VMEM((blocks, BQ, LN), jnp.bfloat16),
                        pltpu.VMEM((blocks, 2*BQ, BQ), jnp.float32)],
        compiler_params=pltpu.CompilerParams(vmem_limit_bytes=48 << 20),
        name="attend",
        cost_estimate=cost(22),
    )(first, x)

def attn_bwd_kernel(length, first_ref, x_ref, do_ref, of_ref, lse_ref, cos_ref, sin_ref, out_ref,
                    q_s, k_s, v_s, do_s, dl_s, dq_s, dk_s, dv_s):
    j = pl.program_id(0)
    blocks = length // BQ
    first = first_ref[0]
    @pl.when(j == 0)
    def _():
        def body(b, carry):
            rows = pl.ds(pl.multiple_of(b * BQ, BQ), BQ)
            q0, q1, k, v = unpack4(*split3(x_ref[rows, :]))
            q_s[b, :BQ, :] = q0.astype(jnp.bfloat16)
            q_s[b, BQ:, :] = q1.astype(jnp.bfloat16)
            k_s[b] = k.astype(jnp.bfloat16)
            v_s[b] = v.astype(jnp.bfloat16)
            for d in range(2):
                parts = unpack4(*split3(do_ref[2*b + d]))
                for n, part in enumerate(parts):
                    at = (n % 2) * BQ + d*128 + (n // 2) * 64
                    do_s[b, at:at+64, :] = part.astype(jnp.bfloat16)
            prod = do_s[b].astype(jnp.float32) * of_ref[b]
            delta = jnp.broadcast_to(jnp.sum(prod, axis=1, keepdims=True), (2*BQ, LN))
            dl_s[b] = jnp.transpose(delta, (1, 0))[:8, :]
            dq_s[b] = jnp.zeros((2*BQ, LN), jnp.float32)
            return carry
        lax.fori_loop(0, blocks, body, 0)
    clean_from = (length // 8 + BQ - 1) // BQ
    clean_to = 3 * length // 4 // BQ
    late = (3 * length // 4 + length // 8) // BQ
    third = 3 * length // 4 // BQ
    stop = jnp.where(j >= third, blocks, late)
    k = k_s[j]
    v = v_s[j]
    dk_s[j] = jnp.zeros((BQ, LN), jnp.float32)
    dv_s[j] = jnp.zeros((BQ, LN), jnp.float32)
    key = j * BQ + lax.broadcasted_iota(jnp.int32, (BQ, 1), 0)

    def step(i, masked):
        q, do = q_s[i], do_s[i]
        s = dotf(k, q, ((1,), (1,)))
        p = jnp.exp2(s * C2 - lse_ref[i, 0:1, :])
        if masked:
            q_index = i * BQ + lax.broadcasted_iota(jnp.int32, (1, BQ), 1)
            ok = (key <= q_index) & (key >= doc_low(q_index, first, length))
            p = jnp.where(jnp.concatenate([ok, ok], axis=1), p, 0.0)
        dp = dotf(v, do, ((1,), (1,)))
        ds = (p * (dp - dl_s[i, 0:1, :])).astype(jnp.bfloat16)
        dv_s[j] += dotf(p.astype(jnp.bfloat16), do, ((1,), (0,)))
        dk_s[j] += dotf(ds, q, ((1,), (0,)))
        dq_s[i] += dotf(ds, k, ((0,), (0,)))

    def loop(lo, hi, masked):
        def body(i, carry):
            step(i, masked)
            return carry
        lax.fori_loop(lo, hi, body, 0)

    step(j, True)
    clean_lo = j + 1
    clean_hi = jnp.where(j >= clean_from, jnp.maximum(clean_to, j + 1), j + 1)
    loop(clean_lo, clean_hi, False)
    loop(clean_hi, stop, True)

    @pl.when(j == blocks - 1)
    def _():
        scale = HD ** -0.5
        def body(b, carry):
            rows = pl.ds(pl.multiple_of(b * BQ, BQ), BQ)
            t = pack4(dq_s[b, :BQ, :] * scale, dq_s[b, BQ:, :] * scale, dk_s[b] * scale, dv_s[b])
            t = jnp.concatenate(t, axis=1)
            cosine, sine, lower = cos_sin3(cos_ref[rows, :], sin_ref[rows, :])
            out_ref[rows, :] = turn(t, cosine, -sine, lower).astype(jnp.bfloat16)
            return carry
        lax.fori_loop(0, blocks, body, 0)

def attn_bwd(first, x, do, of, lse, cos, sin):
    length = x.shape[0]
    blocks = length // BQ
    whole = lambda a: pl.BlockSpec(a.shape, lambda j: (0,) * a.ndim)
    return pl.pallas_call(
        functools.partial(attn_bwd_kernel, length),
        grid=(blocks,),
        in_specs=[pl.BlockSpec(memory_space=pltpu.SMEM)] + [whole(a) for a in (x, do, of, lse, cos, sin)],
        out_specs=pl.BlockSpec((length, 3*LN), lambda j: (0, 0)),
        out_shape=jax.ShapeDtypeStruct((length, 3*LN), jnp.bfloat16),
        scratch_shapes=[pltpu.VMEM((blocks, 2*BQ, LN), jnp.bfloat16),
                        pltpu.VMEM((blocks, BQ, LN), jnp.bfloat16),
                        pltpu.VMEM((blocks, BQ, LN), jnp.bfloat16),
                        pltpu.VMEM((blocks, 2*BQ, LN), jnp.bfloat16),
                        pltpu.VMEM((blocks, 8, 2*BQ), jnp.float32),
                        pltpu.VMEM((blocks, 2*BQ, LN), jnp.float32),
                        pltpu.VMEM((blocks, BQ, LN), jnp.float32),
                        pltpu.VMEM((blocks, BQ, LN), jnp.float32)],
        compiler_params=pltpu.CompilerParams(vmem_limit_bytes=56 << 20),
        name="attend_back",
        cost_estimate=cost(31),
    )(first, x, do, of, lse, cos, sin)


def widen(table):
    lane = lane_iota(table.shape[0])
    second = jnp.where(lane < 96, pltpu.roll(table, 96, 1), pltpu.roll(table, 16, 1))
    third = jnp.where(lane < 112, pltpu.roll(table, 112, 1), pltpu.roll(table, 32, 1))
    return second, third


def cos_sin3(cos, sin):
    lane = lane_iota(cos.shape[0])
    live = lane < 32
    cos_two, cos_three = widen(cos)
    sin_two, sin_three = widen(sin)
    cosine = jnp.concatenate([cos, cos_two, jnp.where(live, cos_three, 1.0)], axis=1)
    sine = jnp.concatenate([sin, sin_two, jnp.where(live, sin_three, 0.0)], axis=1)
    wide = lax.broadcasted_iota(jnp.int32, cosine.shape, 1)
    lower = (wide % HD) < HD // 2
    return cosine, jnp.where(lower, -sine, sine), lower


def turn(values, cosine, sine, lower):
    width = values.shape[1]
    swapped = jnp.where(
        lower, pltpu.roll(values, width - HD // 2, 1), pltpu.roll(values, HD // 2, 1)
    )
    return values * cosine + swapped * sine


def full_spec(array):
    rank = array.ndim
    return pl.BlockSpec(array.shape, lambda *_: (0,) * rank)


def qkv_kernel(parts, rows, place_ref, *refs):
    blocks = refs[:parts]
    gain_ref, w_ref, cos_ref, sin_ref, a_ref, out_ref = refs[parts:]
    tokens = blocks[0].shape[0] // rows
    for k in range(parts):
        z = lax.rem(place_ref[0] + (parts - k), parts)
        stream = blocks[k][...].astype(jnp.float32)
        factor = lax.rsqrt(jnp.mean(stream * stream, axis=-1, keepdims=True) + EPS)
        normed = (stream * factor * gain_ref[...]).astype(jnp.bfloat16)
        at = pl.ds(pl.multiple_of(z * tokens, tokens), tokens)
        for r in range(rows):
            a_ref[r, at, :] = normed[r * tokens : (r + 1) * tokens]
        product = dotf(normed, w_ref[...], ((1,), (0,)))
        for r in range(rows):
            cosine, sine, lower = cos_sin3(cos_ref[r, at, :], sin_ref[r, at, :])
            for h in range(product.shape[1] // (3 * LN)):
                piece = product[r * tokens : (r + 1) * tokens, h * 3 * LN : (h + 1) * 3 * LN]
                out_ref[h * rows + r, at, :] = turn(piece, cosine, sine, lower).astype(jnp.bfloat16)


def qkv_call(place, blocks, gain, weight, cos, sin, rows):
    parts = len(blocks)
    count, width = blocks[0].shape
    tokens = count // rows * parts
    groups = weight.shape[1] // (3 * LN)
    operands = (*blocks, gain, weight, cos, sin)
    return pl.pallas_call(
        partial(qkv_kernel, parts, rows),
        grid=(1,),
        in_specs=[pl.BlockSpec(memory_space=pltpu.SMEM)] + [full_spec(v) for v in operands],
        out_specs=[
            pl.BlockSpec((rows, tokens, width), lambda i: (0, 0, 0)),
            pl.BlockSpec((groups * rows, tokens, 3 * LN), lambda i: (0, 0, 0)),
        ],
        out_shape=[
            jax.ShapeDtypeStruct((rows, tokens, width), jnp.bfloat16),
            jax.ShapeDtypeStruct((groups * rows, tokens, 3 * LN), jnp.bfloat16),
        ],
        compiler_params=pltpu.CompilerParams(vmem_limit_bytes=48 << 20),
        name="norm_qkv",
        cost_estimate=cost(7),
    )(place, *operands)


def thirds(values):
    return values[:, :LN], values[:, LN : 2 * LN], values[:, 2 * LN :]


def join_pairs(left, right):
    l0, l1, l2 = thirds(left)
    r0, r1, r2 = thirds(right)
    low = lane_iota(left.shape[0]) < 64
    s0, s1, s2 = (pltpu.roll(v, 64, 1) for v in (r0, r1, r2))
    firsts = (l0, jnp.where(low, l1, s0), jnp.where(low, s0, s1))
    m1, m2 = pltpu.roll(l1, 64, 1), pltpu.roll(l2, 64, 1)
    lasts = (jnp.where(low, m1, m2), jnp.where(low, m2, r1), r2)
    return jnp.concatenate(firsts, axis=1), jnp.concatenate(lasts, axis=1)


def out_kernel(rows, parts, o_ref, w_ref, tok_ref, gain_ref, mid_ref, b_ref, oo_ref, o_s):
    half = o_ref.shape[1]
    for r in range(rows):
        for z in range(parts):
            left = o_ref[r * parts + z].astype(jnp.float32)
            right = o_ref[(rows + r) * parts + z].astype(jnp.float32)
            for n, piece in enumerate(join_pairs(left, right)):
                at = (2 * r + n) * half
                o_s[at : at + half, z * 3 * LN : (z + 1) * 3 * LN] = piece.astype(jnp.bfloat16)
    attended = o_s[...]
    oo_ref[...] = attended
    middle = tok_ref[...].astype(jnp.float32) + dotf(attended, w_ref[...], ((1,), (1,)))
    mid_ref[...] = middle
    factor = lax.rsqrt(jnp.mean(middle * middle, axis=-1, keepdims=True) + EPS)
    b_ref[...] = (middle * factor * gain_ref[...]).astype(jnp.bfloat16)


def out_call(o_parts, weight, tokens, gain, rows):
    count, width = tokens.shape
    inner = weight.shape[1]
    operands = (o_parts, weight, tokens, gain)
    shapes = [
        jax.ShapeDtypeStruct((count, width), jnp.float32),
        jax.ShapeDtypeStruct((count, width), jnp.bfloat16),
        jax.ShapeDtypeStruct((count, inner), jnp.bfloat16),
    ]
    return pl.pallas_call(
        partial(out_kernel, rows, o_parts.shape[0] // (2 * rows)),
        grid=(1,),
        in_specs=[full_spec(v) for v in operands],
        out_specs=[full_spec(v) for v in shapes],
        out_shape=shapes,
        scratch_shapes=[pltpu.VMEM((count, inner), jnp.bfloat16)],
        compiler_params=pltpu.CompilerParams(vmem_limit_bytes=48 << 20),
        name="out_norm",
        cost_estimate=cost(4),
    )(*operands)


def split_pairs(firsts, lasts):
    f0, f1, f2 = thirds(firsts)
    g0, g1, g2 = thirds(lasts)
    low = lane_iota(firsts.shape[0]) < 64
    t0, t1 = pltpu.roll(g0, 64, 1), pltpu.roll(g1, 64, 1)
    left = (f0, jnp.where(low, f1, t0), jnp.where(low, t0, t1))
    u1, u2 = pltpu.roll(f1, 64, 1), pltpu.roll(f2, 64, 1)
    right = (jnp.where(low, u1, u2), jnp.where(low, u2, g1), g2)
    return jnp.concatenate(left, axis=1), jnp.concatenate(right, axis=1)


def mid_back_kernel(
    rows, parts, keep_ref, fx_ref, fy_ref, px_ref, py_ref, mid_ref, cot_ref, gain_ref, w_ref,
    gmid_ref, go_ref, do_ref, gg_ref
):
    half = px_ref.shape[0]
    wide = lambda v: v.astype(jnp.float32)
    db = jnp.concatenate(
        [
            keep_ref[:half] + wide(fx_ref[:half]) + wide(py_ref[...]),
            keep_ref[half:] + wide(fy_ref[:half]) + wide(px_ref[...]),
        ],
        axis=0,
    )
    middle = mid_ref[...]
    factor = lax.rsqrt(jnp.mean(middle * middle, axis=-1, keepdims=True) + EPS)
    scaled = db * gain_ref[...]
    inner = jnp.mean(scaled * middle, axis=-1, keepdims=True)
    grad = cot_ref[...].astype(jnp.float32) + factor * scaled - middle * (factor**3 * inner)
    gmid_ref[...] = grad
    gg_ref[...] = jnp.sum(db * middle * factor, axis=0, keepdims=True)
    low = grad.astype(jnp.bfloat16)
    go_ref[...] = low
    back = dotf(low, w_ref[...], ((1,), (0,)))
    half = do_ref.shape[1]
    for r in range(rows):
        for z in range(parts):
            cols = slice(z * 3 * LN, (z + 1) * 3 * LN)
            at = 2 * r * half
            left, right = split_pairs(back[at : at + half, cols], back[at + half : at + 2 * half, cols])
            do_ref[r * parts + z] = left.astype(jnp.bfloat16)
            do_ref[(rows + r) * parts + z] = right.astype(jnp.bfloat16)


def mid_back_call(pieces, middle, cot, gain, weight, rows, parts):
    count, width = middle.shape
    operands = (*pieces, middle, cot, gain, weight)
    shapes = [
        jax.ShapeDtypeStruct((count, width), jnp.float32),
        jax.ShapeDtypeStruct((count, width), jnp.bfloat16),
        jax.ShapeDtypeStruct((2 * rows * parts, count // rows // 2, 3 * LN), jnp.bfloat16),
        jax.ShapeDtypeStruct((1, width), jnp.float32),
    ]
    return pl.pallas_call(
        partial(mid_back_kernel, rows, parts),
        grid=(1,),
        in_specs=[pl.BlockSpec((count, width), lambda i: (0, 0))] + [full_spec(v) for v in operands[1:]],
        out_specs=[full_spec(v) for v in shapes],
        out_shape=shapes,
        compiler_params=pltpu.CompilerParams(vmem_limit_bytes=48 << 20),
        name="mid_back",
        cost_estimate=cost(5),
    )(*operands)


def da_kernel(parts, rows, place_ref, *refs):
    blocks = refs[:parts]
    d_ref, w_ref, da_ref, gg_ref = refs[parts:]
    tokens = blocks[0].shape[0] // rows
    groups = d_ref.shape[0]
    total = jnp.zeros(gg_ref.shape, jnp.float32)
    for k in range(parts):
        z = lax.rem(place_ref[0] + (parts - k), parts)
        at = pl.ds(pl.multiple_of(z * tokens, tokens), tokens)
        left = jnp.concatenate(
            [jnp.concatenate([d_ref[g, r, at, :] for r in range(rows)], axis=0) for g in range(groups)],
            axis=1,
        )
        back = dotf(left, w_ref[...], ((1,), (1,)))
        stream = blocks[k][...].astype(jnp.float32)
        factor = lax.rsqrt(jnp.mean(stream * stream, axis=-1, keepdims=True) + EPS)
        total = total + jnp.sum(back * stream * factor, axis=0, keepdims=True)
        count = rows * tokens
        da_ref[pl.ds(pl.multiple_of(z * count, count), count), :] = back.astype(jnp.bfloat16)
    gg_ref[...] = total


def da_call(place, blocks, grads, weight, rows):
    parts = len(blocks)
    count, width = blocks[0].shape
    operands = (*blocks, grads, weight)
    shapes = [
        jax.ShapeDtypeStruct((parts * count, width), jnp.bfloat16),
        jax.ShapeDtypeStruct((1, width), jnp.float32),
    ]
    return pl.pallas_call(
        partial(da_kernel, parts, rows),
        grid=(1,),
        in_specs=[pl.BlockSpec(memory_space=pltpu.SMEM)] + [full_spec(v) for v in operands],
        out_specs=[full_spec(v) for v in shapes],
        out_shape=shapes,
        compiler_params=pltpu.CompilerParams(vmem_limit_bytes=48 << 20),
        name="da_part",
        cost_estimate=cost(6),
    )(place, *operands)


def cut_kernel(gate_ref, up_ref, down_ref, out_ref):
    for n in range(out_ref.shape[0]):
        at = slice(n * LN, (n + 1) * LN)
        out_ref[n, :, :LN] = gate_ref[:, at]
        out_ref[n, :, LN : 2 * LN] = up_ref[:, at]
        out_ref[n, :, 2 * LN :] = jnp.transpose(down_ref[at, :].astype(jnp.float32)).astype(jnp.bfloat16)


def cut_call(gate, up, down):
    shape = jax.ShapeDtypeStruct((gate.shape[1] // LN, gate.shape[0], 3 * LN), jnp.bfloat16)
    operands = (gate, up, down)
    return pl.pallas_call(
        cut_kernel,
        grid=(1,),
        in_specs=[full_spec(v) for v in operands],
        out_specs=full_spec(shape),
        out_shape=shape,
        name="cut_units",
        cost_estimate=cost(3),
    )(*operands)


def uncut_kernel(in_ref, gate_ref, up_ref, down_ref):
    for n in range(in_ref.shape[0]):
        at = slice(n * LN, (n + 1) * LN)
        gate_ref[:, at] = in_ref[n, :, :LN].astype(jnp.float32)
        up_ref[:, at] = in_ref[n, :, LN : 2 * LN].astype(jnp.float32)
        down_ref[at, :] = jnp.transpose(in_ref[n, :, 2 * LN :].astype(jnp.float32))


def uncut_call(value):
    units, rows = value.shape[0] * LN, value.shape[1]
    shapes = [jax.ShapeDtypeStruct(s, jnp.float32) for s in ((rows, units), (rows, units), (units, rows))]
    return pl.pallas_call(
        uncut_kernel,
        grid=(1,),
        in_specs=[full_spec(value)],
        out_specs=[full_spec(v) for v in shapes],
        out_shape=shapes,
        name="uncut_units",
        cost_estimate=cost(3),
    )(value)


def place_kernel(parts, turned, at_ref, mine_ref, other_ref, out_ref):
    size = mine_ref.shape[1]
    z = at_ref[3]
    for c, ref in enumerate((mine_ref, other_ref)):
        for n in range(parts):
            y, x = at_ref[0] ^ (n // 2), at_ref[1] ^ (n % 2)
            rows = pl.multiple_of(((y * 2 + x) * 2 + (at_ref[2] ^ c)) * size, size)
            for k in range(ref.shape[0] // parts):
                count = ref.shape[0] // parts
                source = lax.rem(z + (count - k), count) if turned else k
                cols = pl.multiple_of(source * 3 * LN, 3 * LN)
                out_ref[pl.ds(rows, size), pl.ds(cols, 3 * LN)] = ref[n * count + k]


def place_call(at, mine, other, turned):
    size = mine.shape[1]
    shape = jax.ShapeDtypeStruct((8 * size, mine.shape[0] // 4 * mine.shape[2]), mine.dtype)
    return pl.pallas_call(
        partial(place_kernel, 4, turned),
        grid=(1,),
        in_specs=[pl.BlockSpec(memory_space=pltpu.SMEM), full_spec(mine), full_spec(other)],
        out_specs=full_spec(shape),
        out_shape=shape,
        compiler_params=pltpu.CompilerParams(vmem_limit_bytes=32 << 20),
        name="place_out",
        cost_estimate=cost(3),
    )(at, mine, other)


def fill_square(refs, out_ref):
    own, xn, yn, first, last = refs
    half = first.shape[0]
    out_ref[0, :half], out_ref[0, half:] = own[:half], own[half:]
    out_ref[1, :half], out_ref[1, half:] = xn[:half], first[...]
    out_ref[2, :half], out_ref[2, half:] = yn[half:], last[...]
    out_ref[3, :half], out_ref[3, half:] = xn[half:], yn[:half]


def down_back_kernel(*refs):
    pieces, (w0_ref, w1_ref, out_ref, g_s) = refs[:5], refs[5:]

    @pl.when(pl.program_id(0) == 0)
    def _():
        fill_square(pieces, g_s)

    weight = jnp.concatenate([w0_ref[0, :, 2 * LN :], w1_ref[0, :, 2 * LN :]], axis=1)

    def body(m, carry):
        out_ref[0, m] = dotf(g_s[m], weight, ((1,), (0,)))
        return carry

    lax.fori_loop(0, 4, body, 0)


def unit_spec(weight):
    return pl.BlockSpec((1,) + weight.shape[1:], lambda z: (z, 0, 0))


def down_back_call(pieces, mine, other):
    count, width = pieces[0].shape
    parts = mine.shape[0]
    shape = jax.ShapeDtypeStruct((parts, 4, count, 2 * LN), jnp.float32)
    return pl.pallas_call(
        down_back_kernel,
        grid=(parts,),
        in_specs=[full_spec(v) for v in pieces] + [unit_spec(mine), unit_spec(other)],
        out_specs=pl.BlockSpec((1, 4, count, 2 * LN), lambda z: (z, 0, 0, 0)),
        out_shape=shape,
        scratch_shapes=[pltpu.VMEM((4, count, width), jnp.bfloat16)],
        compiler_params=pltpu.CompilerParams(vmem_limit_bytes=40 << 20),
        name="down_back",
        cost_estimate=cost(8),
    )(*pieces, mine, other)


def emit_square(acc_ref, keep_ref, sx_ref, sy_ref):
    count = sx_ref.shape[0]
    keep_ref[:count] = acc_ref[0]
    keep_ref[count:] = acc_ref[3]
    sx_ref[...] = acc_ref[1].astype(jnp.bfloat16)
    sy_ref[...] = acc_ref[2].astype(jnp.bfloat16)


def units_kernel(*refs):
    pieces, (w0_ref, w1_ref, dh_ref) = refs[:5], refs[5:8]
    dgu_ref, hid_ref, keep_ref, sx_ref, sy_ref, b_s, acc_s = refs[8:]
    step = pl.program_id(0)

    @pl.when(step == 0)
    def _():
        fill_square(pieces, b_s)

    def body(m, carry):
        b = b_s[m]
        total = None
        for n, w_ref in enumerate((w0_ref, w1_ref)):
            weight = w_ref[0, :, : 2 * LN]
            both = dotf(b, weight, ((1,), (0,)))
            gate, up = both[:, :LN], both[:, LN:]
            dh = dh_ref[0, m, :, n * LN : (n + 1) * LN]
            sigma = 1.0 / (1.0 + jnp.exp(-gate))
            silu = gate * sigma
            hid_ref[0, m, :, n * LN : (n + 1) * LN] = (silu * up).astype(jnp.bfloat16)
            grad_gate = dh * up * sigma * (1.0 + gate * (1.0 - sigma))
            grads = jnp.concatenate([grad_gate, dh * silu], axis=1).astype(jnp.bfloat16)
            dgu_ref[0, n, m] = grads
            back = dotf(grads, weight, ((1,), (1,)))
            total = back if total is None else total + back

        @pl.when(step == 0)
        def _():
            acc_s[m] = total

        @pl.when(step > 0)
        def _():
            acc_s[m] += total

        return carry

    lax.fori_loop(0, 4, body, 0)

    @pl.when(step == pl.num_programs(0) - 1)
    def _():
        emit_square(acc_s, keep_ref, sx_ref, sy_ref)


def square_shapes(count, width):
    return [
        jax.ShapeDtypeStruct((2 * count, width), jnp.float32),
        jax.ShapeDtypeStruct((count, width), jnp.bfloat16),
        jax.ShapeDtypeStruct((count, width), jnp.bfloat16),
    ]


def units_call(pieces, mine, other, grad_hidden):
    count, width = pieces[0].shape
    parts = mine.shape[0]
    low = jnp.bfloat16
    shapes = [
        jax.ShapeDtypeStruct((parts, 2, 4, count, 2 * LN), low),
        jax.ShapeDtypeStruct((parts, 4, count, 2 * LN), low),
    ] + square_shapes(count, width)
    return pl.pallas_call(
        units_kernel,
        grid=(parts,),
        in_specs=[full_spec(v) for v in pieces]
        + [unit_spec(mine), unit_spec(other), pl.BlockSpec((1, 4, count, 2 * LN), lambda z: (z, 0, 0, 0))],
        out_specs=[
            pl.BlockSpec((1, 2, 4, count, 2 * LN), lambda z: (z, 0, 0, 0, 0)),
            pl.BlockSpec((1, 4, count, 2 * LN), lambda z: (z, 0, 0, 0)),
        ]
        + [full_spec(v) for v in shapes[2:]],
        out_shape=shapes,
        scratch_shapes=[pltpu.VMEM((4, count, width), low), pltpu.VMEM((4, count, width), jnp.float32)],
        compiler_params=pltpu.CompilerParams(vmem_limit_bytes=56 << 20),
        name="units",
        cost_estimate=cost(26),
    )(*pieces, mine, other, grad_hidden)


def down_kernel(hid_ref, w0_ref, w1_ref, keep_ref, sx_ref, sy_ref, acc_s):
    step = pl.program_id(0)
    weight = jnp.concatenate([w0_ref[0, :, 2 * LN :], w1_ref[0, :, 2 * LN :]], axis=1)

    def body(m, carry):
        total = dotf(hid_ref[0, m], weight, ((1,), (1,)))

        @pl.when(step == 0)
        def _():
            acc_s[m] = total

        @pl.when(step > 0)
        def _():
            acc_s[m] += total

        return carry

    lax.fori_loop(0, 4, body, 0)

    @pl.when(step == pl.num_programs(0) - 1)
    def _():
        emit_square(acc_s, keep_ref, sx_ref, sy_ref)


def down_call(hidden, mine, other):
    parts, _, count, _ = hidden.shape
    width = mine.shape[1]
    shapes = square_shapes(count, width)
    return pl.pallas_call(
        down_kernel,
        grid=(parts,),
        in_specs=[pl.BlockSpec((1,) + hidden.shape[1:], lambda z: (z, 0, 0, 0)), unit_spec(mine), unit_spec(other)],
        out_specs=[full_spec(v) for v in shapes],
        out_shape=shapes,
        scratch_shapes=[pltpu.VMEM((4, count, width), jnp.float32)],
        compiler_params=pltpu.CompilerParams(vmem_limit_bytes=40 << 20),
        name="down",
        cost_estimate=cost(11),
    )(hidden, mine, other)


def unit_grads_kernel(place_ref, *refs):
    b_pieces, g_pieces = refs[:5], refs[5:10]
    dgu_ref, hid_ref, mine_ref, other_ref, fill_s, b_s, g_s = refs[10:]
    count = fill_s.shape[1]

    @pl.when(pl.program_id(0) == 0)
    def _():
        for pieces, side in ((b_pieces, b_s), (g_pieces, g_s)):
            fill_square(pieces, fill_s)
            for m in range(4):
                side[:, m * count : (m + 1) * count] = jnp.transpose(fill_s[m])

    hidden = hid_ref[0].reshape(4 * count, 2 * LN)
    grads = [dgu_ref[0, n].reshape(4 * count, 2 * LN) for n in range(2)]
    rows = b_s.shape[0] // 4

    def body(m, carry):
        at = pl.ds(pl.multiple_of(m * rows, rows), rows)
        left, right = b_s[at, :], g_s[at, :]
        down = dotf(right, hidden, ((1,), (0,)))
        for n, out_ref in enumerate((mine_ref, other_ref)):
            out_ref[0, at, : 2 * LN] = dotf(left, grads[n], ((1,), (0,))).astype(jnp.bfloat16)
            out_ref[0, at, 2 * LN :] = down[:, n * LN : (n + 1) * LN].astype(jnp.bfloat16)
        return carry

    lax.fori_loop(0, 4, body, 0)


def unit_grads_call(place, b_pieces, g_pieces, grads, hidden):
    count, width = b_pieces[0].shape
    parts = hidden.shape[0]
    low = jnp.bfloat16
    operands = (*b_pieces, *g_pieces)
    return pl.pallas_call(
        unit_grads_kernel,
        grid_spec=pltpu.PrefetchScalarGridSpec(
            num_scalar_prefetch=1,
            grid=(parts,),
            in_specs=[full_spec(v) for v in operands]
            + [
                pl.BlockSpec((1,) + grads.shape[1:], lambda k, at: (k, 0, 0, 0, 0)),
                pl.BlockSpec((1,) + hidden.shape[1:], lambda k, at: (k, 0, 0, 0)),
            ],
            out_specs=[pl.BlockSpec((1, width, 3 * LN), lambda k, at: (k, 0, 0))] * 2,
            scratch_shapes=[pltpu.VMEM((4, count, width), low)]
            + [pltpu.VMEM((width, 4 * count), low)] * 2,
        ),
        out_shape=[jax.ShapeDtypeStruct((parts, width, 3 * LN), low)] * 2,
        compiler_params=pltpu.CompilerParams(vmem_limit_bytes=56 << 20),
        name="unit_grads",
        cost_estimate=cost(19),
    )(place, *operands, grads, hidden)


def qkv_grads_kernel(a_ref, d_ref, out_ref):
    left = jnp.transpose(a_ref[...])
    for g in range(d_ref.shape[0]):
        cols = slice(g * 3 * LN, (g + 1) * 3 * LN)
        out_ref[:, cols] = dotf(left, d_ref[g], ((1,), (0,))).astype(out_ref.dtype)


def qkv_grads_call(normed, grads):
    count, width = normed.shape
    shape = jax.ShapeDtypeStruct((width, grads.shape[0] * 3 * LN), jnp.bfloat16)
    tile = 2 * LN
    return pl.pallas_call(
        qkv_grads_kernel,
        grid=(width // tile,),
        in_specs=[pl.BlockSpec((count, tile), lambda i: (0, i)), full_spec(grads)],
        out_specs=pl.BlockSpec((tile, shape.shape[1]), lambda i: (i, 0)),
        out_shape=shape,
        compiler_params=pltpu.CompilerParams(vmem_limit_bytes=32 << 20),
        name="qkv_grads",
        cost_estimate=cost(5),
    )(normed, grads)


def out_grads_kernel(at_ref, go_ref, o_ref, out_ref, full_s):
    tile = 2 * LN
    right = o_ref[...]
    for n in range(full_s.shape[0] // tile):
        left = jnp.transpose(go_ref[:, n * tile : (n + 1) * tile])
        full_s[n * tile : (n + 1) * tile, :] = dotf(left, right, ((1,), (0,))).astype(jnp.bfloat16)
    half = out_ref.shape[2]
    size = 2 * half
    order = ((0, 0, 0), (0, 0, 1), (0, 1, 0), (1, 1, 0), (1, 0, 1), (1, 1, 1), (0, 1, 1), (1, 0, 0))
    for c in range(2):
        for n, (y, x, last) in enumerate(order):
            block = ((at_ref[0] ^ y) * 2 + (at_ref[1] ^ x)) * 2 + (at_ref[2] ^ c)
            rows = pl.multiple_of(block * size + last * half, 32)
            out_ref[c, n] = full_s[pl.ds(rows, half), :]


def out_grads_call(at, grad, attended):
    width, inner = grad.shape[1], attended.shape[1]
    shape = jax.ShapeDtypeStruct((2, 8, width // 16, inner), jnp.bfloat16)
    return pl.pallas_call(
        out_grads_kernel,
        grid=(1,),
        in_specs=[pl.BlockSpec(memory_space=pltpu.SMEM), full_spec(grad), full_spec(attended)],
        out_specs=full_spec(shape),
        out_shape=shape,
        scratch_shapes=[pltpu.VMEM((width, inner), jnp.bfloat16)],
        compiler_params=pltpu.CompilerParams(vmem_limit_bytes=32 << 20),
        name="out_grads",
        cost_estimate=cost(3),
    )(at, grad, attended)


EVERY = ("y", "x", "c", "z")
SWAP = ((0, 1), (1, 0))


def swap(value, axis):
    return lax.ppermute(value, axis, SWAP)


def gather_blocks(value, size):
    shift = lambda k: [(i, (i + k) % size) for i in range(size)]
    return [value] + [lax.ppermute(value, "z", shift(k)) for k in range(1, size)]


def gather_sides(value):
    return swap(value, "x"), swap(value, "y")


def gather_corner(xn, yn):
    half = xn.shape[0] // 2
    return swap(yn[:half], "x"), swap(xn[half:], "y")


def gather_square(value):
    sides = gather_sides(value)
    return (value, *sides, *gather_corner(*sides))


def reduce_square(keep, send_x, send_y):
    return reduce_square_rest(keep, swap(send_x, "x"), swap(send_y, "y"))


def reduce_square_rest(keep, from_x, from_y):
    low = jnp.bfloat16
    half = from_x.shape[0] // 2
    pass_y = swap((keep[3 * half :] + from_x[half:].astype(jnp.float32)).astype(low), "y")
    pass_x = swap((keep[2 * half : 3 * half] + from_y[half:].astype(jnp.float32)).astype(low), "x")
    return keep, from_x, from_y, pass_x, pass_y


def total_square(pieces):
    keep, from_x, from_y, pass_x, pass_y = pieces
    half = pass_x.shape[0]
    wide = lambda v: v.astype(jnp.float32)
    return jnp.concatenate(
        [
            keep[:half] + wide(from_x[:half]) + wide(pass_y),
            keep[half : 2 * half] + wide(from_y[:half]) + wide(pass_x),
        ],
        axis=0,
    )


def reduce_line(part, at, size, between=None):
    block = lambda k: lax.dynamic_index_in_dim(part, jnp.clip(at + k, 0, size - 1), 0, keepdims=False)
    wide = lambda v: v.astype(jnp.float32)
    up, down = None, None
    for step in range(1, size):
        k = size - step
        send_up, send_down = block(k), block(-k)
        if up is not None:
            send_up = (wide(send_up) + wide(up)).astype(part.dtype)
            send_down = (wide(send_down) + wide(down)).astype(part.dtype)
        up = lax.ppermute(send_up, "z", [(i, i + 1) for i in range(step)])
        down = lax.ppermute(send_down, "z", [(size - 1 - i, size - 2 - i) for i in range(step)])
        if between is not None:
            up, down = between(step, up, down)
    return wide(block(0)) + wide(up) + wide(down)


def all_to_all(value, axes):
    return lax.all_to_all(value, axes, 0, 0, tiled=True)


def tie(*values):
    return lax.optimization_barrier(values)


def fast_local(sizes, *args):
    (tokens, cotangent, segments, positions, norm_in, w_query, w_key, w_value, w_out, norm_mid, w_gate, w_up, w_down) = args
    nz = sizes["z"]
    devices = sizes["y"] * sizes["x"] * sizes["c"] * nz
    plane = devices // nz
    rows, span, width = tokens.shape
    count = rows * span
    chunk = segments.shape[1]
    length = chunk * sizes["x"] * sizes["c"]
    x_at, c_at, z_at = lax.axis_index("x"), lax.axis_index("c"), lax.axis_index("z")
    place = z_at.reshape(1).astype(jnp.int32)
    at = jnp.stack([lax.axis_index("y"), x_at, c_at, z_at]).astype(jnp.int32)

    gains = jnp.concatenate([norm_in, norm_mid], axis=1)
    share = norm_in.shape[1]
    gains = jnp.pad(gains, ((0, 0), (0, LN - 2 * share)))
    gains = all_to_all(jnp.broadcast_to(gains, (nz, LN)), "z")

    own, gains, w_o = tie(tokens.reshape(count, width), gains, w_out[0].T)
    blocks = gather_blocks(own, nz)
    w_o = jnp.stack(gather_blocks(w_o, nz))

    gains = all_to_all(jnp.broadcast_to(gains, (plane, nz, LN)).reshape(plane * nz, LN), ("y", "x", "c"))
    gain_in = gains[:, :share].reshape(1, width)
    gain_mid = gains[:, share : 2 * share].reshape(1, width)

    kv_local = w_key.shape[2] // HD
    per_head = lambda w: w[0].reshape(w.shape[1], kv_local, -1)
    w_qkv = jnp.concatenate([per_head(w_query), per_head(w_key), per_head(w_value)], axis=2)
    w_qkv = lax.all_gather(w_qkv.reshape(w_qkv.shape[0], -1), ("y", "x", "c"), axis=0, tiled=True)

    gate, up, down, _ = tie(w_gate[0], w_up[0], w_down[0], gains)
    w_ff = all_to_all(cut_call(gate, up, down), ("y", "x", "c"))
    w_ff = w_ff.reshape(width, 3 * LN)

    last = (x_at * sizes["c"] + c_at + 1) * chunk - 1
    begin = last - positions[:, -1] - jnp.where(segments[:, -1] == 2, 3 * length // 4, 0)
    lanes = jnp.arange(LN, dtype=jnp.int32) % (HD // 2)
    frequency = THETA ** (-(2.0 * lanes.astype(jnp.float32)) / HD)
    token_angle = positions.astype(jnp.float32)[:, :, None] * frequency
    first = lax.dynamic_slice_in_dim(begin, c_at, 1).astype(jnp.int32)
    index = jnp.arange(length, dtype=jnp.int32)
    row_angle = (index - doc_low(index, first[0], length)).astype(jnp.float32)[:, None] * frequency
    token_cos, token_sin = jnp.cos(token_angle), jnp.sin(token_angle)
    row_cos, row_sin = jnp.cos(row_angle), jnp.sin(row_angle)

    sides = gather_sides(w_o)
    blocks[1], *sides = tie(blocks[1], *sides)
    w_o = jnp.concatenate([w_o, *sides, *gather_corner(*sides)], axis=0)
    w_o = (w_o, swap(w_o, "c"))
    normed, qkv = qkv_call(place, blocks, gain_in, w_qkv, token_cos, token_sin, rows)
    qkv = all_to_all(qkv, ("x", "c")).reshape(length, 3 * LN)

    w_ff, _ = tie(w_ff, normed)
    w_mine = lax.all_gather(w_ff, "z", axis=0, tiled=True)
    cot_low = cotangent.reshape(count, width)
    cot_first, _ = tie(cot_low, qkv)
    cot_sides = gather_sides(cot_first)

    attended, attended_float, log_total = attn_fwd(first, qkv)
    attended, *cot_sides = tie(attended, *cot_sides)
    attended = all_to_all(attended, ("x", "c", "z"))
    w_o = place_call(at, *w_o, True)
    attended, *corner = tie(attended, *gather_corner(*cot_sides))
    cot_pieces = (cot_low, *cot_sides, *corner)
    middle, normed_b, attended_low = out_call(attended, w_o, own, gain_mid, rows)
    w_mine, _ = tie(w_mine, normed_b)
    w_mine = w_mine.reshape(nz, width, 3 * LN)
    w_other = swap(w_mine, "c")
    b_pieces = gather_square(normed_b)

    grad_hidden = down_back_call(cot_pieces, w_mine, w_other)
    grad_gu, hidden, *sends = units_call(b_pieces, w_mine, w_other, grad_hidden)
    from_x, from_y = swap(sends[1], "x"), swap(sends[2], "y")
    ff_mine, ff_other = unit_grads_call(place, b_pieces, cot_pieces, grad_gu, hidden)
    from_x, from_y, ff_mine, ff_other = tie(from_x, from_y, ff_mine, ff_other)
    grad_b = reduce_square_rest(sends[0], from_x, from_y)
    grad_ff = ff_mine.astype(jnp.float32) + swap(ff_other, "c").astype(jnp.float32)
    grad_ff = grad_ff.astype(jnp.bfloat16).reshape(nz * width, 3 * LN)
    grad_ff = lax.psum_scatter(grad_ff, "z", scatter_dimension=0, tiled=True)
    grad_mid, grad_low, grad_o, gain_grad_mid = mid_back_call(
        grad_b, middle, cot_low, gain_mid, w_o, rows, nz
    )
    grad_o = all_to_all(grad_o, ("x", "c", "z"))

    grad_wo = out_grads_call(at, grad_low, attended_low)
    grad_wo = grad_wo[0].astype(jnp.float32) + swap(grad_wo[1], "c").astype(jnp.float32)
    step = width // 16
    flat_wo = grad_wo.reshape(8 * step, -1)
    keep_wo = jnp.concatenate([flat_wo[: 2 * step], flat_wo[6 * step :]], axis=0)
    grad_wo = total_square(
        reduce_square(
            keep_wo,
            flat_wo[2 * step : 4 * step].astype(jnp.bfloat16),
            flat_wo[4 * step : 6 * step].astype(jnp.bfloat16),
        )
    ).astype(jnp.bfloat16)
    grad_wo = jnp.stack([grad_wo[:, z * 3 * LN : (z + 1) * 3 * LN] for z in range(nz)])

    grad_qkv = attn_bwd(first, qkv, grad_o, attended_float, log_total, row_cos, row_sin)
    grad_qkv = all_to_all(grad_qkv.reshape(-1, chunk, 3 * LN), ("x", "c"))
    grad_qkv = grad_qkv.reshape(kv_local, rows, chunk, 3 * LN)
    part, gain_grad_in = da_call(place, blocks, grad_qkv, w_qkv, rows)
    grad_wqkv = qkv_grads_call(
        normed.reshape(rows * chunk, width), grad_qkv.reshape(kv_local, rows * chunk, 3 * LN)
    )
    grad_wqkv = lax.psum_scatter(grad_wqkv, ("y", "x", "c"), scatter_dimension=0, tiled=True)
    gain_grads = jnp.concatenate(
        [gain_grad_in.reshape(devices, share), gain_grad_mid.reshape(devices, share)], axis=1
    )
    gain_grads = jnp.pad(gain_grads, ((0, 0), (0, LN - 2 * share)))
    late = {"ff": grad_ff}

    def between(step, up, down):
        if step == 1:
            late["hidden"], _, _ = tie(hidden, up, down)
            late["wo"] = all_to_all(grad_wo, "z")
            late["gain"] = all_to_all(gain_grads, EVERY)
        if step == nz - 2:
            up, down, late["wo"], late["gain"] = tie(up, down, late["wo"], late["gain"])
        if step == nz - 2:
            late["ff"], _ = tie(late["ff"], up)
            late["ff"] = all_to_all(late["ff"].reshape(plane, width // plane, 3 * LN), ("y", "x", "c"))
        if step == nz - 1:
            up, down, late["ff"] = tie(up, down, late["ff"])
        return up, down

    grad_a = reduce_line(part.reshape(nz, count, width), z_at, nz, between)
    grad_ff = late["ff"]
    out = middle + total_square(reduce_square(*down_call(late["hidden"], w_mine, w_other)))
    grad_wo = jnp.sum(late["wo"].astype(jnp.float32), axis=0)
    gain_grads = jnp.sum(late["gain"], axis=0, keepdims=True)

    stream = own.astype(jnp.float32)
    factor = lax.rsqrt(jnp.mean(stream * stream, axis=-1, keepdims=True) + EPS)
    back_in, _ = norm_back(stream, factor, gain_in, grad_a)
    grad_tokens = grad_mid + back_in
    grad_wqkv = grad_wqkv.astype(jnp.float32).reshape(-1, kv_local, 4 * HD)
    flat = lambda g: g.reshape(1, g.shape[0], -1)
    grad_gate, grad_up, grad_down = uncut_call(grad_ff)
    return (
        out.reshape(tokens.shape),
        grad_tokens.reshape(tokens.shape),
        gain_grads[:, :share],
        flat(grad_wqkv[:, :, : 2 * HD]),
        flat(grad_wqkv[:, :, 2 * HD : 3 * HD]),
        flat(grad_wqkv[:, :, 3 * HD :]),
        grad_wo.T[None],
        gain_grads[:, share : 2 * share],
        grad_gate[None],
        grad_up[None],
        grad_down[None],
    )


def fast_solution(mesh, cores):
    batch, seq, kv = mesh.devices.shape
    fine = Mesh(mesh.devices.reshape(batch, seq // cores, cores, kv), EVERY)
    sizes = dict(fine.shape)
    row_spec = P("y", ("x", "c", "z"), None)
    seq_spec = P("y", ("x", "c"))
    gain_spec = P(None, EVERY)
    in_w = P(None, ("y", "x", "c"), "z")
    out_w = P(None, "z", ("y", "x", "c"))
    in_specs = (row_spec, row_spec, seq_spec, seq_spec, gain_spec, in_w, in_w, in_w, out_w, gain_spec, in_w, in_w, out_w)
    out_specs = (row_spec, row_spec, gain_spec, in_w, in_w, in_w, out_w, gain_spec, in_w, in_w, out_w)
    return jax.shard_map(
        partial(fast_local, sizes), mesh=fine, in_specs=in_specs, out_specs=out_specs, check_vma=False
    )


def solution(mesh):
    batch, seq, kv = (mesh.shape[name] for name in ("batch", "seq", "kv"))
    general = general_solution(mesh)
    if (batch, seq) != (2, 4):
        return general
    fast = fast_solution(mesh, 2)

    def run(*args):
        rows, length, width = args[0].shape
        kv_heads, q_heads = args[6].shape[2] // HD, args[5].shape[2] // HD
        fits = (
            rows == 2 * batch
            and kv_heads == 2 * kv
            and q_heads == 2 * kv_heads
            and length == 128 * seq * kv
            and length % (4 * BQ) == 0
            and width % LN == 0
            and 2 * width // (batch * seq * kv) <= LN
            and args[10].shape[2] == LN * batch * seq * kv
        )
        return (fast if fits else general)(*args)

    return run
```

```python
import functools
import math
from functools import partial

import jax
import jax.numpy as jnp
from jax import lax
from jax.experimental import pallas as pl
from jax.experimental.pallas import tpu as pltpu
from jax.sharding import Mesh
from jax.sharding import PartitionSpec as P

HD = 96
LAYERS = 1


EPS = 1e-05
THETA = 100000.0
BIG_NEG = -1e30


def rotary(positions_row):
    half_width = HD // 2
    frequency = THETA ** (-(2.0 * jnp.arange(half_width, dtype=jnp.float32)) / HD)
    angles = positions_row.astype(jnp.float32)[:, None] * frequency[None, :]
    cosine = jnp.concatenate([jnp.cos(angles), jnp.cos(angles)], axis=1)
    sine_table = jnp.concatenate([jnp.sin(angles), jnp.sin(angles)], axis=1)
    return (cosine, sine_table)


def rotate(head_vals, cosine, sine_table):
    half_width = head_vals.shape[-1] // 2
    swapped = jnp.concatenate([-head_vals[..., half_width:], head_vals[..., :half_width]], axis=-1)
    return head_vals * cosine[:, None, :] + swapped * sine_table[:, None, :]


def rms_norm(stream, gain):
    factor = lax.rsqrt(jnp.mean(stream * stream, axis=-1, keepdims=True) + EPS)
    return (stream * factor * gain, factor)


def norm_back(stream, factor, gain, upstream):
    scaled_grad = upstream * gain
    inner_mean = jnp.mean(scaled_grad * stream, axis=-1, keepdims=True)
    grad_stream = factor * scaled_grad - stream * factor**3 * inner_mean
    return (grad_stream, jnp.sum(upstream * stream * factor, axis=0))


def key_width(key_count):
    return math.gcd(key_count, 1024)


def contract(left_side, right_side, left_dim, right_dim):
    return lax.dot_general(
        left_side,
        right_side,
        (((left_dim,), (right_dim,)), ((), ())),
        preferred_element_type=jnp.float32,
    )


def spread(shard_rows):
    return lax.all_gather(shard_rows, "kv", axis=0, tiled=True)


def token_sum(pairs):
    summed = None
    for left_part, right_part, right_dim in pairs:
        product = contract(left_part, right_part, 1, right_dim)
        summed = product if summed is None else summed + product
    return lax.psum_scatter(
        summed.astype(jnp.bfloat16), "kv", scatter_dimension=0, tiled=True
    ).astype(jnp.float32)


def split_block(kv_both, seg_keys, offset, step_width, kv_local, head_size):
    kv_block = lax.dynamic_slice_in_dim(kv_both, offset, step_width, 0)
    key_block = kv_block[:, : kv_local * head_size].reshape(step_width, kv_local, head_size)
    value_block = kv_block[:, kv_local * head_size :].reshape(step_width, kv_local, head_size)
    seg_block = lax.dynamic_slice_in_dim(seg_keys, offset, step_width, 0)
    return (key_block, value_block, seg_block)


def forward_row(queries, seg_query, fold_state, kv_both, seg_keys, first_query, key_start):
    key_count = kv_both.shape[0]
    step_width = key_width(key_count)
    query_count, kv_local, group_size, head_size = queries.shape
    query_index = first_query + jnp.arange(query_count, dtype=jnp.int32)
    score_scale = head_size ** (-0.5)

    def forward_one_step(step_index, inner_state):
        running_max, weight_total, value_total = inner_state
        offset = step_index * step_width
        key_block, value_block, seg_block = split_block(
            kv_both, seg_keys, offset, step_width, kv_local, head_size
        )
        key_index = offset + jnp.arange(step_width, dtype=jnp.int32)
        allowed = (seg_query[:, None] == seg_block[None, :]) & (
            key_index[None, :] <= query_index[:, None]
        )
        scores = (
            jnp.einsum("qkgd,pkd->kgqp", queries, key_block, preferred_element_type=jnp.float32)
            * score_scale
        )
        scores = jnp.where(allowed, scores, BIG_NEG)
        new_max = jnp.maximum(running_max, jnp.max(scores, axis=-1))
        weights = jnp.where(allowed, jnp.exp(scores - new_max[..., None]), 0.0)
        rescale = jnp.exp(running_max - new_max)
        weight_total = rescale * weight_total + jnp.sum(weights, axis=-1)
        update = jnp.einsum(
            "kgqp,pkd->qkgd",
            weights.astype(jnp.bfloat16),
            value_block,
            preferred_element_type=jnp.float32,
        )
        value_total = jnp.transpose(rescale, (2, 0, 1))[..., None] * value_total + update
        return (new_max, weight_total, value_total)

    return lax.fori_loop(0, key_count // step_width, forward_one_step, fold_state)


def forward_fold(queries, seg_query, first_query, fold_state, pieces, key_start):
    kv_both, seg_keys = pieces
    row_fn = partial(forward_row, first_query=first_query, key_start=key_start)
    return jax.vmap(row_fn, in_axes=(0, 0, 0, 1, 1))(
        queries, seg_query, fold_state, kv_both, seg_keys
    )


def backward_row(
    queries,
    grad_attn,
    log_total,
    row_delta,
    seg_query,
    fold_state,
    kv_both,
    seg_keys,
    first_query,
    key_start,
):
    key_count = kv_both.shape[0]
    step_width = key_width(key_count)
    query_count, kv_local, group_size, head_size = queries.shape
    query_index = first_query + jnp.arange(query_count, dtype=jnp.int32)
    score_scale = head_size ** (-0.5)

    def backward_one_step(step_index, inner_state):
        grad_queries, grad_buffer = inner_state
        offset = step_index * step_width
        key_block, value_block, seg_block = split_block(
            kv_both, seg_keys, offset, step_width, kv_local, head_size
        )
        key_index = offset + jnp.arange(step_width, dtype=jnp.int32)
        allowed = (seg_query[:, None] == seg_block[None, :]) & (
            key_index[None, :] <= query_index[:, None]
        )
        scores = (
            jnp.einsum("qkgd,pkd->kgqp", queries, key_block, preferred_element_type=jnp.float32)
            * score_scale
        )
        probs_block = jnp.where(allowed, jnp.exp(scores - log_total[..., None]), 0.0)
        grad_probs = jnp.einsum(
            "qkgd,pkd->kgqp", grad_attn, value_block, preferred_element_type=jnp.float32
        )
        grad_scores = (probs_block * (grad_probs - row_delta[..., None])).astype(jnp.bfloat16)
        grad_queries = (
            grad_queries
            + jnp.einsum(
                "kgqp,pkd->qkgd", grad_scores, key_block, preferred_element_type=jnp.float32
            )
            * score_scale
        )
        grad_keys = (
            jnp.einsum("kgqp,qkgd->pkd", grad_scores, queries, preferred_element_type=jnp.float32)
            * score_scale
        )
        grad_values = jnp.einsum(
            "kgqp,qkgd->pkd",
            probs_block.astype(jnp.bfloat16),
            grad_attn,
            preferred_element_type=jnp.float32,
        )
        joined = jnp.concatenate(
            [grad_keys.reshape(step_width, -1), grad_values.reshape(step_width, -1)], axis=1
        )
        grad_buffer = lax.dynamic_update_slice_in_dim(grad_buffer, joined, offset, 0)
        return (grad_queries, grad_buffer)

    return lax.fori_loop(0, key_count // step_width, backward_one_step, fold_state)


def backward_fold(
    queries, grad_attn, log_total, row_delta, seg_query, first_query, fold_state, pieces, key_start
):
    kv_both, seg_keys = pieces
    row_fn = partial(backward_row, first_query=first_query, key_start=key_start)
    return jax.vmap(row_fn, in_axes=(0, 0, 0, 0, 0, 0, 1, 1))(
        queries, grad_attn, log_total, row_delta, seg_query, fold_state, kv_both, seg_keys
    )


def layer_forward(stream, gain_pair, matrices, seg_info, tables):
    gain_in, gain_mid = gain_pair
    w_query, w_key, w_value, w_out, w_gate, w_up, w_down = matrices
    seg_query, seg_keys = seg_info
    cosine, sine_table = tables
    row_count = seg_query.shape[0]
    kv_local = w_key.shape[1] // HD
    head_local = w_query.shape[1] // HD
    group_size = head_local // kv_local
    normed_a, factor_a = rms_norm(stream, gain_in)
    spread_a = spread(normed_a.astype(jnp.bfloat16))
    flat_count = spread_a.shape[0]
    token_count = flat_count // row_count
    raw_queries = jnp.dot(spread_a, w_query, preferred_element_type=jnp.float32).reshape(
        flat_count, head_local, HD
    )
    queries = (
        rotate(raw_queries, cosine, sine_table)
        .astype(jnp.bfloat16)
        .reshape(token_count, row_count, kv_local, group_size, HD)
    )
    queries = jnp.transpose(queries, (1, 0, 2, 3, 4))
    raw_keys = jnp.dot(spread_a, w_key, preferred_element_type=jnp.float32).reshape(
        flat_count, kv_local, HD
    )
    keys_low = (
        rotate(raw_keys, cosine, sine_table).astype(jnp.bfloat16).reshape(flat_count, kv_local * HD)
    )
    values_low = jnp.dot(spread_a, w_value, preferred_element_type=jnp.float32).astype(jnp.bfloat16)
    kv_both = jnp.concatenate([keys_low, values_low], axis=1).reshape(
        token_count, row_count, 2 * kv_local * HD
    )
    first_query = lax.axis_index("seq") * token_count
    start_state = (
        jnp.full((row_count, kv_local, group_size, token_count), BIG_NEG, jnp.float32),
        jnp.zeros((row_count, kv_local, group_size, token_count), jnp.float32),
        jnp.zeros((row_count, token_count, kv_local, group_size, HD), jnp.float32),
    )
    running_max, weight_total, value_total = forward_fold(
        queries,
        seg_query,
        first_query,
        start_state,
        (
            lax.all_gather(kv_both, "seq", axis=0, tiled=True),
            lax.all_gather(seg_keys, "seq", axis=0, tiled=True),
        ),
        jnp.int32(0),
    )
    attn_float = value_total / jnp.transpose(weight_total, (0, 3, 1, 2))[..., None]
    log_total = running_max + jnp.log(weight_total)
    attn_low = (
        jnp.transpose(attn_float, (1, 0, 2, 3, 4))
        .reshape(flat_count, head_local * HD)
        .astype(jnp.bfloat16)
    )
    stream_mid = stream + token_sum(((attn_low, w_out, 0),))
    normed_b, factor_b = rms_norm(stream_mid, gain_mid)
    spread_b = spread(normed_b.astype(jnp.bfloat16))
    gate_val = jnp.dot(spread_b, w_gate, preferred_element_type=jnp.float32)
    up_val = jnp.dot(spread_b, w_up, preferred_element_type=jnp.float32)
    hidden = (jax.nn.silu(gate_val) * up_val).astype(jnp.bfloat16)
    stream_out = stream_mid + token_sum(((hidden, w_down, 0),))
    saved_state = (
        stream,
        factor_a,
        spread_a,
        queries,
        kv_both,
        attn_float,
        attn_low,
        log_total,
        stream_mid,
        factor_b,
        spread_b,
        gate_val,
        up_val,
        hidden,
    )
    return (stream_out, saved_state)


def layer_backward(saved_state, grad_stream, gain_pair, matrices, seg_info, tables):
    (
        stream,
        factor_a,
        spread_a,
        queries,
        kv_both,
        attn_float,
        attn_low,
        log_total,
        stream_mid,
        factor_b,
        spread_b,
        gate_val,
        up_val,
        hidden,
    ) = saved_state
    gain_in, gain_mid = gain_pair
    w_query, w_key, w_value, w_out, w_gate, w_up, w_down = matrices
    seg_query, seg_keys = seg_info
    cosine, sine_table = tables
    row_count, token_count, kv_local, group_size, head_size = queries.shape
    head_local = kv_local * group_size
    flat_count = row_count * token_count
    grad_low = spread(grad_stream.astype(jnp.bfloat16))
    grad_down_w = contract(hidden, grad_low, 0, 0)
    grad_hidden = contract(grad_low, w_down, 1, 1)
    sigmoid_gate = jax.nn.sigmoid(gate_val)
    silu_gate = gate_val * sigmoid_gate
    grad_gate_low = (
        grad_hidden * up_val * sigmoid_gate * (1.0 + gate_val * (1.0 - sigmoid_gate))
    ).astype(jnp.bfloat16)
    grad_up_low = (grad_hidden * silu_gate).astype(jnp.bfloat16)
    grad_gate_w = contract(spread_b, grad_gate_low, 0, 0)
    grad_up_w = contract(spread_b, grad_up_low, 0, 0)
    grad_normed_b = token_sum(((grad_gate_low, w_gate, 1), (grad_up_low, w_up, 1)))
    back_mid, grad_gain_mid = norm_back(stream_mid, factor_b, gain_mid, grad_normed_b)
    grad_mid = grad_stream + back_mid
    grad_attn_full = spread(grad_mid.astype(jnp.bfloat16))
    grad_out_w = contract(attn_low, grad_attn_full, 0, 0)
    grad_attn = (
        contract(grad_attn_full, w_out, 1, 1)
        .astype(jnp.bfloat16)
        .reshape(token_count, row_count, kv_local, group_size, head_size)
    )
    grad_attn = jnp.transpose(grad_attn, (1, 0, 2, 3, 4))
    row_delta = jnp.transpose(jnp.sum(grad_attn * attn_float, axis=-1), (0, 2, 3, 1))
    first_query = lax.axis_index("seq") * token_count
    row_length = token_count * lax.axis_size("seq")
    start_state = (
        jnp.zeros((row_count, token_count, kv_local, group_size, head_size), jnp.float32),
        jnp.zeros((row_count, row_length, 2 * kv_local * head_size), jnp.float32),
    )
    grad_queries, grad_buffer = backward_fold(
        queries,
        grad_attn,
        log_total,
        row_delta,
        seg_query,
        first_query,
        start_state,
        (
            lax.all_gather(kv_both, "seq", axis=0, tiled=True),
            lax.all_gather(seg_keys, "seq", axis=0, tiled=True),
        ),
        jnp.int32(0),
    )
    grad_kv = lax.psum_scatter(
        grad_buffer.astype(jnp.bfloat16), "seq", scatter_dimension=1, tiled=True
    ).astype(jnp.float32)
    grad_kv = jnp.transpose(grad_kv, (1, 0, 2)).reshape(flat_count, 2 * kv_local * head_size)
    grad_queries = jnp.transpose(grad_queries, (1, 0, 2, 3, 4)).reshape(
        flat_count, head_local, head_size
    )
    grad_q_low = (
        rotate(grad_queries, cosine, -sine_table)
        .astype(jnp.bfloat16)
        .reshape(flat_count, head_local * head_size)
    )
    grad_k_low = (
        rotate(
            grad_kv[:, : kv_local * head_size].reshape(flat_count, kv_local, head_size),
            cosine,
            -sine_table,
        )
        .astype(jnp.bfloat16)
        .reshape(flat_count, kv_local * head_size)
    )
    grad_v_low = grad_kv[:, kv_local * head_size :].astype(jnp.bfloat16)
    grad_query_w = contract(spread_a, grad_q_low, 0, 0)
    grad_key_w = contract(spread_a, grad_k_low, 0, 0)
    grad_value_w = contract(spread_a, grad_v_low, 0, 0)
    grad_normed_a = token_sum(
        ((grad_q_low, w_query, 1), (grad_k_low, w_key, 1), (grad_v_low, w_value, 1))
    )
    back_in, grad_gain_in = norm_back(stream, factor_a, gain_in, grad_normed_a)
    grad_input = grad_mid + back_in
    weight_grads = (
        lax.psum_scatter(
            grad_query_w.astype(jnp.bfloat16), ("batch", "seq"), scatter_dimension=0, tiled=True
        ).astype(jnp.float32),
        lax.psum_scatter(
            grad_key_w.astype(jnp.bfloat16), ("batch", "seq"), scatter_dimension=0, tiled=True
        ).astype(jnp.float32),
        lax.psum_scatter(
            grad_value_w.astype(jnp.bfloat16), ("batch", "seq"), scatter_dimension=0, tiled=True
        ).astype(jnp.float32),
        lax.psum_scatter(
            grad_out_w.astype(jnp.bfloat16), ("batch", "seq"), scatter_dimension=1, tiled=True
        ).astype(jnp.float32),
        lax.psum_scatter(
            grad_gate_w.astype(jnp.bfloat16), ("batch", "seq"), scatter_dimension=0, tiled=True
        ).astype(jnp.float32),
        lax.psum_scatter(
            grad_up_w.astype(jnp.bfloat16), ("batch", "seq"), scatter_dimension=0, tiled=True
        ).astype(jnp.float32),
        lax.psum_scatter(
            grad_down_w.astype(jnp.bfloat16), ("batch", "seq"), scatter_dimension=1, tiled=True
        ).astype(jnp.float32),
    )
    return (grad_input, weight_grads, grad_gain_in, grad_gain_mid)


def to_flat(shard_rows):
    row_count, token_part, width = shard_rows.shape
    return jnp.transpose(shard_rows.astype(jnp.float32), (1, 0, 2)).reshape(
        token_part * row_count, width
    )


def from_flat(flat_rows, row_count):
    token_part = flat_rows.shape[0] // row_count
    return jnp.transpose(flat_rows.reshape(token_part, row_count, flat_rows.shape[1]), (1, 0, 2))


def general_local(
    tokens,
    cotangent,
    segments,
    positions,
    norm_in,
    w_query,
    w_key,
    w_value,
    w_out,
    norm_mid,
    w_gate,
    w_up,
    w_down,
):
    gains_in, gains_mid = (
        lax.all_gather(norm_in, ("batch", "seq", "kv"), axis=1, tiled=True),
        lax.all_gather(norm_mid, ("batch", "seq", "kv"), axis=1, tiled=True),
    )
    row_count = tokens.shape[0]
    seg_info = (segments, jnp.transpose(segments, (1, 0)))
    tables = rotary(jnp.transpose(positions, (1, 0)).reshape(-1))

    def fetch_layer(layer_index):
        return (
            lax.all_gather(w_query[layer_index], ("batch", "seq"), axis=0, tiled=True),
            lax.all_gather(w_key[layer_index], ("batch", "seq"), axis=0, tiled=True),
            lax.all_gather(w_value[layer_index], ("batch", "seq"), axis=0, tiled=True),
            lax.all_gather(w_out[layer_index], ("batch", "seq"), axis=1, tiled=True),
            lax.all_gather(w_gate[layer_index], ("batch", "seq"), axis=0, tiled=True),
            lax.all_gather(w_up[layer_index], ("batch", "seq"), axis=0, tiled=True),
            lax.all_gather(w_down[layer_index], ("batch", "seq"), axis=1, tiled=True),
        )

    stream = to_flat(tokens)
    fetched = []
    states = []
    layer_index = 0
    matrices = fetch_layer(layer_index)
    layer_inputs = [stream]
    stream, saved_state = layer_forward(
        stream, (gains_in[layer_index], gains_mid[layer_index]), matrices, seg_info, tables
    )
    fetched.append(matrices)
    states.append(saved_state)
    grad_stream = to_flat(cotangent)
    grads_in = []
    grads_mid = []
    weight_lists = []
    for layer_index in reversed(range(LAYERS)):
        gain_pair = (gains_in[layer_index], gains_mid[layer_index])
        matrices = fetch_layer(layer_index)
        saved_state = layer_forward(
            layer_inputs[layer_index], gain_pair, matrices, seg_info, tables
        )[1]
        grad_stream, weight_grads, grad_gain_in, grad_gain_mid = layer_backward(
            saved_state, grad_stream, gain_pair, matrices, seg_info, tables
        )
        grads_in.insert(0, grad_gain_in)
        grads_mid.insert(0, grad_gain_mid)
        weight_lists.insert(0, weight_grads)
    gain_grads_in, gain_grads_mid = (
        lax.psum_scatter(
            jnp.stack(grads_in), ("batch", "seq", "kv"), scatter_dimension=1, tiled=True
        ),
        lax.psum_scatter(
            jnp.stack(grads_mid), ("batch", "seq", "kv"), scatter_dimension=1, tiled=True
        ),
    )
    stacked_grads = [
        jnp.stack([grad_set[member] for grad_set in weight_lists]) for member in range(7)
    ]
    return (
        from_flat(stream, row_count),
        from_flat(grad_stream, row_count),
        gain_grads_in,
        stacked_grads[0],
        stacked_grads[1],
        stacked_grads[2],
        stacked_grads[3],
        gain_grads_mid,
        stacked_grads[4],
        stacked_grads[5],
        stacked_grads[6],
    )


def general_solution(mesh):
    in_specs = (
        P("batch", ("seq", "kv"), None),
        P("batch", ("seq", "kv"), None),
        P("batch", "seq"),
        P("batch", "seq"),
        P(None, ("batch", "seq", "kv")),
        P(None, ("batch", "seq"), "kv"),
        P(None, ("batch", "seq"), "kv"),
        P(None, ("batch", "seq"), "kv"),
        P(None, "kv", ("batch", "seq")),
        P(None, ("batch", "seq", "kv")),
        P(None, ("batch", "seq"), "kv"),
        P(None, ("batch", "seq"), "kv"),
        P(None, "kv", ("batch", "seq")),
    )
    out_specs = (
        P("batch", ("seq", "kv"), None),
        P("batch", ("seq", "kv"), None),
        P(None, ("batch", "seq", "kv")),
        P(None, ("batch", "seq"), "kv"),
        P(None, ("batch", "seq"), "kv"),
        P(None, ("batch", "seq"), "kv"),
        P(None, "kv", ("batch", "seq")),
        P(None, ("batch", "seq", "kv")),
        P(None, ("batch", "seq"), "kv"),
        P(None, ("batch", "seq"), "kv"),
        P(None, "kv", ("batch", "seq")),
    )
    return jax.shard_map(general_local, mesh=mesh, in_specs=in_specs, out_specs=out_specs, check_vma=False)


LN = 128
NEG=-1e30
C2 = (96 ** -0.5) * 1.4426950408889634

def cost(microseconds):
    return pl.CostEstimate(
        flops=microseconds * 10**9, bytes_accessed=microseconds * 3 * 10**6, transcendentals=0
    )


def lane_iota(rows):
    return lax.broadcasted_iota(jnp.int32, (rows, LN), 1)

def unpack4(t0, t1, t2):
    lane = lane_iota(t0.shape[0])
    live = lane < HD
    zero = jnp.zeros_like(t0)
    a = t0
    b = pltpu.roll(jnp.where(lane >= 96, t0, t1), 32, 1)
    c = pltpu.roll(jnp.where(lane >= 64, t1, t2), 64, 1)
    d = pltpu.roll(t2, 96, 1)
    return tuple(jnp.where(live, v, zero) for v in (a, b, c, d))

def pack4(a, b, c, d):
    lane = lane_iota(a.shape[0])
    b, c, d = pltpu.roll(b, 96, 1), pltpu.roll(c, 64, 1), pltpu.roll(d, 32, 1)
    return (jnp.where(lane < 96, a, b), jnp.where(lane < 64, b, c), jnp.where(lane < 32, c, d))

def split3(x):
    x = x.astype(jnp.float32)
    return x[:, :LN], x[:, LN:2*LN], x[:, 2*LN:]

def doc_low(index, first, length):
    second = first + 3 * length // 4
    return jnp.where(index >= second, second, jnp.where(index >= first, first, 0))

BQ = 256

def dotf(a, b, dims):
    return lax.dot_general(a, b, (dims, ((), ())), preferred_element_type=jnp.float32)

def attn_fwd_kernel(length, first_ref, x_ref, o_ref, of_ref, lse_ref, q_s, k_s, v_s, s_s):
    i = pl.program_id(0)
    blocks = length // BQ
    first = first_ref[0]
    @pl.when(i == 0)
    def _():
        def body(j, carry):
            rows = pl.ds(pl.multiple_of(j * BQ, BQ), BQ)
            q0, q1, k, v = unpack4(*split3(x_ref[rows, :]))
            q_s[j, :BQ, :] = q0.astype(jnp.bfloat16)
            q_s[j, BQ:, :] = q1.astype(jnp.bfloat16)
            k_s[j] = k.astype(jnp.bfloat16)
            v_s[j] = v.astype(jnp.bfloat16)
            return carry
        lax.fori_loop(0, blocks, body, 0)
    q = q_s[i]
    clean_from = (length // 8 + BQ - 1) // BQ
    clean_to = 3 * length // 4 // BQ
    late = (3 * length // 4 + length // 8) // BQ
    start = jnp.where(i >= late, 3 * length // 4 // BQ, 0)
    head_masked = jnp.where(i < clean_to, jnp.minimum(clean_from, i), i)
    q_index = i * BQ + lax.broadcasted_iota(jnp.int32, (BQ, 1), 0)
    low = doc_low(q_index, first, length)

    def halves(v, op):
        return op(v[:, :LN], v[:, LN:])

    def score(j, top, masked):
        s = dotf(q, k_s[j], ((1,), (1,)))
        if masked:
            key = j * BQ + lax.broadcasted_iota(jnp.int32, (1, BQ), 1)
            ok = (key <= q_index) & (key >= low)
            s = jnp.where(jnp.concatenate([ok, ok], axis=0), s, NEG)
        s_s[j] = s
        return jnp.maximum(top, halves(s, jnp.maximum))

    top = jnp.full((2 * BQ, LN), NEG, jnp.float32)
    top = lax.fori_loop(start, head_masked, lambda j, t: score(j, t, True), top)
    top = lax.fori_loop(jnp.maximum(head_masked, start), i, lambda j, t: score(j, t, False), top)
    top = score(i, top, True)
    m = jnp.max(top, axis=1, keepdims=True) * C2

    def add(j, state):
        total, acc = state
        p = jnp.exp2(s_s[j] * C2 - m)
        total = total + halves(p, jnp.add)
        acc = acc + dotf(p.astype(jnp.bfloat16), v_s[j], ((1,), (0,)))
        return total, acc

    zero = jnp.zeros((2 * BQ, LN), jnp.float32)
    total, acc = lax.fori_loop(start, i + 1, add, (zero, zero))
    total = jnp.sum(total, axis=1, keepdims=True)
    out = acc / total
    lse = jnp.broadcast_to(m + jnp.log2(total), (2 * BQ, LN))
    lse_ref[0] = jnp.transpose(lse, (1, 0))[:8, :]
    of_ref[0] = out
    for d in range(2):
        parts = []
        for h in range(2):
            parts.append(out[BQ*0 + d*128 + h*64: d*128 + h*64 + 64])
            parts.append(out[BQ + d*128 + h*64: BQ + d*128 + h*64 + 64])
        t = pack4(*parts)
        for n in range(3):
            o_ref[d, :, n*LN:(n+1)*LN] = t[n].astype(jnp.bfloat16)

def attn_fwd(first, x):
    length = x.shape[0]
    blocks = length // BQ
    return pl.pallas_call(
        functools.partial(attn_fwd_kernel, length),
        grid=(blocks,),
        in_specs=[pl.BlockSpec(memory_space=pltpu.SMEM),
                  pl.BlockSpec((length, 3*LN), lambda i: (0, 0))],
        out_specs=[pl.BlockSpec((2, 64, 3*LN), lambda i: (i, 0, 0)),
                   pl.BlockSpec((1, 2*BQ, LN), lambda i: (i, 0, 0)),
                   pl.BlockSpec((1, 8, 2*BQ), lambda i: (i, 0, 0))],
        out_shape=[jax.ShapeDtypeStruct((length//128, 64, 3*LN), jnp.bfloat16),
                   jax.ShapeDtypeStruct((blocks, 2*BQ, LN), jnp.float32),
                   jax.ShapeDtypeStruct((blocks, 8, 2*BQ), jnp.float32)],
        scratch_shapes=[pltpu.VMEM((blocks, 2*BQ, LN), jnp.bfloat16),
                        pltpu.VMEM((blocks, BQ, LN), jnp.bfloat16),
                        pltpu.VMEM((blocks, BQ, LN), jnp.bfloat16),
                        pltpu.VMEM((blocks, 2*BQ, BQ), jnp.float32)],
        compiler_params=pltpu.CompilerParams(vmem_limit_bytes=48 << 20),
        name="attend",
        cost_estimate=cost(22),
    )(first, x)

def attn_bwd_kernel(length, first_ref, x_ref, do_ref, of_ref, lse_ref, cos_ref, sin_ref, out_ref,
                    q_s, k_s, v_s, do_s, dl_s, dq_s, dk_s, dv_s):
    j = pl.program_id(0)
    blocks = length // BQ
    first = first_ref[0]
    @pl.when(j == 0)
    def _():
        def body(b, carry):
            rows = pl.ds(pl.multiple_of(b * BQ, BQ), BQ)
            q0, q1, k, v = unpack4(*split3(x_ref[rows, :]))
            q_s[b, :BQ, :] = q0.astype(jnp.bfloat16)
            q_s[b, BQ:, :] = q1.astype(jnp.bfloat16)
            k_s[b] = k.astype(jnp.bfloat16)
            v_s[b] = v.astype(jnp.bfloat16)
            for d in range(2):
                parts = unpack4(*split3(do_ref[2*b + d]))
                for n, part in enumerate(parts):
                    at = (n % 2) * BQ + d*128 + (n // 2) * 64
                    do_s[b, at:at+64, :] = part.astype(jnp.bfloat16)
            prod = do_s[b].astype(jnp.float32) * of_ref[b]
            delta = jnp.broadcast_to(jnp.sum(prod, axis=1, keepdims=True), (2*BQ, LN))
            dl_s[b] = jnp.transpose(delta, (1, 0))[:8, :]
            dq_s[b] = jnp.zeros((2*BQ, LN), jnp.float32)
            return carry
        lax.fori_loop(0, blocks, body, 0)
    clean_from = (length // 8 + BQ - 1) // BQ
    clean_to = 3 * length // 4 // BQ
    late = (3 * length // 4 + length // 8) // BQ
    third = 3 * length // 4 // BQ
    stop = jnp.where(j >= third, blocks, late)
    k = k_s[j]
    v = v_s[j]
    dk_s[j] = jnp.zeros((BQ, LN), jnp.float32)
    dv_s[j] = jnp.zeros((BQ, LN), jnp.float32)
    key = j * BQ + lax.broadcasted_iota(jnp.int32, (BQ, 1), 0)

    def step(i, masked):
        q, do = q_s[i], do_s[i]
        s = dotf(k, q, ((1,), (1,)))
        p = jnp.exp2(s * C2 - lse_ref[i, 0:1, :])
        if masked:
            q_index = i * BQ + lax.broadcasted_iota(jnp.int32, (1, BQ), 1)
            ok = (key <= q_index) & (key >= doc_low(q_index, first, length))
            p = jnp.where(jnp.concatenate([ok, ok], axis=1), p, 0.0)
        dp = dotf(v, do, ((1,), (1,)))
        ds = (p * (dp - dl_s[i, 0:1, :])).astype(jnp.bfloat16)
        dv_s[j] += dotf(p.astype(jnp.bfloat16), do, ((1,), (0,)))
        dk_s[j] += dotf(ds, q, ((1,), (0,)))
        dq_s[i] += dotf(ds, k, ((0,), (0,)))

    def loop(lo, hi, masked):
        def body(i, carry):
            step(i, masked)
            return carry
        lax.fori_loop(lo, hi, body, 0)

    step(j, True)
    clean_lo = j + 1
    clean_hi = jnp.where(j >= clean_from, jnp.maximum(clean_to, j + 1), j + 1)
    loop(clean_lo, clean_hi, False)
    loop(clean_hi, stop, True)

    @pl.when(j == blocks - 1)
    def _():
        scale = HD ** -0.5
        def body(b, carry):
            rows = pl.ds(pl.multiple_of(b * BQ, BQ), BQ)
            t = pack4(dq_s[b, :BQ, :] * scale, dq_s[b, BQ:, :] * scale, dk_s[b] * scale, dv_s[b])
            t = jnp.concatenate(t, axis=1)
            cosine, sine, lower = cos_sin3(cos_ref[rows, :], sin_ref[rows, :])
            out_ref[rows, :] = turn(t, cosine, -sine, lower).astype(jnp.bfloat16)
            return carry
        lax.fori_loop(0, blocks, body, 0)

def attn_bwd(first, x, do, of, lse, cos, sin):
    length = x.shape[0]
    blocks = length // BQ
    whole = lambda a: pl.BlockSpec(a.shape, lambda j: (0,) * a.ndim)
    return pl.pallas_call(
        functools.partial(attn_bwd_kernel, length),
        grid=(blocks,),
        in_specs=[pl.BlockSpec(memory_space=pltpu.SMEM)] + [whole(a) for a in (x, do, of, lse, cos, sin)],
        out_specs=pl.BlockSpec((length, 3*LN), lambda j: (0, 0)),
        out_shape=jax.ShapeDtypeStruct((length, 3*LN), jnp.bfloat16),
        scratch_shapes=[pltpu.VMEM((blocks, 2*BQ, LN), jnp.bfloat16),
                        pltpu.VMEM((blocks, BQ, LN), jnp.bfloat16),
                        pltpu.VMEM((blocks, BQ, LN), jnp.bfloat16),
                        pltpu.VMEM((blocks, 2*BQ, LN), jnp.bfloat16),
                        pltpu.VMEM((blocks, 8, 2*BQ), jnp.float32),
                        pltpu.VMEM((blocks, 2*BQ, LN), jnp.float32),
                        pltpu.VMEM((blocks, BQ, LN), jnp.float32),
                        pltpu.VMEM((blocks, BQ, LN), jnp.float32)],
        compiler_params=pltpu.CompilerParams(vmem_limit_bytes=56 << 20),
        name="attend_back",
        cost_estimate=cost(31),
    )(first, x, do, of, lse, cos, sin)


def widen(table):
    lane = lane_iota(table.shape[0])
    second = jnp.where(lane < 96, pltpu.roll(table, 96, 1), pltpu.roll(table, 16, 1))
    third = jnp.where(lane < 112, pltpu.roll(table, 112, 1), pltpu.roll(table, 32, 1))
    return second, third


def cos_sin3(cos, sin):
    lane = lane_iota(cos.shape[0])
    live = lane < 32
    cos_two, cos_three = widen(cos)
    sin_two, sin_three = widen(sin)
    cosine = jnp.concatenate([cos, cos_two, jnp.where(live, cos_three, 1.0)], axis=1)
    sine = jnp.concatenate([sin, sin_two, jnp.where(live, sin_three, 0.0)], axis=1)
    wide = lax.broadcasted_iota(jnp.int32, cosine.shape, 1)
    lower = (wide % HD) < HD // 2
    return cosine, jnp.where(lower, -sine, sine), lower


def turn(values, cosine, sine, lower):
    width = values.shape[1]
    swapped = jnp.where(
        lower, pltpu.roll(values, width - HD // 2, 1), pltpu.roll(values, HD // 2, 1)
    )
    return values * cosine + swapped * sine


def full_spec(array):
    rank = array.ndim
    return pl.BlockSpec(array.shape, lambda *_: (0,) * rank)


def qkv_kernel(parts, rows, h_ref, gain_ref, w_ref, cos_ref, sin_ref, a_ref, out_ref):
    count = h_ref.shape[0] // parts
    tokens = count // rows

    def body(z, carry):
        stream = h_ref[pl.ds(pl.multiple_of(z * count, count), count), :].astype(jnp.float32)
        factor = lax.rsqrt(jnp.mean(stream * stream, axis=-1, keepdims=True) + EPS)
        normed = (stream * factor * gain_ref[...]).astype(jnp.bfloat16)
        at = pl.ds(pl.multiple_of(z * tokens, tokens), tokens)
        for r in range(rows):
            a_ref[r, at, :] = normed[r * tokens : (r + 1) * tokens]
        product = dotf(normed, w_ref[...], ((1,), (0,)))
        for r in range(rows):
            cosine, sine, lower = cos_sin3(cos_ref[r, at, :], sin_ref[r, at, :])
            for h in range(product.shape[1] // (3 * LN)):
                piece = product[r * tokens : (r + 1) * tokens, h * 3 * LN : (h + 1) * 3 * LN]
                out_ref[h * rows + r, at, :] = turn(piece, cosine, sine, lower).astype(jnp.bfloat16)
        return carry

    lax.fori_loop(0, parts, body, 0)


def qkv_call(parts, group, gain, weight, cos, sin, rows):
    count, width = group.shape
    tokens = count // rows
    groups = weight.shape[1] // (3 * LN)
    operands = (group, gain, weight, cos, sin)
    return pl.pallas_call(
        partial(qkv_kernel, parts, rows),
        grid=(1,),
        in_specs=[full_spec(v) for v in operands],
        out_specs=[
            pl.BlockSpec((rows, tokens, width), lambda i: (0, 0, 0)),
            pl.BlockSpec((groups * rows, tokens, 3 * LN), lambda i: (0, 0, 0)),
        ],
        out_shape=[
            jax.ShapeDtypeStruct((rows, tokens, width), jnp.bfloat16),
            jax.ShapeDtypeStruct((groups * rows, tokens, 3 * LN), jnp.bfloat16),
        ],
        compiler_params=pltpu.CompilerParams(vmem_limit_bytes=48 << 20),
        name="norm_qkv",
        cost_estimate=cost(7),
    )(*operands)


def thirds(values):
    return values[:, :LN], values[:, LN : 2 * LN], values[:, 2 * LN :]


def join_pairs(left, right):
    l0, l1, l2 = thirds(left)
    r0, r1, r2 = thirds(right)
    low = lane_iota(left.shape[0]) < 64
    s0, s1, s2 = (pltpu.roll(v, 64, 1) for v in (r0, r1, r2))
    firsts = (l0, jnp.where(low, l1, s0), jnp.where(low, s0, s1))
    m1, m2 = pltpu.roll(l1, 64, 1), pltpu.roll(l2, 64, 1)
    lasts = (jnp.where(low, m1, m2), jnp.where(low, m2, r1), r2)
    return jnp.concatenate(firsts, axis=1), jnp.concatenate(lasts, axis=1)


def out_kernel(rows, parts, o_ref, w_ref, tok_ref, gain_ref, mid_ref, b_ref, oo_ref, o_s):
    half = o_ref.shape[1]
    for r in range(rows):
        for z in range(parts):
            left = o_ref[r * parts + z].astype(jnp.float32)
            right = o_ref[(rows + r) * parts + z].astype(jnp.float32)
            for n, piece in enumerate(join_pairs(left, right)):
                at = (2 * r + n) * half
                o_s[at : at + half, z * 3 * LN : (z + 1) * 3 * LN] = piece.astype(jnp.bfloat16)
    attended = o_s[...]
    oo_ref[...] = attended
    middle = tok_ref[...].astype(jnp.float32) + dotf(attended, w_ref[...], ((1,), (1,)))
    mid_ref[...] = middle
    factor = lax.rsqrt(jnp.mean(middle * middle, axis=-1, keepdims=True) + EPS)
    b_ref[...] = (middle * factor * gain_ref[...]).astype(jnp.bfloat16)


def out_call(o_parts, weight, tokens, gain, rows):
    count, width = tokens.shape
    inner = weight.shape[1]
    operands = (o_parts, weight, tokens, gain)
    shapes = [
        jax.ShapeDtypeStruct((count, width), jnp.float32),
        jax.ShapeDtypeStruct((count, width), jnp.bfloat16),
        jax.ShapeDtypeStruct((count, inner), jnp.bfloat16),
    ]
    return pl.pallas_call(
        partial(out_kernel, rows, o_parts.shape[0] // (2 * rows)),
        grid=(1,),
        in_specs=[full_spec(v) for v in operands],
        out_specs=[full_spec(v) for v in shapes],
        out_shape=shapes,
        scratch_shapes=[pltpu.VMEM((count, inner), jnp.bfloat16)],
        compiler_params=pltpu.CompilerParams(vmem_limit_bytes=48 << 20),
        name="out_norm",
        cost_estimate=cost(4),
    )(*operands)


def split_pairs(firsts, lasts):
    f0, f1, f2 = thirds(firsts)
    g0, g1, g2 = thirds(lasts)
    low = lane_iota(firsts.shape[0]) < 64
    t0, t1 = pltpu.roll(g0, 64, 1), pltpu.roll(g1, 64, 1)
    left = (f0, jnp.where(low, f1, t0), jnp.where(low, t0, t1))
    u1, u2 = pltpu.roll(f1, 64, 1), pltpu.roll(f2, 64, 1)
    right = (jnp.where(low, u1, u2), jnp.where(low, u2, g1), g2)
    return jnp.concatenate(left, axis=1), jnp.concatenate(right, axis=1)


def mid_back_kernel(
    rows, parts, keep_ref, fx_ref, fy_ref, px_ref, py_ref, mid_ref, cot_ref, gain_ref, w_ref,
    gmid_ref, go_ref, do_ref, gg_ref
):
    half = px_ref.shape[0]
    wide = lambda v: v.astype(jnp.float32)
    db = jnp.concatenate(
        [
            keep_ref[:half] + wide(fx_ref[:half]) + wide(py_ref[...]),
            keep_ref[half:] + wide(fy_ref[:half]) + wide(px_ref[...]),
        ],
        axis=0,
    )
    middle = mid_ref[...]
    factor = lax.rsqrt(jnp.mean(middle * middle, axis=-1, keepdims=True) + EPS)
    scaled = db * gain_ref[...]
    inner = jnp.mean(scaled * middle, axis=-1, keepdims=True)
    grad = cot_ref[...].astype(jnp.float32) + factor * scaled - middle * (factor**3 * inner)
    gmid_ref[...] = grad
    gg_ref[...] = jnp.sum(db * middle * factor, axis=0, keepdims=True)
    low = grad.astype(jnp.bfloat16)
    go_ref[...] = low
    back = dotf(low, w_ref[...], ((1,), (0,)))
    half = do_ref.shape[1]
    for r in range(rows):
        for z in range(parts):
            cols = slice(z * 3 * LN, (z + 1) * 3 * LN)
            at = 2 * r * half
            left, right = split_pairs(back[at : at + half, cols], back[at + half : at + 2 * half, cols])
            do_ref[r * parts + z] = left.astype(jnp.bfloat16)
            do_ref[(rows + r) * parts + z] = right.astype(jnp.bfloat16)


def mid_back_call(pieces, middle, cot, gain, weight, rows, parts):
    count, width = middle.shape
    operands = (*pieces, middle, cot, gain, weight)
    shapes = [
        jax.ShapeDtypeStruct((count, width), jnp.float32),
        jax.ShapeDtypeStruct((count, width), jnp.bfloat16),
        jax.ShapeDtypeStruct((2 * rows * parts, count // rows // 2, 3 * LN), jnp.bfloat16),
        jax.ShapeDtypeStruct((1, width), jnp.float32),
    ]
    return pl.pallas_call(
        partial(mid_back_kernel, rows, parts),
        grid=(1,),
        in_specs=[pl.BlockSpec((count, width), lambda i: (0, 0))] + [full_spec(v) for v in operands[1:]],
        out_specs=[full_spec(v) for v in shapes],
        out_shape=shapes,
        compiler_params=pltpu.CompilerParams(vmem_limit_bytes=48 << 20),
        name="mid_back",
        cost_estimate=cost(5),
    )(*operands)


def da_kernel(parts, rows, h_ref, d_ref, w_ref, wo_ref, da_ref, gg_ref):
    count = h_ref.shape[0] // parts
    tokens = count // rows
    groups = d_ref.shape[0]
    run = wo_ref.shape[0] // parts
    gg_ref[...] = jnp.zeros_like(gg_ref)

    def body(z, carry):
        at = pl.ds(pl.multiple_of(z * tokens, tokens), tokens)
        left = jnp.concatenate(
            [jnp.concatenate([d_ref[g, r, at, :] for r in range(rows)], axis=0) for g in range(groups)],
            axis=1,
        )
        back = dotf(left, w_ref[...], ((1,), (1,)))
        stream = h_ref[pl.ds(pl.multiple_of(z * count, count), count), :].astype(jnp.float32)
        factor = lax.rsqrt(jnp.mean(stream * stream, axis=-1, keepdims=True) + EPS)
        gg_ref[...] += jnp.sum(back * stream * factor, axis=0, keepdims=True)
        da_ref[z, :count, :] = back.astype(jnp.bfloat16)
        cols = pl.ds(pl.multiple_of(z * 3 * LN, 3 * LN), 3 * LN)
        for n in range(parts):
            da_ref[z, count:, n * 3 * LN : (n + 1) * 3 * LN] = wo_ref[n * run : (n + 1) * run, cols]
        return carry

    lax.fori_loop(0, parts, body, 0)


def da_call(parts, group, grads, weight, grad_wo, rows):
    count, width = group.shape
    operands = (group, grads, weight, grad_wo)
    block = (count + grad_wo.shape[0]) // parts
    shapes = [
        jax.ShapeDtypeStruct((parts, block, width), jnp.bfloat16),
        jax.ShapeDtypeStruct((1, width), jnp.float32),
    ]
    part, gain_grad = pl.pallas_call(
        partial(da_kernel, parts, rows),
        grid=(1,),
        in_specs=[full_spec(v) for v in operands],
        out_specs=[full_spec(v) for v in shapes],
        out_shape=shapes,
        compiler_params=pltpu.CompilerParams(vmem_limit_bytes=48 << 20),
        name="da_part",
        cost_estimate=cost(6),
    )(*operands)
    return part.reshape(parts * block, width), gain_grad


def cut_kernel(gate_ref, up_ref, down_ref, out_ref):
    for n in range(out_ref.shape[0]):
        at = slice(n * LN, (n + 1) * LN)
        out_ref[n, :, :LN] = gate_ref[:, at]
        out_ref[n, :, LN : 2 * LN] = up_ref[:, at]
        out_ref[n, :, 2 * LN :] = jnp.transpose(down_ref[at, :].astype(jnp.float32)).astype(jnp.bfloat16)


def cut_call(gate, up, down):
    shape = jax.ShapeDtypeStruct((gate.shape[1] // LN, gate.shape[0], 3 * LN), jnp.bfloat16)
    operands = (gate, up, down)
    return pl.pallas_call(
        cut_kernel,
        grid=(1,),
        in_specs=[full_spec(v) for v in operands],
        out_specs=full_spec(shape),
        out_shape=shape,
        name="cut_units",
        cost_estimate=cost(3),
    )(*operands)


def uncut_kernel(in_ref, gate_ref, up_ref, down_ref):
    for n in range(in_ref.shape[0]):
        at = slice(n * LN, (n + 1) * LN)
        gate_ref[:, at] = in_ref[n, :, :LN].astype(jnp.float32)
        up_ref[:, at] = in_ref[n, :, LN : 2 * LN].astype(jnp.float32)
        down_ref[at, :] = jnp.transpose(in_ref[n, :, 2 * LN :].astype(jnp.float32))


def uncut_call(value):
    units, rows = value.shape[0] * LN, value.shape[1]
    shapes = [jax.ShapeDtypeStruct(s, jnp.float32) for s in ((rows, units), (rows, units), (units, rows))]
    return pl.pallas_call(
        uncut_kernel,
        grid=(1,),
        in_specs=[full_spec(value)],
        out_specs=[full_spec(v) for v in shapes],
        out_shape=shapes,
        name="uncut_units",
        cost_estimate=cost(3),
    )(value)


def place_kernel(parts, turned, at_ref, mine_ref, other_ref, out_ref):
    size = mine_ref.shape[1]
    z = at_ref[3]
    for c, ref in enumerate((mine_ref, other_ref)):
        for n in range(parts):
            y, x = at_ref[0] ^ (n // 2), at_ref[1] ^ (n % 2)
            rows = pl.multiple_of(((y * 2 + x) * 2 + (at_ref[2] ^ c)) * size, size)
            for k in range(ref.shape[0] // parts):
                count = ref.shape[0] // parts
                source = lax.rem(z + (count - k), count) if turned else k
                cols = pl.multiple_of(source * 3 * LN, 3 * LN)
                out_ref[pl.ds(rows, size), pl.ds(cols, 3 * LN)] = ref[n * count + k]


def place_call(at, mine, other, turned):
    size = mine.shape[1]
    shape = jax.ShapeDtypeStruct((8 * size, mine.shape[0] // 4 * mine.shape[2]), mine.dtype)
    return pl.pallas_call(
        partial(place_kernel, 4, turned),
        grid=(1,),
        in_specs=[pl.BlockSpec(memory_space=pltpu.SMEM), full_spec(mine), full_spec(other)],
        out_specs=full_spec(shape),
        out_shape=shape,
        compiler_params=pltpu.CompilerParams(vmem_limit_bytes=32 << 20),
        name="place_out",
        cost_estimate=cost(3),
    )(at, mine, other)


def fill_square(refs, out_ref):
    own, xn, yn, first, last = refs
    half = first.shape[0]
    out_ref[0, :half], out_ref[0, half:] = own[:half], own[half:]
    out_ref[1, :half], out_ref[1, half:] = xn[:half], first[...]
    out_ref[2, :half], out_ref[2, half:] = yn[half:], last[...]
    out_ref[3, :half], out_ref[3, half:] = xn[half:], yn[:half]


def down_back_kernel(*refs):
    pieces, (w0_ref, w1_ref, out_ref, g_s) = refs[:5], refs[5:]

    @pl.when(pl.program_id(0) == 0)
    def _():
        fill_square(pieces, g_s)

    weight = jnp.concatenate([w0_ref[0, :, 2 * LN :], w1_ref[0, :, 2 * LN :]], axis=1)

    def body(m, carry):
        out_ref[0, m] = dotf(g_s[m], weight, ((1,), (0,)))
        return carry

    lax.fori_loop(0, 4, body, 0)


def unit_spec(weight):
    return pl.BlockSpec((1,) + weight.shape[1:], lambda z: (z, 0, 0))


def down_back_call(pieces, mine, other):
    count, width = pieces[0].shape
    parts = mine.shape[0]
    shape = jax.ShapeDtypeStruct((parts, 4, count, 2 * LN), jnp.float32)
    return pl.pallas_call(
        down_back_kernel,
        grid=(parts,),
        in_specs=[full_spec(v) for v in pieces] + [unit_spec(mine), unit_spec(other)],
        out_specs=pl.BlockSpec((1, 4, count, 2 * LN), lambda z: (z, 0, 0, 0)),
        out_shape=shape,
        scratch_shapes=[pltpu.VMEM((4, count, width), jnp.bfloat16)],
        compiler_params=pltpu.CompilerParams(vmem_limit_bytes=60 << 20),
        name="down_back",
        cost_estimate=cost(8),
    )(*pieces, mine, other)


def emit_square(acc_ref, keep_ref, sx_ref, sy_ref):
    count = sx_ref.shape[0]
    keep_ref[:count] = acc_ref[0]
    keep_ref[count:] = acc_ref[3]
    sx_ref[...] = acc_ref[1].astype(jnp.bfloat16)
    sy_ref[...] = acc_ref[2].astype(jnp.bfloat16)


def units_kernel(*refs):
    pieces, (w0_ref, w1_ref, dh_ref) = refs[:5], refs[5:8]
    dgu_ref, hid_ref, keep_ref, sx_ref, sy_ref, b_s, acc_s = refs[8:]
    step = pl.program_id(0)

    @pl.when(step == 0)
    def _():
        fill_square(pieces, b_s)

    def body(m, carry):
        b = b_s[m]
        total = None
        for n, w_ref in enumerate((w0_ref, w1_ref)):
            weight = w_ref[0, :, : 2 * LN]
            both = dotf(b, weight, ((1,), (0,)))
            gate, up = both[:, :LN], both[:, LN:]
            dh = dh_ref[0, m, :, n * LN : (n + 1) * LN]
            sigma = 1.0 / (1.0 + jnp.exp(-gate))
            silu = gate * sigma
            hid_ref[0, m, :, n * LN : (n + 1) * LN] = (silu * up).astype(jnp.bfloat16)
            grad_gate = dh * up * sigma * (1.0 + gate * (1.0 - sigma))
            grads = jnp.concatenate([grad_gate, dh * silu], axis=1).astype(jnp.bfloat16)
            dgu_ref[0, n, m] = grads
            back = dotf(grads, weight, ((1,), (1,)))
            total = back if total is None else total + back

        @pl.when(step == 0)
        def _():
            acc_s[m] = total

        @pl.when(step > 0)
        def _():
            acc_s[m] += total

        return carry

    lax.fori_loop(0, 4, body, 0)

    @pl.when(step == pl.num_programs(0) - 1)
    def _():
        emit_square(acc_s, keep_ref, sx_ref, sy_ref)


def square_shapes(count, width):
    return [
        jax.ShapeDtypeStruct((2 * count, width), jnp.float32),
        jax.ShapeDtypeStruct((count, width), jnp.bfloat16),
        jax.ShapeDtypeStruct((count, width), jnp.bfloat16),
    ]


def units_call(pieces, mine, other, grad_hidden):
    count, width = pieces[0].shape
    parts = mine.shape[0]
    low = jnp.bfloat16
    shapes = [
        jax.ShapeDtypeStruct((parts, 2, 4, count, 2 * LN), low),
        jax.ShapeDtypeStruct((parts, 4, count, 2 * LN), low),
    ] + square_shapes(count, width)
    return pl.pallas_call(
        units_kernel,
        grid=(parts,),
        in_specs=[full_spec(v) for v in pieces]
        + [unit_spec(mine), unit_spec(other), pl.BlockSpec((1, 4, count, 2 * LN), lambda z: (z, 0, 0, 0))],
        out_specs=[
            pl.BlockSpec((1, 2, 4, count, 2 * LN), lambda z: (z, 0, 0, 0, 0)),
            pl.BlockSpec((1, 4, count, 2 * LN), lambda z: (z, 0, 0, 0)),
        ]
        + [full_spec(v) for v in shapes[2:]],
        out_shape=shapes,
        scratch_shapes=[pltpu.VMEM((4, count, width), low), pltpu.VMEM((4, count, width), jnp.float32)],
        compiler_params=pltpu.CompilerParams(vmem_limit_bytes=60 << 20),
        name="units",
        cost_estimate=cost(26),
    )(*pieces, mine, other, grad_hidden)


def down_kernel(hid_ref, w0_ref, w1_ref, keep_ref, sx_ref, sy_ref, acc_s):
    step = pl.program_id(0)
    weight = jnp.concatenate([w0_ref[0, :, 2 * LN :], w1_ref[0, :, 2 * LN :]], axis=1)

    def body(m, carry):
        total = dotf(hid_ref[0, m], weight, ((1,), (1,)))

        @pl.when(step == 0)
        def _():
            acc_s[m] = total

        @pl.when(step > 0)
        def _():
            acc_s[m] += total

        return carry

    lax.fori_loop(0, 4, body, 0)

    @pl.when(step == pl.num_programs(0) - 1)
    def _():
        emit_square(acc_s, keep_ref, sx_ref, sy_ref)


def down_call(hidden, mine, other):
    parts, _, count, _ = hidden.shape
    width = mine.shape[1]
    shapes = square_shapes(count, width)
    return pl.pallas_call(
        down_kernel,
        grid=(parts,),
        in_specs=[pl.BlockSpec((1,) + hidden.shape[1:], lambda z: (z, 0, 0, 0)), unit_spec(mine), unit_spec(other)],
        out_specs=[full_spec(v) for v in shapes],
        out_shape=shapes,
        scratch_shapes=[pltpu.VMEM((4, count, width), jnp.float32)],
        compiler_params=pltpu.CompilerParams(vmem_limit_bytes=60 << 20),
        name="down",
        cost_estimate=cost(11),
    )(hidden, mine, other)


def unit_grads_kernel(*refs):
    b_pieces, g_pieces = refs[:5], refs[5:10]
    dgu_ref, hid_ref, mine_ref, other_ref, fill_s, b_s, g_s = refs[10:]
    count = fill_s.shape[1]

    @pl.when(pl.program_id(0) == 0)
    def _():
        for pieces, side in ((b_pieces, b_s), (g_pieces, g_s)):
            fill_square(pieces, fill_s)
            for m in range(4):
                side[:, m * count : (m + 1) * count] = jnp.transpose(fill_s[m])

    hidden = hid_ref[0].reshape(4 * count, 2 * LN)
    grads = [dgu_ref[0, n].reshape(4 * count, 2 * LN) for n in range(2)]
    rows = b_s.shape[0] // 4

    def body(m, carry):
        at = pl.ds(pl.multiple_of(m * rows, rows), rows)
        left, right = b_s[at, :], g_s[at, :]
        down = dotf(right, hidden, ((1,), (0,)))
        for n, out_ref in enumerate((mine_ref, other_ref)):
            out_ref[0, at, : 2 * LN] = dotf(left, grads[n], ((1,), (0,))).astype(jnp.bfloat16)
            out_ref[0, at, 2 * LN :] = down[:, n * LN : (n + 1) * LN].astype(jnp.bfloat16)
        return carry

    lax.fori_loop(0, 4, body, 0)


def unit_grads_call(b_pieces, g_pieces, grads, hidden):
    count, width = b_pieces[0].shape
    parts = hidden.shape[0]
    low = jnp.bfloat16
    operands = (*b_pieces, *g_pieces)
    return pl.pallas_call(
        unit_grads_kernel,
        grid=(parts,),
        in_specs=[full_spec(v) for v in operands]
        + [
            pl.BlockSpec((1,) + grads.shape[1:], lambda z: (z, 0, 0, 0, 0)),
            pl.BlockSpec((1,) + hidden.shape[1:], lambda z: (z, 0, 0, 0)),
        ],
        out_specs=[pl.BlockSpec((1, width, 3 * LN), lambda z: (z, 0, 0))] * 2,
        out_shape=[jax.ShapeDtypeStruct((parts, width, 3 * LN), low)] * 2,
        scratch_shapes=[pltpu.VMEM((4, count, width), low)] + [pltpu.VMEM((width, 4 * count), low)] * 2,
        compiler_params=pltpu.CompilerParams(vmem_limit_bytes=60 << 20),
        name="unit_grads",
        cost_estimate=cost(19),
    )(*operands, grads, hidden)


ORDER = ((0, 0, 0), (0, 0, 1), (0, 1, 0), (1, 1, 0), (1, 0, 1), (1, 1, 1), (0, 1, 1), (1, 0, 0))


def row_grads_kernel(at_ref, left_ref, right_ref, mine_ref, other_ref, full_s):
    tile = 2 * LN
    width = right_ref.shape[2]

    def body(n, carry):
        rows = pl.ds(pl.multiple_of(n * tile, tile), tile)
        left = jnp.transpose(left_ref[:, rows])
        for g in range(right_ref.shape[0]):
            piece = dotf(left, right_ref[g], ((1,), (0,)))
            full_s[rows, g * width : (g + 1) * width] = piece.astype(jnp.bfloat16)
        return carry

    lax.fori_loop(0, full_s.shape[0] // tile, body, 0)
    half = mine_ref.shape[1]
    for c, out_ref in enumerate((mine_ref, other_ref)):
        for n, (y, x, last) in enumerate(ORDER):
            block = ((at_ref[0] ^ y) * 2 + (at_ref[1] ^ x)) * 2 + (at_ref[2] ^ c)
            rows = pl.multiple_of(block * 2 * half + last * half, 32)
            out_ref[n] = full_s[pl.ds(rows, half), :]


def row_grads_call(at, left, right, name, time):
    width = left.shape[1]
    cols = right.shape[0] * right.shape[2]
    shape = jax.ShapeDtypeStruct((8, width // 16, cols), jnp.bfloat16)
    return pl.pallas_call(
        row_grads_kernel,
        grid=(1,),
        in_specs=[pl.BlockSpec(memory_space=pltpu.SMEM), full_spec(left), full_spec(right)],
        out_specs=[full_spec(shape)] * 2,
        out_shape=[shape] * 2,
        scratch_shapes=[pltpu.VMEM((width, cols), jnp.bfloat16)],
        compiler_params=pltpu.CompilerParams(vmem_limit_bytes=32 << 20),
        cost_estimate=cost(time),
        name=name,
    )(at, left, right)


def core_sum(mine, other):
    step = mine.shape[1]
    both = (mine.astype(jnp.float32) + other.astype(jnp.float32)).reshape(8 * step, -1)
    keep = jnp.concatenate([both[: 2 * step], both[6 * step :]], axis=0)
    low = both[2 * step : 6 * step].astype(jnp.bfloat16)
    return keep, low[: 2 * step], low[2 * step :]


EVERY = ("y", "x", "c", "z")
SWAP = ((0, 1), (1, 0))


def swap(value, axis):
    return lax.ppermute(value, axis, SWAP)


def gather_blocks(value, size):
    shift = lambda k: [(i, (i + k) % size) for i in range(size)]
    return [value] + [lax.ppermute(value, "z", shift(k)) for k in range(1, size)]


def gather_sides(value):
    return swap(value, "x"), swap(value, "y")


def gather_corner(xn, yn):
    half = xn.shape[0] // 2
    return swap(yn[:half], "x"), swap(xn[half:], "y")


def gather_square(value):
    sides = gather_sides(value)
    return (value, *sides, *gather_corner(*sides))


def reduce_square(keep, send_x, send_y):
    return reduce_square_rest(keep, swap(send_x, "x"), swap(send_y, "y"))


def reduce_square_rest(keep, from_x, from_y):
    low = jnp.bfloat16
    half = from_x.shape[0] // 2
    pass_y = swap((keep[3 * half :] + from_x[half:].astype(jnp.float32)).astype(low), "y")
    pass_x = swap((keep[2 * half : 3 * half] + from_y[half:].astype(jnp.float32)).astype(low), "x")
    return keep, from_x, from_y, pass_x, pass_y


def total_square(pieces):
    keep, from_x, from_y, pass_x, pass_y = pieces
    half = pass_x.shape[0]
    wide = lambda v: v.astype(jnp.float32)
    return jnp.concatenate(
        [
            keep[:half] + wide(from_x[:half]) + wide(pass_y),
            keep[half : 2 * half] + wide(from_y[:half]) + wide(pass_x),
        ],
        axis=0,
    )


def all_to_all(value, axes):
    return lax.all_to_all(value, axes, 0, 0, tiled=True)


def tie(*values):
    return lax.optimization_barrier(values)


def fast_local(sizes, *args):
    (tokens, cotangent, segments, positions, norm_in, w_query, w_key, w_value, w_out, norm_mid, w_gate, w_up, w_down) = args
    nz = sizes["z"]
    devices = sizes["y"] * sizes["x"] * sizes["c"] * nz
    plane = devices // nz
    rows, span, width = tokens.shape
    count = rows * span
    chunk = segments.shape[1]
    length = chunk * sizes["x"] * sizes["c"]
    x_at, c_at, z_at = lax.axis_index("x"), lax.axis_index("c"), lax.axis_index("z")
    at = jnp.stack([lax.axis_index("y"), x_at, c_at, z_at]).astype(jnp.int32)

    own = tokens.reshape(count, width)
    group = lax.all_gather(own, "z", axis=0, tiled=True)
    gains = jnp.concatenate([norm_in, norm_mid], axis=1)
    share = norm_in.shape[1]
    gains = jnp.pad(gains, ((0, 0), (0, LN - 2 * share)))
    gains = all_to_all(jnp.broadcast_to(gains, (devices, LN)), EVERY)

    kv_local = w_key.shape[2] // HD
    per_head = lambda w: w[0].reshape(w.shape[1], kv_local, -1)
    w_qkv = jnp.concatenate([per_head(w_query), per_head(w_key), per_head(w_value)], axis=2)
    w_qkv, w_o = tie(jnp.transpose(w_qkv, (1, 0, 2)), jnp.stack(gather_blocks(w_out[0].T, nz)))
    w_qkv = jnp.concatenate(gather_square(w_qkv), axis=0)
    w_qkv = place_call(at, w_qkv, swap(w_qkv, "c"), False)

    last = (x_at * sizes["c"] + c_at + 1) * chunk - 1
    begin = last - positions[:, -1] - jnp.where(segments[:, -1] == 2, 3 * length // 4, 0)
    lanes = jnp.arange(LN, dtype=jnp.int32) % (HD // 2)
    frequency = THETA ** (-(2.0 * lanes.astype(jnp.float32)) / HD)
    token_angle = positions.astype(jnp.float32)[:, :, None] * frequency
    first = lax.dynamic_slice_in_dim(begin, c_at, 1).astype(jnp.int32)
    index = jnp.arange(length, dtype=jnp.int32)
    row_angle = (index - doc_low(index, first[0], length)).astype(jnp.float32)[:, None] * frequency
    token_cos, token_sin = jnp.cos(token_angle), jnp.sin(token_angle)
    row_cos, row_sin = jnp.cos(row_angle), jnp.sin(row_angle)

    sides = gather_sides(w_o)
    gate, up, down, gains, *tables = tie(
        w_gate[0], w_up[0], w_down[0], gains, token_cos, token_sin, row_cos, row_sin, *sides
    )
    token_cos, token_sin, row_cos, row_sin, *sides = tables
    gain_in = gains[:, :share].reshape(1, width)
    gain_mid = gains[:, share : 2 * share].reshape(1, width)
    w_ff = all_to_all(cut_call(gate, up, down), ("y", "x", "c"))
    w_ff = w_ff.reshape(width, 3 * LN)
    corner = gather_corner(*sides)
    group, w_qkv, w_ff, *corner = tie(group, w_qkv, w_ff, *corner)
    w_o = jnp.concatenate([w_o, *sides, *corner], axis=0)
    w_mine = lax.all_gather(w_ff, "z", axis=0, tiled=True)

    normed, qkv = qkv_call(nz, group, gain_in, w_qkv, token_cos, token_sin, rows)
    qkv = all_to_all(qkv, ("x", "c")).reshape(length, 3 * LN)

    cot_low = cotangent.reshape(count, width)
    cot_first, _ = tie(cot_low, qkv)
    cot_sides = gather_sides(cot_first)

    attended, attended_float, log_total = attn_fwd(first, qkv)
    attended, *cot_sides = tie(attended, *cot_sides)
    attended = all_to_all(attended, ("x", "c", "z"))
    w_o = place_call(at, w_o, swap(w_o, "c"), True)
    w_o, *cot_sides = tie(w_o, *cot_sides)
    attended, *corner = tie(attended, *gather_corner(*cot_sides))
    cot_pieces = (cot_low, *cot_sides, *corner)
    middle, normed_b, attended_low = out_call(attended, w_o, own, gain_mid, rows)
    w_mine, _ = tie(w_mine, normed_b)
    w_mine = w_mine.reshape(nz, width, 3 * LN)
    w_other = swap(w_mine, "c")
    b_sides = gather_sides(normed_b)
    grad_hidden = down_back_call(cot_pieces, w_mine, w_other)
    *b_sides, grad_hidden = tie(*b_sides, grad_hidden)
    b_pieces = (normed_b, *b_sides, *gather_corner(*b_sides))
    grad_gu, hidden, *sends = units_call(b_pieces, w_mine, w_other, grad_hidden)
    from_x, from_y = swap(sends[1], "x"), swap(sends[2], "y")
    ff_mine, ff_other = unit_grads_call(b_pieces, cot_pieces, grad_gu, hidden)
    from_x, from_y, ff_other = tie(from_x, from_y, ff_other)
    grad_b = reduce_square_rest(sends[0], from_x, from_y)
    grad_ff = ff_mine.astype(jnp.float32) + swap(ff_other, "c").astype(jnp.float32)
    grad_ff = grad_ff.astype(jnp.bfloat16).reshape(nz * width, 3 * LN)
    grad_ff, *corner = tie(grad_ff, *grad_b[3:])
    grad_b = (*grad_b[:3], *corner)
    grad_ff = lax.psum_scatter(grad_ff, "z", scatter_dimension=0, tiled=True)
    grad_mid, grad_low, grad_o, gain_grad_mid = mid_back_call(
        grad_b, middle, cot_low, gain_mid, w_o, rows, nz
    )
    grad_o = all_to_all(grad_o, ("x", "c", "z"))
    hidden, _ = tie(hidden, grad_low)
    keep_out, *out_sides = down_call(hidden, w_mine, w_other)
    out_sides = swap(out_sides[0], "x"), swap(out_sides[1], "y")
    wo_mine, wo_other = row_grads_call(at, grad_low, attended_low[None], "out_grads", 3)
    wo_keep, *wo_sides = core_sum(wo_mine, swap(wo_other, "c"))
    wo_sides = swap(wo_sides[0], "x"), swap(wo_sides[1], "y")

    grad_qkv = attn_bwd(first, qkv, grad_o, attended_float, log_total, row_cos, row_sin)
    grad_qkv, *sides = tie(grad_qkv, *out_sides, *wo_sides)
    out = middle + total_square(reduce_square_rest(keep_out, *sides[:2]))
    grad_wo = total_square(reduce_square_rest(wo_keep, *sides[2:])).astype(jnp.bfloat16)
    grad_qkv = all_to_all(grad_qkv.reshape(-1, chunk, 3 * LN), ("x", "c"))
    grad_qkv, grad_ff = tie(grad_qkv, grad_ff)
    grad_ff = all_to_all(grad_ff.reshape(plane, width // plane, 3 * LN), ("y", "x", "c"))
    grad_qkv = grad_qkv.reshape(kv_local, rows, chunk, 3 * LN)
    part, gain_grad_in = da_call(nz, group, grad_qkv, w_qkv, grad_wo, rows)
    part = lax.psum_scatter(part, "z", scatter_dimension=0, tiled=True).astype(jnp.float32)
    grad_a, grad_wo = part[:count], part[count:]
    grad_wo = jnp.concatenate([grad_wo[:, n * 3 * LN : (n + 1) * 3 * LN] for n in range(nz)], axis=0)
    grad_wqkv = row_grads_call(
        at,
        normed.reshape(rows * chunk, width),
        grad_qkv.reshape(kv_local, rows * chunk, 3 * LN),
        "qkv_grads",
        5,
    )
    *grad_wqkv, grad_ff = tie(*grad_wqkv, grad_ff)
    grad_wqkv = reduce_square(*core_sum(grad_wqkv[0], swap(grad_wqkv[1], "c")))
    gain_grads = jnp.concatenate(
        [gain_grad_in.reshape(devices, share), gain_grad_mid.reshape(devices, share)], axis=1
    )
    gain_grads = jnp.pad(gain_grads, ((0, 0), (0, LN - 2 * share)))
    *grad_wqkv, gain_grads = tie(*grad_wqkv, gain_grads)
    grad_wqkv = total_square(grad_wqkv)
    gain_grads = jnp.sum(all_to_all(gain_grads, EVERY), axis=0, keepdims=True)

    stream = own.astype(jnp.float32)
    factor = lax.rsqrt(jnp.mean(stream * stream, axis=-1, keepdims=True) + EPS)
    back_in, _ = norm_back(stream, factor, gain_in, grad_a)
    grad_tokens = grad_mid + back_in
    grad_wqkv = grad_wqkv.reshape(-1, kv_local, 4 * HD)
    flat = lambda g: g.reshape(1, g.shape[0], -1)
    grad_gate, grad_up, grad_down = uncut_call(grad_ff)
    return (
        out.reshape(tokens.shape),
        grad_tokens.reshape(tokens.shape),
        gain_grads[:, :share],
        flat(grad_wqkv[:, :, : 2 * HD]),
        flat(grad_wqkv[:, :, 2 * HD : 3 * HD]),
        flat(grad_wqkv[:, :, 3 * HD :]),
        grad_wo.T[None],
        gain_grads[:, share : 2 * share],
        grad_gate[None],
        grad_up[None],
        grad_down[None],
    )


def fast_solution(mesh, cores):
    batch, seq, kv = mesh.devices.shape
    fine = Mesh(mesh.devices.reshape(batch, seq // cores, cores, kv), EVERY)
    sizes = dict(fine.shape)
    row_spec = P("y", ("x", "c", "z"), None)
    seq_spec = P("y", ("x", "c"))
    gain_spec = P(None, EVERY)
    in_w = P(None, ("y", "x", "c"), "z")
    out_w = P(None, "z", ("y", "x", "c"))
    in_specs = (row_spec, row_spec, seq_spec, seq_spec, gain_spec, in_w, in_w, in_w, out_w, gain_spec, in_w, in_w, out_w)
    out_specs = (row_spec, row_spec, gain_spec, in_w, in_w, in_w, out_w, gain_spec, in_w, in_w, out_w)
    return jax.shard_map(
        partial(fast_local, sizes), mesh=fine, in_specs=in_specs, out_specs=out_specs, check_vma=False
    )


def solution(mesh):
    batch, seq, kv = (mesh.shape[name] for name in ("batch", "seq", "kv"))
    general = general_solution(mesh)
    if (batch, seq) != (2, 4):
        return general
    fast = fast_solution(mesh, 2)

    def run(*args):
        rows, length, width = args[0].shape
        kv_heads, q_heads = args[6].shape[2] // HD, args[5].shape[2] // HD
        fits = (
            rows == 2 * batch
            and kv_heads == 2 * kv
            and q_heads == 2 * kv_heads
            and length == 128 * seq * kv
            and length % (4 * BQ) == 0
            and width % LN == 0
            and 2 * width // (batch * seq * kv) <= LN
            and args[10].shape[2] == LN * batch * seq * kv
        )
        return (fast if fits else general)(*args)

    return run
```

```python
import functools
import math
from functools import partial

import jax
import jax.numpy as jnp
from jax import lax
from jax.experimental import pallas as pl
from jax.experimental.pallas import tpu as pltpu
from jax.sharding import Mesh
from jax.sharding import PartitionSpec as P

HD = 96
LAYERS = 1


EPS = 1e-05
THETA = 100000.0
BIG_NEG = -1e30


def rotary(positions_row):
    half_width = HD // 2
    frequency = THETA ** (-(2.0 * jnp.arange(half_width, dtype=jnp.float32)) / HD)
    angles = positions_row.astype(jnp.float32)[:, None] * frequency[None, :]
    cosine = jnp.concatenate([jnp.cos(angles), jnp.cos(angles)], axis=1)
    sine_table = jnp.concatenate([jnp.sin(angles), jnp.sin(angles)], axis=1)
    return (cosine, sine_table)


def rotate(head_vals, cosine, sine_table):
    half_width = head_vals.shape[-1] // 2
    swapped = jnp.concatenate([-head_vals[..., half_width:], head_vals[..., :half_width]], axis=-1)
    return head_vals * cosine[:, None, :] + swapped * sine_table[:, None, :]


def rms_norm(stream, gain):
    factor = lax.rsqrt(jnp.mean(stream * stream, axis=-1, keepdims=True) + EPS)
    return (stream * factor * gain, factor)


def norm_back(stream, factor, gain, upstream):
    scaled_grad = upstream * gain
    inner_mean = jnp.mean(scaled_grad * stream, axis=-1, keepdims=True)
    grad_stream = factor * scaled_grad - stream * factor**3 * inner_mean
    return (grad_stream, jnp.sum(upstream * stream * factor, axis=0))


def key_width(key_count):
    return math.gcd(key_count, 1024)


def contract(left_side, right_side, left_dim, right_dim):
    return lax.dot_general(
        left_side,
        right_side,
        (((left_dim,), (right_dim,)), ((), ())),
        preferred_element_type=jnp.float32,
    )


def spread(shard_rows):
    return lax.all_gather(shard_rows, "kv", axis=0, tiled=True)


def token_sum(pairs):
    summed = None
    for left_part, right_part, right_dim in pairs:
        product = contract(left_part, right_part, 1, right_dim)
        summed = product if summed is None else summed + product
    return lax.psum_scatter(
        summed.astype(jnp.bfloat16), "kv", scatter_dimension=0, tiled=True
    ).astype(jnp.float32)


def split_block(kv_both, seg_keys, offset, step_width, kv_local, head_size):
    kv_block = lax.dynamic_slice_in_dim(kv_both, offset, step_width, 0)
    key_block = kv_block[:, : kv_local * head_size].reshape(step_width, kv_local, head_size)
    value_block = kv_block[:, kv_local * head_size :].reshape(step_width, kv_local, head_size)
    seg_block = lax.dynamic_slice_in_dim(seg_keys, offset, step_width, 0)
    return (key_block, value_block, seg_block)


def forward_row(queries, seg_query, fold_state, kv_both, seg_keys, first_query, key_start):
    key_count = kv_both.shape[0]
    step_width = key_width(key_count)
    query_count, kv_local, group_size, head_size = queries.shape
    query_index = first_query + jnp.arange(query_count, dtype=jnp.int32)
    score_scale = head_size ** (-0.5)

    def forward_one_step(step_index, inner_state):
        running_max, weight_total, value_total = inner_state
        offset = step_index * step_width
        key_block, value_block, seg_block = split_block(
            kv_both, seg_keys, offset, step_width, kv_local, head_size
        )
        key_index = offset + jnp.arange(step_width, dtype=jnp.int32)
        allowed = (seg_query[:, None] == seg_block[None, :]) & (
            key_index[None, :] <= query_index[:, None]
        )
        scores = (
            jnp.einsum("qkgd,pkd->kgqp", queries, key_block, preferred_element_type=jnp.float32)
            * score_scale
        )
        scores = jnp.where(allowed, scores, BIG_NEG)
        new_max = jnp.maximum(running_max, jnp.max(scores, axis=-1))
        weights = jnp.where(allowed, jnp.exp(scores - new_max[..., None]), 0.0)
        rescale = jnp.exp(running_max - new_max)
        weight_total = rescale * weight_total + jnp.sum(weights, axis=-1)
        update = jnp.einsum(
            "kgqp,pkd->qkgd",
            weights.astype(jnp.bfloat16),
            value_block,
            preferred_element_type=jnp.float32,
        )
        value_total = jnp.transpose(rescale, (2, 0, 1))[..., None] * value_total + update
        return (new_max, weight_total, value_total)

    return lax.fori_loop(0, key_count // step_width, forward_one_step, fold_state)


def forward_fold(queries, seg_query, first_query, fold_state, pieces, key_start):
    kv_both, seg_keys = pieces
    row_fn = partial(forward_row, first_query=first_query, key_start=key_start)
    return jax.vmap(row_fn, in_axes=(0, 0, 0, 1, 1))(
        queries, seg_query, fold_state, kv_both, seg_keys
    )


def backward_row(
    queries,
    grad_attn,
    log_total,
    row_delta,
    seg_query,
    fold_state,
    kv_both,
    seg_keys,
    first_query,
    key_start,
):
    key_count = kv_both.shape[0]
    step_width = key_width(key_count)
    query_count, kv_local, group_size, head_size = queries.shape
    query_index = first_query + jnp.arange(query_count, dtype=jnp.int32)
    score_scale = head_size ** (-0.5)

    def backward_one_step(step_index, inner_state):
        grad_queries, grad_buffer = inner_state
        offset = step_index * step_width
        key_block, value_block, seg_block = split_block(
            kv_both, seg_keys, offset, step_width, kv_local, head_size
        )
        key_index = offset + jnp.arange(step_width, dtype=jnp.int32)
        allowed = (seg_query[:, None] == seg_block[None, :]) & (
            key_index[None, :] <= query_index[:, None]
        )
        scores = (
            jnp.einsum("qkgd,pkd->kgqp", queries, key_block, preferred_element_type=jnp.float32)
            * score_scale
        )
        probs_block = jnp.where(allowed, jnp.exp(scores - log_total[..., None]), 0.0)
        grad_probs = jnp.einsum(
            "qkgd,pkd->kgqp", grad_attn, value_block, preferred_element_type=jnp.float32
        )
        grad_scores = (probs_block * (grad_probs - row_delta[..., None])).astype(jnp.bfloat16)
        grad_queries = (
            grad_queries
            + jnp.einsum(
                "kgqp,pkd->qkgd", grad_scores, key_block, preferred_element_type=jnp.float32
            )
            * score_scale
        )
        grad_keys = (
            jnp.einsum("kgqp,qkgd->pkd", grad_scores, queries, preferred_element_type=jnp.float32)
            * score_scale
        )
        grad_values = jnp.einsum(
            "kgqp,qkgd->pkd",
            probs_block.astype(jnp.bfloat16),
            grad_attn,
            preferred_element_type=jnp.float32,
        )
        joined = jnp.concatenate(
            [grad_keys.reshape(step_width, -1), grad_values.reshape(step_width, -1)], axis=1
        )
        grad_buffer = lax.dynamic_update_slice_in_dim(grad_buffer, joined, offset, 0)
        return (grad_queries, grad_buffer)

    return lax.fori_loop(0, key_count // step_width, backward_one_step, fold_state)


def backward_fold(
    queries, grad_attn, log_total, row_delta, seg_query, first_query, fold_state, pieces, key_start
):
    kv_both, seg_keys = pieces
    row_fn = partial(backward_row, first_query=first_query, key_start=key_start)
    return jax.vmap(row_fn, in_axes=(0, 0, 0, 0, 0, 0, 1, 1))(
        queries, grad_attn, log_total, row_delta, seg_query, fold_state, kv_both, seg_keys
    )


def layer_forward(stream, gain_pair, matrices, seg_info, tables):
    gain_in, gain_mid = gain_pair
    w_query, w_key, w_value, w_out, w_gate, w_up, w_down = matrices
    seg_query, seg_keys = seg_info
    cosine, sine_table = tables
    row_count = seg_query.shape[0]
    kv_local = w_key.shape[1] // HD
    head_local = w_query.shape[1] // HD
    group_size = head_local // kv_local
    normed_a, factor_a = rms_norm(stream, gain_in)
    spread_a = spread(normed_a.astype(jnp.bfloat16))
    flat_count = spread_a.shape[0]
    token_count = flat_count // row_count
    raw_queries = jnp.dot(spread_a, w_query, preferred_element_type=jnp.float32).reshape(
        flat_count, head_local, HD
    )
    queries = (
        rotate(raw_queries, cosine, sine_table)
        .astype(jnp.bfloat16)
        .reshape(token_count, row_count, kv_local, group_size, HD)
    )
    queries = jnp.transpose(queries, (1, 0, 2, 3, 4))
    raw_keys = jnp.dot(spread_a, w_key, preferred_element_type=jnp.float32).reshape(
        flat_count, kv_local, HD
    )
    keys_low = (
        rotate(raw_keys, cosine, sine_table).astype(jnp.bfloat16).reshape(flat_count, kv_local * HD)
    )
    values_low = jnp.dot(spread_a, w_value, preferred_element_type=jnp.float32).astype(jnp.bfloat16)
    kv_both = jnp.concatenate([keys_low, values_low], axis=1).reshape(
        token_count, row_count, 2 * kv_local * HD
    )
    first_query = lax.axis_index("seq") * token_count
    start_state = (
        jnp.full((row_count, kv_local, group_size, token_count), BIG_NEG, jnp.float32),
        jnp.zeros((row_count, kv_local, group_size, token_count), jnp.float32),
        jnp.zeros((row_count, token_count, kv_local, group_size, HD), jnp.float32),
    )
    running_max, weight_total, value_total = forward_fold(
        queries,
        seg_query,
        first_query,
        start_state,
        (
            lax.all_gather(kv_both, "seq", axis=0, tiled=True),
            lax.all_gather(seg_keys, "seq", axis=0, tiled=True),
        ),
        jnp.int32(0),
    )
    attn_float = value_total / jnp.transpose(weight_total, (0, 3, 1, 2))[..., None]
    log_total = running_max + jnp.log(weight_total)
    attn_low = (
        jnp.transpose(attn_float, (1, 0, 2, 3, 4))
        .reshape(flat_count, head_local * HD)
        .astype(jnp.bfloat16)
    )
    stream_mid = stream + token_sum(((attn_low, w_out, 0),))
    normed_b, factor_b = rms_norm(stream_mid, gain_mid)
    spread_b = spread(normed_b.astype(jnp.bfloat16))
    gate_val = jnp.dot(spread_b, w_gate, preferred_element_type=jnp.float32)
    up_val = jnp.dot(spread_b, w_up, preferred_element_type=jnp.float32)
    hidden = (jax.nn.silu(gate_val) * up_val).astype(jnp.bfloat16)
    stream_out = stream_mid + token_sum(((hidden, w_down, 0),))
    saved_state = (
        stream,
        factor_a,
        spread_a,
        queries,
        kv_both,
        attn_float,
        attn_low,
        log_total,
        stream_mid,
        factor_b,
        spread_b,
        gate_val,
        up_val,
        hidden,
    )
    return (stream_out, saved_state)


def layer_backward(saved_state, grad_stream, gain_pair, matrices, seg_info, tables):
    (
        stream,
        factor_a,
        spread_a,
        queries,
        kv_both,
        attn_float,
        attn_low,
        log_total,
        stream_mid,
        factor_b,
        spread_b,
        gate_val,
        up_val,
        hidden,
    ) = saved_state
    gain_in, gain_mid = gain_pair
    w_query, w_key, w_value, w_out, w_gate, w_up, w_down = matrices
    seg_query, seg_keys = seg_info
    cosine, sine_table = tables
    row_count, token_count, kv_local, group_size, head_size = queries.shape
    head_local = kv_local * group_size
    flat_count = row_count * token_count
    grad_low = spread(grad_stream.astype(jnp.bfloat16))
    grad_down_w = contract(hidden, grad_low, 0, 0)
    grad_hidden = contract(grad_low, w_down, 1, 1)
    sigmoid_gate = jax.nn.sigmoid(gate_val)
    silu_gate = gate_val * sigmoid_gate
    grad_gate_low = (
        grad_hidden * up_val * sigmoid_gate * (1.0 + gate_val * (1.0 - sigmoid_gate))
    ).astype(jnp.bfloat16)
    grad_up_low = (grad_hidden * silu_gate).astype(jnp.bfloat16)
    grad_gate_w = contract(spread_b, grad_gate_low, 0, 0)
    grad_up_w = contract(spread_b, grad_up_low, 0, 0)
    grad_normed_b = token_sum(((grad_gate_low, w_gate, 1), (grad_up_low, w_up, 1)))
    back_mid, grad_gain_mid = norm_back(stream_mid, factor_b, gain_mid, grad_normed_b)
    grad_mid = grad_stream + back_mid
    grad_attn_full = spread(grad_mid.astype(jnp.bfloat16))
    grad_out_w = contract(attn_low, grad_attn_full, 0, 0)
    grad_attn = (
        contract(grad_attn_full, w_out, 1, 1)
        .astype(jnp.bfloat16)
        .reshape(token_count, row_count, kv_local, group_size, head_size)
    )
    grad_attn = jnp.transpose(grad_attn, (1, 0, 2, 3, 4))
    row_delta = jnp.transpose(jnp.sum(grad_attn * attn_float, axis=-1), (0, 2, 3, 1))
    first_query = lax.axis_index("seq") * token_count
    row_length = token_count * lax.axis_size("seq")
    start_state = (
        jnp.zeros((row_count, token_count, kv_local, group_size, head_size), jnp.float32),
        jnp.zeros((row_count, row_length, 2 * kv_local * head_size), jnp.float32),
    )
    grad_queries, grad_buffer = backward_fold(
        queries,
        grad_attn,
        log_total,
        row_delta,
        seg_query,
        first_query,
        start_state,
        (
            lax.all_gather(kv_both, "seq", axis=0, tiled=True),
            lax.all_gather(seg_keys, "seq", axis=0, tiled=True),
        ),
        jnp.int32(0),
    )
    grad_kv = lax.psum_scatter(
        grad_buffer.astype(jnp.bfloat16), "seq", scatter_dimension=1, tiled=True
    ).astype(jnp.float32)
    grad_kv = jnp.transpose(grad_kv, (1, 0, 2)).reshape(flat_count, 2 * kv_local * head_size)
    grad_queries = jnp.transpose(grad_queries, (1, 0, 2, 3, 4)).reshape(
        flat_count, head_local, head_size
    )
    grad_q_low = (
        rotate(grad_queries, cosine, -sine_table)
        .astype(jnp.bfloat16)
        .reshape(flat_count, head_local * head_size)
    )
    grad_k_low = (
        rotate(
            grad_kv[:, : kv_local * head_size].reshape(flat_count, kv_local, head_size),
            cosine,
            -sine_table,
        )
        .astype(jnp.bfloat16)
        .reshape(flat_count, kv_local * head_size)
    )
    grad_v_low = grad_kv[:, kv_local * head_size :].astype(jnp.bfloat16)
    grad_query_w = contract(spread_a, grad_q_low, 0, 0)
    grad_key_w = contract(spread_a, grad_k_low, 0, 0)
    grad_value_w = contract(spread_a, grad_v_low, 0, 0)
    grad_normed_a = token_sum(
        ((grad_q_low, w_query, 1), (grad_k_low, w_key, 1), (grad_v_low, w_value, 1))
    )
    back_in, grad_gain_in = norm_back(stream, factor_a, gain_in, grad_normed_a)
    grad_input = grad_mid + back_in
    weight_grads = (
        lax.psum_scatter(
            grad_query_w.astype(jnp.bfloat16), ("batch", "seq"), scatter_dimension=0, tiled=True
        ).astype(jnp.float32),
        lax.psum_scatter(
            grad_key_w.astype(jnp.bfloat16), ("batch", "seq"), scatter_dimension=0, tiled=True
        ).astype(jnp.float32),
        lax.psum_scatter(
            grad_value_w.astype(jnp.bfloat16), ("batch", "seq"), scatter_dimension=0, tiled=True
        ).astype(jnp.float32),
        lax.psum_scatter(
            grad_out_w.astype(jnp.bfloat16), ("batch", "seq"), scatter_dimension=1, tiled=True
        ).astype(jnp.float32),
        lax.psum_scatter(
            grad_gate_w.astype(jnp.bfloat16), ("batch", "seq"), scatter_dimension=0, tiled=True
        ).astype(jnp.float32),
        lax.psum_scatter(
            grad_up_w.astype(jnp.bfloat16), ("batch", "seq"), scatter_dimension=0, tiled=True
        ).astype(jnp.float32),
        lax.psum_scatter(
            grad_down_w.astype(jnp.bfloat16), ("batch", "seq"), scatter_dimension=1, tiled=True
        ).astype(jnp.float32),
    )
    return (grad_input, weight_grads, grad_gain_in, grad_gain_mid)


def to_flat(shard_rows):
    row_count, token_part, width = shard_rows.shape
    return jnp.transpose(shard_rows.astype(jnp.float32), (1, 0, 2)).reshape(
        token_part * row_count, width
    )


def from_flat(flat_rows, row_count):
    token_part = flat_rows.shape[0] // row_count
    return jnp.transpose(flat_rows.reshape(token_part, row_count, flat_rows.shape[1]), (1, 0, 2))


def general_local(
    tokens,
    cotangent,
    segments,
    positions,
    norm_in,
    w_query,
    w_key,
    w_value,
    w_out,
    norm_mid,
    w_gate,
    w_up,
    w_down,
):
    gains_in, gains_mid = (
        lax.all_gather(norm_in, ("batch", "seq", "kv"), axis=1, tiled=True),
        lax.all_gather(norm_mid, ("batch", "seq", "kv"), axis=1, tiled=True),
    )
    row_count = tokens.shape[0]
    seg_info = (segments, jnp.transpose(segments, (1, 0)))
    tables = rotary(jnp.transpose(positions, (1, 0)).reshape(-1))

    def fetch_layer(layer_index):
        return (
            lax.all_gather(w_query[layer_index], ("batch", "seq"), axis=0, tiled=True),
            lax.all_gather(w_key[layer_index], ("batch", "seq"), axis=0, tiled=True),
            lax.all_gather(w_value[layer_index], ("batch", "seq"), axis=0, tiled=True),
            lax.all_gather(w_out[layer_index], ("batch", "seq"), axis=1, tiled=True),
            lax.all_gather(w_gate[layer_index], ("batch", "seq"), axis=0, tiled=True),
            lax.all_gather(w_up[layer_index], ("batch", "seq"), axis=0, tiled=True),
            lax.all_gather(w_down[layer_index], ("batch", "seq"), axis=1, tiled=True),
        )

    stream = to_flat(tokens)
    fetched = []
    states = []
    layer_index = 0
    matrices = fetch_layer(layer_index)
    layer_inputs = [stream]
    stream, saved_state = layer_forward(
        stream, (gains_in[layer_index], gains_mid[layer_index]), matrices, seg_info, tables
    )
    fetched.append(matrices)
    states.append(saved_state)
    grad_stream = to_flat(cotangent)
    grads_in = []
    grads_mid = []
    weight_lists = []
    for layer_index in reversed(range(LAYERS)):
        gain_pair = (gains_in[layer_index], gains_mid[layer_index])
        matrices = fetch_layer(layer_index)
        saved_state = layer_forward(
            layer_inputs[layer_index], gain_pair, matrices, seg_info, tables
        )[1]
        grad_stream, weight_grads, grad_gain_in, grad_gain_mid = layer_backward(
            saved_state, grad_stream, gain_pair, matrices, seg_info, tables
        )
        grads_in.insert(0, grad_gain_in)
        grads_mid.insert(0, grad_gain_mid)
        weight_lists.insert(0, weight_grads)
    gain_grads_in, gain_grads_mid = (
        lax.psum_scatter(
            jnp.stack(grads_in), ("batch", "seq", "kv"), scatter_dimension=1, tiled=True
        ),
        lax.psum_scatter(
            jnp.stack(grads_mid), ("batch", "seq", "kv"), scatter_dimension=1, tiled=True
        ),
    )
    stacked_grads = [
        jnp.stack([grad_set[member] for grad_set in weight_lists]) for member in range(7)
    ]
    return (
        from_flat(stream, row_count),
        from_flat(grad_stream, row_count),
        gain_grads_in,
        stacked_grads[0],
        stacked_grads[1],
        stacked_grads[2],
        stacked_grads[3],
        gain_grads_mid,
        stacked_grads[4],
        stacked_grads[5],
        stacked_grads[6],
    )


def general_solution(mesh):
    in_specs = (
        P("batch", ("seq", "kv"), None),
        P("batch", ("seq", "kv"), None),
        P("batch", "seq"),
        P("batch", "seq"),
        P(None, ("batch", "seq", "kv")),
        P(None, ("batch", "seq"), "kv"),
        P(None, ("batch", "seq"), "kv"),
        P(None, ("batch", "seq"), "kv"),
        P(None, "kv", ("batch", "seq")),
        P(None, ("batch", "seq", "kv")),
        P(None, ("batch", "seq"), "kv"),
        P(None, ("batch", "seq"), "kv"),
        P(None, "kv", ("batch", "seq")),
    )
    out_specs = (
        P("batch", ("seq", "kv"), None),
        P("batch", ("seq", "kv"), None),
        P(None, ("batch", "seq", "kv")),
        P(None, ("batch", "seq"), "kv"),
        P(None, ("batch", "seq"), "kv"),
        P(None, ("batch", "seq"), "kv"),
        P(None, "kv", ("batch", "seq")),
        P(None, ("batch", "seq", "kv")),
        P(None, ("batch", "seq"), "kv"),
        P(None, ("batch", "seq"), "kv"),
        P(None, "kv", ("batch", "seq")),
    )
    return jax.shard_map(general_local, mesh=mesh, in_specs=in_specs, out_specs=out_specs, check_vma=False)


LN = 128
NEG=-1e30
C2 = (96 ** -0.5) * 1.4426950408889634

def cost(microseconds):
    return pl.CostEstimate(
        flops=microseconds * 10**9, bytes_accessed=microseconds * 3 * 10**6, transcendentals=0
    )


def lane_iota(rows):
    return lax.broadcasted_iota(jnp.int32, (rows, LN), 1)

def unpack4(t0, t1, t2):
    lane = lane_iota(t0.shape[0])
    live = lane < HD
    zero = jnp.zeros_like(t0)
    a = t0
    b = pltpu.roll(jnp.where(lane >= 96, t0, t1), 32, 1)
    c = pltpu.roll(jnp.where(lane >= 64, t1, t2), 64, 1)
    d = pltpu.roll(t2, 96, 1)
    return tuple(jnp.where(live, v, zero) for v in (a, b, c, d))

def pack4(a, b, c, d):
    lane = lane_iota(a.shape[0])
    b, c, d = pltpu.roll(b, 96, 1), pltpu.roll(c, 64, 1), pltpu.roll(d, 32, 1)
    return (jnp.where(lane < 96, a, b), jnp.where(lane < 64, b, c), jnp.where(lane < 32, c, d))

def split3(x):
    x = x.astype(jnp.float32)
    return x[:, :LN], x[:, LN:2*LN], x[:, 2*LN:]

def doc_low(index, first, length):
    second = first + 3 * length // 4
    return jnp.where(index >= second, second, jnp.where(index >= first, first, 0))

BQ = 256
BK = 512

def dotf(a, b, dims):
    return lax.dot_general(a, b, (dims, ((), ())), preferred_element_type=jnp.float32)

def attn_fwd_kernel(length, first_ref, x_ref, o_ref, of_ref, lse_ref, q_s, k_s, v_s, s_s):
    i = pl.program_id(0)
    blocks = length // BQ
    first = first_ref[0]

    @pl.when(i == 0)
    def _():
        def body(j, carry):
            rows = pl.ds(pl.multiple_of(j * BQ, BQ), BQ)
            q0, q1, k, v = unpack4(*split3(x_ref[rows, :]))
            q_s[j, :BQ, :] = q0.astype(jnp.bfloat16)
            q_s[j, BQ:, :] = q1.astype(jnp.bfloat16)
            k_s[rows, :] = k.astype(jnp.bfloat16)
            v_s[rows, :] = v.astype(jnp.bfloat16)
            return carry

        lax.fori_loop(0, blocks, body, 0)

    q = q_s[i]
    late = (3 * length // 4 + length // 8) // BQ
    start = jnp.where(i >= late, 3 * length // 4 // BK, 0)
    stop = i * BQ // BK + 1
    q_index = i * BQ + lax.broadcasted_iota(jnp.int32, (BQ, 1), 0)
    low = doc_low(q_index, first, length)

    def fold(v, op):
        out = v[:, :LN]
        for n in range(1, BK // LN):
            out = op(out, v[:, n * LN : (n + 1) * LN])
        return out

    def score(j, top):
        s = dotf(q, k_s[pl.ds(pl.multiple_of(j * BK, BK), BK), :], ((1,), (1,)))
        key = j * BK + lax.broadcasted_iota(jnp.int32, (1, BK), 1)
        ok = (key <= q_index) & (key >= low)
        s = jnp.concatenate([jnp.where(ok, s[:BQ], NEG), jnp.where(ok, s[BQ:], NEG)], axis=0)
        s_s[j] = s
        return jnp.maximum(top, fold(s, jnp.maximum))

    top = lax.fori_loop(start, stop, score, jnp.full((2 * BQ, LN), NEG, jnp.float32))
    m = jnp.max(top, axis=1, keepdims=True) * C2

    def add(j, state):
        p = jnp.exp2(s_s[j] * C2 - m)
        keys = pl.ds(pl.multiple_of(j * BK, BK), BK)
        of_ref[0] += dotf(p.astype(jnp.bfloat16), v_s[keys, :], ((1,), (0,)))
        return state + fold(p, jnp.add)

    zero = jnp.zeros((2 * BQ, LN), jnp.float32)
    of_ref[0] = zero
    total = lax.fori_loop(start, stop, add, zero)
    total = jnp.sum(total, axis=1, keepdims=True)
    out = of_ref[0] / total
    lse = jnp.broadcast_to(m + jnp.log2(total), (2 * BQ, LN))
    lse_ref[0] = jnp.transpose(lse, (1, 0))[:8, :]
    of_ref[0] = out
    for d in range(2):
        at = d * 128
        parts = [out[at + n // 2 * 64 + n % 2 * BQ : at + n // 2 * 64 + n % 2 * BQ + 64] for n in range(4)]
        for n, t in enumerate(pack4(*parts)):
            o_ref[d, :, n * LN : (n + 1) * LN] = t.astype(jnp.bfloat16)


def attn_fwd(first, x):
    length = x.shape[0]
    blocks = length // BQ
    return pl.pallas_call(
        functools.partial(attn_fwd_kernel, length),
        grid=(blocks,),
        in_specs=[pl.BlockSpec(memory_space=pltpu.SMEM),
                  pl.BlockSpec((length, 3*LN), lambda i: (0, 0))],
        out_specs=[pl.BlockSpec((2, 64, 3*LN), lambda i: (i, 0, 0)),
                   pl.BlockSpec((1, 2*BQ, LN), lambda i: (i, 0, 0)),
                   pl.BlockSpec((1, 8, 2*BQ), lambda i: (i, 0, 0))],
        out_shape=[jax.ShapeDtypeStruct((length//128, 64, 3*LN), jnp.bfloat16),
                   jax.ShapeDtypeStruct((blocks, 2*BQ, LN), jnp.float32),
                   jax.ShapeDtypeStruct((blocks, 8, 2*BQ), jnp.float32)],
        scratch_shapes=[pltpu.VMEM((blocks, 2*BQ, LN), jnp.bfloat16),
                        pltpu.VMEM((length, LN), jnp.bfloat16),
                        pltpu.VMEM((length, LN), jnp.bfloat16),
                        pltpu.VMEM((length // BK, 2*BQ, BK), jnp.float32)],
        compiler_params=pltpu.CompilerParams(vmem_limit_bytes=48 << 20),
        name="attend",
        cost_estimate=cost(22),
    )(first, x)

def attn_bwd_kernel(length, first_ref, x_ref, do_ref, of_ref, lse_ref, cos_ref, sin_ref, out_ref,
                    q_s, k_s, v_s, do_s, dl_s, dq_s, dk_s, dv_s):
    j = pl.program_id(0)
    blocks = length // BQ
    first = first_ref[0]
    @pl.when(j == 0)
    def _():
        def body(b, carry):
            rows = pl.ds(pl.multiple_of(b * BQ, BQ), BQ)
            q0, q1, k, v = unpack4(*split3(x_ref[rows, :]))
            q_s[b, :BQ, :] = q0.astype(jnp.bfloat16)
            q_s[b, BQ:, :] = q1.astype(jnp.bfloat16)
            k_s[b] = k.astype(jnp.bfloat16)
            v_s[b] = v.astype(jnp.bfloat16)
            for d in range(2):
                parts = unpack4(*split3(do_ref[2*b + d]))
                for n, part in enumerate(parts):
                    at = (n % 2) * BQ + d*128 + (n // 2) * 64
                    do_s[b, at:at+64, :] = part.astype(jnp.bfloat16)
            prod = do_s[b].astype(jnp.float32) * of_ref[b]
            delta = jnp.broadcast_to(jnp.sum(prod, axis=1, keepdims=True), (2*BQ, LN))
            dl_s[b] = jnp.transpose(delta, (1, 0))[:8, :]
            dq_s[b] = jnp.zeros((2*BQ, LN), jnp.float32)
            return carry
        lax.fori_loop(0, blocks, body, 0)
    late = (3 * length // 4 + length // 8) // BQ
    third = 3 * length // 4 // BQ
    stop = jnp.where(j >= third, blocks, late)
    k = k_s[j]
    v = v_s[j]
    dk_s[j] = jnp.zeros((BQ, LN), jnp.float32)
    dv_s[j] = jnp.zeros((BQ, LN), jnp.float32)
    key = j * BQ + lax.broadcasted_iota(jnp.int32, (BQ, 1), 0)

    def steps(places):
        dk, dv = [], []
        for i in places:
            q, do = q_s[i], do_s[i]
            s = dotf(k, q, ((1,), (1,)))
            dp = dotf(v, do, ((1,), (1,)))
            q_index = i * BQ + lax.broadcasted_iota(jnp.int32, (1, BQ), 1)
            ok = (key <= q_index) & (key >= doc_low(q_index, first, length))
            p = jnp.exp2(s * C2 - lse_ref[i, 0:1, :])
            p = jnp.concatenate([jnp.where(ok, p[:, :BQ], 0.0), jnp.where(ok, p[:, BQ:], 0.0)], axis=1)
            ds = (p * (dp - dl_s[i, 0:1, :])).astype(jnp.bfloat16)
            dv.append(dotf(p.astype(jnp.bfloat16), do, ((1,), (0,))))
            dk.append(dotf(ds, q, ((1,), (0,))))
            dq_s[i] += dotf(ds, k, ((0,), (0,)))
        dv_s[j] += functools.reduce(jnp.add, dv)
        dk_s[j] += functools.reduce(jnp.add, dk)

    pairs = (stop - j) // 2

    def body(n, carry):
        steps((j + 2 * n, j + 2 * n + 1))
        return carry

    lax.fori_loop(0, pairs, body, 0)

    @pl.when(j + 2 * pairs < stop)
    def _():
        steps((stop - 1,))

    @pl.when(j == blocks - 1)
    def _():
        scale = HD ** -0.5
        lower = lane_iota(BQ) < HD // 2

        def turn_back(piece, cosine, sine):
            swapped = jnp.where(lower, -pltpu.roll(piece, LN - HD // 2, 1), pltpu.roll(piece, HD // 2, 1))
            return (piece * cosine - swapped * sine) * scale

        def body(b, carry):
            rows = pl.ds(pl.multiple_of(b * BQ, BQ), BQ)
            cosine, sine = cos_ref[rows, :], sin_ref[rows, :]
            pieces = [turn_back(v, cosine, sine) for v in (dq_s[b, :BQ, :], dq_s[b, BQ:, :], dk_s[b])]
            for n, tile in enumerate(pack4(*pieces, dv_s[b])):
                out_ref[rows, n * LN : (n + 1) * LN] = tile.astype(jnp.bfloat16)
            return carry

        lax.fori_loop(0, blocks, body, 0)


def attn_bwd(first, x, do, of, lse, cos, sin):
    length = x.shape[0]
    blocks = length // BQ
    whole = lambda a: pl.BlockSpec(a.shape, lambda j: (0,) * a.ndim)
    return pl.pallas_call(
        functools.partial(attn_bwd_kernel, length),
        grid=(blocks,),
        in_specs=[pl.BlockSpec(memory_space=pltpu.SMEM)] + [whole(a) for a in (x, do, of, lse, cos, sin)],
        out_specs=pl.BlockSpec((length, 3*LN), lambda j: (0, 0)),
        out_shape=jax.ShapeDtypeStruct((length, 3*LN), jnp.bfloat16),
        scratch_shapes=[pltpu.VMEM((blocks, 2*BQ, LN), jnp.bfloat16),
                        pltpu.VMEM((blocks, BQ, LN), jnp.bfloat16),
                        pltpu.VMEM((blocks, BQ, LN), jnp.bfloat16),
                        pltpu.VMEM((blocks, 2*BQ, LN), jnp.bfloat16),
                        pltpu.VMEM((blocks, 8, 2*BQ), jnp.float32),
                        pltpu.VMEM((blocks, 2*BQ, LN), jnp.float32),
                        pltpu.VMEM((blocks, BQ, LN), jnp.float32),
                        pltpu.VMEM((blocks, BQ, LN), jnp.float32)],
        compiler_params=pltpu.CompilerParams(vmem_limit_bytes=56 << 20),
        name="attend_back",
        cost_estimate=cost(31),
    )(first, x, do, of, lse, cos, sin)


def widen(table):
    lane = lane_iota(table.shape[0])
    second = jnp.where(lane < 96, pltpu.roll(table, 96, 1), pltpu.roll(table, 16, 1))
    third = jnp.where(lane < 112, pltpu.roll(table, 112, 1), pltpu.roll(table, 32, 1))
    return second, third


def cos_sin3(cos, sin):
    lane = lane_iota(cos.shape[0])
    live = lane < 32
    cos_two, cos_three = widen(cos)
    sin_two, sin_three = widen(sin)
    cosine = jnp.concatenate([cos, cos_two, jnp.where(live, cos_three, 1.0)], axis=1)
    lower = (
        (lane < 48) | (lane >= 96),
        (lane < 16) | ((lane >= 64) & (lane < 112)),
        (lane >= 32) & (lane < 80),
    )
    tiles = (sin, sin_two, jnp.where(live, sin_three, 0.0))
    sine = jnp.concatenate([jnp.where(l, -t, t) for l, t in zip(lower, tiles)], axis=1)
    return cosine, sine, lower


def turn(values, cosine, sine, lower):
    width = values.shape[1]
    left, right = pltpu.roll(values, width - HD // 2, 1), pltpu.roll(values, HD // 2, 1)
    swapped = [
        jnp.where(l, left[:, n * LN : (n + 1) * LN], right[:, n * LN : (n + 1) * LN])
        for n, l in enumerate(lower)
    ]
    return values * cosine + jnp.concatenate(swapped, axis=1) * sine


def full_spec(array):
    rank = array.ndim
    return pl.BlockSpec(array.shape, lambda *_: (0,) * rank)


def qkv_kernel(parts, rows, h_ref, gain_ref, w_ref, cos_ref, sin_ref, a_ref, out_ref):
    count = h_ref.shape[0] // parts
    tokens = count // rows

    def body(z, carry):
        stream = h_ref[pl.ds(pl.multiple_of(z * count, count), count), :].astype(jnp.float32)
        factor = lax.rsqrt(jnp.mean(stream * stream, axis=-1, keepdims=True) + EPS)
        normed = (stream * factor * gain_ref[...]).astype(jnp.bfloat16)
        at = pl.ds(pl.multiple_of(z * tokens, tokens), tokens)
        for r in range(rows):
            a_ref[r, at, :] = normed[r * tokens : (r + 1) * tokens]
        product = dotf(normed, w_ref[...], ((1,), (0,)))
        for r in range(rows):
            cosine, sine, lower = cos_sin3(cos_ref[r, at, :], sin_ref[r, at, :])
            for h in range(product.shape[1] // (3 * LN)):
                piece = product[r * tokens : (r + 1) * tokens, h * 3 * LN : (h + 1) * 3 * LN]
                out_ref[h * rows + r, at, :] = turn(piece, cosine, sine, lower).astype(jnp.bfloat16)
        return carry

    lax.fori_loop(0, parts, body, 0)


def qkv_call(parts, group, gain, weight, cos, sin, rows):
    count, width = group.shape
    tokens = count // rows
    groups = weight.shape[1] // (3 * LN)
    operands = (group, gain, weight, cos, sin)
    return pl.pallas_call(
        partial(qkv_kernel, parts, rows),
        grid=(1,),
        in_specs=[full_spec(v) for v in operands],
        out_specs=[
            pl.BlockSpec((rows, tokens, width), lambda i: (0, 0, 0)),
            pl.BlockSpec((groups * rows, tokens, 3 * LN), lambda i: (0, 0, 0)),
        ],
        out_shape=[
            jax.ShapeDtypeStruct((rows, tokens, width), jnp.bfloat16),
            jax.ShapeDtypeStruct((groups * rows, tokens, 3 * LN), jnp.bfloat16),
        ],
        compiler_params=pltpu.CompilerParams(vmem_limit_bytes=48 << 20),
        name="norm_qkv",
        cost_estimate=cost(7),
    )(*operands)


def thirds(values):
    return values[:, :LN], values[:, LN : 2 * LN], values[:, 2 * LN :]


def join_pairs(left, right):
    l0, l1, l2 = thirds(left)
    r0, r1, r2 = thirds(right)
    low = lane_iota(left.shape[0]) < 64
    s0, s1, s2 = (pltpu.roll(v, 64, 1) for v in (r0, r1, r2))
    firsts = (l0, jnp.where(low, l1, s0), jnp.where(low, s0, s1))
    m1, m2 = pltpu.roll(l1, 64, 1), pltpu.roll(l2, 64, 1)
    lasts = (jnp.where(low, m1, m2), jnp.where(low, m2, r1), r2)
    return jnp.concatenate(firsts, axis=1), jnp.concatenate(lasts, axis=1)


def out_kernel(rows, parts, o_ref, w_ref, tok_ref, gain_ref, mid_ref, b_ref, oo_ref, o_s):
    half = o_ref.shape[1]
    for r in range(rows):
        for z in range(parts):
            left = o_ref[r * parts + z].astype(jnp.float32)
            right = o_ref[(rows + r) * parts + z].astype(jnp.float32)
            for n, piece in enumerate(join_pairs(left, right)):
                at = (2 * r + n) * half
                o_s[at : at + half, z * 3 * LN : (z + 1) * 3 * LN] = piece.astype(jnp.bfloat16)
    attended = o_s[...]
    oo_ref[...] = attended
    middle = tok_ref[...].astype(jnp.float32) + dotf(attended, w_ref[...], ((1,), (1,)))
    mid_ref[...] = middle
    factor = lax.rsqrt(jnp.mean(middle * middle, axis=-1, keepdims=True) + EPS)
    b_ref[...] = (middle * factor * gain_ref[...]).astype(jnp.bfloat16)


def out_call(o_parts, weight, tokens, gain, rows):
    count, width = tokens.shape
    inner = weight.shape[1]
    operands = (o_parts, weight, tokens, gain)
    shapes = [
        jax.ShapeDtypeStruct((count, width), jnp.float32),
        jax.ShapeDtypeStruct((count, width), jnp.bfloat16),
        jax.ShapeDtypeStruct((count, inner), jnp.bfloat16),
    ]
    return pl.pallas_call(
        partial(out_kernel, rows, o_parts.shape[0] // (2 * rows)),
        grid=(1,),
        in_specs=[full_spec(v) for v in operands],
        out_specs=[full_spec(v) for v in shapes],
        out_shape=shapes,
        scratch_shapes=[pltpu.VMEM((count, inner), jnp.bfloat16)],
        compiler_params=pltpu.CompilerParams(vmem_limit_bytes=48 << 20),
        name="out_norm",
        cost_estimate=cost(4),
    )(*operands)


def split_pairs(firsts, lasts):
    f0, f1, f2 = thirds(firsts)
    g0, g1, g2 = thirds(lasts)
    low = lane_iota(firsts.shape[0]) < 64
    t0, t1 = pltpu.roll(g0, 64, 1), pltpu.roll(g1, 64, 1)
    left = (f0, jnp.where(low, f1, t0), jnp.where(low, t0, t1))
    u1, u2 = pltpu.roll(f1, 64, 1), pltpu.roll(f2, 64, 1)
    right = (jnp.where(low, u1, u2), jnp.where(low, u2, g1), g2)
    return jnp.concatenate(left, axis=1), jnp.concatenate(right, axis=1)


def mid_back_kernel(
    rows, parts, keep_ref, fx_ref, fy_ref, px_ref, py_ref, mid_ref, cot_ref, gain_ref, w_ref,
    gmid_ref, go_ref, do_ref, gg_ref
):
    half = px_ref.shape[0]
    wide = lambda v: v.astype(jnp.float32)
    db = jnp.concatenate(
        [
            keep_ref[:half] + wide(fx_ref[:half]) + wide(py_ref[...]),
            keep_ref[half:] + wide(fy_ref[:half]) + wide(px_ref[...]),
        ],
        axis=0,
    )
    middle = mid_ref[...]
    factor = lax.rsqrt(jnp.mean(middle * middle, axis=-1, keepdims=True) + EPS)
    scaled = db * gain_ref[...]
    inner = jnp.mean(scaled * middle, axis=-1, keepdims=True)
    grad = cot_ref[...].astype(jnp.float32) + factor * scaled - middle * (factor**3 * inner)
    gmid_ref[...] = grad
    gg_ref[...] = jnp.sum(db * middle * factor, axis=0, keepdims=True)
    low = grad.astype(jnp.bfloat16)
    go_ref[...] = low
    back = dotf(low, w_ref[...], ((1,), (0,)))
    half = do_ref.shape[1]
    for r in range(rows):
        for z in range(parts):
            cols = slice(z * 3 * LN, (z + 1) * 3 * LN)
            at = 2 * r * half
            left, right = split_pairs(back[at : at + half, cols], back[at + half : at + 2 * half, cols])
            do_ref[r * parts + z] = left.astype(jnp.bfloat16)
            do_ref[(rows + r) * parts + z] = right.astype(jnp.bfloat16)


def mid_back_call(pieces, middle, cot, gain, weight, rows, parts):
    count, width = middle.shape
    operands = (*pieces, middle, cot, gain, weight)
    shapes = [
        jax.ShapeDtypeStruct((count, width), jnp.float32),
        jax.ShapeDtypeStruct((count, width), jnp.bfloat16),
        jax.ShapeDtypeStruct((2 * rows * parts, count // rows // 2, 3 * LN), jnp.bfloat16),
        jax.ShapeDtypeStruct((1, width), jnp.float32),
    ]
    return pl.pallas_call(
        partial(mid_back_kernel, rows, parts),
        grid=(1,),
        in_specs=[pl.BlockSpec((count, width), lambda i: (0, 0))] + [full_spec(v) for v in operands[1:]],
        out_specs=[full_spec(v) for v in shapes],
        out_shape=shapes,
        compiler_params=pltpu.CompilerParams(vmem_limit_bytes=48 << 20),
        name="mid_back",
        cost_estimate=cost(5),
    )(*operands)


def da_kernel(parts, rows, h_ref, d_ref, w_ref, wo_ref, da_ref, gg_ref):
    count = h_ref.shape[0] // parts
    tokens = count // rows
    groups = d_ref.shape[0]
    run = wo_ref.shape[0] // parts
    gg_ref[...] = jnp.zeros_like(gg_ref)

    def body(z, carry):
        at = pl.ds(pl.multiple_of(z * tokens, tokens), tokens)
        left = jnp.concatenate(
            [jnp.concatenate([d_ref[g, r, at, :] for r in range(rows)], axis=0) for g in range(groups)],
            axis=1,
        )
        back = dotf(left, w_ref[...], ((1,), (1,)))
        stream = h_ref[pl.ds(pl.multiple_of(z * count, count), count), :].astype(jnp.float32)
        factor = lax.rsqrt(jnp.mean(stream * stream, axis=-1, keepdims=True) + EPS)
        gg_ref[...] += jnp.sum(back * stream * factor, axis=0, keepdims=True)
        da_ref[z, :count, :] = back.astype(jnp.bfloat16)
        cols = pl.ds(pl.multiple_of(z * 3 * LN, 3 * LN), 3 * LN)
        for n in range(parts):
            da_ref[z, count:, n * 3 * LN : (n + 1) * 3 * LN] = wo_ref[n * run : (n + 1) * run, cols]
        return carry

    lax.fori_loop(0, parts, body, 0)


def da_call(parts, group, grads, weight, grad_wo, rows):
    count, width = group.shape
    operands = (group, grads, weight, grad_wo)
    block = (count + grad_wo.shape[0]) // parts
    shapes = [
        jax.ShapeDtypeStruct((parts, block, width), jnp.bfloat16),
        jax.ShapeDtypeStruct((1, width), jnp.float32),
    ]
    part, gain_grad = pl.pallas_call(
        partial(da_kernel, parts, rows),
        grid=(1,),
        in_specs=[full_spec(v) for v in operands],
        out_specs=[full_spec(v) for v in shapes],
        out_shape=shapes,
        compiler_params=pltpu.CompilerParams(vmem_limit_bytes=48 << 20),
        name="da_part",
        cost_estimate=cost(6),
    )(*operands)
    return part.reshape(parts * block, width), gain_grad


def cut_kernel(gate_ref, up_ref, down_ref, out_ref):
    for n in range(out_ref.shape[0]):
        at = slice(n * LN, (n + 1) * LN)
        out_ref[n, :, :LN] = gate_ref[:, at]
        out_ref[n, :, LN : 2 * LN] = up_ref[:, at]
        out_ref[n, :, 2 * LN :] = jnp.transpose(down_ref[at, :].astype(jnp.float32)).astype(jnp.bfloat16)


def cut_call(gate, up, down):
    shape = jax.ShapeDtypeStruct((gate.shape[1] // LN, gate.shape[0], 3 * LN), jnp.bfloat16)
    operands = (gate, up, down)
    return pl.pallas_call(
        cut_kernel,
        grid=(1,),
        in_specs=[full_spec(v) for v in operands],
        out_specs=full_spec(shape),
        out_shape=shape,
        name="cut_units",
        cost_estimate=cost(3),
    )(*operands)


def uncut_kernel(in_ref, gate_ref, up_ref, down_ref):
    for n in range(in_ref.shape[0]):
        at = slice(n * LN, (n + 1) * LN)
        gate_ref[:, at] = in_ref[n, :, :LN].astype(jnp.float32)
        up_ref[:, at] = in_ref[n, :, LN : 2 * LN].astype(jnp.float32)
        down_ref[at, :] = jnp.transpose(in_ref[n, :, 2 * LN :].astype(jnp.float32))


def uncut_call(value):
    units, rows = value.shape[0] * LN, value.shape[1]
    shapes = [jax.ShapeDtypeStruct(s, jnp.float32) for s in ((rows, units), (rows, units), (units, rows))]
    return pl.pallas_call(
        uncut_kernel,
        grid=(1,),
        in_specs=[full_spec(value)],
        out_specs=[full_spec(v) for v in shapes],
        out_shape=shapes,
        name="uncut_units",
        cost_estimate=cost(3),
    )(value)


def place_kernel(parts, turned, at_ref, mine_ref, other_ref, out_ref):
    size = mine_ref.shape[1]
    z = at_ref[3]
    for c, ref in enumerate((mine_ref, other_ref)):
        for n in range(parts):
            y, x = at_ref[0] ^ (n // 2), at_ref[1] ^ (n % 2)
            rows = pl.multiple_of(((y * 2 + x) * 2 + (at_ref[2] ^ c)) * size, size)
            for k in range(ref.shape[0] // parts):
                count = ref.shape[0] // parts
                source = lax.rem(z + (count - k), count) if turned else k
                cols = pl.multiple_of(source * 3 * LN, 3 * LN)
                out_ref[pl.ds(rows, size), pl.ds(cols, 3 * LN)] = ref[n * count + k]


def place_call(at, mine, other, turned):
    size = mine.shape[1]
    shape = jax.ShapeDtypeStruct((8 * size, mine.shape[0] // 4 * mine.shape[2]), mine.dtype)
    return pl.pallas_call(
        partial(place_kernel, 4, turned),
        grid=(1,),
        in_specs=[pl.BlockSpec(memory_space=pltpu.SMEM), full_spec(mine), full_spec(other)],
        out_specs=full_spec(shape),
        out_shape=shape,
        compiler_params=pltpu.CompilerParams(vmem_limit_bytes=32 << 20),
        name="place_out",
        cost_estimate=cost(3),
    )(at, mine, other)


def fill_square(refs, out_ref):
    own, xn, yn, first, last = refs
    half = first.shape[0]
    out_ref[0, :half], out_ref[0, half:] = own[:half], own[half:]
    out_ref[1, :half], out_ref[1, half:] = xn[:half], first[...]
    out_ref[2, :half], out_ref[2, half:] = yn[half:], last[...]
    out_ref[3, :half], out_ref[3, half:] = xn[half:], yn[:half]


def down_back_kernel(*refs):
    pieces, (w0_ref, w1_ref, out_ref, g_s) = refs[:5], refs[5:]

    @pl.when(pl.program_id(0) == 0)
    def _():
        fill_square(pieces, g_s)

    weight = jnp.concatenate([w0_ref[0, :, 2 * LN :], w1_ref[0, :, 2 * LN :]], axis=1)

    count, width = g_s.shape[1:]

    def body(m, carry):
        two = pl.ds(2 * m, 2)
        product = dotf(g_s[two].reshape(2 * count, width), weight, ((1,), (0,)))
        out_ref[0, two] = product.reshape(2, count, 2 * LN)
        return carry

    lax.fori_loop(0, 2, body, 0)


def unit_spec(weight):
    return pl.BlockSpec((1,) + weight.shape[1:], lambda z: (z, 0, 0))


def down_back_call(pieces, mine, other):
    count, width = pieces[0].shape
    parts = mine.shape[0]
    shape = jax.ShapeDtypeStruct((parts, 4, count, 2 * LN), jnp.float32)
    return pl.pallas_call(
        down_back_kernel,
        grid=(parts,),
        in_specs=[full_spec(v) for v in pieces] + [unit_spec(mine), unit_spec(other)],
        out_specs=pl.BlockSpec((1, 4, count, 2 * LN), lambda z: (z, 0, 0, 0)),
        out_shape=shape,
        scratch_shapes=[pltpu.VMEM((4, count, width), jnp.bfloat16)],
        compiler_params=pltpu.CompilerParams(vmem_limit_bytes=60 << 20),
        name="down_back",
        cost_estimate=cost(8),
    )(*pieces, mine, other)


def emit_square(acc_ref, keep_ref, sx_ref, sy_ref):
    count = sx_ref.shape[0]
    keep_ref[:count] = acc_ref[0]
    keep_ref[count:] = acc_ref[3]
    sx_ref[...] = acc_ref[1].astype(jnp.bfloat16)
    sy_ref[...] = acc_ref[2].astype(jnp.bfloat16)


def units_kernel(*refs):
    pieces, (w0_ref, w1_ref, dh_ref) = refs[:5], refs[5:8]
    dgu_ref, hid_ref, keep_ref, sx_ref, sy_ref, b_s, acc_s = refs[8:]
    step = pl.program_id(0)

    @pl.when(step == 0)
    def _():
        fill_square(pieces, b_s)

    count, width = b_s.shape[1:]

    def body(m, carry):
        two = pl.ds(2 * m, 2)
        b = b_s[two].reshape(2 * count, width)
        total = None
        for n, w_ref in enumerate((w0_ref, w1_ref)):
            weight = w_ref[0, :, : 2 * LN]
            both = dotf(b, weight, ((1,), (0,)))
            gate, up = both[:, :LN], both[:, LN:]
            cols = slice(n * LN, (n + 1) * LN)
            dh = dh_ref[0, two, :, cols].reshape(2 * count, LN)
            sigma = 1.0 / (1.0 + jnp.exp(-gate))
            silu = gate * sigma
            hid_ref[0, two, :, cols] = (silu * up).astype(jnp.bfloat16).reshape(2, count, LN)
            grad_gate = dh * up * sigma * (1.0 + gate * (1.0 - sigma))
            grads = jnp.concatenate([grad_gate, dh * silu], axis=1).astype(jnp.bfloat16)
            dgu_ref[0, n, two] = grads.reshape(2, count, 2 * LN)
            back = dotf(grads, weight, ((1,), (1,)))
            total = back if total is None else total + back
        total = total.reshape(2, count, width)

        @pl.when(step == 0)
        def _():
            acc_s[two] = total

        @pl.when(step > 0)
        def _():
            acc_s[two] += total

        return carry

    lax.fori_loop(0, 2, body, 0)

    @pl.when(step == pl.num_programs(0) - 1)
    def _():
        emit_square(acc_s, keep_ref, sx_ref, sy_ref)


def square_shapes(count, width):
    return [
        jax.ShapeDtypeStruct((2 * count, width), jnp.float32),
        jax.ShapeDtypeStruct((count, width), jnp.bfloat16),
        jax.ShapeDtypeStruct((count, width), jnp.bfloat16),
    ]


def units_call(pieces, mine, other, grad_hidden):
    count, width = pieces[0].shape
    parts = mine.shape[0]
    low = jnp.bfloat16
    shapes = [
        jax.ShapeDtypeStruct((parts, 2, 4, count, 2 * LN), low),
        jax.ShapeDtypeStruct((parts, 4, count, 2 * LN), low),
    ] + square_shapes(count, width)
    return pl.pallas_call(
        units_kernel,
        grid=(parts,),
        in_specs=[full_spec(v) for v in pieces]
        + [unit_spec(mine), unit_spec(other), pl.BlockSpec((1, 4, count, 2 * LN), lambda z: (z, 0, 0, 0))],
        out_specs=[
            pl.BlockSpec((1, 2, 4, count, 2 * LN), lambda z: (z, 0, 0, 0, 0)),
            pl.BlockSpec((1, 4, count, 2 * LN), lambda z: (z, 0, 0, 0)),
        ]
        + [full_spec(v) for v in shapes[2:]],
        out_shape=shapes,
        scratch_shapes=[pltpu.VMEM((4, count, width), low), pltpu.VMEM((4, count, width), jnp.float32)],
        compiler_params=pltpu.CompilerParams(vmem_limit_bytes=60 << 20),
        name="units",
        cost_estimate=cost(26),
    )(*pieces, mine, other, grad_hidden)


def down_kernel(hid_ref, w0_ref, w1_ref, keep_ref, sx_ref, sy_ref, acc_s):
    step = pl.program_id(0)
    weight = jnp.concatenate([w0_ref[0, :, 2 * LN :], w1_ref[0, :, 2 * LN :]], axis=1)

    count, width = acc_s.shape[1:]

    def body(m, carry):
        two = pl.ds(2 * m, 2)
        total = dotf(hid_ref[0, two].reshape(2 * count, 2 * LN), weight, ((1,), (1,)))
        total = total.reshape(2, count, width)

        @pl.when(step == 0)
        def _():
            acc_s[two] = total

        @pl.when(step > 0)
        def _():
            acc_s[two] += total

        return carry

    lax.fori_loop(0, 2, body, 0)

    @pl.when(step == pl.num_programs(0) - 1)
    def _():
        emit_square(acc_s, keep_ref, sx_ref, sy_ref)


def down_call(hidden, mine, other):
    parts, _, count, _ = hidden.shape
    width = mine.shape[1]
    shapes = square_shapes(count, width)
    return pl.pallas_call(
        down_kernel,
        grid=(parts,),
        in_specs=[pl.BlockSpec((1,) + hidden.shape[1:], lambda z: (z, 0, 0, 0)), unit_spec(mine), unit_spec(other)],
        out_specs=[full_spec(v) for v in shapes],
        out_shape=shapes,
        scratch_shapes=[pltpu.VMEM((4, count, width), jnp.float32)],
        compiler_params=pltpu.CompilerParams(vmem_limit_bytes=60 << 20),
        name="down",
        cost_estimate=cost(11),
    )(hidden, mine, other)


def unit_grads_kernel(*refs):
    b_pieces, g_pieces = refs[:5], refs[5:10]
    dgu_ref, hid_ref, mine_ref, other_ref, fill_s, b_s, g_s = refs[10:]
    count = fill_s.shape[1]

    @pl.when(pl.program_id(0) == 0)
    def _():
        for pieces, side in ((b_pieces, b_s), (g_pieces, g_s)):
            fill_square(pieces, fill_s)
            for m in range(4):
                side[:, m * count : (m + 1) * count] = jnp.transpose(fill_s[m])

    hidden = hid_ref[0].reshape(4 * count, 2 * LN)
    grads = [dgu_ref[0, n].reshape(4 * count, 2 * LN) for n in range(2)]
    rows = b_s.shape[0] // 4

    def body(m, carry):
        at = pl.ds(pl.multiple_of(m * rows, rows), rows)
        left, right = b_s[at, :], g_s[at, :]
        down = dotf(right, hidden, ((1,), (0,)))
        for n, out_ref in enumerate((mine_ref, other_ref)):
            out_ref[0, at, : 2 * LN] = dotf(left, grads[n], ((1,), (0,))).astype(jnp.bfloat16)
            out_ref[0, at, 2 * LN :] = down[:, n * LN : (n + 1) * LN].astype(jnp.bfloat16)
        return carry

    lax.fori_loop(0, 4, body, 0)


def unit_grads_call(b_pieces, g_pieces, grads, hidden):
    count, width = b_pieces[0].shape
    parts = hidden.shape[0]
    low = jnp.bfloat16
    operands = (*b_pieces, *g_pieces)
    return pl.pallas_call(
        unit_grads_kernel,
        grid=(parts,),
        in_specs=[full_spec(v) for v in operands]
        + [
            pl.BlockSpec((1,) + grads.shape[1:], lambda z: (z, 0, 0, 0, 0)),
            pl.BlockSpec((1,) + hidden.shape[1:], lambda z: (z, 0, 0, 0)),
        ],
        out_specs=[pl.BlockSpec((1, width, 3 * LN), lambda z: (z, 0, 0))] * 2,
        out_shape=[jax.ShapeDtypeStruct((parts, width, 3 * LN), low)] * 2,
        scratch_shapes=[pltpu.VMEM((4, count, width), low)] + [pltpu.VMEM((width, 4 * count), low)] * 2,
        compiler_params=pltpu.CompilerParams(vmem_limit_bytes=60 << 20),
        name="unit_grads",
        cost_estimate=cost(19),
    )(*operands, grads, hidden)


BY_SIDES = tuple((y, x, last) for x in range(2) for y in range(2) for last in range(2))
ORDER = ((0, 0, 0), (0, 0, 1), (0, 1, 0), (1, 1, 0), (1, 0, 1), (1, 1, 1), (0, 1, 1), (1, 0, 0))


def row_grads_kernel(order, at_ref, left_ref, right_ref, mine_ref, other_ref, full_s):
    tile = 2 * LN
    width = right_ref.shape[2]

    def body(n, carry):
        rows = pl.ds(pl.multiple_of(n * tile, tile), tile)
        left = jnp.transpose(left_ref[:, rows])
        for g in range(right_ref.shape[0]):
            piece = dotf(left, right_ref[g], ((1,), (0,)))
            full_s[rows, g * width : (g + 1) * width] = piece.astype(jnp.bfloat16)
        return carry

    lax.fori_loop(0, full_s.shape[0] // tile, body, 0)
    half = mine_ref.shape[1]
    for c, out_ref in enumerate((mine_ref, other_ref)):
        for n, (y, x, last) in enumerate(order):
            block = ((at_ref[0] ^ y) * 2 + (at_ref[1] ^ x)) * 2 + (at_ref[2] ^ c)
            rows = pl.multiple_of(block * 2 * half + last * half, 32)
            out_ref[n] = full_s[pl.ds(rows, half), :]


def row_grads_call(at, left, right, order, name, time):
    width = left.shape[1]
    cols = right.shape[0] * right.shape[2]
    shape = jax.ShapeDtypeStruct((8, width // 16, cols), jnp.bfloat16)
    return pl.pallas_call(
        partial(row_grads_kernel, order),
        grid=(1,),
        in_specs=[pl.BlockSpec(memory_space=pltpu.SMEM), full_spec(left), full_spec(right)],
        out_specs=[full_spec(shape)] * 2,
        out_shape=[shape] * 2,
        scratch_shapes=[pltpu.VMEM((width, cols), jnp.bfloat16)],
        compiler_params=pltpu.CompilerParams(vmem_limit_bytes=32 << 20),
        cost_estimate=cost(time),
        name=name,
    )(at, left, right)


def core_sum(mine, other):
    step = mine.shape[1]
    both = (mine.astype(jnp.float32) + other.astype(jnp.float32)).reshape(8 * step, -1)
    keep = jnp.concatenate([both[: 2 * step], both[6 * step :]], axis=0)
    low = both[2 * step : 6 * step].astype(jnp.bfloat16)
    return keep, low[: 2 * step], low[2 * step :]


EVERY = ("y", "x", "c", "z")
SWAP = ((0, 1), (1, 0))


def swap(value, axis):
    return lax.ppermute(value, axis, SWAP)


def gather_blocks(value, size):
    shift = lambda k: [(i, (i + k) % size) for i in range(size)]
    return [value] + [lax.ppermute(value, "z", shift(k)) for k in range(1, size)]


def gather_sides(value):
    return swap(value, "x"), swap(value, "y")


def gather_corner(xn, yn):
    half = xn.shape[0] // 2
    return swap(yn[:half], "x"), swap(xn[half:], "y")


def gather_square(value):
    sides = gather_sides(value)
    return (value, *sides, *gather_corner(*sides))


def reduce_square(keep, send_x, send_y):
    return reduce_square_rest(keep, swap(send_x, "x"), swap(send_y, "y"))


def reduce_square_rest(keep, from_x, from_y):
    low = jnp.bfloat16
    half = from_x.shape[0] // 2
    pass_y = swap((keep[3 * half :] + from_x[half:].astype(jnp.float32)).astype(low), "y")
    pass_x = swap((keep[2 * half : 3 * half] + from_y[half:].astype(jnp.float32)).astype(low), "x")
    return keep, from_x, from_y, pass_x, pass_y


def total_square(pieces):
    keep, from_x, from_y, pass_x, pass_y = pieces
    half = pass_x.shape[0]
    wide = lambda v: v.astype(jnp.float32)
    return jnp.concatenate(
        [
            keep[:half] + wide(from_x[:half]) + wide(pass_y),
            keep[half : 2 * half] + wide(from_y[:half]) + wide(pass_x),
        ],
        axis=0,
    )


def all_to_all(value, axes):
    return lax.all_to_all(value, axes, 0, 0, tiled=True)


def tie(*values):
    return lax.optimization_barrier(values)


def fast_local(sizes, *args):
    (tokens, cotangent, segments, positions, norm_in, w_query, w_key, w_value, w_out, norm_mid, w_gate, w_up, w_down) = args
    nz = sizes["z"]
    devices = sizes["y"] * sizes["x"] * sizes["c"] * nz
    plane = devices // nz
    rows, span, width = tokens.shape
    count = rows * span
    chunk = segments.shape[1]
    length = chunk * sizes["x"] * sizes["c"]
    x_at, c_at, z_at = lax.axis_index("x"), lax.axis_index("c"), lax.axis_index("z")
    at = jnp.stack([lax.axis_index("y"), x_at, c_at, z_at]).astype(jnp.int32)

    own = tokens.reshape(count, width)
    group = lax.all_gather(own, "z", axis=0, tiled=True)
    gains = jnp.concatenate([norm_in, norm_mid], axis=1)
    share = norm_in.shape[1]
    gains = jnp.pad(gains, ((0, 0), (0, LN - 2 * share)))
    gains = all_to_all(jnp.broadcast_to(gains, (devices, LN)), EVERY)

    kv_local = w_key.shape[2] // HD
    per_head = lambda w: w[0].reshape(w.shape[1], kv_local, -1)
    w_qkv = jnp.concatenate([per_head(w_query), per_head(w_key), per_head(w_value)], axis=2)
    w_qkv, w_o = tie(jnp.transpose(w_qkv, (1, 0, 2)), jnp.stack(gather_blocks(w_out[0].T, nz)))
    w_qkv = jnp.concatenate(gather_square(w_qkv), axis=0)
    w_qkv = place_call(at, w_qkv, swap(w_qkv, "c"), False)

    last = (x_at * sizes["c"] + c_at + 1) * chunk - 1
    begin = last - positions[:, -1] - jnp.where(segments[:, -1] == 2, 3 * length // 4, 0)
    lanes = jnp.arange(LN, dtype=jnp.int32) % (HD // 2)
    frequency = THETA ** (-(2.0 * lanes.astype(jnp.float32)) / HD)
    token_angle = positions.astype(jnp.float32)[:, :, None] * frequency
    first = lax.dynamic_slice_in_dim(begin, c_at, 1).astype(jnp.int32)
    index = jnp.arange(length, dtype=jnp.int32)
    row_angle = (index - doc_low(index, first[0], length)).astype(jnp.float32)[:, None] * frequency
    token_cos, token_sin = jnp.cos(token_angle), jnp.sin(token_angle)
    row_cos, row_sin = jnp.cos(row_angle), jnp.sin(row_angle)

    sides = gather_sides(w_o)
    gate, up, down, gains, *tables = tie(
        w_gate[0], w_up[0], w_down[0], gains, token_cos, token_sin, row_cos, row_sin, *sides
    )
    token_cos, token_sin, row_cos, row_sin, *sides = tables
    gain_in = gains[:, :share].reshape(1, width)
    gain_mid = gains[:, share : 2 * share].reshape(1, width)
    w_ff = all_to_all(cut_call(gate, up, down), ("y", "x", "c"))
    w_ff = w_ff.reshape(width, 3 * LN)
    corner = gather_corner(*sides)
    group, w_qkv, w_ff, *corner = tie(group, w_qkv, w_ff, *corner)
    w_o = jnp.concatenate([w_o, *sides, *corner], axis=0)
    w_mine = lax.all_gather(w_ff, "z", axis=0, tiled=True)

    normed, qkv = qkv_call(nz, group, gain_in, w_qkv, token_cos, token_sin, rows)
    qkv = all_to_all(qkv, ("x", "c")).reshape(length, 3 * LN)

    cot_low = cotangent.reshape(count, width)
    cot_first, _ = tie(cot_low, qkv)
    cot_sides = gather_sides(cot_first)

    attended, attended_float, log_total = attn_fwd(first, qkv)
    attended, *cot_sides = tie(attended, *cot_sides)
    attended = all_to_all(attended, ("x", "c", "z"))
    w_o = place_call(at, w_o, swap(w_o, "c"), True)
    w_o, *cot_sides = tie(w_o, *cot_sides)
    attended, *corner = tie(attended, *gather_corner(*cot_sides))
    cot_pieces = (cot_low, *cot_sides, *corner)
    middle, normed_b, attended_low = out_call(attended, w_o, own, gain_mid, rows)
    w_mine, _ = tie(w_mine, normed_b)
    w_mine = w_mine.reshape(nz, width, 3 * LN)
    w_other = swap(w_mine, "c")
    b_sides = gather_sides(normed_b)
    grad_hidden = down_back_call(cot_pieces, w_mine, w_other)
    *b_sides, grad_hidden = tie(*b_sides, grad_hidden)
    b_pieces = (normed_b, *b_sides, *gather_corner(*b_sides))
    grad_gu, hidden, *sends = units_call(b_pieces, w_mine, w_other, grad_hidden)
    from_x, from_y = swap(sends[1], "x"), swap(sends[2], "y")
    ff_mine, ff_other = unit_grads_call(b_pieces, cot_pieces, grad_gu, hidden)
    from_x, from_y, ff_other = tie(from_x, from_y, ff_other)
    grad_b = reduce_square_rest(sends[0], from_x, from_y)
    grad_ff = ff_mine.astype(jnp.float32) + swap(ff_other, "c").astype(jnp.float32)
    grad_ff = grad_ff.astype(jnp.bfloat16).reshape(nz * width, 3 * LN)
    grad_ff, *corner = tie(grad_ff, *grad_b[3:])
    grad_b = (*grad_b[:3], *corner)
    grad_ff = lax.psum_scatter(grad_ff, "z", scatter_dimension=0, tiled=True)
    grad_mid, grad_low, grad_o, gain_grad_mid = mid_back_call(
        grad_b, middle, cot_low, gain_mid, w_o, rows, nz
    )
    grad_o = all_to_all(grad_o, ("x", "c", "z"))
    hidden, _ = tie(hidden, grad_low)
    keep_out, *out_sides = down_call(hidden, w_mine, w_other)
    out_sides = swap(out_sides[0], "x"), swap(out_sides[1], "y")
    wo_mine, wo_other = row_grads_call(at, grad_low, attended_low[None], BY_SIDES, "out_grads", 3)
    wo_sum = (wo_mine.astype(jnp.float32) + swap(wo_other, "c").astype(jnp.float32)).reshape(width // 2, -1)
    wo_keep, wo_send = wo_sum[: width // 4], wo_sum[width // 4 :].astype(jnp.bfloat16)
    wo_got = swap(wo_send, "x")

    grad_qkv = attn_bwd(first, qkv, grad_o, attended_float, log_total, row_cos, row_sin)
    grad_qkv, wo_got, *out_sides = tie(grad_qkv, wo_got, *out_sides)
    out = middle + total_square(reduce_square_rest(keep_out, *out_sides))
    wo_sum = wo_keep + wo_got.astype(jnp.float32)
    wo_got = swap(wo_sum[width // 8 :].astype(jnp.bfloat16), "y")
    grad_wo = (wo_sum[: width // 8] + wo_got.astype(jnp.float32)).astype(jnp.bfloat16)
    grad_qkv = all_to_all(grad_qkv.reshape(-1, chunk, 3 * LN), ("x", "c"))
    grad_qkv, grad_ff = tie(grad_qkv, grad_ff)
    grad_ff = all_to_all(grad_ff.reshape(plane, width // plane, 3 * LN), ("y", "x", "c"))
    grad_qkv = grad_qkv.reshape(kv_local, rows, chunk, 3 * LN)
    part, gain_grad_in = da_call(nz, group, grad_qkv, w_qkv, grad_wo, rows)
    part = lax.psum_scatter(part, "z", scatter_dimension=0, tiled=True).astype(jnp.float32)
    grad_a, grad_wo = part[:count], part[count:]
    grad_wo = jnp.concatenate([grad_wo[:, n * 3 * LN : (n + 1) * 3 * LN] for n in range(nz)], axis=0)
    grad_wqkv = row_grads_call(
        at,
        normed.reshape(rows * chunk, width),
        grad_qkv.reshape(kv_local, rows * chunk, 3 * LN),
        ORDER,
        "qkv_grads",
        5,
    )
    *grad_wqkv, grad_ff = tie(*grad_wqkv, grad_ff)
    grad_wqkv = reduce_square(*core_sum(grad_wqkv[0], swap(grad_wqkv[1], "c")))
    gain_grads = jnp.concatenate(
        [gain_grad_in.reshape(devices, share), gain_grad_mid.reshape(devices, share)], axis=1
    )
    gain_grads = jnp.pad(gain_grads, ((0, 0), (0, LN - 2 * share)))
    *grad_wqkv, gain_grads = tie(*grad_wqkv, gain_grads)
    grad_wqkv = total_square(grad_wqkv)
    gain_grads = jnp.sum(all_to_all(gain_grads, EVERY), axis=0, keepdims=True)

    stream = own.astype(jnp.float32)
    factor = lax.rsqrt(jnp.mean(stream * stream, axis=-1, keepdims=True) + EPS)
    back_in, _ = norm_back(stream, factor, gain_in, grad_a)
    grad_tokens = grad_mid + back_in
    grad_wqkv = grad_wqkv.reshape(-1, kv_local, 4 * HD)
    flat = lambda g: g.reshape(1, g.shape[0], -1)
    grad_gate, grad_up, grad_down = uncut_call(grad_ff)
    return (
        out.reshape(tokens.shape),
        grad_tokens.reshape(tokens.shape),
        gain_grads[:, :share],
        flat(grad_wqkv[:, :, : 2 * HD]),
        flat(grad_wqkv[:, :, 2 * HD : 3 * HD]),
        flat(grad_wqkv[:, :, 3 * HD :]),
        grad_wo.T[None],
        gain_grads[:, share : 2 * share],
        grad_gate[None],
        grad_up[None],
        grad_down[None],
    )


def fast_solution(mesh, cores):
    batch, seq, kv = mesh.devices.shape
    fine = Mesh(mesh.devices.reshape(batch, seq // cores, cores, kv), EVERY)
    sizes = dict(fine.shape)
    row_spec = P("y", ("x", "c", "z"), None)
    seq_spec = P("y", ("x", "c"))
    gain_spec = P(None, EVERY)
    in_w = P(None, ("y", "x", "c"), "z")
    out_w = P(None, "z", ("y", "x", "c"))
    in_specs = (row_spec, row_spec, seq_spec, seq_spec, gain_spec, in_w, in_w, in_w, out_w, gain_spec, in_w, in_w, out_w)
    out_specs = (row_spec, row_spec, gain_spec, in_w, in_w, in_w, out_w, gain_spec, in_w, in_w, out_w)
    return jax.shard_map(
        partial(fast_local, sizes), mesh=fine, in_specs=in_specs, out_specs=out_specs, check_vma=False
    )


def solution(mesh):
    batch, seq, kv = (mesh.shape[name] for name in ("batch", "seq", "kv"))
    general = general_solution(mesh)
    if (batch, seq) != (2, 4):
        return general
    fast = fast_solution(mesh, 2)

    def run(*args):
        rows, length, width = args[0].shape
        kv_heads, q_heads = args[6].shape[2] // HD, args[5].shape[2] // HD
        fits = (
            rows == 2 * batch
            and kv_heads == 2 * kv
            and q_heads == 2 * kv_heads
            and length == 128 * seq * kv
            and length % (4 * BQ) == 0
            and width % LN == 0
            and 2 * width // (batch * seq * kv) <= LN
            and args[10].shape[2] == LN * batch * seq * kv
        )
        return (fast if fits else general)(*args)

    return run
```

```python
import functools
import math
from functools import partial

import jax
import jax.numpy as jnp
from jax import lax
from jax.experimental import pallas as pl
from jax.experimental.pallas import tpu as pltpu
from jax.sharding import Mesh
from jax.sharding import PartitionSpec as P

HD = 96
LAYERS = 1


EPS = 1e-05
THETA = 100000.0
BIG_NEG = -1e30


def rotary(positions_row):
    half_width = HD // 2
    frequency = THETA ** (-(2.0 * jnp.arange(half_width, dtype=jnp.float32)) / HD)
    angles = positions_row.astype(jnp.float32)[:, None] * frequency[None, :]
    cosine = jnp.concatenate([jnp.cos(angles), jnp.cos(angles)], axis=1)
    sine_table = jnp.concatenate([jnp.sin(angles), jnp.sin(angles)], axis=1)
    return (cosine, sine_table)


def rotate(head_vals, cosine, sine_table):
    half_width = head_vals.shape[-1] // 2
    swapped = jnp.concatenate([-head_vals[..., half_width:], head_vals[..., :half_width]], axis=-1)
    return head_vals * cosine[:, None, :] + swapped * sine_table[:, None, :]


def rms_norm(stream, gain):
    factor = lax.rsqrt(jnp.mean(stream * stream, axis=-1, keepdims=True) + EPS)
    return (stream * factor * gain, factor)


def norm_back(stream, factor, gain, upstream):
    scaled_grad = upstream * gain
    inner_mean = jnp.mean(scaled_grad * stream, axis=-1, keepdims=True)
    grad_stream = factor * scaled_grad - stream * factor**3 * inner_mean
    return (grad_stream, jnp.sum(upstream * stream * factor, axis=0))


def key_width(key_count):
    return math.gcd(key_count, 1024)


def contract(left_side, right_side, left_dim, right_dim):
    return lax.dot_general(
        left_side,
        right_side,
        (((left_dim,), (right_dim,)), ((), ())),
        preferred_element_type=jnp.float32,
    )


def spread(shard_rows):
    return lax.all_gather(shard_rows, "kv", axis=0, tiled=True)


def token_sum(pairs):
    summed = None
    for left_part, right_part, right_dim in pairs:
        product = contract(left_part, right_part, 1, right_dim)
        summed = product if summed is None else summed + product
    return lax.psum_scatter(
        summed.astype(jnp.bfloat16), "kv", scatter_dimension=0, tiled=True
    ).astype(jnp.float32)


def split_block(kv_both, seg_keys, offset, step_width, kv_local, head_size):
    kv_block = lax.dynamic_slice_in_dim(kv_both, offset, step_width, 0)
    key_block = kv_block[:, : kv_local * head_size].reshape(step_width, kv_local, head_size)
    value_block = kv_block[:, kv_local * head_size :].reshape(step_width, kv_local, head_size)
    seg_block = lax.dynamic_slice_in_dim(seg_keys, offset, step_width, 0)
    return (key_block, value_block, seg_block)


def forward_row(queries, seg_query, fold_state, kv_both, seg_keys, first_query, key_start):
    key_count = kv_both.shape[0]
    step_width = key_width(key_count)
    query_count, kv_local, group_size, head_size = queries.shape
    query_index = first_query + jnp.arange(query_count, dtype=jnp.int32)
    score_scale = head_size ** (-0.5)

    def forward_one_step(step_index, inner_state):
        running_max, weight_total, value_total = inner_state
        offset = step_index * step_width
        key_block, value_block, seg_block = split_block(
            kv_both, seg_keys, offset, step_width, kv_local, head_size
        )
        key_index = offset + jnp.arange(step_width, dtype=jnp.int32)
        allowed = (seg_query[:, None] == seg_block[None, :]) & (
            key_index[None, :] <= query_index[:, None]
        )
        scores = (
            jnp.einsum("qkgd,pkd->kgqp", queries, key_block, preferred_element_type=jnp.float32)
            * score_scale
        )
        scores = jnp.where(allowed, scores, BIG_NEG)
        new_max = jnp.maximum(running_max, jnp.max(scores, axis=-1))
        weights = jnp.where(allowed, jnp.exp(scores - new_max[..., None]), 0.0)
        rescale = jnp.exp(running_max - new_max)
        weight_total = rescale * weight_total + jnp.sum(weights, axis=-1)
        update = jnp.einsum(
            "kgqp,pkd->qkgd",
            weights.astype(jnp.bfloat16),
            value_block,
            preferred_element_type=jnp.float32,
        )
        value_total = jnp.transpose(rescale, (2, 0, 1))[..., None] * value_total + update
        return (new_max, weight_total, value_total)

    return lax.fori_loop(0, key_count // step_width, forward_one_step, fold_state)


def forward_fold(queries, seg_query, first_query, fold_state, pieces, key_start):
    kv_both, seg_keys = pieces
    row_fn = partial(forward_row, first_query=first_query, key_start=key_start)
    return jax.vmap(row_fn, in_axes=(0, 0, 0, 1, 1))(
        queries, seg_query, fold_state, kv_both, seg_keys
    )


def backward_row(
    queries,
    grad_attn,
    log_total,
    row_delta,
    seg_query,
    fold_state,
    kv_both,
    seg_keys,
    first_query,
    key_start,
):
    key_count = kv_both.shape[0]
    step_width = key_width(key_count)
    query_count, kv_local, group_size, head_size = queries.shape
    query_index = first_query + jnp.arange(query_count, dtype=jnp.int32)
    score_scale = head_size ** (-0.5)

    def backward_one_step(step_index, inner_state):
        grad_queries, grad_buffer = inner_state
        offset = step_index * step_width
        key_block, value_block, seg_block = split_block(
            kv_both, seg_keys, offset, step_width, kv_local, head_size
        )
        key_index = offset + jnp.arange(step_width, dtype=jnp.int32)
        allowed = (seg_query[:, None] == seg_block[None, :]) & (
            key_index[None, :] <= query_index[:, None]
        )
        scores = (
            jnp.einsum("qkgd,pkd->kgqp", queries, key_block, preferred_element_type=jnp.float32)
            * score_scale
        )
        probs_block = jnp.where(allowed, jnp.exp(scores - log_total[..., None]), 0.0)
        grad_probs = jnp.einsum(
            "qkgd,pkd->kgqp", grad_attn, value_block, preferred_element_type=jnp.float32
        )
        grad_scores = (probs_block * (grad_probs - row_delta[..., None])).astype(jnp.bfloat16)
        grad_queries = (
            grad_queries
            + jnp.einsum(
                "kgqp,pkd->qkgd", grad_scores, key_block, preferred_element_type=jnp.float32
            )
            * score_scale
        )
        grad_keys = (
            jnp.einsum("kgqp,qkgd->pkd", grad_scores, queries, preferred_element_type=jnp.float32)
            * score_scale
        )
        grad_values = jnp.einsum(
            "kgqp,qkgd->pkd",
            probs_block.astype(jnp.bfloat16),
            grad_attn,
            preferred_element_type=jnp.float32,
        )
        joined = jnp.concatenate(
            [grad_keys.reshape(step_width, -1), grad_values.reshape(step_width, -1)], axis=1
        )
        grad_buffer = lax.dynamic_update_slice_in_dim(grad_buffer, joined, offset, 0)
        return (grad_queries, grad_buffer)

    return lax.fori_loop(0, key_count // step_width, backward_one_step, fold_state)


def backward_fold(
    queries, grad_attn, log_total, row_delta, seg_query, first_query, fold_state, pieces, key_start
):
    kv_both, seg_keys = pieces
    row_fn = partial(backward_row, first_query=first_query, key_start=key_start)
    return jax.vmap(row_fn, in_axes=(0, 0, 0, 0, 0, 0, 1, 1))(
        queries, grad_attn, log_total, row_delta, seg_query, fold_state, kv_both, seg_keys
    )


def layer_forward(stream, gain_pair, matrices, seg_info, tables):
    gain_in, gain_mid = gain_pair
    w_query, w_key, w_value, w_out, w_gate, w_up, w_down = matrices
    seg_query, seg_keys = seg_info
    cosine, sine_table = tables
    row_count = seg_query.shape[0]
    kv_local = w_key.shape[1] // HD
    head_local = w_query.shape[1] // HD
    group_size = head_local // kv_local
    normed_a, factor_a = rms_norm(stream, gain_in)
    spread_a = spread(normed_a.astype(jnp.bfloat16))
    flat_count = spread_a.shape[0]
    token_count = flat_count // row_count
    raw_queries = jnp.dot(spread_a, w_query, preferred_element_type=jnp.float32).reshape(
        flat_count, head_local, HD
    )
    queries = (
        rotate(raw_queries, cosine, sine_table)
        .astype(jnp.bfloat16)
        .reshape(token_count, row_count, kv_local, group_size, HD)
    )
    queries = jnp.transpose(queries, (1, 0, 2, 3, 4))
    raw_keys = jnp.dot(spread_a, w_key, preferred_element_type=jnp.float32).reshape(
        flat_count, kv_local, HD
    )
    keys_low = (
        rotate(raw_keys, cosine, sine_table).astype(jnp.bfloat16).reshape(flat_count, kv_local * HD)
    )
    values_low = jnp.dot(spread_a, w_value, preferred_element_type=jnp.float32).astype(jnp.bfloat16)
    kv_both = jnp.concatenate([keys_low, values_low], axis=1).reshape(
        token_count, row_count, 2 * kv_local * HD
    )
    first_query = lax.axis_index("seq") * token_count
    start_state = (
        jnp.full((row_count, kv_local, group_size, token_count), BIG_NEG, jnp.float32),
        jnp.zeros((row_count, kv_local, group_size, token_count), jnp.float32),
        jnp.zeros((row_count, token_count, kv_local, group_size, HD), jnp.float32),
    )
    running_max, weight_total, value_total = forward_fold(
        queries,
        seg_query,
        first_query,
        start_state,
        (
            lax.all_gather(kv_both, "seq", axis=0, tiled=True),
            lax.all_gather(seg_keys, "seq", axis=0, tiled=True),
        ),
        jnp.int32(0),
    )
    attn_float = value_total / jnp.transpose(weight_total, (0, 3, 1, 2))[..., None]
    log_total = running_max + jnp.log(weight_total)
    attn_low = (
        jnp.transpose(attn_float, (1, 0, 2, 3, 4))
        .reshape(flat_count, head_local * HD)
        .astype(jnp.bfloat16)
    )
    stream_mid = stream + token_sum(((attn_low, w_out, 0),))
    normed_b, factor_b = rms_norm(stream_mid, gain_mid)
    spread_b = spread(normed_b.astype(jnp.bfloat16))
    gate_val = jnp.dot(spread_b, w_gate, preferred_element_type=jnp.float32)
    up_val = jnp.dot(spread_b, w_up, preferred_element_type=jnp.float32)
    hidden = (jax.nn.silu(gate_val) * up_val).astype(jnp.bfloat16)
    stream_out = stream_mid + token_sum(((hidden, w_down, 0),))
    saved_state = (
        stream,
        factor_a,
        spread_a,
        queries,
        kv_both,
        attn_float,
        attn_low,
        log_total,
        stream_mid,
        factor_b,
        spread_b,
        gate_val,
        up_val,
        hidden,
    )
    return (stream_out, saved_state)


def layer_backward(saved_state, grad_stream, gain_pair, matrices, seg_info, tables):
    (
        stream,
        factor_a,
        spread_a,
        queries,
        kv_both,
        attn_float,
        attn_low,
        log_total,
        stream_mid,
        factor_b,
        spread_b,
        gate_val,
        up_val,
        hidden,
    ) = saved_state
    gain_in, gain_mid = gain_pair
    w_query, w_key, w_value, w_out, w_gate, w_up, w_down = matrices
    seg_query, seg_keys = seg_info
    cosine, sine_table = tables
    row_count, token_count, kv_local, group_size, head_size = queries.shape
    head_local = kv_local * group_size
    flat_count = row_count * token_count
    grad_low = spread(grad_stream.astype(jnp.bfloat16))
    grad_down_w = contract(hidden, grad_low, 0, 0)
    grad_hidden = contract(grad_low, w_down, 1, 1)
    sigmoid_gate = jax.nn.sigmoid(gate_val)
    silu_gate = gate_val * sigmoid_gate
    grad_gate_low = (
        grad_hidden * up_val * sigmoid_gate * (1.0 + gate_val * (1.0 - sigmoid_gate))
    ).astype(jnp.bfloat16)
    grad_up_low = (grad_hidden * silu_gate).astype(jnp.bfloat16)
    grad_gate_w = contract(spread_b, grad_gate_low, 0, 0)
    grad_up_w = contract(spread_b, grad_up_low, 0, 0)
    grad_normed_b = token_sum(((grad_gate_low, w_gate, 1), (grad_up_low, w_up, 1)))
    back_mid, grad_gain_mid = norm_back(stream_mid, factor_b, gain_mid, grad_normed_b)
    grad_mid = grad_stream + back_mid
    grad_attn_full = spread(grad_mid.astype(jnp.bfloat16))
    grad_out_w = contract(attn_low, grad_attn_full, 0, 0)
    grad_attn = (
        contract(grad_attn_full, w_out, 1, 1)
        .astype(jnp.bfloat16)
        .reshape(token_count, row_count, kv_local, group_size, head_size)
    )
    grad_attn = jnp.transpose(grad_attn, (1, 0, 2, 3, 4))
    row_delta = jnp.transpose(jnp.sum(grad_attn * attn_float, axis=-1), (0, 2, 3, 1))
    first_query = lax.axis_index("seq") * token_count
    row_length = token_count * lax.axis_size("seq")
    start_state = (
        jnp.zeros((row_count, token_count, kv_local, group_size, head_size), jnp.float32),
        jnp.zeros((row_count, row_length, 2 * kv_local * head_size), jnp.float32),
    )
    grad_queries, grad_buffer = backward_fold(
        queries,
        grad_attn,
        log_total,
        row_delta,
        seg_query,
        first_query,
        start_state,
        (
            lax.all_gather(kv_both, "seq", axis=0, tiled=True),
            lax.all_gather(seg_keys, "seq", axis=0, tiled=True),
        ),
        jnp.int32(0),
    )
    grad_kv = lax.psum_scatter(
        grad_buffer.astype(jnp.bfloat16), "seq", scatter_dimension=1, tiled=True
    ).astype(jnp.float32)
    grad_kv = jnp.transpose(grad_kv, (1, 0, 2)).reshape(flat_count, 2 * kv_local * head_size)
    grad_queries = jnp.transpose(grad_queries, (1, 0, 2, 3, 4)).reshape(
        flat_count, head_local, head_size
    )
    grad_q_low = (
        rotate(grad_queries, cosine, -sine_table)
        .astype(jnp.bfloat16)
        .reshape(flat_count, head_local * head_size)
    )
    grad_k_low = (
        rotate(
            grad_kv[:, : kv_local * head_size].reshape(flat_count, kv_local, head_size),
            cosine,
            -sine_table,
        )
        .astype(jnp.bfloat16)
        .reshape(flat_count, kv_local * head_size)
    )
    grad_v_low = grad_kv[:, kv_local * head_size :].astype(jnp.bfloat16)
    grad_query_w = contract(spread_a, grad_q_low, 0, 0)
    grad_key_w = contract(spread_a, grad_k_low, 0, 0)
    grad_value_w = contract(spread_a, grad_v_low, 0, 0)
    grad_normed_a = token_sum(
        ((grad_q_low, w_query, 1), (grad_k_low, w_key, 1), (grad_v_low, w_value, 1))
    )
    back_in, grad_gain_in = norm_back(stream, factor_a, gain_in, grad_normed_a)
    grad_input = grad_mid + back_in
    weight_grads = (
        lax.psum_scatter(
            grad_query_w.astype(jnp.bfloat16), ("batch", "seq"), scatter_dimension=0, tiled=True
        ).astype(jnp.float32),
        lax.psum_scatter(
            grad_key_w.astype(jnp.bfloat16), ("batch", "seq"), scatter_dimension=0, tiled=True
        ).astype(jnp.float32),
        lax.psum_scatter(
            grad_value_w.astype(jnp.bfloat16), ("batch", "seq"), scatter_dimension=0, tiled=True
        ).astype(jnp.float32),
        lax.psum_scatter(
            grad_out_w.astype(jnp.bfloat16), ("batch", "seq"), scatter_dimension=1, tiled=True
        ).astype(jnp.float32),
        lax.psum_scatter(
            grad_gate_w.astype(jnp.bfloat16), ("batch", "seq"), scatter_dimension=0, tiled=True
        ).astype(jnp.float32),
        lax.psum_scatter(
            grad_up_w.astype(jnp.bfloat16), ("batch", "seq"), scatter_dimension=0, tiled=True
        ).astype(jnp.float32),
        lax.psum_scatter(
            grad_down_w.astype(jnp.bfloat16), ("batch", "seq"), scatter_dimension=1, tiled=True
        ).astype(jnp.float32),
    )
    return (grad_input, weight_grads, grad_gain_in, grad_gain_mid)


def to_flat(shard_rows):
    row_count, token_part, width = shard_rows.shape
    return jnp.transpose(shard_rows.astype(jnp.float32), (1, 0, 2)).reshape(
        token_part * row_count, width
    )


def from_flat(flat_rows, row_count):
    token_part = flat_rows.shape[0] // row_count
    return jnp.transpose(flat_rows.reshape(token_part, row_count, flat_rows.shape[1]), (1, 0, 2))


def general_local(
    tokens,
    cotangent,
    segments,
    positions,
    norm_in,
    w_query,
    w_key,
    w_value,
    w_out,
    norm_mid,
    w_gate,
    w_up,
    w_down,
):
    gains_in, gains_mid = (
        lax.all_gather(norm_in, ("batch", "seq", "kv"), axis=1, tiled=True),
        lax.all_gather(norm_mid, ("batch", "seq", "kv"), axis=1, tiled=True),
    )
    row_count = tokens.shape[0]
    seg_info = (segments, jnp.transpose(segments, (1, 0)))
    tables = rotary(jnp.transpose(positions, (1, 0)).reshape(-1))

    def fetch_layer(layer_index):
        return (
            lax.all_gather(w_query[layer_index], ("batch", "seq"), axis=0, tiled=True),
            lax.all_gather(w_key[layer_index], ("batch", "seq"), axis=0, tiled=True),
            lax.all_gather(w_value[layer_index], ("batch", "seq"), axis=0, tiled=True),
            lax.all_gather(w_out[layer_index], ("batch", "seq"), axis=1, tiled=True),
            lax.all_gather(w_gate[layer_index], ("batch", "seq"), axis=0, tiled=True),
            lax.all_gather(w_up[layer_index], ("batch", "seq"), axis=0, tiled=True),
            lax.all_gather(w_down[layer_index], ("batch", "seq"), axis=1, tiled=True),
        )

    stream = to_flat(tokens)
    fetched = []
    states = []
    layer_index = 0
    matrices = fetch_layer(layer_index)
    layer_inputs = [stream]
    stream, saved_state = layer_forward(
        stream, (gains_in[layer_index], gains_mid[layer_index]), matrices, seg_info, tables
    )
    fetched.append(matrices)
    states.append(saved_state)
    grad_stream = to_flat(cotangent)
    grads_in = []
    grads_mid = []
    weight_lists = []
    for layer_index in reversed(range(LAYERS)):
        gain_pair = (gains_in[layer_index], gains_mid[layer_index])
        matrices = fetch_layer(layer_index)
        saved_state = layer_forward(
            layer_inputs[layer_index], gain_pair, matrices, seg_info, tables
        )[1]
        grad_stream, weight_grads, grad_gain_in, grad_gain_mid = layer_backward(
            saved_state, grad_stream, gain_pair, matrices, seg_info, tables
        )
        grads_in.insert(0, grad_gain_in)
        grads_mid.insert(0, grad_gain_mid)
        weight_lists.insert(0, weight_grads)
    gain_grads_in, gain_grads_mid = (
        lax.psum_scatter(
            jnp.stack(grads_in), ("batch", "seq", "kv"), scatter_dimension=1, tiled=True
        ),
        lax.psum_scatter(
            jnp.stack(grads_mid), ("batch", "seq", "kv"), scatter_dimension=1, tiled=True
        ),
    )
    stacked_grads = [
        jnp.stack([grad_set[member] for grad_set in weight_lists]) for member in range(7)
    ]
    return (
        from_flat(stream, row_count),
        from_flat(grad_stream, row_count),
        gain_grads_in,
        stacked_grads[0],
        stacked_grads[1],
        stacked_grads[2],
        stacked_grads[3],
        gain_grads_mid,
        stacked_grads[4],
        stacked_grads[5],
        stacked_grads[6],
    )


def general_solution(mesh):
    in_specs = (
        P("batch", ("seq", "kv"), None),
        P("batch", ("seq", "kv"), None),
        P("batch", "seq"),
        P("batch", "seq"),
        P(None, ("batch", "seq", "kv")),
        P(None, ("batch", "seq"), "kv"),
        P(None, ("batch", "seq"), "kv"),
        P(None, ("batch", "seq"), "kv"),
        P(None, "kv", ("batch", "seq")),
        P(None, ("batch", "seq", "kv")),
        P(None, ("batch", "seq"), "kv"),
        P(None, ("batch", "seq"), "kv"),
        P(None, "kv", ("batch", "seq")),
    )
    out_specs = (
        P("batch", ("seq", "kv"), None),
        P("batch", ("seq", "kv"), None),
        P(None, ("batch", "seq", "kv")),
        P(None, ("batch", "seq"), "kv"),
        P(None, ("batch", "seq"), "kv"),
        P(None, ("batch", "seq"), "kv"),
        P(None, "kv", ("batch", "seq")),
        P(None, ("batch", "seq", "kv")),
        P(None, ("batch", "seq"), "kv"),
        P(None, ("batch", "seq"), "kv"),
        P(None, "kv", ("batch", "seq")),
    )
    return jax.shard_map(general_local, mesh=mesh, in_specs=in_specs, out_specs=out_specs, check_vma=False)


LN = 128
NEG=-1e30
C2 = (96 ** -0.5) * 1.4426950408889634

def cost(microseconds):
    return pl.CostEstimate(
        flops=microseconds * 10**9, bytes_accessed=microseconds * 3 * 10**6, transcendentals=0
    )


def lane_iota(rows):
    return lax.broadcasted_iota(jnp.int32, (rows, LN), 1)

def unpack4(t0, t1, t2):
    lane = lane_iota(t0.shape[0])
    live = lane < HD
    zero = jnp.zeros_like(t0)
    a = t0
    b = pltpu.roll(jnp.where(lane >= 96, t0, t1), 32, 1)
    c = pltpu.roll(jnp.where(lane >= 64, t1, t2), 64, 1)
    d = pltpu.roll(t2, 96, 1)
    return tuple(jnp.where(live, v, zero) for v in (a, b, c, d))

def pack4(a, b, c, d):
    lane = lane_iota(a.shape[0])
    b, c, d = pltpu.roll(b, 96, 1), pltpu.roll(c, 64, 1), pltpu.roll(d, 32, 1)
    return (jnp.where(lane < 96, a, b), jnp.where(lane < 64, b, c), jnp.where(lane < 32, c, d))

def split3(x):
    x = x.astype(jnp.float32)
    return x[:, :LN], x[:, LN:2*LN], x[:, 2*LN:]

def doc_low(index, first, length):
    second = first + 3 * length // 4
    return jnp.where(index >= second, second, jnp.where(index >= first, first, 0))

BQ = 256
BK = 512

def dotf(a, b, dims):
    return lax.dot_general(a, b, (dims, ((), ())), preferred_element_type=jnp.float32)

def attn_fwd_kernel(length, first_ref, x_ref, o_ref, of_ref, lse_ref, q_s, k_s, v_s, s_s):
    i = pl.program_id(0)
    blocks = length // BQ
    first = first_ref[0]

    @pl.when(i == 0)
    def _():
        def body(j, carry):
            rows = pl.ds(pl.multiple_of(j * BQ, BQ), BQ)
            q0, q1, k, v = unpack4(*split3(x_ref[rows, :]))
            q_s[j, :BQ, :] = q0.astype(jnp.bfloat16)
            q_s[j, BQ:, :] = q1.astype(jnp.bfloat16)
            k_s[rows, :] = k.astype(jnp.bfloat16)
            v_s[rows, :] = v.astype(jnp.bfloat16)
            return carry

        lax.fori_loop(0, blocks, body, 0)

    q = q_s[i]
    late = (3 * length // 4 + length // 8) // BQ
    start = jnp.where(i >= late, 3 * length // 4 // BK, 0)
    stop = i * BQ // BK + 1
    q_index = i * BQ + lax.broadcasted_iota(jnp.int32, (BQ, 1), 0)
    low = doc_low(q_index, first, length)

    def fold(v, op):
        out = v[:, :LN]
        for n in range(1, BK // LN):
            out = op(out, v[:, n * LN : (n + 1) * LN])
        return out

    def score(j, top):
        s = dotf(q, k_s[pl.ds(pl.multiple_of(j * BK, BK), BK), :], ((1,), (1,)))
        key = j * BK + lax.broadcasted_iota(jnp.int32, (1, BK), 1)
        ok = (key <= q_index) & (key >= low)
        s = jnp.concatenate([jnp.where(ok, s[:BQ], NEG), jnp.where(ok, s[BQ:], NEG)], axis=0)
        s_s[j] = s
        return jnp.maximum(top, fold(s, jnp.maximum))

    top = lax.fori_loop(start, stop, score, jnp.full((2 * BQ, LN), NEG, jnp.float32))
    m = jnp.max(top, axis=1, keepdims=True) * C2

    def add(j, state):
        p = jnp.exp2(s_s[j] * C2 - m)
        keys = pl.ds(pl.multiple_of(j * BK, BK), BK)
        of_ref[0] += dotf(p.astype(jnp.bfloat16), v_s[keys, :], ((1,), (0,)))
        return state + fold(p, jnp.add)

    zero = jnp.zeros((2 * BQ, LN), jnp.float32)
    of_ref[0] = zero
    total = lax.fori_loop(start, stop, add, zero)
    total = jnp.sum(total, axis=1, keepdims=True)
    out = of_ref[0] / total
    lse = jnp.broadcast_to(m + jnp.log2(total), (2 * BQ, LN))
    lse_ref[0] = jnp.transpose(lse, (1, 0))[:8, :]
    of_ref[0] = out
    for d in range(2):
        at = d * 128
        parts = [out[at + n // 2 * 64 + n % 2 * BQ : at + n // 2 * 64 + n % 2 * BQ + 64] for n in range(4)]
        for n, t in enumerate(pack4(*parts)):
            o_ref[d, :, n * LN : (n + 1) * LN] = t.astype(jnp.bfloat16)


def attn_fwd(first, x):
    length = x.shape[0]
    blocks = length // BQ
    return pl.pallas_call(
        functools.partial(attn_fwd_kernel, length),
        grid=(blocks,),
        in_specs=[pl.BlockSpec(memory_space=pltpu.SMEM),
                  pl.BlockSpec((length, 3*LN), lambda i: (0, 0))],
        out_specs=[pl.BlockSpec((2, 64, 3*LN), lambda i: (i, 0, 0)),
                   pl.BlockSpec((1, 2*BQ, LN), lambda i: (i, 0, 0)),
                   pl.BlockSpec((1, 8, 2*BQ), lambda i: (i, 0, 0))],
        out_shape=[jax.ShapeDtypeStruct((length//128, 64, 3*LN), jnp.bfloat16),
                   jax.ShapeDtypeStruct((blocks, 2*BQ, LN), jnp.float32),
                   jax.ShapeDtypeStruct((blocks, 8, 2*BQ), jnp.float32)],
        scratch_shapes=[pltpu.VMEM((blocks, 2*BQ, LN), jnp.bfloat16),
                        pltpu.VMEM((length, LN), jnp.bfloat16),
                        pltpu.VMEM((length, LN), jnp.bfloat16),
                        pltpu.VMEM((length // BK, 2*BQ, BK), jnp.float32)],
        compiler_params=pltpu.CompilerParams(vmem_limit_bytes=48 << 20),
        name="attend",
        cost_estimate=cost(22),
    )(first, x)

def attn_bwd_kernel(length, first_ref, x_ref, do_ref, of_ref, lse_ref, cos_ref, sin_ref, out_ref,
                    q_s, k_s, v_s, do_s, dl_s, dq_s, dk_s, dv_s):
    j = pl.program_id(0)
    blocks = length // BQ
    first = first_ref[0]
    @pl.when(j == 0)
    def _():
        def body(b, carry):
            rows = pl.ds(pl.multiple_of(b * BQ, BQ), BQ)
            q0, q1, k, v = unpack4(*split3(x_ref[rows, :]))
            q_s[b, :BQ, :] = q0.astype(jnp.bfloat16)
            q_s[b, BQ:, :] = q1.astype(jnp.bfloat16)
            k_s[b] = k.astype(jnp.bfloat16)
            v_s[b] = v.astype(jnp.bfloat16)
            for d in range(2):
                parts = unpack4(*split3(do_ref[2*b + d]))
                for n, part in enumerate(parts):
                    at = (n % 2) * BQ + d*128 + (n // 2) * 64
                    do_s[b, at:at+64, :] = part.astype(jnp.bfloat16)
            prod = do_s[b].astype(jnp.float32) * of_ref[b]
            delta = jnp.broadcast_to(jnp.sum(prod, axis=1, keepdims=True), (2*BQ, LN))
            dl_s[b] = jnp.transpose(delta, (1, 0))[:8, :]
            dq_s[b] = jnp.zeros((2*BQ, LN), jnp.float32)
            return carry
        lax.fori_loop(0, blocks, body, 0)
    late = (3 * length // 4 + length // 8) // BQ
    third = 3 * length // 4 // BQ
    stop = jnp.where(j >= third, blocks, late)
    k = k_s[j]
    v = v_s[j]
    dk_s[j] = jnp.zeros((BQ, LN), jnp.float32)
    dv_s[j] = jnp.zeros((BQ, LN), jnp.float32)
    key = j * BQ + lax.broadcasted_iota(jnp.int32, (BQ, 1), 0)

    def steps(places):
        dk, dv = [], []
        for i in places:
            q, do = q_s[i], do_s[i]
            s = dotf(k, q, ((1,), (1,)))
            dp = dotf(v, do, ((1,), (1,)))
            q_index = i * BQ + lax.broadcasted_iota(jnp.int32, (1, BQ), 1)
            ok = (key <= q_index) & (key >= doc_low(q_index, first, length))
            p = jnp.exp2(s * C2 - lse_ref[i, 0:1, :])
            p = jnp.concatenate([jnp.where(ok, p[:, :BQ], 0.0), jnp.where(ok, p[:, BQ:], 0.0)], axis=1)
            ds = (p * (dp - dl_s[i, 0:1, :])).astype(jnp.bfloat16)
            dv.append(dotf(p.astype(jnp.bfloat16), do, ((1,), (0,))))
            dk.append(dotf(ds, q, ((1,), (0,))))
            dq_s[i] += dotf(ds, k, ((0,), (0,)))
        dv_s[j] += functools.reduce(jnp.add, dv)
        dk_s[j] += functools.reduce(jnp.add, dk)

    pairs = (stop - j) // 2

    def body(n, carry):
        steps((j + 2 * n, j + 2 * n + 1))
        return carry

    lax.fori_loop(0, pairs, body, 0)

    @pl.when(j + 2 * pairs < stop)
    def _():
        steps((stop - 1,))

    @pl.when(j == blocks - 1)
    def _():
        scale = HD ** -0.5
        lower = lane_iota(BQ) < HD // 2

        def turn_back(piece, cosine, sine):
            swapped = jnp.where(lower, -pltpu.roll(piece, LN - HD // 2, 1), pltpu.roll(piece, HD // 2, 1))
            return (piece * cosine - swapped * sine) * scale

        def body(b, carry):
            rows = pl.ds(pl.multiple_of(b * BQ, BQ), BQ)
            cosine, sine = cos_ref[rows, :], sin_ref[rows, :]
            pieces = [turn_back(v, cosine, sine) for v in (dq_s[b, :BQ, :], dq_s[b, BQ:, :], dk_s[b])]
            for n, tile in enumerate(pack4(*pieces, dv_s[b])):
                out_ref[rows, n * LN : (n + 1) * LN] = tile.astype(jnp.bfloat16)
            return carry

        lax.fori_loop(0, blocks, body, 0)


def attn_bwd(first, x, do, of, lse, cos, sin):
    length = x.shape[0]
    blocks = length // BQ
    whole = lambda a: pl.BlockSpec(a.shape, lambda j: (0,) * a.ndim)
    return pl.pallas_call(
        functools.partial(attn_bwd_kernel, length),
        grid=(blocks,),
        in_specs=[pl.BlockSpec(memory_space=pltpu.SMEM)] + [whole(a) for a in (x, do, of, lse, cos, sin)],
        out_specs=pl.BlockSpec((length, 3*LN), lambda j: (0, 0)),
        out_shape=jax.ShapeDtypeStruct((length, 3*LN), jnp.bfloat16),
        scratch_shapes=[pltpu.VMEM((blocks, 2*BQ, LN), jnp.bfloat16),
                        pltpu.VMEM((blocks, BQ, LN), jnp.bfloat16),
                        pltpu.VMEM((blocks, BQ, LN), jnp.bfloat16),
                        pltpu.VMEM((blocks, 2*BQ, LN), jnp.bfloat16),
                        pltpu.VMEM((blocks, 8, 2*BQ), jnp.float32),
                        pltpu.VMEM((blocks, 2*BQ, LN), jnp.float32),
                        pltpu.VMEM((blocks, BQ, LN), jnp.float32),
                        pltpu.VMEM((blocks, BQ, LN), jnp.float32)],
        compiler_params=pltpu.CompilerParams(vmem_limit_bytes=56 << 20),
        name="attend_back",
        cost_estimate=cost(31),
    )(first, x, do, of, lse, cos, sin)


def widen(table):
    lane = lane_iota(table.shape[0])
    second = jnp.where(lane < 96, pltpu.roll(table, 96, 1), pltpu.roll(table, 16, 1))
    third = jnp.where(lane < 112, pltpu.roll(table, 112, 1), pltpu.roll(table, 32, 1))
    return second, third


def cos_sin3(cos, sin):
    lane = lane_iota(cos.shape[0])
    live = lane < 32
    cos_two, cos_three = widen(cos)
    sin_two, sin_three = widen(sin)
    cosine = jnp.concatenate([cos, cos_two, jnp.where(live, cos_three, 1.0)], axis=1)
    lower = (
        (lane < 48) | (lane >= 96),
        (lane < 16) | ((lane >= 64) & (lane < 112)),
        (lane >= 32) & (lane < 80),
    )
    tiles = (sin, sin_two, jnp.where(live, sin_three, 0.0))
    sine = jnp.concatenate([jnp.where(l, -t, t) for l, t in zip(lower, tiles)], axis=1)
    return cosine, sine, lower


def turn(values, cosine, sine, lower):
    width = values.shape[1]
    left, right = pltpu.roll(values, width - HD // 2, 1), pltpu.roll(values, HD // 2, 1)
    swapped = [
        jnp.where(l, left[:, n * LN : (n + 1) * LN], right[:, n * LN : (n + 1) * LN])
        for n, l in enumerate(lower)
    ]
    return values * cosine + jnp.concatenate(swapped, axis=1) * sine


def full_spec(array):
    rank = array.ndim
    return pl.BlockSpec(array.shape, lambda *_: (0,) * rank)


def qkv_kernel(parts, rows, h_ref, gain_ref, w_ref, cos_ref, sin_ref, a_ref, out_ref):
    count = h_ref.shape[0] // parts
    tokens = count // rows

    def body(z, carry):
        stream = h_ref[pl.ds(pl.multiple_of(z * count, count), count), :].astype(jnp.float32)
        factor = lax.rsqrt(jnp.mean(stream * stream, axis=-1, keepdims=True) + EPS)
        normed = (stream * factor * gain_ref[...]).astype(jnp.bfloat16)
        at = pl.ds(pl.multiple_of(z * tokens, tokens), tokens)
        for r in range(rows):
            a_ref[r, at, :] = normed[r * tokens : (r + 1) * tokens]
        product = dotf(normed, w_ref[...], ((1,), (0,)))
        for r in range(rows):
            cosine, sine, lower = cos_sin3(cos_ref[r, at, :], sin_ref[r, at, :])
            for h in range(product.shape[1] // (3 * LN)):
                piece = product[r * tokens : (r + 1) * tokens, h * 3 * LN : (h + 1) * 3 * LN]
                out_ref[h * rows + r, at, :] = turn(piece, cosine, sine, lower).astype(jnp.bfloat16)
        return carry

    lax.fori_loop(0, parts, body, 0)


def qkv_call(parts, group, gain, weight, cos, sin, rows):
    count, width = group.shape
    tokens = count // rows
    groups = weight.shape[1] // (3 * LN)
    operands = (group, gain, weight, cos, sin)
    return pl.pallas_call(
        partial(qkv_kernel, parts, rows),
        grid=(1,),
        in_specs=[full_spec(v) for v in operands],
        out_specs=[
            pl.BlockSpec((rows, tokens, width), lambda i: (0, 0, 0)),
            pl.BlockSpec((groups * rows, tokens, 3 * LN), lambda i: (0, 0, 0)),
        ],
        out_shape=[
            jax.ShapeDtypeStruct((rows, tokens, width), jnp.bfloat16),
            jax.ShapeDtypeStruct((groups * rows, tokens, 3 * LN), jnp.bfloat16),
        ],
        compiler_params=pltpu.CompilerParams(vmem_limit_bytes=48 << 20),
        name="norm_qkv",
        cost_estimate=cost(7),
    )(*operands)


def thirds(values):
    return values[:, :LN], values[:, LN : 2 * LN], values[:, 2 * LN :]


def join_pairs(left, right):
    l0, l1, l2 = thirds(left)
    r0, r1, r2 = thirds(right)
    low = lane_iota(left.shape[0]) < 64
    s0, s1, s2 = (pltpu.roll(v, 64, 1) for v in (r0, r1, r2))
    firsts = (l0, jnp.where(low, l1, s0), jnp.where(low, s0, s1))
    m1, m2 = pltpu.roll(l1, 64, 1), pltpu.roll(l2, 64, 1)
    lasts = (jnp.where(low, m1, m2), jnp.where(low, m2, r1), r2)
    return jnp.concatenate(firsts, axis=1), jnp.concatenate(lasts, axis=1)


def out_kernel(rows, parts, o_ref, w_ref, tok_ref, gain_ref, mid_ref, b_ref, oo_ref, o_s):
    half = o_ref.shape[1]
    for r in range(rows):
        for z in range(parts):
            left = o_ref[r * parts + z].astype(jnp.float32)
            right = o_ref[(rows + r) * parts + z].astype(jnp.float32)
            for n, piece in enumerate(join_pairs(left, right)):
                at = (2 * r + n) * half
                o_s[at : at + half, z * 3 * LN : (z + 1) * 3 * LN] = piece.astype(jnp.bfloat16)
    attended = o_s[...]
    oo_ref[...] = attended
    middle = tok_ref[...].astype(jnp.float32) + dotf(attended, w_ref[...], ((1,), (1,)))
    mid_ref[...] = middle
    factor = lax.rsqrt(jnp.mean(middle * middle, axis=-1, keepdims=True) + EPS)
    b_ref[...] = (middle * factor * gain_ref[...]).astype(jnp.bfloat16)


def out_call(o_parts, weight, tokens, gain, rows):
    count, width = tokens.shape
    inner = weight.shape[1]
    operands = (o_parts, weight, tokens, gain)
    shapes = [
        jax.ShapeDtypeStruct((count, width), jnp.float32),
        jax.ShapeDtypeStruct((count, width), jnp.bfloat16),
        jax.ShapeDtypeStruct((count, inner), jnp.bfloat16),
    ]
    return pl.pallas_call(
        partial(out_kernel, rows, o_parts.shape[0] // (2 * rows)),
        grid=(1,),
        in_specs=[full_spec(v) for v in operands],
        out_specs=[full_spec(v) for v in shapes],
        out_shape=shapes,
        scratch_shapes=[pltpu.VMEM((count, inner), jnp.bfloat16)],
        compiler_params=pltpu.CompilerParams(vmem_limit_bytes=48 << 20),
        name="out_norm",
        cost_estimate=cost(4),
    )(*operands)


def split_pairs(firsts, lasts):
    f0, f1, f2 = thirds(firsts)
    g0, g1, g2 = thirds(lasts)
    low = lane_iota(firsts.shape[0]) < 64
    t0, t1 = pltpu.roll(g0, 64, 1), pltpu.roll(g1, 64, 1)
    left = (f0, jnp.where(low, f1, t0), jnp.where(low, t0, t1))
    u1, u2 = pltpu.roll(f1, 64, 1), pltpu.roll(f2, 64, 1)
    right = (jnp.where(low, u1, u2), jnp.where(low, u2, g1), g2)
    return jnp.concatenate(left, axis=1), jnp.concatenate(right, axis=1)


def mid_back_kernel(
    rows, parts, keep_ref, fx_ref, fy_ref, px_ref, py_ref, mid_ref, cot_ref, gain_ref, w_ref,
    gmid_ref, go_ref, do_ref, gg_ref
):
    half = px_ref.shape[0]
    wide = lambda v: v.astype(jnp.float32)
    db = jnp.concatenate(
        [
            keep_ref[:half] + wide(fx_ref[...]) + wide(py_ref[...]),
            keep_ref[half:] + wide(fy_ref[...]) + wide(px_ref[...]),
        ],
        axis=0,
    )
    middle = mid_ref[...]
    factor = lax.rsqrt(jnp.mean(middle * middle, axis=-1, keepdims=True) + EPS)
    scaled = db * gain_ref[...]
    inner = jnp.mean(scaled * middle, axis=-1, keepdims=True)
    grad = cot_ref[...].astype(jnp.float32) + factor * scaled - middle * (factor**3 * inner)
    gmid_ref[...] = grad
    gg_ref[...] = jnp.sum(db * middle * factor, axis=0, keepdims=True)
    low = grad.astype(jnp.bfloat16)
    go_ref[...] = low
    back = dotf(low, w_ref[...], ((1,), (0,)))
    half = do_ref.shape[1]
    for r in range(rows):
        for z in range(parts):
            cols = slice(z * 3 * LN, (z + 1) * 3 * LN)
            at = 2 * r * half
            left, right = split_pairs(back[at : at + half, cols], back[at + half : at + 2 * half, cols])
            do_ref[r * parts + z] = left.astype(jnp.bfloat16)
            do_ref[(rows + r) * parts + z] = right.astype(jnp.bfloat16)


def mid_back_call(pieces, middle, cot, gain, weight, rows, parts):
    count, width = middle.shape
    operands = (*pieces, middle, cot, gain, weight)
    shapes = [
        jax.ShapeDtypeStruct((count, width), jnp.float32),
        jax.ShapeDtypeStruct((count, width), jnp.bfloat16),
        jax.ShapeDtypeStruct((2 * rows * parts, count // rows // 2, 3 * LN), jnp.bfloat16),
        jax.ShapeDtypeStruct((1, width), jnp.float32),
    ]
    return pl.pallas_call(
        partial(mid_back_kernel, rows, parts),
        grid=(1,),
        in_specs=[pl.BlockSpec((count, width), lambda i: (0, 0))] + [full_spec(v) for v in operands[1:]],
        out_specs=[full_spec(v) for v in shapes],
        out_shape=shapes,
        compiler_params=pltpu.CompilerParams(vmem_limit_bytes=48 << 20),
        name="mid_back",
        cost_estimate=cost(5),
    )(*operands)


def da_kernel(parts, rows, h_ref, d_ref, w_ref, wo_ref, da_ref, gg_ref):
    count = h_ref.shape[0] // parts
    tokens = count // rows
    groups = d_ref.shape[0]
    run = wo_ref.shape[0] // parts
    gg_ref[...] = jnp.zeros_like(gg_ref)

    def body(z, carry):
        at = pl.ds(pl.multiple_of(z * tokens, tokens), tokens)
        left = jnp.concatenate(
            [jnp.concatenate([d_ref[g, r, at, :] for r in range(rows)], axis=0) for g in range(groups)],
            axis=1,
        )
        back = dotf(left, w_ref[...], ((1,), (1,)))
        stream = h_ref[pl.ds(pl.multiple_of(z * count, count), count), :].astype(jnp.float32)
        factor = lax.rsqrt(jnp.mean(stream * stream, axis=-1, keepdims=True) + EPS)
        gg_ref[...] += jnp.sum(back * stream * factor, axis=0, keepdims=True)
        da_ref[z, :count, :] = back.astype(jnp.bfloat16)
        cols = pl.ds(pl.multiple_of(z * 3 * LN, 3 * LN), 3 * LN)
        for n in range(parts):
            da_ref[z, count:, n * 3 * LN : (n + 1) * 3 * LN] = wo_ref[n * run : (n + 1) * run, cols]
        return carry

    lax.fori_loop(0, parts, body, 0)


def da_call(parts, group, grads, weight, grad_wo, rows):
    count, width = group.shape
    operands = (group, grads, weight, grad_wo)
    block = (count + grad_wo.shape[0]) // parts
    shapes = [
        jax.ShapeDtypeStruct((parts, block, width), jnp.bfloat16),
        jax.ShapeDtypeStruct((1, width), jnp.float32),
    ]
    part, gain_grad = pl.pallas_call(
        partial(da_kernel, parts, rows),
        grid=(1,),
        in_specs=[full_spec(v) for v in operands],
        out_specs=[full_spec(v) for v in shapes],
        out_shape=shapes,
        compiler_params=pltpu.CompilerParams(vmem_limit_bytes=48 << 20),
        name="da_part",
        cost_estimate=cost(6),
    )(*operands)
    return part.reshape(parts * block, width), gain_grad


def cut_kernel(gate_ref, up_ref, down_ref, out_ref):
    for n in range(out_ref.shape[0]):
        at = slice(n * LN, (n + 1) * LN)
        out_ref[n, :, :LN] = gate_ref[:, at]
        out_ref[n, :, LN : 2 * LN] = up_ref[:, at]
        out_ref[n, :, 2 * LN :] = jnp.transpose(down_ref[at, :].astype(jnp.float32)).astype(jnp.bfloat16)


def cut_call(gate, up, down):
    shape = jax.ShapeDtypeStruct((gate.shape[1] // LN, gate.shape[0], 3 * LN), jnp.bfloat16)
    operands = (gate, up, down)
    return pl.pallas_call(
        cut_kernel,
        grid=(1,),
        in_specs=[full_spec(v) for v in operands],
        out_specs=full_spec(shape),
        out_shape=shape,
        name="cut_units",
        cost_estimate=cost(3),
    )(*operands)


def uncut_kernel(in_ref, gate_ref, up_ref, down_ref):
    for n in range(in_ref.shape[0]):
        at = slice(n * LN, (n + 1) * LN)
        gate_ref[:, at] = in_ref[n, :, :LN].astype(jnp.float32)
        up_ref[:, at] = in_ref[n, :, LN : 2 * LN].astype(jnp.float32)
        down_ref[at, :] = jnp.transpose(in_ref[n, :, 2 * LN :].astype(jnp.float32))


def uncut_call(value):
    units, rows = value.shape[0] * LN, value.shape[1]
    shapes = [jax.ShapeDtypeStruct(s, jnp.float32) for s in ((rows, units), (rows, units), (units, rows))]
    return pl.pallas_call(
        uncut_kernel,
        grid=(1,),
        in_specs=[full_spec(value)],
        out_specs=[full_spec(v) for v in shapes],
        out_shape=shapes,
        name="uncut_units",
        cost_estimate=cost(3),
    )(value)


def place_kernel(parts, turned, at_ref, mine_ref, other_ref, out_ref):
    size = mine_ref.shape[1]
    z = at_ref[3]
    for c, ref in enumerate((mine_ref, other_ref)):
        for n in range(parts):
            y, x = at_ref[0] ^ (n // 2), at_ref[1] ^ (n % 2)
            rows = pl.multiple_of(((y * 2 + x) * 2 + (at_ref[2] ^ c)) * size, size)
            for k in range(ref.shape[0] // parts):
                count = ref.shape[0] // parts
                source = lax.rem(z + (count - k), count) if turned else k
                cols = pl.multiple_of(source * 3 * LN, 3 * LN)
                out_ref[pl.ds(rows, size), pl.ds(cols, 3 * LN)] = ref[n * count + k]


def place_call(at, mine, other, turned):
    size = mine.shape[1]
    shape = jax.ShapeDtypeStruct((8 * size, mine.shape[0] // 4 * mine.shape[2]), mine.dtype)
    return pl.pallas_call(
        partial(place_kernel, 4, turned),
        grid=(1,),
        in_specs=[pl.BlockSpec(memory_space=pltpu.SMEM), full_spec(mine), full_spec(other)],
        out_specs=full_spec(shape),
        out_shape=shape,
        compiler_params=pltpu.CompilerParams(vmem_limit_bytes=32 << 20),
        name="place_out",
        cost_estimate=cost(3),
    )(at, mine, other)


def fill_sides(refs, out_ref):
    own, xn, yn = refs
    count = own.shape[0]
    half = count // 2
    out_ref[:count] = own[...]
    out_ref[count : count + half], out_ref[count + half : 2 * count] = xn[:half], yn[half:]
    out_ref[2 * count : 2 * count + half], out_ref[2 * count + half : 3 * count] = xn[half:], yn[:half]


def fill_corner(refs, out_ref, at):
    first, last = refs
    half = first.shape[0]
    out_ref[at : at + half], out_ref[at + half : at + 2 * half] = first[...], last[...]


def fill_square(refs, out_ref):
    fill_sides(refs[:3], out_ref)
    fill_corner(refs[3:], out_ref, 3 * refs[0].shape[0])


def unit_spec(weight):
    return pl.BlockSpec((1,) + weight.shape[1:], lambda z: (z, 0, 0))


def row_tiles(rows, tile, body):
    def step(m, carry):
        body(pl.ds(pl.multiple_of(m * tile, tile), tile))
        return carry

    lax.fori_loop(0, rows // tile, step, 0)


def down_back_kernel(*refs):
    pieces, (w0_ref, w1_ref, out_ref, g_s) = refs[:5], refs[5:]

    @pl.when(pl.program_id(0) == 0)
    def _():
        fill_square(pieces, g_s)

    weight = jnp.concatenate([w0_ref[0, :, 2 * LN :], w1_ref[0, :, 2 * LN :]], axis=1)

    def body(at):
        out_ref[0, at] = dotf(g_s[at, :], weight, ((1,), (0,)))

    row_tiles(g_s.shape[0], g_s.shape[0] // 2, body)


def down_back_call(pieces, mine, other):
    count, width = pieces[0].shape
    parts = mine.shape[0]
    shape = jax.ShapeDtypeStruct((parts, 4 * count, 2 * LN), jnp.float32)
    return pl.pallas_call(
        down_back_kernel,
        grid=(parts,),
        in_specs=[full_spec(v) for v in pieces] + [unit_spec(mine), unit_spec(other)],
        out_specs=unit_spec(shape),
        out_shape=shape,
        scratch_shapes=[pltpu.VMEM((4 * count, width), jnp.bfloat16)],
        compiler_params=pltpu.CompilerParams(vmem_limit_bytes=60 << 20),
        name="down_back",
        cost_estimate=cost(8),
    )(*pieces, mine, other)


def units_kernel(count, start, tile, *refs):
    pieces = refs[:2] if start else refs[:3]
    w0_ref, w1_ref, dh_ref, dgu_ref, hid_ref, *sends, b_s, acc_s = refs[len(pieces) :]
    step = pl.program_id(0)

    @pl.when(step == 0)
    def _():
        if start:
            fill_corner(pieces, b_s, 0)
        else:
            fill_sides(pieces, b_s)

    def body(at):
        b = b_s[at, :]
        total = None
        for n, w_ref in enumerate((w0_ref, w1_ref)):
            weight = w_ref[0, :, : 2 * LN]
            both = dotf(b, weight, ((1,), (0,)))
            gate, up = both[:, :LN], both[:, LN:]
            cols = slice(n * LN, (n + 1) * LN)
            dh = dh_ref[0, pl.ds(start + at.start, tile), cols]
            sigma = 1.0 / (1.0 + jnp.exp(-gate))
            silu = gate * sigma
            hid_ref[0, at, cols] = (silu * up).astype(jnp.bfloat16)
            grad_gate = dh * up * sigma * (1.0 + gate * (1.0 - sigma))
            grads = jnp.concatenate([grad_gate, dh * silu], axis=1).astype(jnp.bfloat16)
            dgu_ref[0, n, at] = grads
            back = dotf(grads, weight, ((1,), (1,)))
            total = back if total is None else total + back

        @pl.when(step == 0)
        def _():
            acc_s[at, :] = total

        @pl.when(step > 0)
        def _():
            acc_s[at, :] += total

    row_tiles(b_s.shape[0], tile, body)

    @pl.when(step == pl.num_programs(0) - 1)
    def _():
        half = count // 2
        if start:
            sx_ref, sy_ref = sends
            sx_ref[...] = acc_s[:half].astype(jnp.bfloat16)
            sy_ref[...] = acc_s[half:].astype(jnp.bfloat16)
        else:
            keep_ref, sx_ref, sy_ref = sends
            keep_ref[:count] = acc_s[:count]
            keep_ref[count:] = acc_s[2 * count :]
            sx_ref[...] = acc_s[count : count + half].astype(jnp.bfloat16)
            sy_ref[...] = acc_s[count + half : 2 * count].astype(jnp.bfloat16)


def units_call(pieces, mine, other, grad_hidden, corner):
    parts, width = mine.shape[:2]
    count = grad_hidden.shape[1] // 4
    rows = count if corner else 3 * count
    low = jnp.bfloat16
    shapes = [
        jax.ShapeDtypeStruct((parts, 2, rows, 2 * LN), low),
        jax.ShapeDtypeStruct((parts, rows, 2 * LN), low),
    ]
    if not corner:
        shapes += [jax.ShapeDtypeStruct((2 * count, width), jnp.float32)]
    shapes += [jax.ShapeDtypeStruct((count // 2, width), low)] * 2
    return pl.pallas_call(
        partial(units_kernel, count, 3 * count if corner else 0, count if corner else 3 * count // 2),
        grid=(parts,),
        in_specs=[full_spec(v) for v in pieces] + [unit_spec(mine), unit_spec(other), unit_spec(grad_hidden)],
        out_specs=[
            pl.BlockSpec((1, 2, rows, 2 * LN), lambda z: (z, 0, 0, 0)),
            pl.BlockSpec((1, rows, 2 * LN), lambda z: (z, 0, 0)),
        ]
        + [full_spec(v) for v in shapes[2:]],
        out_shape=shapes,
        scratch_shapes=[pltpu.VMEM((rows, width), low), pltpu.VMEM((rows, width), jnp.float32)],
        compiler_params=pltpu.CompilerParams(vmem_limit_bytes=60 << 20),
        name="units_corner" if corner else "units",
        cost_estimate=cost(8 if corner else 19),
    )(*pieces, mine, other, grad_hidden)


def down_kernel(hid_ref, hid_last_ref, w0_ref, w1_ref, keep_ref, sx_ref, sy_ref, acc_s):
    step = pl.program_id(0)
    weight = jnp.concatenate([w0_ref[0, :, 2 * LN :], w1_ref[0, :, 2 * LN :]], axis=1)
    rows, count = hid_ref.shape[1], hid_last_ref.shape[1]

    def add(at, hidden):
        total = dotf(hidden, weight, ((1,), (1,)))

        @pl.when(step == 0)
        def _():
            acc_s[at, :] = total

        @pl.when(step > 0)
        def _():
            acc_s[at, :] += total

    row_tiles(rows, rows // 2, lambda at: add(at, hid_ref[0, at]))
    add(pl.ds(rows, count), hid_last_ref[0])

    @pl.when(step == pl.num_programs(0) - 1)
    def _():
        half = count // 2
        keep_ref[:count] = acc_s[:count]
        keep_ref[count:] = acc_s[2 * count : 3 * count]
        for n, ref in enumerate((sx_ref, sy_ref)):
            at = n * half
            ref[:half] = acc_s[count + at : count + at + half].astype(jnp.bfloat16)
            ref[half:] = acc_s[3 * count + at : 3 * count + at + half].astype(jnp.bfloat16)


def down_call(hidden, hidden_last, mine, other):
    parts, count, _ = hidden_last.shape
    width = mine.shape[1]
    shapes = [
        jax.ShapeDtypeStruct((2 * count, width), jnp.float32),
        jax.ShapeDtypeStruct((count, width), jnp.bfloat16),
        jax.ShapeDtypeStruct((count, width), jnp.bfloat16),
    ]
    operands = (hidden, hidden_last, mine, other)
    return pl.pallas_call(
        down_kernel,
        grid=(parts,),
        in_specs=[unit_spec(v) for v in operands],
        out_specs=[full_spec(v) for v in shapes],
        out_shape=shapes,
        scratch_shapes=[pltpu.VMEM((4 * count, width), jnp.float32)],
        compiler_params=pltpu.CompilerParams(vmem_limit_bytes=60 << 20),
        name="down",
        cost_estimate=cost(11),
    )(*operands)


def unit_grads_kernel(*refs):
    b_pieces, g_pieces = refs[:5], refs[5:10]
    dgu_ref, dgu_last_ref, hid_ref, hid_last_ref, mine_ref, other_ref, fill_s, b_s, g_s = refs[10:]
    total, width = fill_s.shape
    count = total // 4

    @pl.when(pl.program_id(0) == 0)
    def _():
        for pieces, side in ((b_pieces, b_s), (g_pieces, g_s)):
            fill_square(pieces, fill_s)
            for m in range(4):
                at = slice(m * count, (m + 1) * count)
                side[:, at] = jnp.transpose(fill_s[at, :])

    cut = hid_ref.shape[1]

    def body(at):
        left, right = b_s[at, :], g_s[at, :]
        sum_over = lambda v, a, z: dotf(v[:, :cut], a, ((1,), (0,))) + dotf(v[:, cut:], z, ((1,), (0,)))
        down = sum_over(right, hid_ref[0], hid_last_ref[0])
        for n, out_ref in enumerate((mine_ref, other_ref)):
            out_ref[0, at, : 2 * LN] = sum_over(left, dgu_ref[0, n], dgu_last_ref[0, n]).astype(jnp.bfloat16)
            out_ref[0, at, 2 * LN :] = down[:, n * LN : (n + 1) * LN].astype(jnp.bfloat16)

    row_tiles(width, width // 4, body)


def unit_grads_call(b_pieces, g_pieces, grads, hidden):
    count, width = b_pieces[0].shape
    parts = hidden[0].shape[0]
    low = jnp.bfloat16
    operands = (*b_pieces, *g_pieces)
    return pl.pallas_call(
        unit_grads_kernel,
        grid=(parts,),
        in_specs=[full_spec(v) for v in operands]
        + [pl.BlockSpec((1,) + v.shape[1:], lambda z: (z, 0, 0, 0)) for v in grads]
        + [unit_spec(v) for v in hidden],
        out_specs=[pl.BlockSpec((1, width, 3 * LN), lambda z: (z, 0, 0))] * 2,
        out_shape=[jax.ShapeDtypeStruct((parts, width, 3 * LN), low)] * 2,
        scratch_shapes=[pltpu.VMEM((4 * count, width), low)] + [pltpu.VMEM((width, 4 * count), low)] * 2,
        compiler_params=pltpu.CompilerParams(vmem_limit_bytes=60 << 20),
        name="unit_grads",
        cost_estimate=cost(19),
    )(*operands, *grads, *hidden)


BY_SIDES = tuple((y, x, last) for x in range(2) for y in range(2) for last in range(2))
ORDER = ((0, 0, 0), (0, 0, 1), (0, 1, 0), (1, 1, 0), (1, 0, 1), (1, 1, 1), (0, 1, 1), (1, 0, 0))


def row_grads_kernel(order, at_ref, left_ref, right_ref, mine_ref, other_ref, full_s):
    tile = 2 * LN
    width = right_ref.shape[2]

    def body(n, carry):
        rows = pl.ds(pl.multiple_of(n * tile, tile), tile)
        left = jnp.transpose(left_ref[:, rows])
        for g in range(right_ref.shape[0]):
            piece = dotf(left, right_ref[g], ((1,), (0,)))
            full_s[rows, g * width : (g + 1) * width] = piece.astype(jnp.bfloat16)
        return carry

    lax.fori_loop(0, full_s.shape[0] // tile, body, 0)
    half = mine_ref.shape[1]
    for c, out_ref in enumerate((mine_ref, other_ref)):
        for n, (y, x, last) in enumerate(order):
            block = ((at_ref[0] ^ y) * 2 + (at_ref[1] ^ x)) * 2 + (at_ref[2] ^ c)
            rows = pl.multiple_of(block * 2 * half + last * half, 32)
            out_ref[n] = full_s[pl.ds(rows, half), :]


def row_grads_call(at, left, right, order, name, time):
    width = left.shape[1]
    cols = right.shape[0] * right.shape[2]
    shape = jax.ShapeDtypeStruct((8, width // 16, cols), jnp.bfloat16)
    return pl.pallas_call(
        partial(row_grads_kernel, order),
        grid=(1,),
        in_specs=[pl.BlockSpec(memory_space=pltpu.SMEM), full_spec(left), full_spec(right)],
        out_specs=[full_spec(shape)] * 2,
        out_shape=[shape] * 2,
        scratch_shapes=[pltpu.VMEM((width, cols), jnp.bfloat16)],
        compiler_params=pltpu.CompilerParams(vmem_limit_bytes=32 << 20),
        cost_estimate=cost(time),
        name=name,
    )(at, left, right)


def core_sum(mine, other):
    step = mine.shape[1]
    both = (mine.astype(jnp.float32) + other.astype(jnp.float32)).reshape(8 * step, -1)
    keep = jnp.concatenate([both[: 2 * step], both[6 * step :]], axis=0)
    low = both[2 * step : 6 * step].astype(jnp.bfloat16)
    return keep, low[: 2 * step], low[2 * step :]


EVERY = ("y", "x", "c", "z")
SWAP = ((0, 1), (1, 0))


def swap(value, axis):
    return lax.ppermute(value, axis, SWAP)


def gather_blocks(value, size):
    shift = lambda k: [(i, (i + k) % size) for i in range(size)]
    return [value] + [lax.ppermute(value, "z", shift(k)) for k in range(1, size)]


def gather_sides(value):
    return swap(value, "x"), swap(value, "y")


def gather_corner(xn, yn):
    half = xn.shape[0] // 2
    return swap(yn[:half], "x"), swap(xn[half:], "y")


def gather_square(value):
    sides = gather_sides(value)
    return (value, *sides, *gather_corner(*sides))


def reduce_square(keep, send_x, send_y):
    return reduce_square_rest(keep, swap(send_x, "x"), swap(send_y, "y"))


def reduce_square_rest(keep, from_x, from_y):
    half = from_x.shape[0] // 2
    corner = pass_on(keep, from_x[half:], from_y[half:])
    return keep, from_x[:half], from_y[:half], *corner


def pass_on(keep, corner_x, corner_y):
    low = jnp.bfloat16
    half = corner_x.shape[0]
    pass_y = swap((keep[3 * half :] + corner_x.astype(jnp.float32)).astype(low), "y")
    pass_x = swap((keep[2 * half : 3 * half] + corner_y.astype(jnp.float32)).astype(low), "x")
    return pass_x, pass_y


def total_square(pieces):
    keep, from_x, from_y, pass_x, pass_y = pieces
    half = pass_x.shape[0]
    wide = lambda v: v.astype(jnp.float32)
    return jnp.concatenate(
        [
            keep[:half] + wide(from_x) + wide(pass_y),
            keep[half : 2 * half] + wide(from_y) + wide(pass_x),
        ],
        axis=0,
    )


def all_to_all(value, axes):
    return lax.all_to_all(value, axes, 0, 0, tiled=True)


def tie(*values):
    return lax.optimization_barrier(values)


def fast_local(sizes, *args):
    (tokens, cotangent, segments, positions, norm_in, w_query, w_key, w_value, w_out, norm_mid, w_gate, w_up, w_down) = args
    nz = sizes["z"]
    devices = sizes["y"] * sizes["x"] * sizes["c"] * nz
    plane = devices // nz
    rows, span, width = tokens.shape
    count = rows * span
    chunk = segments.shape[1]
    length = chunk * sizes["x"] * sizes["c"]
    x_at, c_at, z_at = lax.axis_index("x"), lax.axis_index("c"), lax.axis_index("z")
    at = jnp.stack([lax.axis_index("y"), x_at, c_at, z_at]).astype(jnp.int32)

    own = tokens.reshape(count, width)
    group = lax.all_gather(own, "z", axis=0, tiled=True)
    gains = jnp.concatenate([norm_in, norm_mid], axis=1)
    share = norm_in.shape[1]
    gains = jnp.pad(gains, ((0, 0), (0, LN - 2 * share)))
    gains = all_to_all(jnp.broadcast_to(gains, (devices, LN)), EVERY)

    kv_local = w_key.shape[2] // HD
    per_head = lambda w: w[0].reshape(w.shape[1], kv_local, -1)
    w_qkv = jnp.concatenate([per_head(w_query), per_head(w_key), per_head(w_value)], axis=2)
    w_qkv, w_o = tie(jnp.transpose(w_qkv, (1, 0, 2)), jnp.stack(gather_blocks(w_out[0].T, nz)))
    w_qkv = jnp.concatenate(gather_square(w_qkv), axis=0)
    w_qkv = place_call(at, w_qkv, swap(w_qkv, "c"), False)

    last = (x_at * sizes["c"] + c_at + 1) * chunk - 1
    begin = last - positions[:, -1] - jnp.where(segments[:, -1] == 2, 3 * length // 4, 0)
    lanes = jnp.arange(LN, dtype=jnp.int32) % (HD // 2)
    frequency = THETA ** (-(2.0 * lanes.astype(jnp.float32)) / HD)
    token_angle = positions.astype(jnp.float32)[:, :, None] * frequency
    first = lax.dynamic_slice_in_dim(begin, c_at, 1).astype(jnp.int32)
    index = jnp.arange(length, dtype=jnp.int32)
    row_angle = (index - doc_low(index, first[0], length)).astype(jnp.float32)[:, None] * frequency
    token_cos, token_sin = jnp.cos(token_angle), jnp.sin(token_angle)
    row_cos, row_sin = jnp.cos(row_angle), jnp.sin(row_angle)

    sides = gather_sides(w_o)
    gate, up, down, gains, *tables = tie(
        w_gate[0], w_up[0], w_down[0], gains, token_cos, token_sin, row_cos, row_sin, *sides
    )
    token_cos, token_sin, row_cos, row_sin, *sides = tables
    gain_in = gains[:, :share].reshape(1, width)
    gain_mid = gains[:, share : 2 * share].reshape(1, width)
    w_ff = all_to_all(cut_call(gate, up, down), ("y", "x", "c"))
    w_ff = w_ff.reshape(width, 3 * LN)
    corner = gather_corner(*sides)
    group, w_qkv, w_ff = tie(group, w_qkv, w_ff)
    w_mine = lax.all_gather(w_ff, "z", axis=0, tiled=True)

    normed, qkv = qkv_call(nz, group, gain_in, w_qkv, token_cos, token_sin, rows)
    qkv, *corner = tie(qkv, *corner)
    w_o = jnp.concatenate([w_o, *sides, *corner], axis=0)
    qkv = all_to_all(qkv, ("x", "c")).reshape(length, 3 * LN)

    cot_low = cotangent.reshape(count, width)
    cot_first, _ = tie(cot_low, qkv)
    cot_sides = gather_sides(cot_first)

    attended, attended_float, log_total = attn_fwd(first, qkv)
    attended, *cot_sides = tie(attended, *cot_sides)
    attended = all_to_all(attended, ("x", "c", "z"))
    w_o = place_call(at, w_o, swap(w_o, "c"), True)
    w_o, *cot_sides = tie(w_o, *cot_sides)
    attended, *corner = tie(attended, *gather_corner(*cot_sides))
    cot_pieces = (cot_low, *cot_sides, *corner)
    middle, normed_b, attended_low = out_call(attended, w_o, own, gain_mid, rows)
    w_mine, _ = tie(w_mine, normed_b)
    w_mine = w_mine.reshape(nz, width, 3 * LN)
    w_other = swap(w_mine, "c")
    b_sides = gather_sides(normed_b)
    grad_hidden = down_back_call(cot_pieces, w_mine, w_other)
    *b_sides, grad_hidden = tie(*b_sides, grad_hidden)
    b_corner = gather_corner(*b_sides)
    b_pieces = (normed_b, *b_sides, *b_corner)
    grads, hidden, keep_b, *sends = units_call((normed_b, *b_sides), w_mine, w_other, grad_hidden, False)
    from_x, from_y = swap(sends[0], "x"), swap(sends[1], "y")
    grads_last, hidden_last, *sends = units_call(b_corner, w_mine, w_other, grad_hidden, True)
    corner_x, corner_y = swap(sends[0], "x"), swap(sends[1], "y")
    ff_mine, ff_other = unit_grads_call(b_pieces, cot_pieces, (grads, grads_last), (hidden, hidden_last))
    from_x, from_y, corner_x, corner_y, ff_other = tie(from_x, from_y, corner_x, corner_y, ff_other)
    grad_b = (keep_b, from_x, from_y, *pass_on(keep_b, corner_x, corner_y))
    grad_ff = ff_mine.astype(jnp.float32) + swap(ff_other, "c").astype(jnp.float32)
    grad_ff = grad_ff.astype(jnp.bfloat16).reshape(nz * width, 3 * LN)
    grad_ff, *corner = tie(grad_ff, *grad_b[3:])
    grad_b = (*grad_b[:3], *corner)
    grad_ff = lax.psum_scatter(grad_ff, "z", scatter_dimension=0, tiled=True)
    grad_mid, grad_low, grad_o, gain_grad_mid = mid_back_call(
        grad_b, middle, cot_low, gain_mid, w_o, rows, nz
    )
    grad_o = all_to_all(grad_o, ("x", "c", "z"))
    hidden, hidden_last, _ = tie(hidden, hidden_last, grad_low)
    keep_out, *out_sides = down_call(hidden, hidden_last, w_mine, w_other)
    out_sides = swap(out_sides[0], "x"), swap(out_sides[1], "y")
    wo_mine, wo_other = row_grads_call(at, grad_low, attended_low[None], BY_SIDES, "out_grads", 3)
    wo_sum = (wo_mine.astype(jnp.float32) + swap(wo_other, "c").astype(jnp.float32)).reshape(width // 2, -1)
    wo_keep, wo_send = wo_sum[: width // 4], wo_sum[width // 4 :].astype(jnp.bfloat16)
    wo_got = swap(wo_send, "x")

    grad_qkv = attn_bwd(first, qkv, grad_o, attended_float, log_total, row_cos, row_sin)
    grad_qkv, wo_got, *out_sides = tie(grad_qkv, wo_got, *out_sides)
    out = middle + total_square(reduce_square_rest(keep_out, *out_sides))
    wo_sum = wo_keep + wo_got.astype(jnp.float32)
    wo_got = swap(wo_sum[width // 8 :].astype(jnp.bfloat16), "y")
    grad_wo = (wo_sum[: width // 8] + wo_got.astype(jnp.float32)).astype(jnp.bfloat16)
    grad_qkv = all_to_all(grad_qkv.reshape(-1, chunk, 3 * LN), ("x", "c"))
    grad_qkv, grad_ff = tie(grad_qkv, grad_ff)
    grad_ff = all_to_all(grad_ff.reshape(plane, width // plane, 3 * LN), ("y", "x", "c"))
    grad_qkv = grad_qkv.reshape(kv_local, rows, chunk, 3 * LN)
    part, gain_grad_in = da_call(nz, group, grad_qkv, w_qkv, grad_wo, rows)
    part = lax.psum_scatter(part, "z", scatter_dimension=0, tiled=True).astype(jnp.float32)
    grad_a, grad_wo = part[:count], part[count:]
    grad_wo = jnp.concatenate([grad_wo[:, n * 3 * LN : (n + 1) * 3 * LN] for n in range(nz)], axis=0)
    grad_wqkv = row_grads_call(
        at,
        normed.reshape(rows * chunk, width),
        grad_qkv.reshape(kv_local, rows * chunk, 3 * LN),
        ORDER,
        "qkv_grads",
        5,
    )
    *grad_wqkv, grad_ff = tie(*grad_wqkv, grad_ff)
    grad_wqkv = reduce_square(*core_sum(grad_wqkv[0], swap(grad_wqkv[1], "c")))
    gain_grads = jnp.concatenate(
        [gain_grad_in.reshape(devices, share), gain_grad_mid.reshape(devices, share)], axis=1
    )
    gain_grads = jnp.pad(gain_grads, ((0, 0), (0, LN - 2 * share)))
    *grad_wqkv, gain_grads = tie(*grad_wqkv, gain_grads)
    grad_wqkv = total_square(grad_wqkv)
    gain_grads = jnp.sum(all_to_all(gain_grads, EVERY), axis=0, keepdims=True)

    stream = own.astype(jnp.float32)
    factor = lax.rsqrt(jnp.mean(stream * stream, axis=-1, keepdims=True) + EPS)
    back_in, _ = norm_back(stream, factor, gain_in, grad_a)
    grad_tokens = grad_mid + back_in
    grad_wqkv = grad_wqkv.reshape(-1, kv_local, 4 * HD)
    flat = lambda g: g.reshape(1, g.shape[0], -1)
    grad_gate, grad_up, grad_down = uncut_call(grad_ff)
    return (
        out.reshape(tokens.shape),
        grad_tokens.reshape(tokens.shape),
        gain_grads[:, :share],
        flat(grad_wqkv[:, :, : 2 * HD]),
        flat(grad_wqkv[:, :, 2 * HD : 3 * HD]),
        flat(grad_wqkv[:, :, 3 * HD :]),
        grad_wo.T[None],
        gain_grads[:, share : 2 * share],
        grad_gate[None],
        grad_up[None],
        grad_down[None],
    )


def fast_solution(mesh, cores):
    batch, seq, kv = mesh.devices.shape
    fine = Mesh(mesh.devices.reshape(batch, seq // cores, cores, kv), EVERY)
    sizes = dict(fine.shape)
    row_spec = P("y", ("x", "c", "z"), None)
    seq_spec = P("y", ("x", "c"))
    gain_spec = P(None, EVERY)
    in_w = P(None, ("y", "x", "c"), "z")
    out_w = P(None, "z", ("y", "x", "c"))
    in_specs = (row_spec, row_spec, seq_spec, seq_spec, gain_spec, in_w, in_w, in_w, out_w, gain_spec, in_w, in_w, out_w)
    out_specs = (row_spec, row_spec, gain_spec, in_w, in_w, in_w, out_w, gain_spec, in_w, in_w, out_w)
    return jax.shard_map(
        partial(fast_local, sizes), mesh=fine, in_specs=in_specs, out_specs=out_specs, check_vma=False
    )


def solution(mesh):
    batch, seq, kv = (mesh.shape[name] for name in ("batch", "seq", "kv"))
    general = general_solution(mesh)
    if (batch, seq) != (2, 4):
        return general
    fast = fast_solution(mesh, 2)

    def run(*args):
        rows, length, width = args[0].shape
        kv_heads, q_heads = args[6].shape[2] // HD, args[5].shape[2] // HD
        fits = (
            rows == 2 * batch
            and kv_heads == 2 * kv
            and q_heads == 2 * kv_heads
            and length == 128 * seq * kv
            and length % (4 * BQ) == 0
            and width % LN == 0
            and 2 * width // (batch * seq * kv) <= LN
            and args[10].shape[2] == LN * batch * seq * kv
        )
        return (fast if fits else general)(*args)

    return run
```

```python
import functools
import math
from functools import partial

import jax
import jax.numpy as jnp
from jax import lax
from jax.experimental import pallas as pl
from jax.experimental.pallas import tpu as pltpu
from jax.sharding import Mesh
from jax.sharding import PartitionSpec as P

HD = 96
LAYERS = 1


EPS = 1e-05
THETA = 100000.0
BIG_NEG = -1e30


def rotary(positions_row):
    half_width = HD // 2
    frequency = THETA ** (-(2.0 * jnp.arange(half_width, dtype=jnp.float32)) / HD)
    angles = positions_row.astype(jnp.float32)[:, None] * frequency[None, :]
    cosine = jnp.concatenate([jnp.cos(angles), jnp.cos(angles)], axis=1)
    sine_table = jnp.concatenate([jnp.sin(angles), jnp.sin(angles)], axis=1)
    return (cosine, sine_table)


def rotate(head_vals, cosine, sine_table):
    half_width = head_vals.shape[-1] // 2
    swapped = jnp.concatenate([-head_vals[..., half_width:], head_vals[..., :half_width]], axis=-1)
    return head_vals * cosine[:, None, :] + swapped * sine_table[:, None, :]


def rms_norm(stream, gain):
    factor = lax.rsqrt(jnp.mean(stream * stream, axis=-1, keepdims=True) + EPS)
    return (stream * factor * gain, factor)


def norm_back(stream, factor, gain, upstream):
    scaled_grad = upstream * gain
    inner_mean = jnp.mean(scaled_grad * stream, axis=-1, keepdims=True)
    grad_stream = factor * scaled_grad - stream * factor**3 * inner_mean
    return (grad_stream, jnp.sum(upstream * stream * factor, axis=0))


def key_width(key_count):
    return math.gcd(key_count, 1024)


def contract(left_side, right_side, left_dim, right_dim):
    return lax.dot_general(
        left_side,
        right_side,
        (((left_dim,), (right_dim,)), ((), ())),
        preferred_element_type=jnp.float32,
    )


def spread(shard_rows):
    return lax.all_gather(shard_rows, "kv", axis=0, tiled=True)


def token_sum(pairs):
    summed = None
    for left_part, right_part, right_dim in pairs:
        product = contract(left_part, right_part, 1, right_dim)
        summed = product if summed is None else summed + product
    return lax.psum_scatter(
        summed.astype(jnp.bfloat16), "kv", scatter_dimension=0, tiled=True
    ).astype(jnp.float32)


def split_block(kv_both, seg_keys, offset, step_width, kv_local, head_size):
    kv_block = lax.dynamic_slice_in_dim(kv_both, offset, step_width, 0)
    key_block = kv_block[:, : kv_local * head_size].reshape(step_width, kv_local, head_size)
    value_block = kv_block[:, kv_local * head_size :].reshape(step_width, kv_local, head_size)
    seg_block = lax.dynamic_slice_in_dim(seg_keys, offset, step_width, 0)
    return (key_block, value_block, seg_block)


def forward_row(queries, seg_query, fold_state, kv_both, seg_keys, first_query, key_start):
    key_count = kv_both.shape[0]
    step_width = key_width(key_count)
    query_count, kv_local, group_size, head_size = queries.shape
    query_index = first_query + jnp.arange(query_count, dtype=jnp.int32)
    score_scale = head_size ** (-0.5)

    def forward_one_step(step_index, inner_state):
        running_max, weight_total, value_total = inner_state
        offset = step_index * step_width
        key_block, value_block, seg_block = split_block(
            kv_both, seg_keys, offset, step_width, kv_local, head_size
        )
        key_index = offset + jnp.arange(step_width, dtype=jnp.int32)
        allowed = (seg_query[:, None] == seg_block[None, :]) & (
            key_index[None, :] <= query_index[:, None]
        )
        scores = (
            jnp.einsum("qkgd,pkd->kgqp", queries, key_block, preferred_element_type=jnp.float32)
            * score_scale
        )
        scores = jnp.where(allowed, scores, BIG_NEG)
        new_max = jnp.maximum(running_max, jnp.max(scores, axis=-1))
        weights = jnp.where(allowed, jnp.exp(scores - new_max[..., None]), 0.0)
        rescale = jnp.exp(running_max - new_max)
        weight_total = rescale * weight_total + jnp.sum(weights, axis=-1)
        update = jnp.einsum(
            "kgqp,pkd->qkgd",
            weights.astype(jnp.bfloat16),
            value_block,
            preferred_element_type=jnp.float32,
        )
        value_total = jnp.transpose(rescale, (2, 0, 1))[..., None] * value_total + update
        return (new_max, weight_total, value_total)

    return lax.fori_loop(0, key_count // step_width, forward_one_step, fold_state)


def forward_fold(queries, seg_query, first_query, fold_state, pieces, key_start):
    kv_both, seg_keys = pieces
    row_fn = partial(forward_row, first_query=first_query, key_start=key_start)
    return jax.vmap(row_fn, in_axes=(0, 0, 0, 1, 1))(
        queries, seg_query, fold_state, kv_both, seg_keys
    )


def backward_row(
    queries,
    grad_attn,
    log_total,
    row_delta,
    seg_query,
    fold_state,
    kv_both,
    seg_keys,
    first_query,
    key_start,
):
    key_count = kv_both.shape[0]
    step_width = key_width(key_count)
    query_count, kv_local, group_size, head_size = queries.shape
    query_index = first_query + jnp.arange(query_count, dtype=jnp.int32)
    score_scale = head_size ** (-0.5)

    def backward_one_step(step_index, inner_state):
        grad_queries, grad_buffer = inner_state
        offset = step_index * step_width
        key_block, value_block, seg_block = split_block(
            kv_both, seg_keys, offset, step_width, kv_local, head_size
        )
        key_index = offset + jnp.arange(step_width, dtype=jnp.int32)
        allowed = (seg_query[:, None] == seg_block[None, :]) & (
            key_index[None, :] <= query_index[:, None]
        )
        scores = (
            jnp.einsum("qkgd,pkd->kgqp", queries, key_block, preferred_element_type=jnp.float32)
            * score_scale
        )
        probs_block = jnp.where(allowed, jnp.exp(scores - log_total[..., None]), 0.0)
        grad_probs = jnp.einsum(
            "qkgd,pkd->kgqp", grad_attn, value_block, preferred_element_type=jnp.float32
        )
        grad_scores = (probs_block * (grad_probs - row_delta[..., None])).astype(jnp.bfloat16)
        grad_queries = (
            grad_queries
            + jnp.einsum(
                "kgqp,pkd->qkgd", grad_scores, key_block, preferred_element_type=jnp.float32
            )
            * score_scale
        )
        grad_keys = (
            jnp.einsum("kgqp,qkgd->pkd", grad_scores, queries, preferred_element_type=jnp.float32)
            * score_scale
        )
        grad_values = jnp.einsum(
            "kgqp,qkgd->pkd",
            probs_block.astype(jnp.bfloat16),
            grad_attn,
            preferred_element_type=jnp.float32,
        )
        joined = jnp.concatenate(
            [grad_keys.reshape(step_width, -1), grad_values.reshape(step_width, -1)], axis=1
        )
        grad_buffer = lax.dynamic_update_slice_in_dim(grad_buffer, joined, offset, 0)
        return (grad_queries, grad_buffer)

    return lax.fori_loop(0, key_count // step_width, backward_one_step, fold_state)


def backward_fold(
    queries, grad_attn, log_total, row_delta, seg_query, first_query, fold_state, pieces, key_start
):
    kv_both, seg_keys = pieces
    row_fn = partial(backward_row, first_query=first_query, key_start=key_start)
    return jax.vmap(row_fn, in_axes=(0, 0, 0, 0, 0, 0, 1, 1))(
        queries, grad_attn, log_total, row_delta, seg_query, fold_state, kv_both, seg_keys
    )


def layer_forward(stream, gain_pair, matrices, seg_info, tables):
    gain_in, gain_mid = gain_pair
    w_query, w_key, w_value, w_out, w_gate, w_up, w_down = matrices
    seg_query, seg_keys = seg_info
    cosine, sine_table = tables
    row_count = seg_query.shape[0]
    kv_local = w_key.shape[1] // HD
    head_local = w_query.shape[1] // HD
    group_size = head_local // kv_local
    normed_a, factor_a = rms_norm(stream, gain_in)
    spread_a = spread(normed_a.astype(jnp.bfloat16))
    flat_count = spread_a.shape[0]
    token_count = flat_count // row_count
    raw_queries = jnp.dot(spread_a, w_query, preferred_element_type=jnp.float32).reshape(
        flat_count, head_local, HD
    )
    queries = (
        rotate(raw_queries, cosine, sine_table)
        .astype(jnp.bfloat16)
        .reshape(token_count, row_count, kv_local, group_size, HD)
    )
    queries = jnp.transpose(queries, (1, 0, 2, 3, 4))
    raw_keys = jnp.dot(spread_a, w_key, preferred_element_type=jnp.float32).reshape(
        flat_count, kv_local, HD
    )
    keys_low = (
        rotate(raw_keys, cosine, sine_table).astype(jnp.bfloat16).reshape(flat_count, kv_local * HD)
    )
    values_low = jnp.dot(spread_a, w_value, preferred_element_type=jnp.float32).astype(jnp.bfloat16)
    kv_both = jnp.concatenate([keys_low, values_low], axis=1).reshape(
        token_count, row_count, 2 * kv_local * HD
    )
    first_query = lax.axis_index("seq") * token_count
    start_state = (
        jnp.full((row_count, kv_local, group_size, token_count), BIG_NEG, jnp.float32),
        jnp.zeros((row_count, kv_local, group_size, token_count), jnp.float32),
        jnp.zeros((row_count, token_count, kv_local, group_size, HD), jnp.float32),
    )
    running_max, weight_total, value_total = forward_fold(
        queries,
        seg_query,
        first_query,
        start_state,
        (
            lax.all_gather(kv_both, "seq", axis=0, tiled=True),
            lax.all_gather(seg_keys, "seq", axis=0, tiled=True),
        ),
        jnp.int32(0),
    )
    attn_float = value_total / jnp.transpose(weight_total, (0, 3, 1, 2))[..., None]
    log_total = running_max + jnp.log(weight_total)
    attn_low = (
        jnp.transpose(attn_float, (1, 0, 2, 3, 4))
        .reshape(flat_count, head_local * HD)
        .astype(jnp.bfloat16)
    )
    stream_mid = stream + token_sum(((attn_low, w_out, 0),))
    normed_b, factor_b = rms_norm(stream_mid, gain_mid)
    spread_b = spread(normed_b.astype(jnp.bfloat16))
    gate_val = jnp.dot(spread_b, w_gate, preferred_element_type=jnp.float32)
    up_val = jnp.dot(spread_b, w_up, preferred_element_type=jnp.float32)
    hidden = (jax.nn.silu(gate_val) * up_val).astype(jnp.bfloat16)
    stream_out = stream_mid + token_sum(((hidden, w_down, 0),))
    saved_state = (
        stream,
        factor_a,
        spread_a,
        queries,
        kv_both,
        attn_float,
        attn_low,
        log_total,
        stream_mid,
        factor_b,
        spread_b,
        gate_val,
        up_val,
        hidden,
    )
    return (stream_out, saved_state)


def layer_backward(saved_state, grad_stream, gain_pair, matrices, seg_info, tables):
    (
        stream,
        factor_a,
        spread_a,
        queries,
        kv_both,
        attn_float,
        attn_low,
        log_total,
        stream_mid,
        factor_b,
        spread_b,
        gate_val,
        up_val,
        hidden,
    ) = saved_state
    gain_in, gain_mid = gain_pair
    w_query, w_key, w_value, w_out, w_gate, w_up, w_down = matrices
    seg_query, seg_keys = seg_info
    cosine, sine_table = tables
    row_count, token_count, kv_local, group_size, head_size = queries.shape
    head_local = kv_local * group_size
    flat_count = row_count * token_count
    grad_low = spread(grad_stream.astype(jnp.bfloat16))
    grad_down_w = contract(hidden, grad_low, 0, 0)
    grad_hidden = contract(grad_low, w_down, 1, 1)
    sigmoid_gate = jax.nn.sigmoid(gate_val)
    silu_gate = gate_val * sigmoid_gate
    grad_gate_low = (
        grad_hidden * up_val * sigmoid_gate * (1.0 + gate_val * (1.0 - sigmoid_gate))
    ).astype(jnp.bfloat16)
    grad_up_low = (grad_hidden * silu_gate).astype(jnp.bfloat16)
    grad_gate_w = contract(spread_b, grad_gate_low, 0, 0)
    grad_up_w = contract(spread_b, grad_up_low, 0, 0)
    grad_normed_b = token_sum(((grad_gate_low, w_gate, 1), (grad_up_low, w_up, 1)))
    back_mid, grad_gain_mid = norm_back(stream_mid, factor_b, gain_mid, grad_normed_b)
    grad_mid = grad_stream + back_mid
    grad_attn_full = spread(grad_mid.astype(jnp.bfloat16))
    grad_out_w = contract(attn_low, grad_attn_full, 0, 0)
    grad_attn = (
        contract(grad_attn_full, w_out, 1, 1)
        .astype(jnp.bfloat16)
        .reshape(token_count, row_count, kv_local, group_size, head_size)
    )
    grad_attn = jnp.transpose(grad_attn, (1, 0, 2, 3, 4))
    row_delta = jnp.transpose(jnp.sum(grad_attn * attn_float, axis=-1), (0, 2, 3, 1))
    first_query = lax.axis_index("seq") * token_count
    row_length = token_count * lax.axis_size("seq")
    start_state = (
        jnp.zeros((row_count, token_count, kv_local, group_size, head_size), jnp.float32),
        jnp.zeros((row_count, row_length, 2 * kv_local * head_size), jnp.float32),
    )
    grad_queries, grad_buffer = backward_fold(
        queries,
        grad_attn,
        log_total,
        row_delta,
        seg_query,
        first_query,
        start_state,
        (
            lax.all_gather(kv_both, "seq", axis=0, tiled=True),
            lax.all_gather(seg_keys, "seq", axis=0, tiled=True),
        ),
        jnp.int32(0),
    )
    grad_kv = lax.psum_scatter(
        grad_buffer.astype(jnp.bfloat16), "seq", scatter_dimension=1, tiled=True
    ).astype(jnp.float32)
    grad_kv = jnp.transpose(grad_kv, (1, 0, 2)).reshape(flat_count, 2 * kv_local * head_size)
    grad_queries = jnp.transpose(grad_queries, (1, 0, 2, 3, 4)).reshape(
        flat_count, head_local, head_size
    )
    grad_q_low = (
        rotate(grad_queries, cosine, -sine_table)
        .astype(jnp.bfloat16)
        .reshape(flat_count, head_local * head_size)
    )
    grad_k_low = (
        rotate(
            grad_kv[:, : kv_local * head_size].reshape(flat_count, kv_local, head_size),
            cosine,
            -sine_table,
        )
        .astype(jnp.bfloat16)
        .reshape(flat_count, kv_local * head_size)
    )
    grad_v_low = grad_kv[:, kv_local * head_size :].astype(jnp.bfloat16)
    grad_query_w = contract(spread_a, grad_q_low, 0, 0)
    grad_key_w = contract(spread_a, grad_k_low, 0, 0)
    grad_value_w = contract(spread_a, grad_v_low, 0, 0)
    grad_normed_a = token_sum(
        ((grad_q_low, w_query, 1), (grad_k_low, w_key, 1), (grad_v_low, w_value, 1))
    )
    back_in, grad_gain_in = norm_back(stream, factor_a, gain_in, grad_normed_a)
    grad_input = grad_mid + back_in
    weight_grads = (
        lax.psum_scatter(
            grad_query_w.astype(jnp.bfloat16), ("batch", "seq"), scatter_dimension=0, tiled=True
        ).astype(jnp.float32),
        lax.psum_scatter(
            grad_key_w.astype(jnp.bfloat16), ("batch", "seq"), scatter_dimension=0, tiled=True
        ).astype(jnp.float32),
        lax.psum_scatter(
            grad_value_w.astype(jnp.bfloat16), ("batch", "seq"), scatter_dimension=0, tiled=True
        ).astype(jnp.float32),
        lax.psum_scatter(
            grad_out_w.astype(jnp.bfloat16), ("batch", "seq"), scatter_dimension=1, tiled=True
        ).astype(jnp.float32),
        lax.psum_scatter(
            grad_gate_w.astype(jnp.bfloat16), ("batch", "seq"), scatter_dimension=0, tiled=True
        ).astype(jnp.float32),
        lax.psum_scatter(
            grad_up_w.astype(jnp.bfloat16), ("batch", "seq"), scatter_dimension=0, tiled=True
        ).astype(jnp.float32),
        lax.psum_scatter(
            grad_down_w.astype(jnp.bfloat16), ("batch", "seq"), scatter_dimension=1, tiled=True
        ).astype(jnp.float32),
    )
    return (grad_input, weight_grads, grad_gain_in, grad_gain_mid)


def to_flat(shard_rows):
    row_count, token_part, width = shard_rows.shape
    return jnp.transpose(shard_rows.astype(jnp.float32), (1, 0, 2)).reshape(
        token_part * row_count, width
    )


def from_flat(flat_rows, row_count):
    token_part = flat_rows.shape[0] // row_count
    return jnp.transpose(flat_rows.reshape(token_part, row_count, flat_rows.shape[1]), (1, 0, 2))


def general_local(
    tokens,
    cotangent,
    segments,
    positions,
    norm_in,
    w_query,
    w_key,
    w_value,
    w_out,
    norm_mid,
    w_gate,
    w_up,
    w_down,
):
    gains_in, gains_mid = (
        lax.all_gather(norm_in, ("batch", "seq", "kv"), axis=1, tiled=True),
        lax.all_gather(norm_mid, ("batch", "seq", "kv"), axis=1, tiled=True),
    )
    row_count = tokens.shape[0]
    seg_info = (segments, jnp.transpose(segments, (1, 0)))
    tables = rotary(jnp.transpose(positions, (1, 0)).reshape(-1))

    def fetch_layer(layer_index):
        return (
            lax.all_gather(w_query[layer_index], ("batch", "seq"), axis=0, tiled=True),
            lax.all_gather(w_key[layer_index], ("batch", "seq"), axis=0, tiled=True),
            lax.all_gather(w_value[layer_index], ("batch", "seq"), axis=0, tiled=True),
            lax.all_gather(w_out[layer_index], ("batch", "seq"), axis=1, tiled=True),
            lax.all_gather(w_gate[layer_index], ("batch", "seq"), axis=0, tiled=True),
            lax.all_gather(w_up[layer_index], ("batch", "seq"), axis=0, tiled=True),
            lax.all_gather(w_down[layer_index], ("batch", "seq"), axis=1, tiled=True),
        )

    stream = to_flat(tokens)
    fetched = []
    states = []
    layer_index = 0
    matrices = fetch_layer(layer_index)
    layer_inputs = [stream]
    stream, saved_state = layer_forward(
        stream, (gains_in[layer_index], gains_mid[layer_index]), matrices, seg_info, tables
    )
    fetched.append(matrices)
    states.append(saved_state)
    grad_stream = to_flat(cotangent)
    grads_in = []
    grads_mid = []
    weight_lists = []
    for layer_index in reversed(range(LAYERS)):
        gain_pair = (gains_in[layer_index], gains_mid[layer_index])
        matrices = fetch_layer(layer_index)
        saved_state = layer_forward(
            layer_inputs[layer_index], gain_pair, matrices, seg_info, tables
        )[1]
        grad_stream, weight_grads, grad_gain_in, grad_gain_mid = layer_backward(
            saved_state, grad_stream, gain_pair, matrices, seg_info, tables
        )
        grads_in.insert(0, grad_gain_in)
        grads_mid.insert(0, grad_gain_mid)
        weight_lists.insert(0, weight_grads)
    gain_grads_in, gain_grads_mid = (
        lax.psum_scatter(
            jnp.stack(grads_in), ("batch", "seq", "kv"), scatter_dimension=1, tiled=True
        ),
        lax.psum_scatter(
            jnp.stack(grads_mid), ("batch", "seq", "kv"), scatter_dimension=1, tiled=True
        ),
    )
    stacked_grads = [
        jnp.stack([grad_set[member] for grad_set in weight_lists]) for member in range(7)
    ]
    return (
        from_flat(stream, row_count),
        from_flat(grad_stream, row_count),
        gain_grads_in,
        stacked_grads[0],
        stacked_grads[1],
        stacked_grads[2],
        stacked_grads[3],
        gain_grads_mid,
        stacked_grads[4],
        stacked_grads[5],
        stacked_grads[6],
    )


def general_solution(mesh):
    in_specs = (
        P("batch", ("seq", "kv"), None),
        P("batch", ("seq", "kv"), None),
        P("batch", "seq"),
        P("batch", "seq"),
        P(None, ("batch", "seq", "kv")),
        P(None, ("batch", "seq"), "kv"),
        P(None, ("batch", "seq"), "kv"),
        P(None, ("batch", "seq"), "kv"),
        P(None, "kv", ("batch", "seq")),
        P(None, ("batch", "seq", "kv")),
        P(None, ("batch", "seq"), "kv"),
        P(None, ("batch", "seq"), "kv"),
        P(None, "kv", ("batch", "seq")),
    )
    out_specs = (
        P("batch", ("seq", "kv"), None),
        P("batch", ("seq", "kv"), None),
        P(None, ("batch", "seq", "kv")),
        P(None, ("batch", "seq"), "kv"),
        P(None, ("batch", "seq"), "kv"),
        P(None, ("batch", "seq"), "kv"),
        P(None, "kv", ("batch", "seq")),
        P(None, ("batch", "seq", "kv")),
        P(None, ("batch", "seq"), "kv"),
        P(None, ("batch", "seq"), "kv"),
        P(None, "kv", ("batch", "seq")),
    )
    return jax.shard_map(general_local, mesh=mesh, in_specs=in_specs, out_specs=out_specs, check_vma=False)


LN = 128
NEG=-1e30
C2 = (96 ** -0.5) * 1.4426950408889634

def cost(microseconds):
    return pl.CostEstimate(
        flops=microseconds * 10**9, bytes_accessed=microseconds * 3 * 10**6, transcendentals=0
    )


def lane_iota(rows):
    return lax.broadcasted_iota(jnp.int32, (rows, LN), 1)

def unpack4(t0, t1, t2):
    lane = lane_iota(t0.shape[0])
    live = lane < HD
    zero = jnp.zeros_like(t0)
    a = t0
    b = pltpu.roll(jnp.where(lane >= 96, t0, t1), 32, 1)
    c = pltpu.roll(jnp.where(lane >= 64, t1, t2), 64, 1)
    d = pltpu.roll(t2, 96, 1)
    return tuple(jnp.where(live, v, zero) for v in (a, b, c, d))

def pack4(a, b, c, d):
    lane = lane_iota(a.shape[0])
    b, c, d = pltpu.roll(b, 96, 1), pltpu.roll(c, 64, 1), pltpu.roll(d, 32, 1)
    return (jnp.where(lane < 96, a, b), jnp.where(lane < 64, b, c), jnp.where(lane < 32, c, d))

def split3(x):
    x = x.astype(jnp.float32)
    return x[:, :LN], x[:, LN:2*LN], x[:, 2*LN:]

def doc_low(index, first, length):
    second = first + 3 * length // 4
    return jnp.where(index >= second, second, jnp.where(index >= first, first, 0))

BQ = 256
BK = 512

def dotf(a, b, dims):
    return lax.dot_general(a, b, (dims, ((), ())), preferred_element_type=jnp.float32)

def attn_fwd_kernel(length, first_ref, x_ref, o_ref, of_ref, lse_ref, q_s, k_s, v_s, s_s):
    i = pl.program_id(0)
    blocks = length // BQ
    first = first_ref[0]

    @pl.when(i == 0)
    def _():
        def body(j, carry):
            rows = pl.ds(pl.multiple_of(j * BQ, BQ), BQ)
            q0, q1, k, v = unpack4(*split3(x_ref[rows, :]))
            q_s[j, :BQ, :] = q0.astype(jnp.bfloat16)
            q_s[j, BQ:, :] = q1.astype(jnp.bfloat16)
            k_s[rows, :] = k.astype(jnp.bfloat16)
            v_s[rows, :] = v.astype(jnp.bfloat16)
            return carry

        lax.fori_loop(0, blocks, body, 0)

    q = q_s[i]
    late = (3 * length // 4 + length // 8) // BQ
    start = jnp.where(i >= late, 3 * length // 4 // BK, 0)
    stop = i * BQ // BK + 1
    q_index = i * BQ + lax.broadcasted_iota(jnp.int32, (BQ, 1), 0)
    low = doc_low(q_index, first, length)

    def fold(v, op):
        out = v[:, :LN]
        for n in range(1, BK // LN):
            out = op(out, v[:, n * LN : (n + 1) * LN])
        return out

    def score(j, top):
        s = dotf(q, k_s[pl.ds(pl.multiple_of(j * BK, BK), BK), :], ((1,), (1,)))
        key = j * BK + lax.broadcasted_iota(jnp.int32, (1, BK), 1)
        ok = (key <= q_index) & (key >= low)
        s = jnp.concatenate([jnp.where(ok, s[:BQ], NEG), jnp.where(ok, s[BQ:], NEG)], axis=0)
        s_s[j] = s
        return jnp.maximum(top, fold(s, jnp.maximum))

    top = lax.fori_loop(start, stop, score, jnp.full((2 * BQ, LN), NEG, jnp.float32))
    m = jnp.max(top, axis=1, keepdims=True) * C2

    def add(j, state):
        p = jnp.exp2(s_s[j] * C2 - m)
        keys = pl.ds(pl.multiple_of(j * BK, BK), BK)
        of_ref[0] += dotf(p.astype(jnp.bfloat16), v_s[keys, :], ((1,), (0,)))
        return state + fold(p, jnp.add)

    zero = jnp.zeros((2 * BQ, LN), jnp.float32)
    of_ref[0] = zero
    total = lax.fori_loop(start, stop, add, zero)
    total = jnp.sum(total, axis=1, keepdims=True)
    out = of_ref[0] / total
    lse = jnp.broadcast_to(m + jnp.log2(total), (2 * BQ, LN))
    lse_ref[0] = jnp.transpose(lse, (1, 0))[:8, :]
    of_ref[0] = out
    for d in range(2):
        at = d * 128
        parts = [out[at + n // 2 * 64 + n % 2 * BQ : at + n // 2 * 64 + n % 2 * BQ + 64] for n in range(4)]
        for n, t in enumerate(pack4(*parts)):
            o_ref[d, :, n * LN : (n + 1) * LN] = t.astype(jnp.bfloat16)


def attn_fwd(first, x):
    length = x.shape[0]
    blocks = length // BQ
    return pl.pallas_call(
        functools.partial(attn_fwd_kernel, length),
        grid=(blocks,),
        in_specs=[pl.BlockSpec(memory_space=pltpu.SMEM),
                  pl.BlockSpec((length, 3*LN), lambda i: (0, 0))],
        out_specs=[pl.BlockSpec((2, 64, 3*LN), lambda i: (i, 0, 0)),
                   pl.BlockSpec((1, 2*BQ, LN), lambda i: (i, 0, 0)),
                   pl.BlockSpec((1, 8, 2*BQ), lambda i: (i, 0, 0))],
        out_shape=[jax.ShapeDtypeStruct((length//128, 64, 3*LN), jnp.bfloat16),
                   jax.ShapeDtypeStruct((blocks, 2*BQ, LN), jnp.float32),
                   jax.ShapeDtypeStruct((blocks, 8, 2*BQ), jnp.float32)],
        scratch_shapes=[pltpu.VMEM((blocks, 2*BQ, LN), jnp.bfloat16),
                        pltpu.VMEM((length, LN), jnp.bfloat16),
                        pltpu.VMEM((length, LN), jnp.bfloat16),
                        pltpu.VMEM((length // BK, 2*BQ, BK), jnp.float32)],
        compiler_params=pltpu.CompilerParams(vmem_limit_bytes=48 << 20),
        name="attend",
        cost_estimate=cost(22),
    )(first, x)

def attn_bwd_kernel(length, first_ref, x_ref, do_ref, of_ref, lse_ref, cos_ref, sin_ref, out_ref,
                    q_s, k_s, v_s, do_s, dl_s, dq_s, dk_s, dv_s):
    j = pl.program_id(0)
    blocks = length // BQ
    first = first_ref[0]
    @pl.when(j == 0)
    def _():
        def body(b, carry):
            rows = pl.ds(pl.multiple_of(b * BQ, BQ), BQ)
            q0, q1, k, v = unpack4(*split3(x_ref[rows, :]))
            q_s[b, :BQ, :] = q0.astype(jnp.bfloat16)
            q_s[b, BQ:, :] = q1.astype(jnp.bfloat16)
            k_s[b] = k.astype(jnp.bfloat16)
            v_s[b] = v.astype(jnp.bfloat16)
            for d in range(2):
                parts = unpack4(*split3(do_ref[2*b + d]))
                for n, part in enumerate(parts):
                    at = (n % 2) * BQ + d*128 + (n // 2) * 64
                    do_s[b, at:at+64, :] = part.astype(jnp.bfloat16)
            prod = do_s[b].astype(jnp.float32) * of_ref[b]
            delta = jnp.broadcast_to(jnp.sum(prod, axis=1, keepdims=True), (2*BQ, LN))
            dl_s[b] = jnp.transpose(delta, (1, 0))[:8, :]
            dq_s[b] = jnp.zeros((2*BQ, LN), jnp.float32)
            return carry
        lax.fori_loop(0, blocks, body, 0)
    late = (3 * length // 4 + length // 8) // BQ
    third = 3 * length // 4 // BQ
    stop = jnp.where(j >= third, blocks, late)
    k = k_s[j]
    v = v_s[j]
    dk_s[j] = jnp.zeros((BQ, LN), jnp.float32)
    dv_s[j] = jnp.zeros((BQ, LN), jnp.float32)
    key = j * BQ + lax.broadcasted_iota(jnp.int32, (BQ, 1), 0)

    def steps(places):
        dk, dv = [], []
        for i in places:
            q, do = q_s[i], do_s[i]
            s = dotf(k, q, ((1,), (1,)))
            dp = dotf(v, do, ((1,), (1,)))
            q_index = i * BQ + lax.broadcasted_iota(jnp.int32, (1, BQ), 1)
            ok = (key <= q_index) & (key >= doc_low(q_index, first, length))
            p = jnp.exp2(s * C2 - lse_ref[i, 0:1, :])
            p = jnp.concatenate([jnp.where(ok, p[:, :BQ], 0.0), jnp.where(ok, p[:, BQ:], 0.0)], axis=1)
            ds = (p * (dp - dl_s[i, 0:1, :])).astype(jnp.bfloat16)
            dv.append(dotf(p.astype(jnp.bfloat16), do, ((1,), (0,))))
            dk.append(dotf(ds, q, ((1,), (0,))))
            dq_s[i] += dotf(ds, k, ((0,), (0,)))
        dv_s[j] += functools.reduce(jnp.add, dv)
        dk_s[j] += functools.reduce(jnp.add, dk)

    pairs = (stop - j) // 2

    def body(n, carry):
        steps((j + 2 * n, j + 2 * n + 1))
        return carry

    lax.fori_loop(0, pairs, body, 0)

    @pl.when(j + 2 * pairs < stop)
    def _():
        steps((stop - 1,))

    @pl.when(j == blocks - 1)
    def _():
        scale = HD ** -0.5
        lower = lane_iota(BQ) < HD // 2

        def turn_back(piece, cosine, sine):
            swapped = jnp.where(lower, -pltpu.roll(piece, LN - HD // 2, 1), pltpu.roll(piece, HD // 2, 1))
            return (piece * cosine - swapped * sine) * scale

        def body(b, carry):
            rows = pl.ds(pl.multiple_of(b * BQ, BQ), BQ)
            cosine, sine = cos_ref[rows, :], sin_ref[rows, :]
            pieces = [turn_back(v, cosine, sine) for v in (dq_s[b, :BQ, :], dq_s[b, BQ:, :], dk_s[b])]
            for n, tile in enumerate(pack4(*pieces, dv_s[b])):
                out_ref[rows, n * LN : (n + 1) * LN] = tile.astype(jnp.bfloat16)
            return carry

        lax.fori_loop(0, blocks, body, 0)


def attn_bwd(first, x, do, of, lse, cos, sin):
    length = x.shape[0]
    blocks = length // BQ
    whole = lambda a: pl.BlockSpec(a.shape, lambda j: (0,) * a.ndim)
    return pl.pallas_call(
        functools.partial(attn_bwd_kernel, length),
        grid=(blocks,),
        in_specs=[pl.BlockSpec(memory_space=pltpu.SMEM)] + [whole(a) for a in (x, do, of, lse, cos, sin)],
        out_specs=pl.BlockSpec((length, 3*LN), lambda j: (0, 0)),
        out_shape=jax.ShapeDtypeStruct((length, 3*LN), jnp.bfloat16),
        scratch_shapes=[pltpu.VMEM((blocks, 2*BQ, LN), jnp.bfloat16),
                        pltpu.VMEM((blocks, BQ, LN), jnp.bfloat16),
                        pltpu.VMEM((blocks, BQ, LN), jnp.bfloat16),
                        pltpu.VMEM((blocks, 2*BQ, LN), jnp.bfloat16),
                        pltpu.VMEM((blocks, 8, 2*BQ), jnp.float32),
                        pltpu.VMEM((blocks, 2*BQ, LN), jnp.float32),
                        pltpu.VMEM((blocks, BQ, LN), jnp.float32),
                        pltpu.VMEM((blocks, BQ, LN), jnp.float32)],
        compiler_params=pltpu.CompilerParams(vmem_limit_bytes=56 << 20),
        name="attend_back",
        cost_estimate=cost(31),
    )(first, x, do, of, lse, cos, sin)


def widen(table):
    lane = lane_iota(table.shape[0])
    second = jnp.where(lane < 96, pltpu.roll(table, 96, 1), pltpu.roll(table, 16, 1))
    third = jnp.where(lane < 112, pltpu.roll(table, 112, 1), pltpu.roll(table, 32, 1))
    return second, third


def cos_sin3(cos, sin):
    lane = lane_iota(cos.shape[0])
    live = lane < 32
    cos_two, cos_three = widen(cos)
    sin_two, sin_three = widen(sin)
    cosine = jnp.concatenate([cos, cos_two, jnp.where(live, cos_three, 1.0)], axis=1)
    lower = (
        (lane < 48) | (lane >= 96),
        (lane < 16) | ((lane >= 64) & (lane < 112)),
        (lane >= 32) & (lane < 80),
    )
    tiles = (sin, sin_two, jnp.where(live, sin_three, 0.0))
    sine = jnp.concatenate([jnp.where(l, -t, t) for l, t in zip(lower, tiles)], axis=1)
    return cosine, sine, lower


def turn(values, cosine, sine, lower):
    width = values.shape[1]
    left, right = pltpu.roll(values, width - HD // 2, 1), pltpu.roll(values, HD // 2, 1)
    swapped = [
        jnp.where(l, left[:, n * LN : (n + 1) * LN], right[:, n * LN : (n + 1) * LN])
        for n, l in enumerate(lower)
    ]
    return values * cosine + jnp.concatenate(swapped, axis=1) * sine


def full_spec(array):
    rank = array.ndim
    return pl.BlockSpec(array.shape, lambda *_: (0,) * rank)


def qkv_kernel(parts, rows, h_ref, gain_ref, w_ref, cos_ref, sin_ref, a_ref, out_ref):
    count = h_ref.shape[0] // parts
    tokens = count // rows

    def body(z, carry):
        stream = h_ref[pl.ds(pl.multiple_of(z * count, count), count), :].astype(jnp.float32)
        factor = lax.rsqrt(jnp.mean(stream * stream, axis=-1, keepdims=True) + EPS)
        normed = (stream * factor * gain_ref[...]).astype(jnp.bfloat16)
        at = pl.ds(pl.multiple_of(z * tokens, tokens), tokens)
        for r in range(rows):
            a_ref[r, at, :] = normed[r * tokens : (r + 1) * tokens]
        product = dotf(normed, w_ref[...], ((1,), (0,)))
        for r in range(rows):
            cosine, sine, lower = cos_sin3(cos_ref[r, at, :], sin_ref[r, at, :])
            for h in range(product.shape[1] // (3 * LN)):
                piece = product[r * tokens : (r + 1) * tokens, h * 3 * LN : (h + 1) * 3 * LN]
                out_ref[h * rows + r, at, :] = turn(piece, cosine, sine, lower).astype(jnp.bfloat16)
        return carry

    lax.fori_loop(0, parts, body, 0)


def qkv_call(parts, group, gain, weight, cos, sin, rows):
    count, width = group.shape
    tokens = count // rows
    groups = weight.shape[1] // (3 * LN)
    operands = (group, gain, weight, cos, sin)
    return pl.pallas_call(
        partial(qkv_kernel, parts, rows),
        grid=(1,),
        in_specs=[full_spec(v) for v in operands],
        out_specs=[
            pl.BlockSpec((rows, tokens, width), lambda i: (0, 0, 0)),
            pl.BlockSpec((groups * rows, tokens, 3 * LN), lambda i: (0, 0, 0)),
        ],
        out_shape=[
            jax.ShapeDtypeStruct((rows, tokens, width), jnp.bfloat16),
            jax.ShapeDtypeStruct((groups * rows, tokens, 3 * LN), jnp.bfloat16),
        ],
        compiler_params=pltpu.CompilerParams(vmem_limit_bytes=48 << 20),
        name="norm_qkv",
        cost_estimate=cost(7),
    )(*operands)


def thirds(values):
    return values[:, :LN], values[:, LN : 2 * LN], values[:, 2 * LN :]


def join_pairs(left, right):
    l0, l1, l2 = thirds(left)
    r0, r1, r2 = thirds(right)
    low = lane_iota(left.shape[0]) < 64
    s0, s1, s2 = (pltpu.roll(v, 64, 1) for v in (r0, r1, r2))
    firsts = (l0, jnp.where(low, l1, s0), jnp.where(low, s0, s1))
    m1, m2 = pltpu.roll(l1, 64, 1), pltpu.roll(l2, 64, 1)
    lasts = (jnp.where(low, m1, m2), jnp.where(low, m2, r1), r2)
    return jnp.concatenate(firsts, axis=1), jnp.concatenate(lasts, axis=1)


def out_kernel(rows, parts, o_ref, w_ref, tok_ref, gain_ref, mid_ref, b_ref, oo_ref, o_s):
    half = o_ref.shape[1]
    for r in range(rows):
        for z in range(parts):
            left = o_ref[r * parts + z].astype(jnp.float32)
            right = o_ref[(rows + r) * parts + z].astype(jnp.float32)
            for n, piece in enumerate(join_pairs(left, right)):
                at = (2 * r + n) * half
                o_s[at : at + half, z * 3 * LN : (z + 1) * 3 * LN] = piece.astype(jnp.bfloat16)
    attended = o_s[...]
    oo_ref[...] = attended
    middle = tok_ref[...].astype(jnp.float32) + dotf(attended, w_ref[...], ((1,), (1,)))
    mid_ref[...] = middle
    factor = lax.rsqrt(jnp.mean(middle * middle, axis=-1, keepdims=True) + EPS)
    b_ref[...] = (middle * factor * gain_ref[...]).astype(jnp.bfloat16)


def out_call(o_parts, weight, tokens, gain, rows):
    count, width = tokens.shape
    inner = weight.shape[1]
    operands = (o_parts, weight, tokens, gain)
    shapes = [
        jax.ShapeDtypeStruct((count, width), jnp.float32),
        jax.ShapeDtypeStruct((count, width), jnp.bfloat16),
        jax.ShapeDtypeStruct((count, inner), jnp.bfloat16),
    ]
    return pl.pallas_call(
        partial(out_kernel, rows, o_parts.shape[0] // (2 * rows)),
        grid=(1,),
        in_specs=[full_spec(v) for v in operands],
        out_specs=[full_spec(v) for v in shapes],
        out_shape=shapes,
        scratch_shapes=[pltpu.VMEM((count, inner), jnp.bfloat16)],
        compiler_params=pltpu.CompilerParams(vmem_limit_bytes=48 << 20),
        name="out_norm",
        cost_estimate=cost(4),
    )(*operands)


def split_pairs(firsts, lasts):
    f0, f1, f2 = thirds(firsts)
    g0, g1, g2 = thirds(lasts)
    low = lane_iota(firsts.shape[0]) < 64
    t0, t1 = pltpu.roll(g0, 64, 1), pltpu.roll(g1, 64, 1)
    left = (f0, jnp.where(low, f1, t0), jnp.where(low, t0, t1))
    u1, u2 = pltpu.roll(f1, 64, 1), pltpu.roll(f2, 64, 1)
    right = (jnp.where(low, u1, u2), jnp.where(low, u2, g1), g2)
    return jnp.concatenate(left, axis=1), jnp.concatenate(right, axis=1)


def mid_back_kernel(
    rows, parts, keep_ref, fx_ref, fy_ref, px_ref, py_ref, mid_ref, cot_ref, gain_ref, w_ref,
    gmid_ref, go_ref, do_ref, gg_ref
):
    half = px_ref.shape[0]
    wide = lambda v: v.astype(jnp.float32)
    db = jnp.concatenate(
        [
            keep_ref[:half] + wide(fx_ref[...]) + wide(py_ref[...]),
            keep_ref[half:] + wide(fy_ref[...]) + wide(px_ref[...]),
        ],
        axis=0,
    )
    middle = mid_ref[...]
    factor = lax.rsqrt(jnp.mean(middle * middle, axis=-1, keepdims=True) + EPS)
    scaled = db * gain_ref[...]
    inner = jnp.mean(scaled * middle, axis=-1, keepdims=True)
    grad = cot_ref[...].astype(jnp.float32) + factor * scaled - middle * (factor**3 * inner)
    gmid_ref[...] = grad
    gg_ref[...] = jnp.sum(db * middle * factor, axis=0, keepdims=True)
    low = grad.astype(jnp.bfloat16)
    go_ref[...] = low
    back = dotf(low, w_ref[...], ((1,), (0,)))
    half = do_ref.shape[1]
    for r in range(rows):
        for z in range(parts):
            cols = slice(z * 3 * LN, (z + 1) * 3 * LN)
            at = 2 * r * half
            left, right = split_pairs(back[at : at + half, cols], back[at + half : at + 2 * half, cols])
            do_ref[r * parts + z] = left.astype(jnp.bfloat16)
            do_ref[(rows + r) * parts + z] = right.astype(jnp.bfloat16)


def mid_back_call(pieces, middle, cot, gain, weight, rows, parts):
    count, width = middle.shape
    operands = (*pieces, middle, cot, gain, weight)
    shapes = [
        jax.ShapeDtypeStruct((count, width), jnp.float32),
        jax.ShapeDtypeStruct((count, width), jnp.bfloat16),
        jax.ShapeDtypeStruct((2 * rows * parts, count // rows // 2, 3 * LN), jnp.bfloat16),
        jax.ShapeDtypeStruct((1, width), jnp.float32),
    ]
    return pl.pallas_call(
        partial(mid_back_kernel, rows, parts),
        grid=(1,),
        in_specs=[pl.BlockSpec((count, width), lambda i: (0, 0))] + [full_spec(v) for v in operands[1:]],
        out_specs=[full_spec(v) for v in shapes],
        out_shape=shapes,
        compiler_params=pltpu.CompilerParams(vmem_limit_bytes=48 << 20),
        name="mid_back",
        cost_estimate=cost(5),
    )(*operands)


def da_kernel(parts, rows, h_ref, d_ref, w_ref, wo_ref, da_ref, gg_ref):
    count = h_ref.shape[0] // parts
    tokens = count // rows
    groups = d_ref.shape[0]
    run = wo_ref.shape[0] // parts
    gg_ref[...] = jnp.zeros_like(gg_ref)

    def body(z, carry):
        at = pl.ds(pl.multiple_of(z * tokens, tokens), tokens)
        left = jnp.concatenate(
            [jnp.concatenate([d_ref[g, r, at, :] for r in range(rows)], axis=0) for g in range(groups)],
            axis=1,
        )
        back = dotf(left, w_ref[...], ((1,), (1,)))
        stream = h_ref[pl.ds(pl.multiple_of(z * count, count), count), :].astype(jnp.float32)
        factor = lax.rsqrt(jnp.mean(stream * stream, axis=-1, keepdims=True) + EPS)
        gg_ref[...] += jnp.sum(back * stream * factor, axis=0, keepdims=True)
        da_ref[z, :count, :] = back.astype(jnp.bfloat16)
        cols = pl.ds(pl.multiple_of(z * 3 * LN, 3 * LN), 3 * LN)
        for n in range(parts):
            da_ref[z, count:, n * 3 * LN : (n + 1) * 3 * LN] = wo_ref[n * run : (n + 1) * run, cols]
        return carry

    lax.fori_loop(0, parts, body, 0)


def da_call(parts, group, grads, weight, grad_wo, rows):
    count, width = group.shape
    operands = (group, grads, weight, grad_wo)
    block = (count + grad_wo.shape[0]) // parts
    shapes = [
        jax.ShapeDtypeStruct((parts, block, width), jnp.bfloat16),
        jax.ShapeDtypeStruct((1, width), jnp.float32),
    ]
    part, gain_grad = pl.pallas_call(
        partial(da_kernel, parts, rows),
        grid=(1,),
        in_specs=[full_spec(v) for v in operands],
        out_specs=[full_spec(v) for v in shapes],
        out_shape=shapes,
        compiler_params=pltpu.CompilerParams(vmem_limit_bytes=48 << 20),
        name="da_part",
        cost_estimate=cost(6),
    )(*operands)
    return part.reshape(parts * block, width), gain_grad


def cut_kernel(gate_ref, up_ref, down_ref, out_ref):
    def body(n, carry):
        at = pl.ds(pl.multiple_of(n * LN, LN), LN)
        out_ref[n, :, :LN] = gate_ref[:, at]
        out_ref[n, :, LN : 2 * LN] = up_ref[:, at]
        out_ref[n, :, 2 * LN :] = jnp.transpose(down_ref[at, :].astype(jnp.float32)).astype(jnp.bfloat16)
        return carry

    lax.fori_loop(0, out_ref.shape[0], body, 0)


def cut_call(gate, up, down):
    shape = jax.ShapeDtypeStruct((gate.shape[1] // LN, gate.shape[0], 3 * LN), jnp.bfloat16)
    operands = (gate, up, down)
    return pl.pallas_call(
        cut_kernel,
        grid=(1,),
        in_specs=[full_spec(v) for v in operands],
        out_specs=full_spec(shape),
        out_shape=shape,
        name="cut_units",
        cost_estimate=cost(3),
    )(*operands)


def uncut_kernel(in_ref, gate_ref, up_ref, down_ref):
    def body(n, carry):
        at = pl.ds(pl.multiple_of(n * LN, LN), LN)
        gate_ref[:, at] = in_ref[n, :, :LN].astype(jnp.float32)
        up_ref[:, at] = in_ref[n, :, LN : 2 * LN].astype(jnp.float32)
        down_ref[at, :] = jnp.transpose(in_ref[n, :, 2 * LN :].astype(jnp.float32))
        return carry

    lax.fori_loop(0, in_ref.shape[0], body, 0)


def uncut_call(value):
    units, rows = value.shape[0] * LN, value.shape[1]
    shapes = [jax.ShapeDtypeStruct(s, jnp.float32) for s in ((rows, units), (rows, units), (units, rows))]
    return pl.pallas_call(
        uncut_kernel,
        grid=(1,),
        in_specs=[full_spec(value)],
        out_specs=[full_spec(v) for v in shapes],
        out_shape=shapes,
        name="uncut_units",
        cost_estimate=cost(3),
    )(value)


def place_kernel(parts, turned, at_ref, mine_ref, other_ref, out_ref):
    size = mine_ref.shape[1]
    z = at_ref[3]
    for c, ref in enumerate((mine_ref, other_ref)):
        for n in range(parts):
            y, x = at_ref[0] ^ (n // 2), at_ref[1] ^ (n % 2)
            rows = pl.multiple_of(((y * 2 + x) * 2 + (at_ref[2] ^ c)) * size, size)
            for k in range(ref.shape[0] // parts):
                count = ref.shape[0] // parts
                source = lax.rem(z + (count - k), count) if turned else k
                cols = pl.multiple_of(source * 3 * LN, 3 * LN)
                out_ref[pl.ds(rows, size), pl.ds(cols, 3 * LN)] = ref[n * count + k]


def place_call(at, mine, other, turned):
    size = mine.shape[1]
    shape = jax.ShapeDtypeStruct((8 * size, mine.shape[0] // 4 * mine.shape[2]), mine.dtype)
    return pl.pallas_call(
        partial(place_kernel, 4, turned),
        grid=(1,),
        in_specs=[pl.BlockSpec(memory_space=pltpu.SMEM), full_spec(mine), full_spec(other)],
        out_specs=full_spec(shape),
        out_shape=shape,
        compiler_params=pltpu.CompilerParams(vmem_limit_bytes=32 << 20),
        name="place_out",
        cost_estimate=cost(3),
    )(at, mine, other)


def fill_sides(refs, out_ref):
    own, xn, yn = refs
    count = own.shape[0]
    half = count // 2
    out_ref[:count] = own[...]
    out_ref[count : count + half], out_ref[count + half : 2 * count] = xn[:half], yn[half:]
    out_ref[2 * count : 2 * count + half], out_ref[2 * count + half : 3 * count] = xn[half:], yn[:half]


def fill_corner(refs, out_ref, at):
    first, last = refs
    half = first.shape[0]
    out_ref[at : at + half], out_ref[at + half : at + 2 * half] = first[...], last[...]


def fill_square(refs, out_ref):
    fill_sides(refs[:3], out_ref)
    fill_corner(refs[3:], out_ref, 3 * refs[0].shape[0])


def unit_spec(weight):
    return pl.BlockSpec((1,) + weight.shape[1:], lambda z: (z, 0, 0))


def row_tiles(rows, tile, body):
    def step(m, carry):
        body(pl.ds(pl.multiple_of(m * tile, tile), tile))
        return carry

    lax.fori_loop(0, rows // tile, step, 0)


def down_back_kernel(*refs):
    pieces, (w0_ref, w1_ref, out_ref, g_s) = refs[:5], refs[5:]

    @pl.when(pl.program_id(0) == 0)
    def _():
        fill_square(pieces, g_s)

    weight = jnp.concatenate([w0_ref[0, :, 2 * LN :], w1_ref[0, :, 2 * LN :]], axis=1)

    def body(at):
        out_ref[0, at] = dotf(g_s[at, :], weight, ((1,), (0,)))

    row_tiles(g_s.shape[0], g_s.shape[0] // 2, body)


def down_back_call(pieces, mine, other):
    count, width = pieces[0].shape
    parts = mine.shape[0]
    shape = jax.ShapeDtypeStruct((parts, 4 * count, 2 * LN), jnp.float32)
    return pl.pallas_call(
        down_back_kernel,
        grid=(parts,),
        in_specs=[full_spec(v) for v in pieces] + [unit_spec(mine), unit_spec(other)],
        out_specs=unit_spec(shape),
        out_shape=shape,
        scratch_shapes=[pltpu.VMEM((4 * count, width), jnp.bfloat16)],
        compiler_params=pltpu.CompilerParams(vmem_limit_bytes=60 << 20),
        name="down_back",
        cost_estimate=cost(8),
    )(*pieces, mine, other)


def units_kernel(count, start, tile, *refs):
    pieces = refs[:2] if start else refs[:3]
    w0_ref, w1_ref, dh_ref, dgu_ref, hid_ref, *sends, b_s, acc_s = refs[len(pieces) :]
    step = pl.program_id(0)

    @pl.when(step == 0)
    def _():
        if start:
            fill_corner(pieces, b_s, 0)
        else:
            fill_sides(pieces, b_s)

    def body(at):
        b = b_s[at, :]
        total = None
        for n, w_ref in enumerate((w0_ref, w1_ref)):
            weight = w_ref[0, :, : 2 * LN]
            both = dotf(b, weight, ((1,), (0,)))
            gate, up = both[:, :LN], both[:, LN:]
            cols = slice(n * LN, (n + 1) * LN)
            dh = dh_ref[0, pl.ds(start + at.start, tile), cols]
            sigma = 1.0 / (1.0 + jnp.exp(-gate))
            silu = gate * sigma
            hid_ref[0, at, cols] = (silu * up).astype(jnp.bfloat16)
            grad_gate = dh * up * sigma * (1.0 + gate * (1.0 - sigma))
            grads = jnp.concatenate([grad_gate, dh * silu], axis=1).astype(jnp.bfloat16)
            dgu_ref[0, n, at] = grads
            back = dotf(grads, weight, ((1,), (1,)))
            total = back if total is None else total + back

        @pl.when(step == 0)
        def _():
            acc_s[at, :] = total

        @pl.when(step > 0)
        def _():
            acc_s[at, :] += total

    row_tiles(b_s.shape[0], tile, body)

    @pl.when(step == pl.num_programs(0) - 1)
    def _():
        half = count // 2
        if start:
            sx_ref, sy_ref = sends
            sx_ref[...] = acc_s[:half].astype(jnp.bfloat16)
            sy_ref[...] = acc_s[half:].astype(jnp.bfloat16)
        else:
            keep_ref, sx_ref, sy_ref = sends
            keep_ref[:count] = acc_s[:count]
            keep_ref[count:] = acc_s[2 * count :]
            sx_ref[...] = acc_s[count : count + half].astype(jnp.bfloat16)
            sy_ref[...] = acc_s[count + half : 2 * count].astype(jnp.bfloat16)


def units_call(pieces, mine, other, grad_hidden, corner):
    parts, width = mine.shape[:2]
    count = grad_hidden.shape[1] // 4
    rows = count if corner else 3 * count
    low = jnp.bfloat16
    shapes = [
        jax.ShapeDtypeStruct((parts, 2, rows, 2 * LN), low),
        jax.ShapeDtypeStruct((parts, rows, 2 * LN), low),
    ]
    if not corner:
        shapes += [jax.ShapeDtypeStruct((2 * count, width), jnp.float32)]
    shapes += [jax.ShapeDtypeStruct((count // 2, width), low)] * 2
    return pl.pallas_call(
        partial(units_kernel, count, 3 * count if corner else 0, count),
        grid=(parts,),
        in_specs=[full_spec(v) for v in pieces] + [unit_spec(mine), unit_spec(other), unit_spec(grad_hidden)],
        out_specs=[
            pl.BlockSpec((1, 2, rows, 2 * LN), lambda z: (z, 0, 0, 0)),
            pl.BlockSpec((1, rows, 2 * LN), lambda z: (z, 0, 0)),
        ]
        + [full_spec(v) for v in shapes[2:]],
        out_shape=shapes,
        scratch_shapes=[pltpu.VMEM((rows, width), low), pltpu.VMEM((rows, width), jnp.float32)],
        compiler_params=pltpu.CompilerParams(vmem_limit_bytes=60 << 20),
        name="units_corner" if corner else "units",
        cost_estimate=cost(8 if corner else 19),
    )(*pieces, mine, other, grad_hidden)


def down_kernel(hid_ref, hid_last_ref, w0_ref, w1_ref, keep_ref, sx_ref, sy_ref, acc_s):
    step = pl.program_id(0)
    weight = jnp.concatenate([w0_ref[0, :, 2 * LN :], w1_ref[0, :, 2 * LN :]], axis=1)
    rows, count = hid_ref.shape[1], hid_last_ref.shape[1]

    def add(at, hidden):
        total = dotf(hidden, weight, ((1,), (1,)))

        @pl.when(step == 0)
        def _():
            acc_s[at, :] = total

        @pl.when(step > 0)
        def _():
            acc_s[at, :] += total

    row_tiles(rows, count, lambda at: add(at, hid_ref[0, at]))
    add(pl.ds(rows, count), hid_last_ref[0])

    @pl.when(step == pl.num_programs(0) - 1)
    def _():
        half = count // 2
        keep_ref[:count] = acc_s[:count]
        keep_ref[count:] = acc_s[2 * count : 3 * count]
        for n, ref in enumerate((sx_ref, sy_ref)):
            at = n * half
            ref[:half] = acc_s[count + at : count + at + half].astype(jnp.bfloat16)
            ref[half:] = acc_s[3 * count + at : 3 * count + at + half].astype(jnp.bfloat16)


def down_call(hidden, hidden_last, mine, other):
    parts, count, _ = hidden_last.shape
    width = mine.shape[1]
    shapes = [
        jax.ShapeDtypeStruct((2 * count, width), jnp.float32),
        jax.ShapeDtypeStruct((count, width), jnp.bfloat16),
        jax.ShapeDtypeStruct((count, width), jnp.bfloat16),
    ]
    operands = (hidden, hidden_last, mine, other)
    return pl.pallas_call(
        down_kernel,
        grid=(parts,),
        in_specs=[unit_spec(v) for v in operands],
        out_specs=[full_spec(v) for v in shapes],
        out_shape=shapes,
        scratch_shapes=[pltpu.VMEM((4 * count, width), jnp.float32)],
        compiler_params=pltpu.CompilerParams(vmem_limit_bytes=60 << 20),
        name="down",
        cost_estimate=cost(11),
    )(*operands)


def unit_grads_kernel(*refs):
    b_pieces, g_pieces = refs[:5], refs[5:10]
    dgu_ref, dgu_last_ref, hid_ref, hid_last_ref, mine_ref, other_ref, fill_s, b_s, g_s = refs[10:]
    total, width = fill_s.shape
    count = total // 4

    @pl.when(pl.program_id(0) == 0)
    def _():
        for pieces, side in ((b_pieces, b_s), (g_pieces, g_s)):
            fill_square(pieces, fill_s)
            for m in range(4):
                at = slice(m * count, (m + 1) * count)
                side[:, at] = jnp.transpose(fill_s[at, :])

    cut = hid_ref.shape[1]

    def body(at):
        left, right = b_s[at, :], g_s[at, :]
        sum_over = lambda v, a, z: dotf(v[:, :cut], a, ((1,), (0,))) + dotf(v[:, cut:], z, ((1,), (0,)))
        down = sum_over(right, hid_ref[0], hid_last_ref[0])
        for n, out_ref in enumerate((mine_ref, other_ref)):
            out_ref[0, at, : 2 * LN] = sum_over(left, dgu_ref[0, n], dgu_last_ref[0, n]).astype(jnp.bfloat16)
            out_ref[0, at, 2 * LN :] = down[:, n * LN : (n + 1) * LN].astype(jnp.bfloat16)

    row_tiles(width, width // 4, body)


def unit_grads_call(b_pieces, g_pieces, grads, hidden):
    count, width = b_pieces[0].shape
    parts = hidden[0].shape[0]
    low = jnp.bfloat16
    operands = (*b_pieces, *g_pieces)
    return pl.pallas_call(
        unit_grads_kernel,
        grid=(parts,),
        in_specs=[full_spec(v) for v in operands]
        + [pl.BlockSpec((1,) + v.shape[1:], lambda z: (z, 0, 0, 0)) for v in grads]
        + [unit_spec(v) for v in hidden],
        out_specs=[pl.BlockSpec((1, width, 3 * LN), lambda z: (z, 0, 0))] * 2,
        out_shape=[jax.ShapeDtypeStruct((parts, width, 3 * LN), low)] * 2,
        scratch_shapes=[pltpu.VMEM((4 * count, width), low)] + [pltpu.VMEM((width, 4 * count), low)] * 2,
        compiler_params=pltpu.CompilerParams(vmem_limit_bytes=60 << 20),
        name="unit_grads",
        cost_estimate=cost(19),
    )(*operands, *grads, *hidden)


BY_SIDES = tuple((y, x, last) for x in range(2) for y in range(2) for last in range(2))
ORDER = ((0, 0, 0), (0, 0, 1), (0, 1, 0), (1, 1, 0), (1, 0, 1), (1, 1, 1), (0, 1, 1), (1, 0, 0))


def row_grads_kernel(order, at_ref, left_ref, right_ref, mine_ref, other_ref, full_s):
    tile = 2 * LN
    width = right_ref.shape[2]

    def body(n, carry):
        rows = pl.ds(pl.multiple_of(n * tile, tile), tile)
        left = jnp.transpose(left_ref[:, rows])
        for g in range(right_ref.shape[0]):
            piece = dotf(left, right_ref[g], ((1,), (0,)))
            full_s[rows, g * width : (g + 1) * width] = piece.astype(jnp.bfloat16)
        return carry

    lax.fori_loop(0, full_s.shape[0] // tile, body, 0)
    half = mine_ref.shape[1]
    for c, out_ref in enumerate((mine_ref, other_ref)):
        for n, (y, x, last) in enumerate(order):
            block = ((at_ref[0] ^ y) * 2 + (at_ref[1] ^ x)) * 2 + (at_ref[2] ^ c)
            rows = pl.multiple_of(block * 2 * half + last * half, 32)
            out_ref[n] = full_s[pl.ds(rows, half), :]


def row_grads_call(at, left, right, order, name, time):
    width = left.shape[1]
    cols = right.shape[0] * right.shape[2]
    shape = jax.ShapeDtypeStruct((8, width // 16, cols), jnp.bfloat16)
    return pl.pallas_call(
        partial(row_grads_kernel, order),
        grid=(1,),
        in_specs=[pl.BlockSpec(memory_space=pltpu.SMEM), full_spec(left), full_spec(right)],
        out_specs=[full_spec(shape)] * 2,
        out_shape=[shape] * 2,
        scratch_shapes=[pltpu.VMEM((width, cols), jnp.bfloat16)],
        compiler_params=pltpu.CompilerParams(vmem_limit_bytes=32 << 20),
        cost_estimate=cost(time),
        name=name,
    )(at, left, right)


def core_sum(mine, other):
    step = mine.shape[1]
    both = (mine.astype(jnp.float32) + other.astype(jnp.float32)).reshape(8 * step, -1)
    keep = jnp.concatenate([both[: 2 * step], both[6 * step :]], axis=0)
    low = both[2 * step : 6 * step].astype(jnp.bfloat16)
    return keep, low[: 2 * step], low[2 * step :]


EVERY = ("y", "x", "c", "z")
SWAP = ((0, 1), (1, 0))


def swap(value, axis):
    return lax.ppermute(value, axis, SWAP)


def gather_blocks(value, size):
    shift = lambda k: [(i, (i + k) % size) for i in range(size)]
    return [value] + [lax.ppermute(value, "z", shift(k)) for k in range(1, size)]


def gather_sides(value):
    return swap(value, "x"), swap(value, "y")


def gather_corner(xn, yn):
    half = xn.shape[0] // 2
    return swap(yn[:half], "x"), swap(xn[half:], "y")


def gather_square(value):
    sides = gather_sides(value)
    return (value, *sides, *gather_corner(*sides))


def reduce_square(keep, send_x, send_y):
    return reduce_square_rest(keep, swap(send_x, "x"), swap(send_y, "y"))


def reduce_square_rest(keep, from_x, from_y):
    half = from_x.shape[0] // 2
    corner = pass_on(keep, from_x[half:], from_y[half:])
    return keep, from_x[:half], from_y[:half], *corner


def pass_on(keep, corner_x, corner_y):
    low = jnp.bfloat16
    half = corner_x.shape[0]
    pass_y = swap((keep[3 * half :] + corner_x.astype(jnp.float32)).astype(low), "y")
    pass_x = swap((keep[2 * half : 3 * half] + corner_y.astype(jnp.float32)).astype(low), "x")
    return pass_x, pass_y


def total_square(pieces):
    keep, from_x, from_y, pass_x, pass_y = pieces
    half = pass_x.shape[0]
    wide = lambda v: v.astype(jnp.float32)
    return jnp.concatenate(
        [
            keep[:half] + wide(from_x) + wide(pass_y),
            keep[half : 2 * half] + wide(from_y) + wide(pass_x),
        ],
        axis=0,
    )


def all_to_all(value, axes):
    return lax.all_to_all(value, axes, 0, 0, tiled=True)


def tie(*values):
    return lax.optimization_barrier(values)


def fast_local(sizes, *args):
    (tokens, cotangent, segments, positions, norm_in, w_query, w_key, w_value, w_out, norm_mid, w_gate, w_up, w_down) = args
    nz = sizes["z"]
    devices = sizes["y"] * sizes["x"] * sizes["c"] * nz
    plane = devices // nz
    rows, span, width = tokens.shape
    count = rows * span
    chunk = segments.shape[1]
    length = chunk * sizes["x"] * sizes["c"]
    x_at, c_at, z_at = lax.axis_index("x"), lax.axis_index("c"), lax.axis_index("z")
    at = jnp.stack([lax.axis_index("y"), x_at, c_at, z_at]).astype(jnp.int32)

    own = tokens.reshape(count, width)
    group = lax.all_gather(own, "z", axis=0, tiled=True)
    gains = jnp.concatenate([norm_in, norm_mid], axis=1)
    share = norm_in.shape[1]
    gains = jnp.pad(gains, ((0, 0), (0, LN - 2 * share)))
    gains = all_to_all(jnp.broadcast_to(gains, (devices, LN)), EVERY)

    kv_local = w_key.shape[2] // HD
    per_head = lambda w: w[0].reshape(w.shape[1], kv_local, -1)
    w_qkv = jnp.concatenate([per_head(w_query), per_head(w_key), per_head(w_value)], axis=2)
    w_qkv, w_o = tie(jnp.transpose(w_qkv, (1, 0, 2)), jnp.stack(gather_blocks(w_out[0].T, nz)))
    w_qkv = jnp.concatenate(gather_square(w_qkv), axis=0)
    w_qkv = place_call(at, w_qkv, swap(w_qkv, "c"), False)

    last = (x_at * sizes["c"] + c_at + 1) * chunk - 1
    begin = last - positions[:, -1] - jnp.where(segments[:, -1] == 2, 3 * length // 4, 0)
    lanes = jnp.arange(LN, dtype=jnp.int32) % (HD // 2)
    frequency = THETA ** (-(2.0 * lanes.astype(jnp.float32)) / HD)
    token_angle = positions.astype(jnp.float32)[:, :, None] * frequency
    first = lax.dynamic_slice_in_dim(begin, c_at, 1).astype(jnp.int32)
    index = jnp.arange(length, dtype=jnp.int32)
    row_angle = (index - doc_low(index, first[0], length)).astype(jnp.float32)[:, None] * frequency
    token_cos, token_sin = jnp.cos(token_angle), jnp.sin(token_angle)
    row_cos, row_sin = jnp.cos(row_angle), jnp.sin(row_angle)

    sides = gather_sides(w_o)
    gate, up, down, gains, *tables = tie(
        w_gate[0], w_up[0], w_down[0], gains, token_cos, token_sin, row_cos, row_sin, *sides
    )
    token_cos, token_sin, row_cos, row_sin, *sides = tables
    gain_in = gains[:, :share].reshape(1, width)
    gain_mid = gains[:, share : 2 * share].reshape(1, width)
    w_ff = all_to_all(cut_call(gate, up, down), ("y", "x", "c"))
    w_ff = w_ff.reshape(width, 3 * LN)
    corner = gather_corner(*sides)
    group, w_qkv, w_ff = tie(group, w_qkv, w_ff)
    w_mine = lax.all_gather(w_ff, "z", axis=0, tiled=True)

    normed, qkv = qkv_call(nz, group, gain_in, w_qkv, token_cos, token_sin, rows)
    qkv, *corner = tie(qkv, *corner)
    w_o = jnp.concatenate([w_o, *sides, *corner], axis=0)
    qkv = all_to_all(qkv, ("x", "c")).reshape(length, 3 * LN)

    cot_low = cotangent.reshape(count, width)
    cot_first, _ = tie(cot_low, qkv)
    cot_sides = gather_sides(cot_first)

    attended, attended_float, log_total = attn_fwd(first, qkv)
    attended, *cot_sides = tie(attended, *cot_sides)
    attended = all_to_all(attended, ("x", "c", "z"))
    w_o = place_call(at, w_o, swap(w_o, "c"), True)
    w_o, *cot_sides = tie(w_o, *cot_sides)
    attended, *corner = tie(attended, *gather_corner(*cot_sides))
    cot_pieces = (cot_low, *cot_sides, *corner)
    middle, normed_b, attended_low = out_call(attended, w_o, own, gain_mid, rows)
    w_mine, _ = tie(w_mine, normed_b)
    w_mine = w_mine.reshape(nz, width, 3 * LN)
    w_other = swap(w_mine, "c")
    b_sides = gather_sides(normed_b)
    grad_hidden = down_back_call(cot_pieces, w_mine, w_other)
    *b_sides, grad_hidden = tie(*b_sides, grad_hidden)
    b_corner = gather_corner(*b_sides)
    b_pieces = (normed_b, *b_sides, *b_corner)
    grads, hidden, keep_b, *sends = units_call((normed_b, *b_sides), w_mine, w_other, grad_hidden, False)
    from_x, from_y = swap(sends[0], "x"), swap(sends[1], "y")
    grads_last, hidden_last, *sends = units_call(b_corner, w_mine, w_other, grad_hidden, True)
    corner_x, corner_y = swap(sends[0], "x"), swap(sends[1], "y")
    ff_mine, ff_other = unit_grads_call(b_pieces, cot_pieces, (grads, grads_last), (hidden, hidden_last))
    from_x, from_y, corner_x, corner_y, ff_other = tie(from_x, from_y, corner_x, corner_y, ff_other)
    grad_b = (keep_b, from_x, from_y, *pass_on(keep_b, corner_x, corner_y))
    grad_ff = ff_mine.astype(jnp.float32) + swap(ff_other, "c").astype(jnp.float32)
    grad_ff = grad_ff.astype(jnp.bfloat16).reshape(nz * width, 3 * LN)
    grad_ff, *corner = tie(grad_ff, *grad_b[3:])
    grad_b = (*grad_b[:3], *corner)
    grad_ff = lax.psum_scatter(grad_ff, "z", scatter_dimension=0, tiled=True)
    grad_mid, grad_low, grad_o, gain_grad_mid = mid_back_call(
        grad_b, middle, cot_low, gain_mid, w_o, rows, nz
    )
    grad_o = all_to_all(grad_o, ("x", "c", "z"))
    hidden, hidden_last, _ = tie(hidden, hidden_last, grad_low)
    keep_out, *out_sides = down_call(hidden, hidden_last, w_mine, w_other)
    out_sides = swap(out_sides[0], "x"), swap(out_sides[1], "y")
    wo_mine, wo_other = row_grads_call(at, grad_low, attended_low[None], BY_SIDES, "out_grads", 3)
    wo_sum = (wo_mine.astype(jnp.float32) + swap(wo_other, "c").astype(jnp.float32)).reshape(width // 2, -1)
    wo_keep, wo_send = wo_sum[: width // 4], wo_sum[width // 4 :].astype(jnp.bfloat16)
    wo_got = swap(wo_send, "x")

    grad_qkv = attn_bwd(first, qkv, grad_o, attended_float, log_total, row_cos, row_sin)
    grad_qkv, wo_got, *out_sides = tie(grad_qkv, wo_got, *out_sides)
    out = middle + total_square(reduce_square_rest(keep_out, *out_sides))
    wo_sum = wo_keep + wo_got.astype(jnp.float32)
    wo_got = swap(wo_sum[width // 8 :].astype(jnp.bfloat16), "y")
    grad_wo = (wo_sum[: width // 8] + wo_got.astype(jnp.float32)).astype(jnp.bfloat16)
    grad_qkv = all_to_all(grad_qkv.reshape(-1, chunk, 3 * LN), ("x", "c"))
    grad_qkv, grad_ff = tie(grad_qkv, grad_ff)
    grad_ff = all_to_all(grad_ff.reshape(plane, width // plane, 3 * LN), ("y", "x", "c"))
    grad_qkv = grad_qkv.reshape(kv_local, rows, chunk, 3 * LN)
    part, gain_grad_in = da_call(nz, group, grad_qkv, w_qkv, grad_wo, rows)
    part = lax.psum_scatter(part, "z", scatter_dimension=0, tiled=True).astype(jnp.float32)
    grad_a, grad_wo = part[:count], part[count:]
    grad_wo = jnp.concatenate([grad_wo[:, n * 3 * LN : (n + 1) * 3 * LN] for n in range(nz)], axis=0)
    grad_wqkv = row_grads_call(
        at,
        normed.reshape(rows * chunk, width),
        grad_qkv.reshape(kv_local, rows * chunk, 3 * LN),
        ORDER,
        "qkv_grads",
        5,
    )
    *grad_wqkv, grad_ff = tie(*grad_wqkv, grad_ff)
    grad_wqkv = reduce_square(*core_sum(grad_wqkv[0], swap(grad_wqkv[1], "c")))
    gain_grads = jnp.concatenate(
        [gain_grad_in.reshape(devices, share), gain_grad_mid.reshape(devices, share)], axis=1
    )
    gain_grads = jnp.pad(gain_grads, ((0, 0), (0, LN - 2 * share)))
    *grad_wqkv, gain_grads = tie(*grad_wqkv, gain_grads)
    grad_wqkv = total_square(grad_wqkv)
    gain_grads = jnp.sum(all_to_all(gain_grads, EVERY), axis=0, keepdims=True)

    stream = own.astype(jnp.float32)
    factor = lax.rsqrt(jnp.mean(stream * stream, axis=-1, keepdims=True) + EPS)
    back_in, _ = norm_back(stream, factor, gain_in, grad_a)
    grad_tokens = grad_mid + back_in
    grad_wqkv = grad_wqkv.reshape(-1, kv_local, 4 * HD)
    flat = lambda g: g.reshape(1, g.shape[0], -1)
    grad_gate, grad_up, grad_down = uncut_call(grad_ff)
    return (
        out.reshape(tokens.shape),
        grad_tokens.reshape(tokens.shape),
        gain_grads[:, :share],
        flat(grad_wqkv[:, :, : 2 * HD]),
        flat(grad_wqkv[:, :, 2 * HD : 3 * HD]),
        flat(grad_wqkv[:, :, 3 * HD :]),
        grad_wo.T[None],
        gain_grads[:, share : 2 * share],
        grad_gate[None],
        grad_up[None],
        grad_down[None],
    )


def fast_solution(mesh, cores):
    batch, seq, kv = mesh.devices.shape
    fine = Mesh(mesh.devices.reshape(batch, seq // cores, cores, kv), EVERY)
    sizes = dict(fine.shape)
    row_spec = P("y", ("x", "c", "z"), None)
    seq_spec = P("y", ("x", "c"))
    gain_spec = P(None, EVERY)
    in_w = P(None, ("y", "x", "c"), "z")
    out_w = P(None, "z", ("y", "x", "c"))
    in_specs = (row_spec, row_spec, seq_spec, seq_spec, gain_spec, in_w, in_w, in_w, out_w, gain_spec, in_w, in_w, out_w)
    out_specs = (row_spec, row_spec, gain_spec, in_w, in_w, in_w, out_w, gain_spec, in_w, in_w, out_w)
    return jax.shard_map(
        partial(fast_local, sizes), mesh=fine, in_specs=in_specs, out_specs=out_specs, check_vma=False
    )


def solution(mesh):
    batch, seq, kv = (mesh.shape[name] for name in ("batch", "seq", "kv"))
    general = general_solution(mesh)
    if (batch, seq) != (2, 4):
        return general
    fast = fast_solution(mesh, 2)

    def run(*args):
        rows, length, width = args[0].shape
        kv_heads, q_heads = args[6].shape[2] // HD, args[5].shape[2] // HD
        fits = (
            rows == 2 * batch
            and kv_heads == 2 * kv
            and q_heads == 2 * kv_heads
            and length == 128 * seq * kv
            and length % (4 * BQ) == 0
            and width % LN == 0
            and 2 * width // (batch * seq * kv) <= LN
            and args[10].shape[2] == LN * batch * seq * kv
        )
        return (fast if fits else general)(*args)

    return run
```

```python
import functools
import math
from functools import partial

import jax
import jax.numpy as jnp
from jax import lax
from jax.experimental import pallas as pl
from jax.experimental.pallas import tpu as pltpu
from jax.sharding import Mesh
from jax.sharding import PartitionSpec as P

HD = 96
LAYERS = 1


EPS = 1e-05
THETA = 100000.0
BIG_NEG = -1e30


def rotary(positions_row):
    half_width = HD // 2
    frequency = THETA ** (-(2.0 * jnp.arange(half_width, dtype=jnp.float32)) / HD)
    angles = positions_row.astype(jnp.float32)[:, None] * frequency[None, :]
    cosine = jnp.concatenate([jnp.cos(angles), jnp.cos(angles)], axis=1)
    sine_table = jnp.concatenate([jnp.sin(angles), jnp.sin(angles)], axis=1)
    return (cosine, sine_table)


def rotate(head_vals, cosine, sine_table):
    half_width = head_vals.shape[-1] // 2
    swapped = jnp.concatenate([-head_vals[..., half_width:], head_vals[..., :half_width]], axis=-1)
    return head_vals * cosine[:, None, :] + swapped * sine_table[:, None, :]


def rms_norm(stream, gain):
    factor = lax.rsqrt(jnp.mean(stream * stream, axis=-1, keepdims=True) + EPS)
    return (stream * factor * gain, factor)


def norm_back(stream, factor, gain, upstream):
    scaled_grad = upstream * gain
    inner_mean = jnp.mean(scaled_grad * stream, axis=-1, keepdims=True)
    grad_stream = factor * scaled_grad - stream * factor**3 * inner_mean
    return (grad_stream, jnp.sum(upstream * stream * factor, axis=0))


def key_width(key_count):
    return math.gcd(key_count, 1024)


def contract(left_side, right_side, left_dim, right_dim):
    return lax.dot_general(
        left_side,
        right_side,
        (((left_dim,), (right_dim,)), ((), ())),
        preferred_element_type=jnp.float32,
    )


def spread(shard_rows):
    return lax.all_gather(shard_rows, "kv", axis=0, tiled=True)


def token_sum(pairs):
    summed = None
    for left_part, right_part, right_dim in pairs:
        product = contract(left_part, right_part, 1, right_dim)
        summed = product if summed is None else summed + product
    return lax.psum_scatter(
        summed.astype(jnp.bfloat16), "kv", scatter_dimension=0, tiled=True
    ).astype(jnp.float32)


def split_block(kv_both, seg_keys, offset, step_width, kv_local, head_size):
    kv_block = lax.dynamic_slice_in_dim(kv_both, offset, step_width, 0)
    key_block = kv_block[:, : kv_local * head_size].reshape(step_width, kv_local, head_size)
    value_block = kv_block[:, kv_local * head_size :].reshape(step_width, kv_local, head_size)
    seg_block = lax.dynamic_slice_in_dim(seg_keys, offset, step_width, 0)
    return (key_block, value_block, seg_block)


def forward_row(queries, seg_query, fold_state, kv_both, seg_keys, first_query, key_start):
    key_count = kv_both.shape[0]
    step_width = key_width(key_count)
    query_count, kv_local, group_size, head_size = queries.shape
    query_index = first_query + jnp.arange(query_count, dtype=jnp.int32)
    score_scale = head_size ** (-0.5)

    def forward_one_step(step_index, inner_state):
        running_max, weight_total, value_total = inner_state
        offset = step_index * step_width
        key_block, value_block, seg_block = split_block(
            kv_both, seg_keys, offset, step_width, kv_local, head_size
        )
        key_index = offset + jnp.arange(step_width, dtype=jnp.int32)
        allowed = (seg_query[:, None] == seg_block[None, :]) & (
            key_index[None, :] <= query_index[:, None]
        )
        scores = (
            jnp.einsum("qkgd,pkd->kgqp", queries, key_block, preferred_element_type=jnp.float32)
            * score_scale
        )
        scores = jnp.where(allowed, scores, BIG_NEG)
        new_max = jnp.maximum(running_max, jnp.max(scores, axis=-1))
        weights = jnp.where(allowed, jnp.exp(scores - new_max[..., None]), 0.0)
        rescale = jnp.exp(running_max - new_max)
        weight_total = rescale * weight_total + jnp.sum(weights, axis=-1)
        update = jnp.einsum(
            "kgqp,pkd->qkgd",
            weights.astype(jnp.bfloat16),
            value_block,
            preferred_element_type=jnp.float32,
        )
        value_total = jnp.transpose(rescale, (2, 0, 1))[..., None] * value_total + update
        return (new_max, weight_total, value_total)

    return lax.fori_loop(0, key_count // step_width, forward_one_step, fold_state)


def forward_fold(queries, seg_query, first_query, fold_state, pieces, key_start):
    kv_both, seg_keys = pieces
    row_fn = partial(forward_row, first_query=first_query, key_start=key_start)
    return jax.vmap(row_fn, in_axes=(0, 0, 0, 1, 1))(
        queries, seg_query, fold_state, kv_both, seg_keys
    )


def backward_row(
    queries,
    grad_attn,
    log_total,
    row_delta,
    seg_query,
    fold_state,
    kv_both,
    seg_keys,
    first_query,
    key_start,
):
    key_count = kv_both.shape[0]
    step_width = key_width(key_count)
    query_count, kv_local, group_size, head_size = queries.shape
    query_index = first_query + jnp.arange(query_count, dtype=jnp.int32)
    score_scale = head_size ** (-0.5)

    def backward_one_step(step_index, inner_state):
        grad_queries, grad_buffer = inner_state
        offset = step_index * step_width
        key_block, value_block, seg_block = split_block(
            kv_both, seg_keys, offset, step_width, kv_local, head_size
        )
        key_index = offset + jnp.arange(step_width, dtype=jnp.int32)
        allowed = (seg_query[:, None] == seg_block[None, :]) & (
            key_index[None, :] <= query_index[:, None]
        )
        scores = (
            jnp.einsum("qkgd,pkd->kgqp", queries, key_block, preferred_element_type=jnp.float32)
            * score_scale
        )
        probs_block = jnp.where(allowed, jnp.exp(scores - log_total[..., None]), 0.0)
        grad_probs = jnp.einsum(
            "qkgd,pkd->kgqp", grad_attn, value_block, preferred_element_type=jnp.float32
        )
        grad_scores = (probs_block * (grad_probs - row_delta[..., None])).astype(jnp.bfloat16)
        grad_queries = (
            grad_queries
            + jnp.einsum(
                "kgqp,pkd->qkgd", grad_scores, key_block, preferred_element_type=jnp.float32
            )
            * score_scale
        )
        grad_keys = (
            jnp.einsum("kgqp,qkgd->pkd", grad_scores, queries, preferred_element_type=jnp.float32)
            * score_scale
        )
        grad_values = jnp.einsum(
            "kgqp,qkgd->pkd",
            probs_block.astype(jnp.bfloat16),
            grad_attn,
            preferred_element_type=jnp.float32,
        )
        joined = jnp.concatenate(
            [grad_keys.reshape(step_width, -1), grad_values.reshape(step_width, -1)], axis=1
        )
        grad_buffer = lax.dynamic_update_slice_in_dim(grad_buffer, joined, offset, 0)
        return (grad_queries, grad_buffer)

    return lax.fori_loop(0, key_count // step_width, backward_one_step, fold_state)


def backward_fold(
    queries, grad_attn, log_total, row_delta, seg_query, first_query, fold_state, pieces, key_start
):
    kv_both, seg_keys = pieces
    row_fn = partial(backward_row, first_query=first_query, key_start=key_start)
    return jax.vmap(row_fn, in_axes=(0, 0, 0, 0, 0, 0, 1, 1))(
        queries, grad_attn, log_total, row_delta, seg_query, fold_state, kv_both, seg_keys
    )


def layer_forward(stream, gain_pair, matrices, seg_info, tables):
    gain_in, gain_mid = gain_pair
    w_query, w_key, w_value, w_out, w_gate, w_up, w_down = matrices
    seg_query, seg_keys = seg_info
    cosine, sine_table = tables
    row_count = seg_query.shape[0]
    kv_local = w_key.shape[1] // HD
    head_local = w_query.shape[1] // HD
    group_size = head_local // kv_local
    normed_a, factor_a = rms_norm(stream, gain_in)
    spread_a = spread(normed_a.astype(jnp.bfloat16))
    flat_count = spread_a.shape[0]
    token_count = flat_count // row_count
    raw_queries = jnp.dot(spread_a, w_query, preferred_element_type=jnp.float32).reshape(
        flat_count, head_local, HD
    )
    queries = (
        rotate(raw_queries, cosine, sine_table)
        .astype(jnp.bfloat16)
        .reshape(token_count, row_count, kv_local, group_size, HD)
    )
    queries = jnp.transpose(queries, (1, 0, 2, 3, 4))
    raw_keys = jnp.dot(spread_a, w_key, preferred_element_type=jnp.float32).reshape(
        flat_count, kv_local, HD
    )
    keys_low = (
        rotate(raw_keys, cosine, sine_table).astype(jnp.bfloat16).reshape(flat_count, kv_local * HD)
    )
    values_low = jnp.dot(spread_a, w_value, preferred_element_type=jnp.float32).astype(jnp.bfloat16)
    kv_both = jnp.concatenate([keys_low, values_low], axis=1).reshape(
        token_count, row_count, 2 * kv_local * HD
    )
    first_query = lax.axis_index("seq") * token_count
    start_state = (
        jnp.full((row_count, kv_local, group_size, token_count), BIG_NEG, jnp.float32),
        jnp.zeros((row_count, kv_local, group_size, token_count), jnp.float32),
        jnp.zeros((row_count, token_count, kv_local, group_size, HD), jnp.float32),
    )
    running_max, weight_total, value_total = forward_fold(
        queries,
        seg_query,
        first_query,
        start_state,
        (
            lax.all_gather(kv_both, "seq", axis=0, tiled=True),
            lax.all_gather(seg_keys, "seq", axis=0, tiled=True),
        ),
        jnp.int32(0),
    )
    attn_float = value_total / jnp.transpose(weight_total, (0, 3, 1, 2))[..., None]
    log_total = running_max + jnp.log(weight_total)
    attn_low = (
        jnp.transpose(attn_float, (1, 0, 2, 3, 4))
        .reshape(flat_count, head_local * HD)
        .astype(jnp.bfloat16)
    )
    stream_mid = stream + token_sum(((attn_low, w_out, 0),))
    normed_b, factor_b = rms_norm(stream_mid, gain_mid)
    spread_b = spread(normed_b.astype(jnp.bfloat16))
    gate_val = jnp.dot(spread_b, w_gate, preferred_element_type=jnp.float32)
    up_val = jnp.dot(spread_b, w_up, preferred_element_type=jnp.float32)
    hidden = (jax.nn.silu(gate_val) * up_val).astype(jnp.bfloat16)
    stream_out = stream_mid + token_sum(((hidden, w_down, 0),))
    saved_state = (
        stream,
        factor_a,
        spread_a,
        queries,
        kv_both,
        attn_float,
        attn_low,
        log_total,
        stream_mid,
        factor_b,
        spread_b,
        gate_val,
        up_val,
        hidden,
    )
    return (stream_out, saved_state)


def layer_backward(saved_state, grad_stream, gain_pair, matrices, seg_info, tables):
    (
        stream,
        factor_a,
        spread_a,
        queries,
        kv_both,
        attn_float,
        attn_low,
        log_total,
        stream_mid,
        factor_b,
        spread_b,
        gate_val,
        up_val,
        hidden,
    ) = saved_state
    gain_in, gain_mid = gain_pair
    w_query, w_key, w_value, w_out, w_gate, w_up, w_down = matrices
    seg_query, seg_keys = seg_info
    cosine, sine_table = tables
    row_count, token_count, kv_local, group_size, head_size = queries.shape
    head_local = kv_local * group_size
    flat_count = row_count * token_count
    grad_low = spread(grad_stream.astype(jnp.bfloat16))
    grad_down_w = contract(hidden, grad_low, 0, 0)
    grad_hidden = contract(grad_low, w_down, 1, 1)
    sigmoid_gate = jax.nn.sigmoid(gate_val)
    silu_gate = gate_val * sigmoid_gate
    grad_gate_low = (
        grad_hidden * up_val * sigmoid_gate * (1.0 + gate_val * (1.0 - sigmoid_gate))
    ).astype(jnp.bfloat16)
    grad_up_low = (grad_hidden * silu_gate).astype(jnp.bfloat16)
    grad_gate_w = contract(spread_b, grad_gate_low, 0, 0)
    grad_up_w = contract(spread_b, grad_up_low, 0, 0)
    grad_normed_b = token_sum(((grad_gate_low, w_gate, 1), (grad_up_low, w_up, 1)))
    back_mid, grad_gain_mid = norm_back(stream_mid, factor_b, gain_mid, grad_normed_b)
    grad_mid = grad_stream + back_mid
    grad_attn_full = spread(grad_mid.astype(jnp.bfloat16))
    grad_out_w = contract(attn_low, grad_attn_full, 0, 0)
    grad_attn = (
        contract(grad_attn_full, w_out, 1, 1)
        .astype(jnp.bfloat16)
        .reshape(token_count, row_count, kv_local, group_size, head_size)
    )
    grad_attn = jnp.transpose(grad_attn, (1, 0, 2, 3, 4))
    row_delta = jnp.transpose(jnp.sum(grad_attn * attn_float, axis=-1), (0, 2, 3, 1))
    first_query = lax.axis_index("seq") * token_count
    row_length = token_count * lax.axis_size("seq")
    start_state = (
        jnp.zeros((row_count, token_count, kv_local, group_size, head_size), jnp.float32),
        jnp.zeros((row_count, row_length, 2 * kv_local * head_size), jnp.float32),
    )
    grad_queries, grad_buffer = backward_fold(
        queries,
        grad_attn,
        log_total,
        row_delta,
        seg_query,
        first_query,
        start_state,
        (
            lax.all_gather(kv_both, "seq", axis=0, tiled=True),
            lax.all_gather(seg_keys, "seq", axis=0, tiled=True),
        ),
        jnp.int32(0),
    )
    grad_kv = lax.psum_scatter(
        grad_buffer.astype(jnp.bfloat16), "seq", scatter_dimension=1, tiled=True
    ).astype(jnp.float32)
    grad_kv = jnp.transpose(grad_kv, (1, 0, 2)).reshape(flat_count, 2 * kv_local * head_size)
    grad_queries = jnp.transpose(grad_queries, (1, 0, 2, 3, 4)).reshape(
        flat_count, head_local, head_size
    )
    grad_q_low = (
        rotate(grad_queries, cosine, -sine_table)
        .astype(jnp.bfloat16)
        .reshape(flat_count, head_local * head_size)
    )
    grad_k_low = (
        rotate(
            grad_kv[:, : kv_local * head_size].reshape(flat_count, kv_local, head_size),
            cosine,
            -sine_table,
        )
        .astype(jnp.bfloat16)
        .reshape(flat_count, kv_local * head_size)
    )
    grad_v_low = grad_kv[:, kv_local * head_size :].astype(jnp.bfloat16)
    grad_query_w = contract(spread_a, grad_q_low, 0, 0)
    grad_key_w = contract(spread_a, grad_k_low, 0, 0)
    grad_value_w = contract(spread_a, grad_v_low, 0, 0)
    grad_normed_a = token_sum(
        ((grad_q_low, w_query, 1), (grad_k_low, w_key, 1), (grad_v_low, w_value, 1))
    )
    back_in, grad_gain_in = norm_back(stream, factor_a, gain_in, grad_normed_a)
    grad_input = grad_mid + back_in
    weight_grads = (
        lax.psum_scatter(
            grad_query_w.astype(jnp.bfloat16), ("batch", "seq"), scatter_dimension=0, tiled=True
        ).astype(jnp.float32),
        lax.psum_scatter(
            grad_key_w.astype(jnp.bfloat16), ("batch", "seq"), scatter_dimension=0, tiled=True
        ).astype(jnp.float32),
        lax.psum_scatter(
            grad_value_w.astype(jnp.bfloat16), ("batch", "seq"), scatter_dimension=0, tiled=True
        ).astype(jnp.float32),
        lax.psum_scatter(
            grad_out_w.astype(jnp.bfloat16), ("batch", "seq"), scatter_dimension=1, tiled=True
        ).astype(jnp.float32),
        lax.psum_scatter(
            grad_gate_w.astype(jnp.bfloat16), ("batch", "seq"), scatter_dimension=0, tiled=True
        ).astype(jnp.float32),
        lax.psum_scatter(
            grad_up_w.astype(jnp.bfloat16), ("batch", "seq"), scatter_dimension=0, tiled=True
        ).astype(jnp.float32),
        lax.psum_scatter(
            grad_down_w.astype(jnp.bfloat16), ("batch", "seq"), scatter_dimension=1, tiled=True
        ).astype(jnp.float32),
    )
    return (grad_input, weight_grads, grad_gain_in, grad_gain_mid)


def to_flat(shard_rows):
    row_count, token_part, width = shard_rows.shape
    return jnp.transpose(shard_rows.astype(jnp.float32), (1, 0, 2)).reshape(
        token_part * row_count, width
    )


def from_flat(flat_rows, row_count):
    token_part = flat_rows.shape[0] // row_count
    return jnp.transpose(flat_rows.reshape(token_part, row_count, flat_rows.shape[1]), (1, 0, 2))


def general_local(
    tokens,
    cotangent,
    segments,
    positions,
    norm_in,
    w_query,
    w_key,
    w_value,
    w_out,
    norm_mid,
    w_gate,
    w_up,
    w_down,
):
    gains_in, gains_mid = (
        lax.all_gather(norm_in, ("batch", "seq", "kv"), axis=1, tiled=True),
        lax.all_gather(norm_mid, ("batch", "seq", "kv"), axis=1, tiled=True),
    )
    row_count = tokens.shape[0]
    seg_info = (segments, jnp.transpose(segments, (1, 0)))
    tables = rotary(jnp.transpose(positions, (1, 0)).reshape(-1))

    def fetch_layer(layer_index):
        return (
            lax.all_gather(w_query[layer_index], ("batch", "seq"), axis=0, tiled=True),
            lax.all_gather(w_key[layer_index], ("batch", "seq"), axis=0, tiled=True),
            lax.all_gather(w_value[layer_index], ("batch", "seq"), axis=0, tiled=True),
            lax.all_gather(w_out[layer_index], ("batch", "seq"), axis=1, tiled=True),
            lax.all_gather(w_gate[layer_index], ("batch", "seq"), axis=0, tiled=True),
            lax.all_gather(w_up[layer_index], ("batch", "seq"), axis=0, tiled=True),
            lax.all_gather(w_down[layer_index], ("batch", "seq"), axis=1, tiled=True),
        )

    stream = to_flat(tokens)
    fetched = []
    states = []
    layer_index = 0
    matrices = fetch_layer(layer_index)
    layer_inputs = [stream]
    stream, saved_state = layer_forward(
        stream, (gains_in[layer_index], gains_mid[layer_index]), matrices, seg_info, tables
    )
    fetched.append(matrices)
    states.append(saved_state)
    grad_stream = to_flat(cotangent)
    grads_in = []
    grads_mid = []
    weight_lists = []
    for layer_index in reversed(range(LAYERS)):
        gain_pair = (gains_in[layer_index], gains_mid[layer_index])
        matrices = fetch_layer(layer_index)
        saved_state = layer_forward(
            layer_inputs[layer_index], gain_pair, matrices, seg_info, tables
        )[1]
        grad_stream, weight_grads, grad_gain_in, grad_gain_mid = layer_backward(
            saved_state, grad_stream, gain_pair, matrices, seg_info, tables
        )
        grads_in.insert(0, grad_gain_in)
        grads_mid.insert(0, grad_gain_mid)
        weight_lists.insert(0, weight_grads)
    gain_grads_in, gain_grads_mid = (
        lax.psum_scatter(
            jnp.stack(grads_in), ("batch", "seq", "kv"), scatter_dimension=1, tiled=True
        ),
        lax.psum_scatter(
            jnp.stack(grads_mid), ("batch", "seq", "kv"), scatter_dimension=1, tiled=True
        ),
    )
    stacked_grads = [
        jnp.stack([grad_set[member] for grad_set in weight_lists]) for member in range(7)
    ]
    return (
        from_flat(stream, row_count),
        from_flat(grad_stream, row_count),
        gain_grads_in,
        stacked_grads[0],
        stacked_grads[1],
        stacked_grads[2],
        stacked_grads[3],
        gain_grads_mid,
        stacked_grads[4],
        stacked_grads[5],
        stacked_grads[6],
    )


def general_solution(mesh):
    in_specs = (
        P("batch", ("seq", "kv"), None),
        P("batch", ("seq", "kv"), None),
        P("batch", "seq"),
        P("batch", "seq"),
        P(None, ("batch", "seq", "kv")),
        P(None, ("batch", "seq"), "kv"),
        P(None, ("batch", "seq"), "kv"),
        P(None, ("batch", "seq"), "kv"),
        P(None, "kv", ("batch", "seq")),
        P(None, ("batch", "seq", "kv")),
        P(None, ("batch", "seq"), "kv"),
        P(None, ("batch", "seq"), "kv"),
        P(None, "kv", ("batch", "seq")),
    )
    out_specs = (
        P("batch", ("seq", "kv"), None),
        P("batch", ("seq", "kv"), None),
        P(None, ("batch", "seq", "kv")),
        P(None, ("batch", "seq"), "kv"),
        P(None, ("batch", "seq"), "kv"),
        P(None, ("batch", "seq"), "kv"),
        P(None, "kv", ("batch", "seq")),
        P(None, ("batch", "seq", "kv")),
        P(None, ("batch", "seq"), "kv"),
        P(None, ("batch", "seq"), "kv"),
        P(None, "kv", ("batch", "seq")),
    )
    return jax.shard_map(general_local, mesh=mesh, in_specs=in_specs, out_specs=out_specs, check_vma=False)


LN = 128
NEG=-1e30
C2 = (96 ** -0.5) * 1.4426950408889634

def cost(microseconds):
    return pl.CostEstimate(
        flops=microseconds * 10**9, bytes_accessed=microseconds * 3 * 10**6, transcendentals=0
    )


def lane_iota(rows):
    return lax.broadcasted_iota(jnp.int32, (rows, LN), 1)

def unpack4(t0, t1, t2):
    lane = lane_iota(t0.shape[0])
    live = lane < HD
    zero = jnp.zeros_like(t0)
    a = t0
    b = pltpu.roll(jnp.where(lane >= 96, t0, t1), 32, 1)
    c = pltpu.roll(jnp.where(lane >= 64, t1, t2), 64, 1)
    d = pltpu.roll(t2, 96, 1)
    return tuple(jnp.where(live, v, zero) for v in (a, b, c, d))

def pack4(a, b, c, d):
    lane = lane_iota(a.shape[0])
    b, c, d = pltpu.roll(b, 96, 1), pltpu.roll(c, 64, 1), pltpu.roll(d, 32, 1)
    return (jnp.where(lane < 96, a, b), jnp.where(lane < 64, b, c), jnp.where(lane < 32, c, d))

def split3(x):
    x = x.astype(jnp.float32)
    return x[:, :LN], x[:, LN:2*LN], x[:, 2*LN:]

def doc_low(index, first, length):
    second = first + 3 * length // 4
    return jnp.where(index >= second, second, jnp.where(index >= first, first, 0))

BQ = 256
BK = 512

def dotf(a, b, dims):
    return lax.dot_general(a, b, (dims, ((), ())), preferred_element_type=jnp.float32)

def attn_fwd_kernel(length, first_ref, x_ref, o_ref, of_ref, lse_ref, q_s, k_s, v_s, s_s):
    i = pl.program_id(0)
    blocks = length // BQ
    first = first_ref[0]

    @pl.when(i == 0)
    def _():
        def body(j, carry):
            rows = pl.ds(pl.multiple_of(j * BQ, BQ), BQ)
            q0, q1, k, v = unpack4(*split3(x_ref[rows, :]))
            q_s[j, :BQ, :] = q0.astype(jnp.bfloat16)
            q_s[j, BQ:, :] = q1.astype(jnp.bfloat16)
            k_s[rows, :] = k.astype(jnp.bfloat16)
            v_s[rows, :] = v.astype(jnp.bfloat16)
            return carry

        lax.fori_loop(0, blocks, body, 0)

    q = q_s[i]
    late = (3 * length // 4 + length // 8) // BQ
    start = jnp.where(i >= late, 3 * length // 4 // BK, 0)
    stop = i * BQ // BK + 1
    q_index = i * BQ + lax.broadcasted_iota(jnp.int32, (BQ, 1), 0)
    low = doc_low(q_index, first, length)

    def fold(v, op):
        out = v[:, :LN]
        for n in range(1, BK // LN):
            out = op(out, v[:, n * LN : (n + 1) * LN])
        return out

    def score(j, top):
        s = dotf(q, k_s[pl.ds(pl.multiple_of(j * BK, BK), BK), :], ((1,), (1,)))
        key = j * BK + lax.broadcasted_iota(jnp.int32, (1, BK), 1)
        ok = (key <= q_index) & (key >= low)
        s = jnp.concatenate([jnp.where(ok, s[:BQ], NEG), jnp.where(ok, s[BQ:], NEG)], axis=0)
        s_s[j] = s
        return jnp.maximum(top, fold(s, jnp.maximum))

    top = lax.fori_loop(start, stop, score, jnp.full((2 * BQ, LN), NEG, jnp.float32))
    m = jnp.max(top, axis=1, keepdims=True) * C2

    def add(j, state):
        p = jnp.exp2(s_s[j] * C2 - m)
        keys = pl.ds(pl.multiple_of(j * BK, BK), BK)
        of_ref[0] += dotf(p.astype(jnp.bfloat16), v_s[keys, :], ((1,), (0,)))
        return state + fold(p, jnp.add)

    zero = jnp.zeros((2 * BQ, LN), jnp.float32)
    of_ref[0] = zero
    total = lax.fori_loop(start, stop, add, zero)
    total = jnp.sum(total, axis=1, keepdims=True)
    out = of_ref[0] / total
    lse = jnp.broadcast_to(m + jnp.log2(total), (2 * BQ, LN))
    lse_ref[0] = jnp.transpose(lse, (1, 0))[:8, :]
    of_ref[0] = out
    for d in range(2):
        at = d * 128
        parts = [out[at + n // 2 * 64 + n % 2 * BQ : at + n // 2 * 64 + n % 2 * BQ + 64] for n in range(4)]
        for n, t in enumerate(pack4(*parts)):
            o_ref[d, :, n * LN : (n + 1) * LN] = t.astype(jnp.bfloat16)


def attn_fwd(first, x):
    length = x.shape[0]
    blocks = length // BQ
    return pl.pallas_call(
        functools.partial(attn_fwd_kernel, length),
        grid=(blocks,),
        in_specs=[pl.BlockSpec(memory_space=pltpu.SMEM),
                  pl.BlockSpec((length, 3*LN), lambda i: (0, 0))],
        out_specs=[pl.BlockSpec((2, 64, 3*LN), lambda i: (i, 0, 0)),
                   pl.BlockSpec((1, 2*BQ, LN), lambda i: (i, 0, 0)),
                   pl.BlockSpec((1, 8, 2*BQ), lambda i: (i, 0, 0))],
        out_shape=[jax.ShapeDtypeStruct((length//128, 64, 3*LN), jnp.bfloat16),
                   jax.ShapeDtypeStruct((blocks, 2*BQ, LN), jnp.float32),
                   jax.ShapeDtypeStruct((blocks, 8, 2*BQ), jnp.float32)],
        scratch_shapes=[pltpu.VMEM((blocks, 2*BQ, LN), jnp.bfloat16),
                        pltpu.VMEM((length, LN), jnp.bfloat16),
                        pltpu.VMEM((length, LN), jnp.bfloat16),
                        pltpu.VMEM((length // BK, 2*BQ, BK), jnp.float32)],
        compiler_params=pltpu.CompilerParams(vmem_limit_bytes=48 << 20),
        name="attend",
        cost_estimate=cost(22),
    )(first, x)

def attn_bwd_kernel(length, first_ref, x_ref, do_ref, of_ref, lse_ref, cos_ref, sin_ref, out_ref,
                    q_s, k_s, v_s, do_s, dl_s, dq_s, dk_s, dv_s):
    j = pl.program_id(0)
    blocks = length // BQ
    first = first_ref[0]
    @pl.when(j == 0)
    def _():
        def body(b, carry):
            rows = pl.ds(pl.multiple_of(b * BQ, BQ), BQ)
            q0, q1, k, v = unpack4(*split3(x_ref[rows, :]))
            q_s[b, :BQ, :] = q0.astype(jnp.bfloat16)
            q_s[b, BQ:, :] = q1.astype(jnp.bfloat16)
            k_s[b] = k.astype(jnp.bfloat16)
            v_s[b] = v.astype(jnp.bfloat16)
            for d in range(2):
                parts = unpack4(*split3(do_ref[2*b + d]))
                for n, part in enumerate(parts):
                    at = (n % 2) * BQ + d*128 + (n // 2) * 64
                    do_s[b, at:at+64, :] = part.astype(jnp.bfloat16)
            prod = do_s[b].astype(jnp.float32) * of_ref[b]
            delta = jnp.broadcast_to(jnp.sum(prod, axis=1, keepdims=True), (2*BQ, LN))
            dl_s[b] = jnp.transpose(delta, (1, 0))[:8, :]
            dq_s[b] = jnp.zeros((2*BQ, LN), jnp.float32)
            return carry
        lax.fori_loop(0, blocks, body, 0)
    late = (3 * length // 4 + length // 8) // BQ
    third = 3 * length // 4 // BQ
    stop = jnp.where(j >= third, blocks, late)
    k = k_s[j]
    v = v_s[j]
    dk_s[j] = jnp.zeros((BQ, LN), jnp.float32)
    dv_s[j] = jnp.zeros((BQ, LN), jnp.float32)
    key = j * BQ + lax.broadcasted_iota(jnp.int32, (BQ, 1), 0)

    def steps(places):
        dk, dv = [], []
        for i in places:
            q, do = q_s[i], do_s[i]
            s = dotf(k, q, ((1,), (1,)))
            dp = dotf(v, do, ((1,), (1,)))
            q_index = i * BQ + lax.broadcasted_iota(jnp.int32, (1, BQ), 1)
            ok = (key <= q_index) & (key >= doc_low(q_index, first, length))
            p = jnp.exp2(s * C2 - lse_ref[i, 0:1, :])
            p = jnp.concatenate([jnp.where(ok, p[:, :BQ], 0.0), jnp.where(ok, p[:, BQ:], 0.0)], axis=1)
            ds = (p * (dp - dl_s[i, 0:1, :])).astype(jnp.bfloat16)
            dv.append(dotf(p.astype(jnp.bfloat16), do, ((1,), (0,))))
            dk.append(dotf(ds, q, ((1,), (0,))))
            dq_s[i] += dotf(ds, k, ((0,), (0,)))
        dv_s[j] += functools.reduce(jnp.add, dv)
        dk_s[j] += functools.reduce(jnp.add, dk)

    pairs = (stop - j) // 2

    def body(n, carry):
        steps((j + 2 * n, j + 2 * n + 1))
        return carry

    lax.fori_loop(0, pairs, body, 0)

    @pl.when(j + 2 * pairs < stop)
    def _():
        steps((stop - 1,))

    @pl.when(j == blocks - 1)
    def _():
        scale = HD ** -0.5
        lower = lane_iota(BQ) < HD // 2

        def turn_back(piece, cosine, sine):
            swapped = jnp.where(lower, -pltpu.roll(piece, LN - HD // 2, 1), pltpu.roll(piece, HD // 2, 1))
            return (piece * cosine - swapped * sine) * scale

        def body(b, carry):
            rows = pl.ds(pl.multiple_of(b * BQ, BQ), BQ)
            cosine, sine = cos_ref[rows, :], sin_ref[rows, :]
            pieces = [turn_back(v, cosine, sine) for v in (dq_s[b, :BQ, :], dq_s[b, BQ:, :], dk_s[b])]
            for n, tile in enumerate(pack4(*pieces, dv_s[b])):
                out_ref[rows, n * LN : (n + 1) * LN] = tile.astype(jnp.bfloat16)
            return carry

        lax.fori_loop(0, blocks, body, 0)


def attn_bwd(first, x, do, of, lse, cos, sin):
    length = x.shape[0]
    blocks = length // BQ
    whole = lambda a: pl.BlockSpec(a.shape, lambda j: (0,) * a.ndim)
    return pl.pallas_call(
        functools.partial(attn_bwd_kernel, length),
        grid=(blocks,),
        in_specs=[pl.BlockSpec(memory_space=pltpu.SMEM)] + [whole(a) for a in (x, do, of, lse, cos, sin)],
        out_specs=pl.BlockSpec((length, 3*LN), lambda j: (0, 0)),
        out_shape=jax.ShapeDtypeStruct((length, 3*LN), jnp.bfloat16),
        scratch_shapes=[pltpu.VMEM((blocks, 2*BQ, LN), jnp.bfloat16),
                        pltpu.VMEM((blocks, BQ, LN), jnp.bfloat16),
                        pltpu.VMEM((blocks, BQ, LN), jnp.bfloat16),
                        pltpu.VMEM((blocks, 2*BQ, LN), jnp.bfloat16),
                        pltpu.VMEM((blocks, 8, 2*BQ), jnp.float32),
                        pltpu.VMEM((blocks, 2*BQ, LN), jnp.float32),
                        pltpu.VMEM((blocks, BQ, LN), jnp.float32),
                        pltpu.VMEM((blocks, BQ, LN), jnp.float32)],
        compiler_params=pltpu.CompilerParams(vmem_limit_bytes=56 << 20),
        name="attend_back",
        cost_estimate=cost(31),
    )(first, x, do, of, lse, cos, sin)


def widen(table):
    lane = lane_iota(table.shape[0])
    second = jnp.where(lane < 96, pltpu.roll(table, 96, 1), pltpu.roll(table, 16, 1))
    third = jnp.where(lane < 112, pltpu.roll(table, 112, 1), pltpu.roll(table, 32, 1))
    return second, third


def cos_sin3(cos, sin):
    lane = lane_iota(cos.shape[0])
    live = lane < 32
    cos_two, cos_three = widen(cos)
    sin_two, sin_three = widen(sin)
    cosine = jnp.concatenate([cos, cos_two, jnp.where(live, cos_three, 1.0)], axis=1)
    lower = (
        (lane < 48) | (lane >= 96),
        (lane < 16) | ((lane >= 64) & (lane < 112)),
        (lane >= 32) & (lane < 80),
    )
    tiles = (sin, sin_two, jnp.where(live, sin_three, 0.0))
    sine = jnp.concatenate([jnp.where(l, -t, t) for l, t in zip(lower, tiles)], axis=1)
    return cosine, sine, lower


def turn(values, cosine, sine, lower):
    width = values.shape[1]
    left, right = pltpu.roll(values, width - HD // 2, 1), pltpu.roll(values, HD // 2, 1)
    swapped = [
        jnp.where(l, left[:, n * LN : (n + 1) * LN], right[:, n * LN : (n + 1) * LN])
        for n, l in enumerate(lower)
    ]
    return values * cosine + jnp.concatenate(swapped, axis=1) * sine


def full_spec(array):
    rank = array.ndim
    return pl.BlockSpec(array.shape, lambda *_: (0,) * rank)


def qkv_kernel(parts, rows, h_ref, gain_ref, w_ref, cos_ref, sin_ref, a_ref, out_ref):
    count = h_ref.shape[0] // parts
    tokens = count // rows

    def body(z, carry):
        stream = h_ref[pl.ds(pl.multiple_of(z * count, count), count), :].astype(jnp.float32)
        factor = lax.rsqrt(jnp.mean(stream * stream, axis=-1, keepdims=True) + EPS)
        normed = (stream * factor * gain_ref[...]).astype(jnp.bfloat16)
        at = pl.ds(pl.multiple_of(z * tokens, tokens), tokens)
        for r in range(rows):
            a_ref[r, at, :] = normed[r * tokens : (r + 1) * tokens]
        product = dotf(normed, w_ref[...], ((1,), (0,)))
        for r in range(rows):
            cosine, sine, lower = cos_sin3(cos_ref[r, at, :], sin_ref[r, at, :])
            for h in range(product.shape[1] // (3 * LN)):
                piece = product[r * tokens : (r + 1) * tokens, h * 3 * LN : (h + 1) * 3 * LN]
                out_ref[h * rows + r, at, :] = turn(piece, cosine, sine, lower).astype(jnp.bfloat16)
        return carry

    lax.fori_loop(0, parts, body, 0)


def qkv_call(parts, group, gain, weight, cos, sin, rows):
    count, width = group.shape
    tokens = count // rows
    groups = weight.shape[1] // (3 * LN)
    operands = (group, gain, weight, cos, sin)
    return pl.pallas_call(
        partial(qkv_kernel, parts, rows),
        grid=(1,),
        in_specs=[full_spec(v) for v in operands],
        out_specs=[
            pl.BlockSpec((rows, tokens, width), lambda i: (0, 0, 0)),
            pl.BlockSpec((groups * rows, tokens, 3 * LN), lambda i: (0, 0, 0)),
        ],
        out_shape=[
            jax.ShapeDtypeStruct((rows, tokens, width), jnp.bfloat16),
            jax.ShapeDtypeStruct((groups * rows, tokens, 3 * LN), jnp.bfloat16),
        ],
        compiler_params=pltpu.CompilerParams(vmem_limit_bytes=48 << 20),
        name="norm_qkv",
        cost_estimate=cost(7),
    )(*operands)


def thirds(values):
    return values[:, :LN], values[:, LN : 2 * LN], values[:, 2 * LN :]


def join_pairs(left, right):
    l0, l1, l2 = thirds(left)
    r0, r1, r2 = thirds(right)
    low = lane_iota(left.shape[0]) < 64
    s0, s1, s2 = (pltpu.roll(v, 64, 1) for v in (r0, r1, r2))
    firsts = (l0, jnp.where(low, l1, s0), jnp.where(low, s0, s1))
    m1, m2 = pltpu.roll(l1, 64, 1), pltpu.roll(l2, 64, 1)
    lasts = (jnp.where(low, m1, m2), jnp.where(low, m2, r1), r2)
    return jnp.concatenate(firsts, axis=1), jnp.concatenate(lasts, axis=1)


def out_kernel(rows, parts, o_ref, w_ref, tok_ref, gain_ref, mid_ref, b_ref, oo_ref, o_s):
    half = o_ref.shape[1]
    for r in range(rows):
        for z in range(parts):
            left = o_ref[r * parts + z].astype(jnp.float32)
            right = o_ref[(rows + r) * parts + z].astype(jnp.float32)
            for n, piece in enumerate(join_pairs(left, right)):
                at = (2 * r + n) * half
                o_s[at : at + half, z * 3 * LN : (z + 1) * 3 * LN] = piece.astype(jnp.bfloat16)
    attended = o_s[...]
    oo_ref[...] = attended
    middle = tok_ref[...].astype(jnp.float32) + dotf(attended, w_ref[...], ((1,), (1,)))
    mid_ref[...] = middle
    factor = lax.rsqrt(jnp.mean(middle * middle, axis=-1, keepdims=True) + EPS)
    b_ref[...] = (middle * factor * gain_ref[...]).astype(jnp.bfloat16)


def out_call(o_parts, weight, tokens, gain, rows):
    count, width = tokens.shape
    inner = weight.shape[1]
    operands = (o_parts, weight, tokens, gain)
    shapes = [
        jax.ShapeDtypeStruct((count, width), jnp.float32),
        jax.ShapeDtypeStruct((count, width), jnp.bfloat16),
        jax.ShapeDtypeStruct((count, inner), jnp.bfloat16),
    ]
    return pl.pallas_call(
        partial(out_kernel, rows, o_parts.shape[0] // (2 * rows)),
        grid=(1,),
        in_specs=[full_spec(v) for v in operands],
        out_specs=[full_spec(v) for v in shapes],
        out_shape=shapes,
        scratch_shapes=[pltpu.VMEM((count, inner), jnp.bfloat16)],
        compiler_params=pltpu.CompilerParams(vmem_limit_bytes=48 << 20),
        name="out_norm",
        cost_estimate=cost(4),
    )(*operands)


def split_pairs(firsts, lasts):
    f0, f1, f2 = thirds(firsts)
    g0, g1, g2 = thirds(lasts)
    low = lane_iota(firsts.shape[0]) < 64
    t0, t1 = pltpu.roll(g0, 64, 1), pltpu.roll(g1, 64, 1)
    left = (f0, jnp.where(low, f1, t0), jnp.where(low, t0, t1))
    u1, u2 = pltpu.roll(f1, 64, 1), pltpu.roll(f2, 64, 1)
    right = (jnp.where(low, u1, u2), jnp.where(low, u2, g1), g2)
    return jnp.concatenate(left, axis=1), jnp.concatenate(right, axis=1)


def mid_back_kernel(
    rows, parts, keep_ref, fx_ref, fy_ref, px_ref, py_ref, mid_ref, cot_ref, gain_ref, w_ref,
    gmid_ref, go_ref, do_ref, gg_ref
):
    half = px_ref.shape[0]
    wide = lambda v: v.astype(jnp.float32)
    db = jnp.concatenate(
        [
            keep_ref[:half] + wide(fx_ref[...]) + wide(py_ref[...]),
            keep_ref[half:] + wide(fy_ref[...]) + wide(px_ref[...]),
        ],
        axis=0,
    )
    middle = mid_ref[...]
    factor = lax.rsqrt(jnp.mean(middle * middle, axis=-1, keepdims=True) + EPS)
    scaled = db * gain_ref[...]
    inner = jnp.mean(scaled * middle, axis=-1, keepdims=True)
    grad = cot_ref[...].astype(jnp.float32) + factor * scaled - middle * (factor**3 * inner)
    gmid_ref[...] = grad
    gg_ref[...] = jnp.sum(db * middle * factor, axis=0, keepdims=True)
    low = grad.astype(jnp.bfloat16)
    go_ref[...] = low
    back = dotf(low, w_ref[...], ((1,), (0,)))
    half = do_ref.shape[1]
    for r in range(rows):
        for z in range(parts):
            cols = slice(z * 3 * LN, (z + 1) * 3 * LN)
            at = 2 * r * half
            left, right = split_pairs(back[at : at + half, cols], back[at + half : at + 2 * half, cols])
            do_ref[r * parts + z] = left.astype(jnp.bfloat16)
            do_ref[(rows + r) * parts + z] = right.astype(jnp.bfloat16)


def mid_back_call(pieces, middle, cot, gain, weight, rows, parts):
    count, width = middle.shape
    operands = (*pieces, middle, cot, gain, weight)
    shapes = [
        jax.ShapeDtypeStruct((count, width), jnp.float32),
        jax.ShapeDtypeStruct((count, width), jnp.bfloat16),
        jax.ShapeDtypeStruct((2 * rows * parts, count // rows // 2, 3 * LN), jnp.bfloat16),
        jax.ShapeDtypeStruct((1, width), jnp.float32),
    ]
    return pl.pallas_call(
        partial(mid_back_kernel, rows, parts),
        grid=(1,),
        in_specs=[pl.BlockSpec((count, width), lambda i: (0, 0))] + [full_spec(v) for v in operands[1:]],
        out_specs=[full_spec(v) for v in shapes],
        out_shape=shapes,
        compiler_params=pltpu.CompilerParams(vmem_limit_bytes=48 << 20),
        name="mid_back",
        cost_estimate=cost(5),
    )(*operands)


def da_kernel(parts, rows, h_ref, d_ref, w_ref, wo_ref, da_ref, gg_ref):
    count = h_ref.shape[0] // parts
    tokens = count // rows
    groups = d_ref.shape[0]
    run = wo_ref.shape[0] // parts
    gg_ref[...] = jnp.zeros_like(gg_ref)

    def body(z, carry):
        at = pl.ds(pl.multiple_of(z * tokens, tokens), tokens)
        left = jnp.concatenate(
            [jnp.concatenate([d_ref[g, r, at, :] for r in range(rows)], axis=0) for g in range(groups)],
            axis=1,
        )
        back = dotf(left, w_ref[...], ((1,), (1,)))
        stream = h_ref[pl.ds(pl.multiple_of(z * count, count), count), :].astype(jnp.float32)
        factor = lax.rsqrt(jnp.mean(stream * stream, axis=-1, keepdims=True) + EPS)
        gg_ref[...] += jnp.sum(back * stream * factor, axis=0, keepdims=True)
        da_ref[z, :count, :] = back.astype(jnp.bfloat16)
        cols = pl.ds(pl.multiple_of(z * 3 * LN, 3 * LN), 3 * LN)
        for n in range(parts):
            da_ref[z, count:, n * 3 * LN : (n + 1) * 3 * LN] = wo_ref[n * run : (n + 1) * run, cols]
        return carry

    lax.fori_loop(0, parts, body, 0)


def da_call(parts, group, grads, weight, grad_wo, rows):
    count, width = group.shape
    operands = (group, grads, weight, grad_wo)
    block = (count + grad_wo.shape[0]) // parts
    shapes = [
        jax.ShapeDtypeStruct((parts, block, width), jnp.bfloat16),
        jax.ShapeDtypeStruct((1, width), jnp.float32),
    ]
    part, gain_grad = pl.pallas_call(
        partial(da_kernel, parts, rows),
        grid=(1,),
        in_specs=[full_spec(v) for v in operands],
        out_specs=[full_spec(v) for v in shapes],
        out_shape=shapes,
        compiler_params=pltpu.CompilerParams(vmem_limit_bytes=48 << 20),
        name="da_part",
        cost_estimate=cost(6),
    )(*operands)
    return part.reshape(parts * block, width), gain_grad


def cut_kernel(gate_ref, up_ref, down_ref, out_ref):
    def body(n, carry):
        at = pl.ds(pl.multiple_of(n * LN, LN), LN)
        out_ref[n, :, :LN] = gate_ref[:, at]
        out_ref[n, :, LN : 2 * LN] = up_ref[:, at]
        out_ref[n, :, 2 * LN :] = jnp.transpose(down_ref[at, :].astype(jnp.float32)).astype(jnp.bfloat16)
        return carry

    lax.fori_loop(0, out_ref.shape[0], body, 0)


def cut_call(gate, up, down):
    shape = jax.ShapeDtypeStruct((gate.shape[1] // LN, gate.shape[0], 3 * LN), jnp.bfloat16)
    operands = (gate, up, down)
    return pl.pallas_call(
        cut_kernel,
        grid=(1,),
        in_specs=[full_spec(v) for v in operands],
        out_specs=full_spec(shape),
        out_shape=shape,
        name="cut_units",
        cost_estimate=cost(3),
    )(*operands)


def uncut_kernel(in_ref, gate_ref, up_ref, down_ref):
    def body(n, carry):
        at = pl.ds(pl.multiple_of(n * LN, LN), LN)
        gate_ref[:, at] = in_ref[n, :, :LN].astype(jnp.float32)
        up_ref[:, at] = in_ref[n, :, LN : 2 * LN].astype(jnp.float32)
        down_ref[at, :] = jnp.transpose(in_ref[n, :, 2 * LN :].astype(jnp.float32))
        return carry

    lax.fori_loop(0, in_ref.shape[0], body, 0)


def uncut_call(value):
    units, rows = value.shape[0] * LN, value.shape[1]
    shapes = [jax.ShapeDtypeStruct(s, jnp.float32) for s in ((rows, units), (rows, units), (units, rows))]
    return pl.pallas_call(
        uncut_kernel,
        grid=(1,),
        in_specs=[full_spec(value)],
        out_specs=[full_spec(v) for v in shapes],
        out_shape=shapes,
        name="uncut_units",
        cost_estimate=cost(3),
    )(value)


def place_kernel(parts, turned, at_ref, mine_ref, other_ref, out_ref):
    size = mine_ref.shape[1]
    z = at_ref[3]
    for c, ref in enumerate((mine_ref, other_ref)):
        for n in range(parts):
            y, x = at_ref[0] ^ (n // 2), at_ref[1] ^ (n % 2)
            rows = pl.multiple_of(((y * 2 + x) * 2 + (at_ref[2] ^ c)) * size, size)
            for k in range(ref.shape[0] // parts):
                count = ref.shape[0] // parts
                source = lax.rem(z + (count - k), count) if turned else k
                cols = pl.multiple_of(source * 3 * LN, 3 * LN)
                out_ref[pl.ds(rows, size), pl.ds(cols, 3 * LN)] = ref[n * count + k]


def place_call(at, mine, other, turned):
    size = mine.shape[1]
    shape = jax.ShapeDtypeStruct((8 * size, mine.shape[0] // 4 * mine.shape[2]), mine.dtype)
    return pl.pallas_call(
        partial(place_kernel, 4, turned),
        grid=(1,),
        in_specs=[pl.BlockSpec(memory_space=pltpu.SMEM), full_spec(mine), full_spec(other)],
        out_specs=full_spec(shape),
        out_shape=shape,
        compiler_params=pltpu.CompilerParams(vmem_limit_bytes=32 << 20),
        name="place_out",
        cost_estimate=cost(3),
    )(at, mine, other)


def fill_sides(refs, out_ref):
    own, xn, yn = refs
    count = own.shape[0]
    half = count // 2
    out_ref[:count] = own[...]
    out_ref[count : count + half], out_ref[count + half : 2 * count] = xn[:half], yn[half:]
    out_ref[2 * count : 2 * count + half], out_ref[2 * count + half : 3 * count] = xn[half:], yn[:half]


def fill_corner(refs, out_ref, at):
    first, last = refs
    half = first.shape[0]
    out_ref[at : at + half], out_ref[at + half : at + 2 * half] = first[...], last[...]


def fill_square(refs, out_ref):
    fill_sides(refs[:3], out_ref)
    fill_corner(refs[3:], out_ref, 3 * refs[0].shape[0])


def unit_spec(weight):
    return pl.BlockSpec((1,) + weight.shape[1:], lambda z: (z, 0, 0))


def row_tiles(rows, tile, body):
    def step(m, carry):
        body(pl.ds(pl.multiple_of(m * tile, tile), tile))
        return carry

    lax.fori_loop(0, rows // tile, step, 0)


def down_back_kernel(*refs):
    pieces, (w0_ref, w1_ref, out_ref, g_s) = refs[:5], refs[5:]

    @pl.when(pl.program_id(0) == 0)
    def _():
        fill_square(pieces, g_s)

    weight = jnp.concatenate([w0_ref[0, :, 2 * LN :], w1_ref[0, :, 2 * LN :]], axis=1)

    def body(at):
        out_ref[0, at] = dotf(g_s[at, :], weight, ((1,), (0,)))

    row_tiles(g_s.shape[0], g_s.shape[0] // 2, body)


def down_back_call(pieces, mine, other):
    count, width = pieces[0].shape
    parts = mine.shape[0]
    shape = jax.ShapeDtypeStruct((parts, 4 * count, 2 * LN), jnp.float32)
    return pl.pallas_call(
        down_back_kernel,
        grid=(parts,),
        in_specs=[full_spec(v) for v in pieces] + [unit_spec(mine), unit_spec(other)],
        out_specs=unit_spec(shape),
        out_shape=shape,
        scratch_shapes=[pltpu.VMEM((4 * count, width), jnp.bfloat16)],
        compiler_params=pltpu.CompilerParams(vmem_limit_bytes=60 << 20),
        name="down_back",
        cost_estimate=cost(8),
    )(*pieces, mine, other)


def units_kernel(count, start, tile, *refs):
    pieces = refs[:2] if start else refs[:3]
    w0_ref, w1_ref, dh_ref, dgu_ref, hid_ref, *sends, b_s, acc_s = refs[len(pieces) :]
    step = pl.program_id(0)

    @pl.when(step == 0)
    def _():
        if start:
            fill_corner(pieces, b_s, 0)
        else:
            fill_sides(pieces, b_s)

    def body(at):
        b = b_s[at, :]
        total = None
        for n, w_ref in enumerate((w0_ref, w1_ref)):
            weight = w_ref[0, :, : 2 * LN]
            both = dotf(b, weight, ((1,), (0,)))
            gate, up = both[:, :LN], both[:, LN:]
            cols = slice(n * LN, (n + 1) * LN)
            dh = dh_ref[0, pl.ds(start + at.start, tile), cols]
            sigma = 1.0 / (1.0 + jnp.exp(-gate))
            silu = gate * sigma
            hid_ref[0, at, cols] = (silu * up).astype(jnp.bfloat16)
            grad_gate = dh * up * sigma * (1.0 + gate * (1.0 - sigma))
            grads = jnp.concatenate([grad_gate, dh * silu], axis=1).astype(jnp.bfloat16)
            dgu_ref[0, n, at] = grads
            back = dotf(grads, weight, ((1,), (1,)))
            total = back if total is None else total + back

        @pl.when(step == 0)
        def _():
            acc_s[at, :] = total

        @pl.when(step > 0)
        def _():
            acc_s[at, :] += total

    row_tiles(b_s.shape[0], tile, body)

    @pl.when(step == pl.num_programs(0) - 1)
    def _():
        half = count // 2
        if start:
            sx_ref, sy_ref = sends
            sx_ref[...] = acc_s[:half].astype(jnp.bfloat16)
            sy_ref[...] = acc_s[half:].astype(jnp.bfloat16)
        else:
            keep_ref, sx_ref, sy_ref = sends
            keep_ref[:count] = acc_s[:count]
            keep_ref[count:] = acc_s[2 * count :]
            sx_ref[...] = acc_s[count : count + half].astype(jnp.bfloat16)
            sy_ref[...] = acc_s[count + half : 2 * count].astype(jnp.bfloat16)


def units_call(pieces, mine, other, grad_hidden, corner):
    parts, width = mine.shape[:2]
    count = grad_hidden.shape[1] // 4
    rows = count if corner else 3 * count
    low = jnp.bfloat16
    shapes = [
        jax.ShapeDtypeStruct((parts, 2, rows, 2 * LN), low),
        jax.ShapeDtypeStruct((parts, rows, 2 * LN), low),
    ]
    if not corner:
        shapes += [jax.ShapeDtypeStruct((2 * count, width), jnp.float32)]
    shapes += [jax.ShapeDtypeStruct((count // 2, width), low)] * 2
    return pl.pallas_call(
        partial(units_kernel, count, 3 * count if corner else 0, count if corner else 3 * count // 2),
        grid=(parts,),
        in_specs=[full_spec(v) for v in pieces] + [unit_spec(mine), unit_spec(other), unit_spec(grad_hidden)],
        out_specs=[
            pl.BlockSpec((1, 2, rows, 2 * LN), lambda z: (z, 0, 0, 0)),
            pl.BlockSpec((1, rows, 2 * LN), lambda z: (z, 0, 0)),
        ]
        + [full_spec(v) for v in shapes[2:]],
        out_shape=shapes,
        scratch_shapes=[pltpu.VMEM((rows, width), low), pltpu.VMEM((rows, width), jnp.float32)],
        compiler_params=pltpu.CompilerParams(vmem_limit_bytes=60 << 20),
        name="units_corner" if corner else "units",
        cost_estimate=cost(8 if corner else 19),
    )(*pieces, mine, other, grad_hidden)


def down_kernel(hid_ref, hid_last_ref, w0_ref, w1_ref, keep_ref, sx_ref, sy_ref, acc_s):
    step = pl.program_id(0)
    weight = jnp.concatenate([w0_ref[0, :, 2 * LN :], w1_ref[0, :, 2 * LN :]], axis=1)
    rows, count = hid_ref.shape[1], hid_last_ref.shape[1]

    def add(at, hidden):
        total = dotf(hidden, weight, ((1,), (1,)))

        @pl.when(step == 0)
        def _():
            acc_s[at, :] = total

        @pl.when(step > 0)
        def _():
            acc_s[at, :] += total

    row_tiles(rows, count, lambda at: add(at, hid_ref[0, at]))
    add(pl.ds(rows, count), hid_last_ref[0])

    @pl.when(step == pl.num_programs(0) - 1)
    def _():
        half = count // 2
        keep_ref[:count] = acc_s[:count]
        keep_ref[count:] = acc_s[2 * count : 3 * count]
        for n, ref in enumerate((sx_ref, sy_ref)):
            at = n * half
            ref[:half] = acc_s[count + at : count + at + half].astype(jnp.bfloat16)
            ref[half:] = acc_s[3 * count + at : 3 * count + at + half].astype(jnp.bfloat16)


def down_call(hidden, hidden_last, mine, other):
    parts, count, _ = hidden_last.shape
    width = mine.shape[1]
    shapes = [
        jax.ShapeDtypeStruct((2 * count, width), jnp.float32),
        jax.ShapeDtypeStruct((count, width), jnp.bfloat16),
        jax.ShapeDtypeStruct((count, width), jnp.bfloat16),
    ]
    operands = (hidden, hidden_last, mine, other)
    return pl.pallas_call(
        down_kernel,
        grid=(parts,),
        in_specs=[unit_spec(v) for v in operands],
        out_specs=[full_spec(v) for v in shapes],
        out_shape=shapes,
        scratch_shapes=[pltpu.VMEM((4 * count, width), jnp.float32)],
        compiler_params=pltpu.CompilerParams(vmem_limit_bytes=60 << 20),
        name="down",
        cost_estimate=cost(11),
    )(*operands)


def unit_grads_kernel(*refs):
    b_pieces, g_pieces = refs[:5], refs[5:10]
    dgu_ref, dgu_last_ref, hid_ref, hid_last_ref, mine_ref, other_ref, fill_s, b_s, g_s = refs[10:]
    total, width = fill_s.shape
    count = total // 4

    @pl.when(pl.program_id(0) == 0)
    def _():
        for pieces, side in ((b_pieces, b_s), (g_pieces, g_s)):
            fill_square(pieces, fill_s)
            for m in range(4):
                at = slice(m * count, (m + 1) * count)
                side[:, at] = jnp.transpose(fill_s[at, :])

    cut = hid_ref.shape[1]

    def body(at):
        left, right = b_s[at, :], g_s[at, :]
        sum_over = lambda v, a, z: dotf(v[:, :cut], a, ((1,), (0,))) + dotf(v[:, cut:], z, ((1,), (0,)))
        down = sum_over(right, hid_ref[0], hid_last_ref[0])
        for n, out_ref in enumerate((mine_ref, other_ref)):
            out_ref[0, at, : 2 * LN] = sum_over(left, dgu_ref[0, n], dgu_last_ref[0, n]).astype(jnp.bfloat16)
            out_ref[0, at, 2 * LN :] = down[:, n * LN : (n + 1) * LN].astype(jnp.bfloat16)

    row_tiles(width, width // 4, body)


def unit_grads_call(b_pieces, g_pieces, grads, hidden):
    count, width = b_pieces[0].shape
    parts = hidden[0].shape[0]
    low = jnp.bfloat16
    operands = (*b_pieces, *g_pieces)
    return pl.pallas_call(
        unit_grads_kernel,
        grid=(parts,),
        in_specs=[full_spec(v) for v in operands]
        + [pl.BlockSpec((1,) + v.shape[1:], lambda z: (z, 0, 0, 0)) for v in grads]
        + [unit_spec(v) for v in hidden],
        out_specs=[pl.BlockSpec((1, width, 3 * LN), lambda z: (z, 0, 0))] * 2,
        out_shape=[jax.ShapeDtypeStruct((parts, width, 3 * LN), low)] * 2,
        scratch_shapes=[pltpu.VMEM((4 * count, width), low)] + [pltpu.VMEM((width, 4 * count), low)] * 2,
        compiler_params=pltpu.CompilerParams(vmem_limit_bytes=60 << 20),
        name="unit_grads",
        cost_estimate=cost(19),
    )(*operands, *grads, *hidden)


BY_SIDES = tuple((y, x, last) for x in range(2) for y in range(2) for last in range(2))
ORDER = ((0, 0, 0), (0, 0, 1), (0, 1, 0), (1, 1, 0), (1, 0, 1), (1, 1, 1), (0, 1, 1), (1, 0, 0))


def row_grads_kernel(order, at_ref, left_ref, right_ref, mine_ref, other_ref, full_s):
    tile = 2 * LN
    width = right_ref.shape[2]

    def body(n, carry):
        rows = pl.ds(pl.multiple_of(n * tile, tile), tile)
        left = jnp.transpose(left_ref[:, rows])
        for g in range(right_ref.shape[0]):
            piece = dotf(left, right_ref[g], ((1,), (0,)))
            full_s[rows, g * width : (g + 1) * width] = piece.astype(jnp.bfloat16)
        return carry

    lax.fori_loop(0, full_s.shape[0] // tile, body, 0)
    half = mine_ref.shape[1]
    for c, out_ref in enumerate((mine_ref, other_ref)):
        for n, (y, x, last) in enumerate(order):
            block = ((at_ref[0] ^ y) * 2 + (at_ref[1] ^ x)) * 2 + (at_ref[2] ^ c)
            rows = pl.multiple_of(block * 2 * half + last * half, 32)
            out_ref[n] = full_s[pl.ds(rows, half), :]


def row_grads_call(at, left, right, order, name, time):
    width = left.shape[1]
    cols = right.shape[0] * right.shape[2]
    shape = jax.ShapeDtypeStruct((8, width // 16, cols), jnp.bfloat16)
    return pl.pallas_call(
        partial(row_grads_kernel, order),
        grid=(1,),
        in_specs=[pl.BlockSpec(memory_space=pltpu.SMEM), full_spec(left), full_spec(right)],
        out_specs=[full_spec(shape)] * 2,
        out_shape=[shape] * 2,
        scratch_shapes=[pltpu.VMEM((width, cols), jnp.bfloat16)],
        compiler_params=pltpu.CompilerParams(vmem_limit_bytes=32 << 20),
        cost_estimate=cost(time),
        name=name,
    )(at, left, right)


def core_sum(mine, other):
    step = mine.shape[1]
    both = (mine.astype(jnp.float32) + other.astype(jnp.float32)).reshape(8 * step, -1)
    keep = jnp.concatenate([both[: 2 * step], both[6 * step :]], axis=0)
    low = both[2 * step : 6 * step].astype(jnp.bfloat16)
    return keep, low[: 2 * step], low[2 * step :]


EVERY = ("y", "x", "c", "z")
SWAP = ((0, 1), (1, 0))


def swap(value, axis):
    return lax.ppermute(value, axis, SWAP)


def gather_blocks(value, size):
    shift = lambda k: [(i, (i + k) % size) for i in range(size)]
    return [value] + [lax.ppermute(value, "z", shift(k)) for k in range(1, size)]


def gather_sides(value):
    return swap(value, "x"), swap(value, "y")


def gather_corner(xn, yn):
    half = xn.shape[0] // 2
    return swap(yn[:half], "x"), swap(xn[half:], "y")


def gather_square(value):
    sides = gather_sides(value)
    return (value, *sides, *gather_corner(*sides))


def reduce_square(keep, send_x, send_y):
    return reduce_square_rest(keep, swap(send_x, "x"), swap(send_y, "y"))


def reduce_square_rest(keep, from_x, from_y):
    half = from_x.shape[0] // 2
    corner = pass_on(keep, from_x[half:], from_y[half:])
    return keep, from_x[:half], from_y[:half], *corner


def pass_on(keep, corner_x, corner_y):
    low = jnp.bfloat16
    half = corner_x.shape[0]
    pass_y = swap((keep[3 * half :] + corner_x.astype(jnp.float32)).astype(low), "y")
    pass_x = swap((keep[2 * half : 3 * half] + corner_y.astype(jnp.float32)).astype(low), "x")
    return pass_x, pass_y


def total_square(pieces):
    keep, from_x, from_y, pass_x, pass_y = pieces
    half = pass_x.shape[0]
    wide = lambda v: v.astype(jnp.float32)
    return jnp.concatenate(
        [
            keep[:half] + wide(from_x) + wide(pass_y),
            keep[half : 2 * half] + wide(from_y) + wide(pass_x),
        ],
        axis=0,
    )


def all_to_all(value, axes):
    return lax.all_to_all(value, axes, 0, 0, tiled=True)


def tie(*values):
    return lax.optimization_barrier(values)


def fast_local(sizes, *args):
    (tokens, cotangent, segments, positions, norm_in, w_query, w_key, w_value, w_out, norm_mid, w_gate, w_up, w_down) = args
    nz = sizes["z"]
    devices = sizes["y"] * sizes["x"] * sizes["c"] * nz
    plane = devices // nz
    rows, span, width = tokens.shape
    count = rows * span
    chunk = segments.shape[1]
    length = chunk * sizes["x"] * sizes["c"]
    x_at, c_at, z_at = lax.axis_index("x"), lax.axis_index("c"), lax.axis_index("z")
    at = jnp.stack([lax.axis_index("y"), x_at, c_at, z_at]).astype(jnp.int32)

    own = tokens.reshape(count, width)
    group = lax.all_gather(own, "z", axis=0, tiled=True)
    gains = jnp.concatenate([norm_in, norm_mid], axis=1)
    share = norm_in.shape[1]
    gains = jnp.pad(gains, ((0, 0), (0, LN - 2 * share)))
    gains = all_to_all(jnp.broadcast_to(gains, (devices, LN)), EVERY)

    kv_local = w_key.shape[2] // HD
    per_head = lambda w: w[0].reshape(w.shape[1], kv_local, -1)
    w_qkv = jnp.concatenate([per_head(w_query), per_head(w_key), per_head(w_value)], axis=2)
    w_qkv, w_o = tie(jnp.transpose(w_qkv, (1, 0, 2)), jnp.stack(gather_blocks(w_out[0].T, nz)))
    w_qkv = jnp.concatenate(gather_square(w_qkv), axis=0)
    w_qkv = place_call(at, w_qkv, swap(w_qkv, "c"), False)

    last = (x_at * sizes["c"] + c_at + 1) * chunk - 1
    begin = last - positions[:, -1] - jnp.where(segments[:, -1] == 2, 3 * length // 4, 0)
    lanes = jnp.arange(LN, dtype=jnp.int32) % (HD // 2)
    frequency = THETA ** (-(2.0 * lanes.astype(jnp.float32)) / HD)
    token_angle = positions.astype(jnp.float32)[:, :, None] * frequency
    first = lax.dynamic_slice_in_dim(begin, c_at, 1).astype(jnp.int32)
    index = jnp.arange(length, dtype=jnp.int32)
    row_angle = (index - doc_low(index, first[0], length)).astype(jnp.float32)[:, None] * frequency
    token_cos, token_sin = jnp.cos(token_angle), jnp.sin(token_angle)
    row_cos, row_sin = jnp.cos(row_angle), jnp.sin(row_angle)

    sides = gather_sides(w_o)
    gate, up, down, gains, *tables = tie(
        w_gate[0], w_up[0], w_down[0], gains, token_cos, token_sin, row_cos, row_sin, *sides
    )
    token_cos, token_sin, row_cos, row_sin, *sides = tables
    gain_in = gains[:, :share].reshape(1, width)
    gain_mid = gains[:, share : 2 * share].reshape(1, width)
    w_ff = all_to_all(cut_call(gate, up, down), ("y", "x", "c"))
    w_ff = w_ff.reshape(width, 3 * LN)
    corner = gather_corner(*sides)
    group, w_qkv, w_ff = tie(group, w_qkv, w_ff)
    w_mine = lax.all_gather(w_ff, "z", axis=0, tiled=True)

    normed, qkv = qkv_call(nz, group, gain_in, w_qkv, token_cos, token_sin, rows)
    qkv, *corner = tie(qkv, *corner)
    w_o = jnp.concatenate([w_o, *sides, *corner], axis=0)
    qkv = all_to_all(qkv, ("x", "c")).reshape(length, 3 * LN)

    cot_low = cotangent.reshape(count, width)
    cot_first, _ = tie(cot_low, qkv)
    cot_sides = gather_sides(cot_first)

    attended, attended_float, log_total = attn_fwd(first, qkv)
    attended, *cot_sides = tie(attended, *cot_sides)
    attended = all_to_all(attended, ("x", "c", "z"))
    w_o = place_call(at, w_o, swap(w_o, "c"), True)
    w_o, *cot_sides = tie(w_o, *cot_sides)
    attended, *corner = tie(attended, *gather_corner(*cot_sides))
    cot_pieces = (cot_low, *cot_sides, *corner)
    middle, normed_b, attended_low = out_call(attended, w_o, own, gain_mid, rows)
    w_mine, _ = tie(w_mine, normed_b)
    w_mine = w_mine.reshape(nz, width, 3 * LN)
    w_other = swap(w_mine, "c")
    b_sides = gather_sides(normed_b)
    grad_hidden = down_back_call(cot_pieces, w_mine, w_other)
    *b_sides, grad_hidden = tie(*b_sides, grad_hidden)
    b_corner = gather_corner(*b_sides)
    b_pieces = (normed_b, *b_sides, *b_corner)
    grads, hidden, keep_b, *sends = units_call((normed_b, *b_sides), w_mine, w_other, grad_hidden, False)
    from_x, from_y = swap(sends[0], "x"), swap(sends[1], "y")
    grads_last, hidden_last, *sends = units_call(b_corner, w_mine, w_other, grad_hidden, True)
    corner_x, corner_y = swap(sends[0], "x"), swap(sends[1], "y")
    ff_mine, ff_other = unit_grads_call(b_pieces, cot_pieces, (grads, grads_last), (hidden, hidden_last))
    from_x, from_y, corner_x, corner_y, ff_other = tie(from_x, from_y, corner_x, corner_y, ff_other)
    grad_b = (keep_b, from_x, from_y, *pass_on(keep_b, corner_x, corner_y))
    grad_ff = ff_mine.astype(jnp.float32) + swap(ff_other, "c").astype(jnp.float32)
    grad_ff = grad_ff.astype(jnp.bfloat16).reshape(nz * width, 3 * LN)
    grad_ff, *corner = tie(grad_ff, *grad_b[3:])
    grad_b = (*grad_b[:3], *corner)
    grad_ff = lax.psum_scatter(grad_ff, "z", scatter_dimension=0, tiled=True)
    grad_mid, grad_low, grad_o, gain_grad_mid = mid_back_call(
        grad_b, middle, cot_low, gain_mid, w_o, rows, nz
    )
    grad_o = all_to_all(grad_o, ("x", "c", "z"))
    hidden, hidden_last, _ = tie(hidden, hidden_last, grad_low)
    keep_out, *out_sides = down_call(hidden, hidden_last, w_mine, w_other)
    out_sides = swap(out_sides[0], "x"), swap(out_sides[1], "y")
    wo_mine, wo_other = row_grads_call(at, grad_low, attended_low[None], BY_SIDES, "out_grads", 3)
    wo_sum = (wo_mine.astype(jnp.float32) + swap(wo_other, "c").astype(jnp.float32)).reshape(width // 2, -1)
    wo_keep, wo_send = wo_sum[: width // 4], wo_sum[width // 4 :].astype(jnp.bfloat16)
    wo_got = swap(wo_send, "x")

    grad_qkv = attn_bwd(first, qkv, grad_o, attended_float, log_total, row_cos, row_sin)
    grad_qkv, wo_got, *out_sides = tie(grad_qkv, wo_got, *out_sides)
    out = middle + total_square(reduce_square_rest(keep_out, *out_sides))
    wo_sum = wo_keep + wo_got.astype(jnp.float32)
    wo_got = swap(wo_sum[width // 8 :].astype(jnp.bfloat16), "y")
    grad_wo = (wo_sum[: width // 8] + wo_got.astype(jnp.float32)).astype(jnp.bfloat16)
    grad_qkv = all_to_all(grad_qkv.reshape(-1, chunk, 3 * LN), ("x", "c"))
    grad_qkv, grad_ff = tie(grad_qkv, grad_ff)
    grad_ff = all_to_all(grad_ff.reshape(plane, width // plane, 3 * LN), ("y", "x", "c"))
    grad_qkv = grad_qkv.reshape(kv_local, rows, chunk, 3 * LN)
    part, gain_grad_in = da_call(nz, group, grad_qkv, w_qkv, grad_wo, rows)
    part = lax.psum_scatter(part, "z", scatter_dimension=0, tiled=True).astype(jnp.float32)
    grad_a, grad_wo = part[:count], part[count:]
    grad_wo = jnp.concatenate([grad_wo[:, n * 3 * LN : (n + 1) * 3 * LN] for n in range(nz)], axis=0)
    grad_wqkv = row_grads_call(
        at,
        normed.reshape(rows * chunk, width),
        grad_qkv.reshape(kv_local, rows * chunk, 3 * LN),
        ORDER,
        "qkv_grads",
        5,
    )
    *grad_wqkv, grad_ff = tie(*grad_wqkv, grad_ff)
    grad_wqkv = reduce_square(*core_sum(grad_wqkv[0], swap(grad_wqkv[1], "c")))
    gain_grads = jnp.concatenate(
        [gain_grad_in.reshape(devices, share), gain_grad_mid.reshape(devices, share)], axis=1
    )
    gain_grads = jnp.pad(gain_grads, ((0, 0), (0, LN - 2 * share)))
    *grad_wqkv, gain_grads = tie(*grad_wqkv, gain_grads)
    grad_wqkv = total_square(grad_wqkv)
    gain_grads = jnp.sum(all_to_all(gain_grads, EVERY), axis=0, keepdims=True)

    stream = own.astype(jnp.float32)
    factor = lax.rsqrt(jnp.mean(stream * stream, axis=-1, keepdims=True) + EPS)
    back_in, _ = norm_back(stream, factor, gain_in, grad_a)
    grad_tokens = grad_mid + back_in
    grad_wqkv = grad_wqkv.reshape(-1, kv_local, 4 * HD)
    flat = lambda g: g.reshape(1, g.shape[0], -1)
    grad_gate, grad_up, grad_down = uncut_call(grad_ff)
    return (
        out.reshape(tokens.shape),
        grad_tokens.reshape(tokens.shape),
        gain_grads[:, :share],
        flat(grad_wqkv[:, :, : 2 * HD]),
        flat(grad_wqkv[:, :, 2 * HD : 3 * HD]),
        flat(grad_wqkv[:, :, 3 * HD :]),
        grad_wo.T[None],
        gain_grads[:, share : 2 * share],
        grad_gate[None],
        grad_up[None],
        grad_down[None],
    )


def fast_solution(mesh, cores):
    batch, seq, kv = mesh.devices.shape
    fine = Mesh(mesh.devices.reshape(batch, seq // cores, cores, kv), EVERY)
    sizes = dict(fine.shape)
    row_spec = P("y", ("x", "c", "z"), None)
    seq_spec = P("y", ("x", "c"))
    gain_spec = P(None, EVERY)
    in_w = P(None, ("y", "x", "c"), "z")
    out_w = P(None, "z", ("y", "x", "c"))
    in_specs = (row_spec, row_spec, seq_spec, seq_spec, gain_spec, in_w, in_w, in_w, out_w, gain_spec, in_w, in_w, out_w)
    out_specs = (row_spec, row_spec, gain_spec, in_w, in_w, in_w, out_w, gain_spec, in_w, in_w, out_w)
    return jax.shard_map(
        partial(fast_local, sizes), mesh=fine, in_specs=in_specs, out_specs=out_specs, check_vma=False
    )


def solution(mesh):
    batch, seq, kv = (mesh.shape[name] for name in ("batch", "seq", "kv"))
    general = general_solution(mesh)
    if (batch, seq) != (2, 4):
        return general
    fast = fast_solution(mesh, 2)

    def run(*args):
        rows, length, width = args[0].shape
        kv_heads, q_heads = args[6].shape[2] // HD, args[5].shape[2] // HD
        fits = (
            rows == 2 * batch
            and kv_heads == 2 * kv
            and q_heads == 2 * kv_heads
            and length == 128 * seq * kv
            and length % (4 * BQ) == 0
            and width % LN == 0
            and 2 * width // (batch * seq * kv) <= LN
            and args[10].shape[2] == LN * batch * seq * kv
        )
        return (fast if fits else general)(*args)

    return run
```
